32 devices in a mesh: batch: 4 (over y, x), ctx: 8 (over z, core).
Axes of the slice: x: 2, y: 2, z: 4, core: 2. Of those that a mesh axis runs over, the one named last changes fastest.
Arguments:
- block_in: bfloat16 [4, 1024, 1152], P('batch', 'ctx'), may hold values from -6 to 6
- positions: int32 [4, 1024], P('batch', 'ctx'), may hold values from 0 to 1023, as said below
- counts: int32 [4], P('batch'), may hold values from 768 to 1024, as said below
- cotangent: bfloat16 [4, 1024, 1152], P('batch', 'ctx'), may hold values from -6 to 6
- gain_input: bfloat16 [1152], P('ctx'), may hold values from 0.099609375 to 1.8984375
- w_query: bfloat16 [1152, 1024], P('ctx'), may hold values from -0.1875 to 0.1875
- w_key: bfloat16 [1152, 256], P('ctx'), may hold values from -0.1875 to 0.1875
- w_value: bfloat16 [1152, 256], P('ctx'), may hold values from -0.1875 to 0.1875
- gain_query: bfloat16 [256], P('ctx'), may hold values from 0.099609375 to 1.8984375
- gain_key: bfloat16 [256], P('ctx'), may hold values from 0.099609375 to 1.8984375
- w_output: bfloat16 [1024, 1152], P('ctx'), may hold values from -0.1875 to 0.1875
- gain_attn: bfloat16 [1152], P('ctx'), may hold values from 0.099609375 to 1.8984375
- gain_ffn: bfloat16 [1152], P('ctx'), may hold values from 0.099609375 to 1.8984375
- w_gate: bfloat16 [1152, 6912], P('ctx'), may hold values from -0.1875 to 0.1875
- w_up: bfloat16 [1152, 6912], P('ctx'), may hold values from -0.1875 to 0.1875
- w_down: bfloat16 [6912, 1152], P('ctx'), may hold values from -0.078125 to 0.078125
- gain_final: bfloat16 [1152], P('ctx'), may hold values from 0.099609375 to 1.8984375
Outputs:
- block_out: bfloat16 [4, 1024, 1152], P('batch', 'ctx')
- grad_in: bfloat16 [4, 1024, 1152], P('batch', 'ctx')
- grad_gain_input: float32 [1152], P('ctx')
- grad_w_query: float32 [1152, 1024], P('ctx')
- grad_w_key: float32 [1152, 256], P('ctx')
- grad_w_value: float32 [1152, 256], P('ctx')
- grad_gain_query: float32 [256], P('ctx')
- grad_gain_key: float32 [256], P('ctx')
- grad_w_output: float32 [1024, 1152], P('ctx')
- grad_gain_attn: float32 [1152], P('ctx')
- grad_gain_ffn: float32 [1152], P('ctx')
- grad_w_gate: float32 [1152, 6912], P('ctx')
- grad_w_up: float32 [1152, 6912], P('ctx')
- grad_w_down: float32 [6912, 1152], P('ctx')
- grad_gain_final: float32 [1152], P('ctx')
The draws below stay inside these ranges and needn't reach their ends.
Inputs may be any that keep to these rules, and one draw needn't show every extreme that they name: positions[r, i] is 0 where a document begins and one more than positions[r, i - 1] elsewhere; from token counts[r] on, the padding forms one more document beginning at 0; in every draw some row is a single document without padding. `counts`: in every draw some row has no padding and some row has exactly 256 padded tokens.
All inputs are finite; a program needn't handle non-finite values.
Results may differ from the reference program's by a relative error of at most 0.023.
Values may be sent and summed in bfloat16 or wider, within the bound.
A program may use at most 192 MiB of HBM per device.

```python
import jax
import jax.numpy as jnp
from jax import lax

D = 1152
NH = 4
HD = 256
FF = 6912
WINDOW = 512
DOC_MIN = 1024
QW = 1024
ROW_LEN = 1024
ROWS = 4


def layout_draw(key):
    base_key = jax.random.fold_in(key, 4111)
    key_cut, key_full, key_level, key_extra = jax.random.split(base_key, 4)
    least_len = min(DOC_MIN, ROW_LEN)
    row_index = jnp.arange(ROWS, dtype=jnp.int32)
    cut_back = jax.random.randint(key_cut, (ROWS,), 0, ROW_LEN // 4 + 1)
    full_row = jax.random.randint(key_full, (), 0, ROWS)
    short_row = (full_row + 1) % ROWS
    cut_back = jnp.where(row_index == full_row, 0, cut_back)
    cut_back = jnp.where(row_index == short_row, ROW_LEN // 4, cut_back)
    counts = (ROW_LEN - cut_back).astype(jnp.int32)
    doc_slots = ROW_LEN // least_len
    levels = doc_slots.bit_length() - 1
    level_draw = jax.random.randint(key_level, (ROWS, doc_slots), 0, levels + 1)
    extra_len = jax.random.randint(key_extra, (ROWS, doc_slots), 0, least_len)
    doc_lengths = least_len * jnp.left_shift(jnp.ones_like(level_draw), level_draw) + extra_len
    slot_index = jnp.arange(doc_slots, dtype=jnp.int32)
    whole_doc = (row_index[:, None] == full_row) & (slot_index[None, :] == 0)
    doc_lengths = jnp.where(whole_doc, ROW_LEN, doc_lengths)
    doc_ends = jnp.cumsum(doc_lengths, axis=1)
    doc_starts = doc_ends - doc_lengths
    token_index = jnp.arange(ROW_LEN, dtype=jnp.int32)
    has_begun = doc_starts[:, :, None] <= token_index[None, None, :]
    doc_start = jnp.max(jnp.where(has_begun, doc_starts[:, :, None], 0), axis=1)
    inside = token_index[None, :] < counts[:, None]
    doc_start = jnp.where(inside, doc_start, counts[:, None])
    positions = (token_index[None, :] - doc_start).astype(jnp.int32)
    return (counts, positions)


def draw_positions(key, part):
    return layout_draw(key)[1]


def draw_counts(key, part):
    return layout_draw(key)[0]


def raised(drawn, rng, source, target, parts, factor):
    def block_of(position):
        return (jnp.arange(drawn.shape[position]) // (drawn.shape[position] // parts)).reshape((-1,) + (1,) * (drawn.ndim - 1 - position))

    one_side = jax.random.permutation(rng, parts)[block_of(target)]
    second = (block_of(target) + parts // 2) % parts
    return jnp.where((block_of(source) == one_side) | (block_of(source) == second), factor * drawn, drawn)


def shard_levels(key, shape, pieces, smallest, top_value):
    def one(dim, shards_of):
        steps = jax.random.uniform(jax.random.fold_in(jax.random.fold_in(key, 6), dim), (shards_of,), jnp.float32, smallest / len(pieces), top_value / len(pieces))
        return jnp.repeat(jnp.exp(steps), shape[dim] // shards_of).reshape((-1,) + (1,) * (len(shape) - dim - 1))

    loudness = one(*pieces[0])
    for cut in pieces[1:]:
        loudness = loudness * one(*cut)
    return loudness


def bell_draw(key, extent, scale, limit, cuts=(), kind=jnp.bfloat16):
    values = scale * jax.random.normal(key, extent, jnp.float32)
    if cuts:
        values = values * shard_levels(key, extent, cuts, -0.22, 0.18)
    return jnp.clip(values, -limit, limit).astype(kind)


def bell_draw_with(stream_key, extent, deviation, most, shards, heavy, kind=jnp.bfloat16):
    entries = deviation * jax.random.normal(stream_key, extent, jnp.float32)
    if shards:
        entries = entries * shard_levels(stream_key, extent, shards, -0.22, 0.18)
    return jnp.clip(raised(entries, jax.random.fold_in(stream_key, 3), *heavy), -most, most).astype(kind)


def setup_inputs(seed: int = 0) -> dict:
    arg_keys = jax.random.split(jax.random.key(seed), 18)
    return {
        "block_in": bell_draw_with(arg_keys[0], (ROWS, ROW_LEN, D), 1.0, 6.0, ((0, 4), (1, 8)), (1, 2, 8, 2.0)),
        "positions": draw_positions(jax.random.fold_in(arg_keys[17], 71), 0),
        "counts": draw_counts(jax.random.fold_in(arg_keys[17], 71), 0),
        "cotangent": bell_draw(arg_keys[3], (ROWS, ROW_LEN, D), 1.0, 6.0, ((0, 4), (1, 8))),
        "gain_input": jnp.clip(1.0 + 0.18 * jax.random.normal(arg_keys[4], (D,), jnp.float32), 0.099609375, 1.8984375).astype(jnp.bfloat16),
        "w_query": bell_draw(arg_keys[5], (D, QW), D ** -0.5, 0.1875, ((0, 8),)),
        "w_key": bell_draw(arg_keys[6], (D, HD), D ** -0.5, 0.1875, ((0, 8),)),
        "w_value": bell_draw(arg_keys[7], (D, HD), D ** -0.5, 0.1875, ((0, 8),)),
        "gain_query": jnp.clip(1.0 + 0.18 * jax.random.normal(arg_keys[8], (HD,), jnp.float32), 0.099609375, 1.8984375).astype(jnp.bfloat16),
        "gain_key": jnp.clip(1.0 + 0.18 * jax.random.normal(arg_keys[9], (HD,), jnp.float32), 0.099609375, 1.8984375).astype(jnp.bfloat16),
        "w_output": bell_draw(arg_keys[10], (QW, D), QW ** -0.5, 0.1875, ((0, 8),)),
        "gain_attn": jnp.clip(1.0 + 0.18 * jax.random.normal(arg_keys[11], (D,), jnp.float32), 0.099609375, 1.8984375).astype(jnp.bfloat16),
        "gain_ffn": jnp.clip(1.0 + 0.18 * jax.random.normal(arg_keys[12], (D,), jnp.float32), 0.099609375, 1.8984375).astype(jnp.bfloat16),
        "w_gate": bell_draw(arg_keys[13], (D, FF), D ** -0.5, 0.1875, ((0, 8),)),
        "w_up": bell_draw(arg_keys[14], (D, FF), D ** -0.5, 0.1875, ((0, 8),)),
        "w_down": bell_draw(arg_keys[15], (FF, D), FF ** -0.5, 0.078125, ((0, 8),)),
        "gain_final": jnp.clip(1.0 + 0.18 * jax.random.normal(arg_keys[16], (D,), jnp.float32), 0.099609375, 1.8984375).astype(jnp.bfloat16),
    }


EPS = 1e-06
BASE = 10000.0
MASKED = -1e+30
HIGH = lax.Precision.HIGHEST

@jax.custom_vjp
def low(v):
    return lax.optimization_barrier(v.astype(jnp.bfloat16)).astype(jnp.float32)

@jax.custom_vjp
def low_back(v):
    return v

def low_keep(v):
    return (low(v), None)

def low_pass(kept, grad):
    return (grad,)

def back_keep(v):
    return (v, None)

def back_low(kept, grad):
    return (low(grad),)
low.defvjp(low_keep, low_pass)
low_back.defvjp(back_keep, back_low)

def normed(vector, gain_vec):
    return vector * lax.rsqrt(lax.optimization_barrier(jnp.mean(vector * vector, axis=-1, keepdims=True)) + EPS) * gain_vec

def rotate(vector, angles):
    half_size = vector.shape[-1] // 2
    cosine = jnp.cos(angles)
    sine_part = jnp.sin(angles)
    first_half = vector[..., :half_size]
    second = vector[..., half_size:]
    return jnp.concatenate([first_half * cosine - second * sine_part, second * cosine + first_half * sine_part], axis=-1)

def matmul_high(inputs, weight):
    return jnp.dot(inputs, weight, precision=HIGH, preferred_element_type=jnp.float32)

def row_forward(params, row_in, row_pos, row_count):
    gain_in_f, query_w, key_w, value_w, gain_q, gain_k, output_w, gain_at, gain_ff, gate_w, up_w, down_w, gain_fin = params
    length = row_in.shape[0]
    act_in = low(normed(row_in, gain_in_f))
    query_raw = low_back(matmul_high(act_in, query_w)).reshape(length, NH, HD)
    key_raw = low_back(matmul_high(act_in, key_w))
    value_all = low(low_back(matmul_high(act_in, value_w)))
    inv_freq = BASE ** (-jnp.arange(0, HD, 2, dtype=jnp.float32) / HD)
    angles = row_pos.astype(jnp.float32)[:, None] * inv_freq[None, :]
    query_all = low(rotate(normed(query_raw, gain_q), angles[:, None, :]))
    key_all = low(rotate(normed(key_raw, gain_k), angles))
    block_len = min(512, length)
    key_pad = jnp.concatenate([jnp.zeros((WINDOW, HD), key_all.dtype), key_all], axis=0)
    value_pad = jnp.concatenate([jnp.zeros((WINDOW, HD), value_all.dtype), value_all], axis=0)
    local_query = jnp.arange(block_len, dtype=jnp.int32)
    local_key = jnp.arange(block_len + WINDOW, dtype=jnp.int32)
    distance = local_query[:, None] + WINDOW - local_key[None, :]

    def one_block(block_start):
        query_blk = lax.dynamic_slice_in_dim(query_all, block_start, block_len, 0)
        key_blk = lax.dynamic_slice_in_dim(key_pad, block_start, block_len + WINDOW, 0)
        value_blk = lax.dynamic_slice_in_dim(value_pad, block_start, block_len + WINDOW, 0)
        pos_blk = lax.dynamic_slice_in_dim(row_pos, block_start, block_len, 0)
        scores = low_back(jnp.einsum('bhd,kd->hbk', query_blk, key_blk, precision=HIGH) * HD ** (-0.5))
        allowed = (distance >= 0) & (distance < WINDOW) & (distance <= pos_blk[:, None])
        scores = jnp.where(allowed[None], scores, MASKED)
        attn_prob = low(jax.nn.softmax(scores, axis=-1))
        return jnp.einsum('hbk,kd->bhd', attn_prob, value_blk, precision=HIGH)
    starts = jnp.arange(length // block_len, dtype=jnp.int32) * block_len
    attended = lax.map(jax.checkpoint(one_block), starts).reshape(length, NH * HD)
    attended = low(low_back(attended))
    attn_proj = low_back(matmul_high(attended, output_w))
    middle = row_in + normed(attn_proj, gain_at)
    ffn_in = low(normed(middle, gain_ff))
    gate_val = low_back(matmul_high(ffn_in, gate_w))
    up_val = low_back(matmul_high(ffn_in, up_w))
    mixed_low = low(jax.nn.gelu(gate_val, approximate=True) * up_val)
    ffn_proj = low_back(matmul_high(mixed_low, down_w))
    final_sum = middle + normed(ffn_proj, gain_fin)
    valid_mask = (jnp.arange(length, dtype=jnp.int32) < row_count).astype(final_sum.dtype)
    return final_sum * valid_mask[:, None]

def reference(block_in, positions, counts, cotangent, gain_input, w_query, w_key, w_value, gain_query, gain_key, w_output, gain_attn, gain_ffn, w_gate, w_up, w_down, gain_final):
    weights = tuple((weight_arg.astype(jnp.float32) for weight_arg in (gain_input, w_query, w_key, w_value, gain_query, gain_key, w_output, gain_attn, gain_ffn, w_gate, w_up, w_down, gain_final)))
    inputs = block_in.astype(jnp.float32)
    upstream = cotangent.astype(jnp.float32)

    def forward(all_in, params):

        def row_step(row_carry, row_data):
            row_in, row_pos, row_count = row_data
            return (row_carry, jax.checkpoint(row_forward)(params, row_in, row_pos, row_count))
        _, outputs = lax.scan(row_step, jnp.zeros((), jnp.float32), (all_in, positions, counts))
        return outputs
    outputs, pull_back = jax.vjp(forward, inputs, weights)
    grad_inputs, grad_weights = pull_back(upstream)
    grad_gain_input, grad_w_query, grad_w_key, grad_w_value, grad_gain_query, grad_gain_key, grad_w_output, grad_gain_attn, grad_gain_ffn, grad_w_gate, grad_w_up, grad_w_down, grad_gain_final = grad_weights
    return (outputs.astype(jnp.bfloat16), grad_inputs.astype(jnp.bfloat16), grad_gain_input, grad_w_query, grad_w_key, grad_w_value, grad_gain_query, grad_gain_key, grad_w_output, grad_gain_attn, grad_gain_ffn, grad_w_gate, grad_w_up, grad_w_down, grad_gain_final)
```

```python
import functools

import jax
import jax.numpy as jnp
from jax import lax
from jax.experimental import pallas as pl
from jax.experimental.pallas import tpu as pltpu
from jax.sharding import PartitionSpec as P

WINDOW = 512


EPS = 1e-06
BASE = 10000.0
MASKED = -1e30
BF16 = jnp.bfloat16
F32 = jnp.float32
MESH = pl.DeviceIdType.MESH


def normed(vector, gain_vec):
    return vector * lax.rsqrt(jnp.mean(vector * vector, axis=-1, keepdims=True) + EPS) * gain_vec


def rotate(vector, angles):
    half_size = vector.shape[-1] // 2
    cosine = jnp.cos(angles)
    sine_part = jnp.sin(angles)
    first_half = vector[..., :half_size]
    second = vector[..., half_size:]
    return jnp.concatenate(
        [first_half * cosine - second * sine_part, second * cosine + first_half * sine_part],
        axis=-1,
    )


def project(inputs, weight):
    return lax.dot_general(inputs, weight, (((1,), (0,)), ((), ())), preferred_element_type=F32)


def project_back(upstream, weight):
    return lax.dot_general(upstream, weight, (((1,), (1,)), ((), ())), preferred_element_type=F32)


def weight_grad(inputs, upstream):
    return lax.dot_general(inputs, upstream, (((0,), (0,)), ((), ())), preferred_element_type=F32)


def gated_gelu(gate_val, up_val):
    return jax.nn.gelu(gate_val, approximate=True) * up_val


def batch_kernel(size, kinds, *refs):
    count = len(kinds)
    sources, results = refs[:count], refs[count : 2 * count]
    send_sem, recv_sem, own_sem = refs[2 * count :]
    me = lax.axis_index("batch")
    barrier = pltpu.get_barrier_semaphore()
    for step in range(1, size):
        pl.semaphore_signal(
            barrier, inc=1, device_id={"batch": lax.rem(me + step, size)}, device_id_type=MESH
        )
    pl.semaphore_wait(barrier, size - 1)
    copies = []
    for step in range(1, size):
        peer = lax.rem(me + step, size)
        for item in range(count):
            source = sources[item].at[peer] if kinds[item] else sources[item]
            copies.append(
                pltpu.make_async_remote_copy(
                    src_ref=source,
                    dst_ref=results[item].at[me],
                    send_sem=send_sem.at[item, step - 1],
                    recv_sem=recv_sem.at[item, step - 1],
                    device_id={"batch": peer},
                    device_id_type=MESH,
                )
            )
    for copy in copies:
        copy.start()
    own = []
    for item in range(count):
        source = sources[item].at[me] if kinds[item] else sources[item]
        own.append(pltpu.make_async_copy(source, results[item].at[me], own_sem.at[item]))
    for copy in own:
        copy.start()
    for copy in own:
        copy.wait()
    for copy in copies:
        copy.wait()


def batch_exchange(name, collective_id, size, whole=(), slots=()):
    arrays = list(whole) + list(slots)
    kinds = [0] * len(whole) + [1] * len(slots)
    count = len(arrays)
    shapes = [
        jax.ShapeDtypeStruct(a.shape if k else (size, *a.shape), a.dtype)
        for a, k in zip(arrays, kinds)
    ]
    return pl.pallas_call(
        functools.partial(batch_kernel, size, kinds),
        name=name,
        out_shape=shapes,
        in_specs=[pl.BlockSpec(memory_space=pltpu.VMEM)] * count,
        out_specs=[pl.BlockSpec(memory_space=pltpu.VMEM)] * count,
        scratch_shapes=[
            pltpu.SemaphoreType.DMA((count, size - 1)),
            pltpu.SemaphoreType.DMA((count, size - 1)),
            pltpu.SemaphoreType.DMA((count,)),
        ],
        compiler_params=pltpu.CompilerParams(collective_id=collective_id, has_side_effects=True),
    )(*arrays)


def halo_kernel(size, depth, direction, source_ref, result_ref, send_sem, recv_sem):
    me = lax.axis_index("ctx")
    barrier = pltpu.get_barrier_semaphore()
    for step in range(1, depth + 1):
        giver = me - direction * step

        @pl.when((giver >= 0) & (giver < size))
        def _():
            pl.semaphore_signal(barrier, inc=1, device_id={"ctx": giver}, device_id_type=MESH)

    takers = jnp.minimum(depth, size - 1 - me) if direction > 0 else jnp.minimum(depth, me)

    @pl.when(takers > 0)
    def _():
        pl.semaphore_wait(barrier, takers)

    def copy(step):
        slot = depth - step
        source = source_ref if direction > 0 else source_ref.at[slot]
        return pltpu.make_async_remote_copy(
            src_ref=source,
            dst_ref=result_ref.at[slot],
            send_sem=send_sem.at[step - 1],
            recv_sem=recv_sem.at[step - 1],
            device_id={"ctx": jnp.clip(me + direction * step, 0, size - 1)},
            device_id_type=MESH,
        )

    for step in range(depth, 0, -1):
        taker = me + direction * step

        @pl.when((taker >= 0) & (taker < size))
        def _():
            copy(step).start()

    for step in range(1, depth + 1):
        taker = me + direction * step
        giver = me - direction * step

        @pl.when((giver < 0) | (giver >= size))
        def _():
            result_ref[depth - step] = jnp.zeros(result_ref.shape[1:], result_ref.dtype)

        @pl.when((giver >= 0) & (giver < size))
        def _():
            copy(step).wait_recv()

        @pl.when((taker >= 0) & (taker < size))
        def _():
            copy(step).wait_send()


def halo_exchange(name, collective_id, size, depth, direction, block):
    return pl.pallas_call(
        functools.partial(halo_kernel, size, depth, direction),
        name=name,
        out_shape=jax.ShapeDtypeStruct((depth, *block.shape[-2:]), block.dtype),
        in_specs=[pl.BlockSpec(memory_space=pltpu.VMEM)],
        out_specs=pl.BlockSpec(memory_space=pltpu.VMEM),
        scratch_shapes=[pltpu.SemaphoreType.DMA((depth,)), pltpu.SemaphoreType.DMA((depth,))],
        compiler_params=pltpu.CompilerParams(collective_id=collective_id, has_side_effects=True),
    )(block)


def gathered(shard):
    return lax.all_gather(shard, "ctx", axis=0, tiled=True)


def scattered(whole):
    return lax.psum_scatter(whole.astype(BF16), "ctx", scatter_dimension=0, tiled=True)


def local(
    n_batch,
    n_ctx,
    block_in,
    positions,
    counts,
    cotangent,
    gain_input,
    w_query,
    w_key,
    w_value,
    gain_query,
    gain_key,
    w_output,
    gain_attn,
    gain_ffn,
    w_gate,
    w_up,
    w_down,
    gain_final,
):
    block_in = block_in[0]
    positions = positions[0]
    cotangent = cotangent[0]
    tok_count, model_width = block_in.shape
    width_shard = w_query.shape[0]
    query_width = w_query.shape[1]
    head_size = w_key.shape[1]
    head_count = query_width // head_size
    hidden = w_gate.shape[1]
    hidden_shard = w_down.shape[0]
    piece = hidden_shard // n_batch
    hidden_part = piece * n_ctx
    halo_depth = (WINDOW + tok_count - 2) // tok_count
    batch_at = lax.axis_index("batch")
    ctx_at = lax.axis_index("ctx")
    all_tok = n_batch * tok_count

    gains = jnp.concatenate(
        [gain_input, gain_attn, gain_ffn, gain_final, gain_query, gain_key]
    )
    gains_all = lax.all_gather(gains, "ctx", axis=0).astype(F32)

    def gain_at(start, length):
        return gains_all[:, start : start + length].reshape(1, -1)

    head_shard = gain_query.shape[0]
    full_gain_in = gain_at(0, width_shard)
    full_gain_attn = gain_at(width_shard, width_shard)
    full_gain_ffn = gain_at(2 * width_shard, width_shard)
    full_gain_final = gain_at(3 * width_shard, width_shard)
    full_gain_q = gain_at(4 * width_shard, head_shard)
    full_gain_k = gain_at(4 * width_shard + head_shard, head_shard)

    def own_columns(weight):
        parts = weight.reshape(width_shard, n_ctx, n_batch, piece)
        mine = lax.dynamic_index_in_dim(parts, batch_at, axis=2, keepdims=False)
        return mine.reshape(width_shard, hidden_part)

    wide_qkv = gathered(jnp.concatenate([w_query, w_key, w_value], axis=1))
    full_output = gathered(w_output)
    part_gate = gathered(own_columns(w_gate))
    part_up = gathered(own_columns(w_up))
    part_down = gathered(lax.dynamic_slice_in_dim(w_down, batch_at * piece, piece, 0))

    first_token = ctx_at * tok_count
    token_place = first_token + jnp.arange(tok_count, dtype=jnp.int32)
    valid_mask = (token_place < counts[0]).astype(F32)[:, None]
    resid_in = block_in.astype(F32)
    act_in = normed(resid_in, full_gain_in).astype(BF16)
    qkv_raw = project(act_in, wide_qkv)
    query_raw = qkv_raw[:, :query_width].reshape(tok_count, head_count, head_size)
    key_raw = qkv_raw[:, query_width : query_width + head_size]
    value_low = qkv_raw[:, query_width + head_size :].astype(BF16)
    inv_freq = BASE ** (-jnp.arange(0, head_size, 2, dtype=F32) / head_size)
    angles = positions.astype(F32)[:, None] * inv_freq

    def query_path(raw_query, gain_vec):
        return rotate(normed(raw_query, gain_vec), angles[:, None, :])

    def key_path(raw_key, gain_vec):
        return rotate(normed(raw_key, gain_vec), angles)

    query_rot = query_path(query_raw, full_gain_q).astype(BF16)
    key_rot = key_path(key_raw, full_gain_k).astype(BF16)
    own_pair = jnp.concatenate([key_rot, value_low], axis=-1)
    halo = halo_exchange("halo_out", 1, n_ctx, halo_depth, 1, own_pair)
    context = jnp.concatenate([halo.reshape(halo_depth * tok_count, -1), own_pair], axis=0)
    ctx_keys = context[:, :head_size]
    ctx_values = context[:, head_size:]
    key_total = (halo_depth + 1) * tok_count
    distance = (
        jnp.arange(tok_count, dtype=jnp.int32)[:, None]
        + halo_depth * tok_count
        - jnp.arange(key_total, dtype=jnp.int32)[None, :]
    )
    allowed = (distance >= 0) & (distance < WINDOW) & (distance <= positions[:, None])
    score_scale = head_size ** (-0.5)
    raw_scores = jnp.einsum("thd,kd->htk", query_rot, ctx_keys, preferred_element_type=F32)
    scores = jnp.where(allowed[None], raw_scores * score_scale, MASKED)
    exp_scores = jnp.exp(scores - jnp.max(scores, axis=-1, keepdims=True))
    attn_prob = exp_scores / jnp.sum(exp_scores, axis=-1, keepdims=True)
    prob_low = attn_prob.astype(BF16)
    attended = jnp.einsum("htk,kd->thd", prob_low, ctx_values, preferred_element_type=F32)
    attn_low = attended.reshape(tok_count, query_width).astype(BF16)
    attn_proj = project(attn_low, full_output)
    middle = resid_in + normed(attn_proj, full_gain_attn)
    ffn_in = normed(middle, full_gain_ffn).astype(BF16)

    ffn_in_all, act_in_all, attn_all = batch_exchange(
        "gather_in", 2, n_batch, whole=(ffn_in, act_in, attn_low)
    )
    ffn_in_all = ffn_in_all.reshape(all_tok, model_width)
    act_in_all = act_in_all.reshape(all_tok, model_width)
    attn_all = attn_all.reshape(all_tok, query_width)
    gate_pre = project(ffn_in_all, part_gate)
    up_pre = project(ffn_in_all, part_up)
    mixed_low = gated_gelu(gate_pre, up_pre).astype(BF16)
    proj_part = project(mixed_low, part_down).astype(BF16)
    (proj_parts,) = batch_exchange(
        "sum_out", 3, n_batch, slots=(proj_part.reshape(n_batch, tok_count, model_width),)
    )
    ffn_proj = jnp.sum(proj_parts.astype(F32), axis=0)
    final_sum = middle + normed(ffn_proj, full_gain_final)
    block_out = (final_sum * valid_mask).astype(BF16)

    grad_final = cotangent.astype(F32) * valid_mask
    _, pull_final = jax.vjp(normed, ffn_proj, full_gain_final)
    grad_ffn_proj, grad_gain_final = pull_final(grad_final)
    (grad_ffn_low,) = batch_exchange("gather_grad", 4, n_batch, whole=(grad_ffn_proj.astype(BF16),))
    grad_ffn_low = grad_ffn_low.reshape(all_tok, model_width)
    grad_w_down = scattered(weight_grad(mixed_low, grad_ffn_low))
    grad_mixed = project_back(grad_ffn_low, part_down)
    _, pull_gelu = jax.vjp(gated_gelu, gate_pre, up_pre)
    grad_gate, grad_up = pull_gelu(grad_mixed)
    grad_gate_low = grad_gate.astype(BF16)
    grad_up_low = grad_up.astype(BF16)
    grad_w_gate = scattered(weight_grad(ffn_in_all, grad_gate_low))
    grad_w_up = scattered(weight_grad(ffn_in_all, grad_up_low))
    back_part = project_back(grad_gate_low, part_gate) + project_back(grad_up_low, part_up)
    (back_parts,) = batch_exchange(
        "sum_back", 5, n_batch, slots=(back_part.astype(BF16).reshape(n_batch, tok_count, model_width),)
    )
    grad_ffn_in = jnp.sum(back_parts.astype(F32), axis=0)
    _, pull_ffn_norm = jax.vjp(normed, middle, full_gain_ffn)
    grad_middle_part, grad_gain_ffn = pull_ffn_norm(grad_ffn_in)
    grad_middle = grad_final + grad_middle_part
    _, pull_attn_norm = jax.vjp(normed, attn_proj, full_gain_attn)
    grad_attn_proj, grad_gain_attn = pull_attn_norm(grad_middle)

    grad_proj_low = grad_attn_proj.astype(BF16)
    grad_attended = (
        project_back(grad_proj_low, full_output)
        .astype(BF16)
        .reshape(tok_count, head_count, head_size)
    )
    grad_prob = jnp.einsum("thd,kd->htk", grad_attended, ctx_values, preferred_element_type=F32)
    row_delta = jnp.sum(attn_prob * grad_prob, axis=-1, keepdims=True)
    grad_scores = (attn_prob * (grad_prob - row_delta)).astype(BF16)
    grad_queries = (
        jnp.einsum("htk,kd->thd", grad_scores, ctx_keys, preferred_element_type=F32) * score_scale
    )
    grad_ctx_keys = (
        jnp.einsum("htk,thd->kd", grad_scores, query_rot, preferred_element_type=F32) * score_scale
    )
    grad_ctx_values = jnp.einsum("htk,thd->kd", prob_low, grad_attended, preferred_element_type=F32)
    grad_context = jnp.concatenate([grad_ctx_keys, grad_ctx_values], axis=-1)
    halo_rows = halo_depth * tok_count
    returned = halo_exchange(
        "halo_back",
        6,
        n_ctx,
        halo_depth,
        -1,
        grad_context[:halo_rows].astype(BF16).reshape(halo_depth, tok_count, 2 * head_size),
    )
    own_grad = grad_context[halo_rows:] + jnp.sum(returned.astype(F32), axis=0)
    grad_value_low = own_grad[:, head_size:].astype(BF16)
    _, pull_key = jax.vjp(key_path, key_raw, full_gain_k)
    grad_key_raw, grad_gain_key = pull_key(own_grad[:, :head_size])
    _, pull_query = jax.vjp(query_path, query_raw, full_gain_q)
    grad_query_raw, grad_gain_query = pull_query(grad_queries)
    grad_qkv_low = jnp.concatenate(
        [
            grad_query_raw.astype(BF16).reshape(tok_count, query_width),
            grad_key_raw.astype(BF16),
            grad_value_low,
        ],
        axis=1,
    )
    grad_act_in = project_back(grad_qkv_low, wide_qkv)
    _, pull_input = jax.vjp(normed, resid_in, full_gain_in)
    grad_in_part, grad_gain_input = pull_input(grad_act_in)
    grad_in = (grad_middle + grad_in_part).astype(BF16)

    def column_slots(upstream):
        return upstream.reshape(tok_count, n_batch, -1).transpose(1, 0, 2)

    qkv_slots, proj_slots = batch_exchange(
        "spread_grads",
        7,
        n_batch,
        slots=(column_slots(grad_qkv_low), column_slots(grad_proj_low)),
    )
    grad_w_output = scattered(weight_grad(attn_all, proj_slots.reshape(all_tok, -1)))
    grad_w_qkv = scattered(weight_grad(act_in_all, qkv_slots.reshape(all_tok, -1)))
    gain_rows = jnp.concatenate(
        [
            grad.reshape(n_ctx, -1)
            for grad in (
                grad_gain_input,
                grad_gain_attn,
                grad_gain_ffn,
                grad_gain_final,
                grad_gain_query,
                grad_gain_key,
            )
        ],
        axis=1,
    )
    gain_sums = lax.psum(gain_rows, ("batch", "ctx"))
    gain_mine = lax.dynamic_index_in_dim(gain_sums, ctx_at, axis=0, keepdims=False)

    (down_all,) = batch_exchange("spread_down", 8, n_batch, whole=(grad_w_down,))
    (gate_all,) = batch_exchange("spread_gate", 9, n_batch, whole=(grad_w_gate,))
    (up_all,) = batch_exchange("spread_up", 10, n_batch, whole=(grad_w_up,))
    qkv_all, output_all = batch_exchange(
        "spread_attn", 11, n_batch, whole=(grad_w_qkv, grad_w_output)
    )

    def columns_back(pieces):
        return pieces.astype(F32).transpose(1, 0, 2).reshape(pieces.shape[1], -1)

    def hidden_back(pieces):
        parts = pieces.reshape(n_batch, width_shard, n_ctx, piece)
        return parts.transpose(1, 2, 0, 3).reshape(width_shard, hidden).astype(F32)

    grad_qkv_shard = columns_back(qkv_all)
    return (
        block_out[None],
        grad_in[None],
        gain_mine[:width_shard],
        grad_qkv_shard[:, :query_width],
        grad_qkv_shard[:, query_width : query_width + head_size],
        grad_qkv_shard[:, query_width + head_size :],
        gain_mine[4 * width_shard : 4 * width_shard + head_shard],
        gain_mine[4 * width_shard + head_shard :],
        columns_back(output_all),
        gain_mine[width_shard : 2 * width_shard],
        gain_mine[2 * width_shard : 3 * width_shard],
        hidden_back(gate_all),
        hidden_back(up_all),
        down_all.reshape(hidden_shard, model_width).astype(F32),
        gain_mine[3 * width_shard : 4 * width_shard],
    )


def solution(mesh):
    matrix = P("ctx", None)
    vector = P("ctx")
    tokens = P("batch", "ctx", None)
    return jax.shard_map(
        functools.partial(local, mesh.shape["batch"], mesh.shape["ctx"]),
        mesh=mesh,
        in_specs=(
            tokens,
            P("batch", "ctx"),
            P("batch"),
            tokens,
            vector,
            matrix,
            matrix,
            matrix,
            vector,
            vector,
            matrix,
            vector,
            vector,
            matrix,
            matrix,
            matrix,
            vector,
        ),
        out_specs=(
            tokens,
            tokens,
            vector,
            matrix,
            matrix,
            matrix,
            vector,
            vector,
            matrix,
            vector,
            vector,
            matrix,
            matrix,
            matrix,
            vector,
        ),
        check_vma=False,
    )
```

```python
import functools

import jax
import jax.numpy as jnp
from jax import lax
from jax.experimental import pallas as pl
from jax.experimental.pallas import tpu as pltpu
from jax.sharding import PartitionSpec as P

WINDOW = 512


EPS = 1e-06
BASE = 10000.0
MASKED = -1e30
BF16 = jnp.bfloat16
F32 = jnp.float32
MESH = pl.DeviceIdType.MESH


def normed(vector, gain_vec):
    return vector * lax.rsqrt(jnp.mean(vector * vector, axis=-1, keepdims=True) + EPS) * gain_vec


def rotate(vector, angles):
    half_size = vector.shape[-1] // 2
    cosine = jnp.cos(angles)
    sine_part = jnp.sin(angles)
    first_half = vector[..., :half_size]
    second = vector[..., half_size:]
    return jnp.concatenate(
        [first_half * cosine - second * sine_part, second * cosine + first_half * sine_part],
        axis=-1,
    )


def project(inputs, weight):
    return lax.dot_general(inputs, weight, (((1,), (0,)), ((), ())), preferred_element_type=F32)


def project_back(upstream, weight):
    return lax.dot_general(upstream, weight, (((1,), (1,)), ((), ())), preferred_element_type=F32)


def weight_grad(inputs, upstream):
    return lax.dot_general(inputs, upstream, (((0,), (0,)), ((), ())), preferred_element_type=F32)


def gated_gelu(gate_val, up_val):
    return jax.nn.gelu(gate_val, approximate=True) * up_val


def batch_kernel(size, kinds, *refs):
    count = len(kinds)
    sources, results = refs[:count], refs[count : 2 * count]
    send_sem, recv_sem, own_sem = refs[2 * count :]
    me = lax.axis_index("batch")
    barrier = pltpu.get_barrier_semaphore()
    for step in range(1, size):
        pl.semaphore_signal(
            barrier, inc=1, device_id={"batch": lax.rem(me + step, size)}, device_id_type=MESH
        )
    pl.semaphore_wait(barrier, size - 1)
    copies = []
    for step in range(1, size):
        peer = lax.rem(me + step, size)
        for item in range(count):
            source = sources[item].at[peer] if kinds[item] else sources[item]
            copies.append(
                pltpu.make_async_remote_copy(
                    src_ref=source,
                    dst_ref=results[item].at[me],
                    send_sem=send_sem.at[item, step - 1],
                    recv_sem=recv_sem.at[item, step - 1],
                    device_id={"batch": peer},
                    device_id_type=MESH,
                )
            )
    for copy in copies:
        copy.start()
    own = []
    for item in range(count):
        source = sources[item].at[me] if kinds[item] else sources[item]
        own.append(pltpu.make_async_copy(source, results[item].at[me], own_sem.at[item]))
    for copy in own:
        copy.start()
    for copy in own:
        copy.wait()
    for copy in copies:
        copy.wait()


def batch_exchange(name, collective_id, size, whole=(), slots=()):
    arrays = list(whole) + list(slots)
    kinds = [0] * len(whole) + [1] * len(slots)
    count = len(arrays)
    shapes = [
        jax.ShapeDtypeStruct(a.shape if k else (size, *a.shape), a.dtype)
        for a, k in zip(arrays, kinds)
    ]
    return pl.pallas_call(
        functools.partial(batch_kernel, size, kinds),
        name=name,
        out_shape=shapes,
        in_specs=[pl.BlockSpec(memory_space=pltpu.VMEM)] * count,
        out_specs=[pl.BlockSpec(memory_space=pltpu.VMEM)] * count,
        scratch_shapes=[
            pltpu.SemaphoreType.DMA((count, size - 1)),
            pltpu.SemaphoreType.DMA((count, size - 1)),
            pltpu.SemaphoreType.DMA((count,)),
        ],
        compiler_params=pltpu.CompilerParams(collective_id=collective_id, has_side_effects=True),
    )(*arrays)


def halo_kernel(size, depth, direction, source_ref, result_ref, send_sem, recv_sem):
    me = lax.axis_index("ctx")
    barrier = pltpu.get_barrier_semaphore()
    for step in range(1, depth + 1):
        giver = me - direction * step

        @pl.when((giver >= 0) & (giver < size))
        def _():
            pl.semaphore_signal(barrier, inc=1, device_id={"ctx": giver}, device_id_type=MESH)

    takers = jnp.minimum(depth, size - 1 - me) if direction > 0 else jnp.minimum(depth, me)

    @pl.when(takers > 0)
    def _():
        pl.semaphore_wait(barrier, takers)

    def copy(step):
        slot = depth - step
        source = source_ref if direction > 0 else source_ref.at[slot]
        return pltpu.make_async_remote_copy(
            src_ref=source,
            dst_ref=result_ref.at[slot],
            send_sem=send_sem.at[step - 1],
            recv_sem=recv_sem.at[step - 1],
            device_id={"ctx": jnp.clip(me + direction * step, 0, size - 1)},
            device_id_type=MESH,
        )

    for step in range(depth, 0, -1):
        taker = me + direction * step

        @pl.when((taker >= 0) & (taker < size))
        def _():
            copy(step).start()

    for step in range(1, depth + 1):
        taker = me + direction * step
        giver = me - direction * step

        @pl.when((giver < 0) | (giver >= size))
        def _():
            result_ref[depth - step] = jnp.zeros(result_ref.shape[1:], result_ref.dtype)

        @pl.when((giver >= 0) & (giver < size))
        def _():
            copy(step).wait_recv()

        @pl.when((taker >= 0) & (taker < size))
        def _():
            copy(step).wait_send()


def halo_exchange(name, collective_id, size, depth, direction, block):
    return pl.pallas_call(
        functools.partial(halo_kernel, size, depth, direction),
        name=name,
        out_shape=jax.ShapeDtypeStruct((depth, *block.shape[-2:]), block.dtype),
        in_specs=[pl.BlockSpec(memory_space=pltpu.VMEM)],
        out_specs=pl.BlockSpec(memory_space=pltpu.VMEM),
        scratch_shapes=[pltpu.SemaphoreType.DMA((depth,)), pltpu.SemaphoreType.DMA((depth,))],
        compiler_params=pltpu.CompilerParams(collective_id=collective_id, has_side_effects=True),
    )(block)


def pick_kernel(n_batch, n_ctx, piece, gate_ref, up_ref, gate_out, up_out):
    me = lax.axis_index("batch")
    for spot in range(n_batch):

        @pl.when(me == spot)
        def _():
            for shard in range(n_ctx):
                start = (shard * n_batch + spot) * piece
                place = pl.ds(shard * piece, piece)
                gate_out[:, place] = gate_ref[:, start : start + piece]
                up_out[:, place] = up_ref[:, start : start + piece]


def pick_columns(n_batch, n_ctx, piece, w_gate, w_up):
    rows = w_gate.shape[0]
    block = 48 if rows % 48 == 0 else rows
    spec = pl.BlockSpec((block, w_gate.shape[1]), lambda i: (i, 0))
    out_spec = pl.BlockSpec((block, n_ctx * piece), lambda i: (i, 0))
    out = jax.ShapeDtypeStruct((rows, n_ctx * piece), w_gate.dtype)
    return pl.pallas_call(
        functools.partial(pick_kernel, n_batch, n_ctx, piece),
        name="pick_columns",
        grid=(rows // block,),
        out_shape=(out, out),
        in_specs=[spec, spec],
        out_specs=[out_spec, out_spec],
    )(w_gate, w_up)


def place_kernel(n_batch, n_ctx, piece, parts_ref, out_ref):
    for shard in range(n_ctx):
        for spot in range(n_batch):
            start = (shard * n_batch + spot) * piece
            out_ref[:, start : start + piece] = parts_ref[
                spot, :, shard * piece : (shard + 1) * piece
            ].astype(F32)


def place_columns(name, n_batch, n_ctx, piece, parts):
    rows = parts.shape[1]
    block = 48 if rows % 48 == 0 else rows
    hidden = n_batch * n_ctx * piece
    return pl.pallas_call(
        functools.partial(place_kernel, n_batch, n_ctx, piece),
        name=name,
        grid=(rows // block,),
        out_shape=jax.ShapeDtypeStruct((rows, hidden), F32),
        in_specs=[pl.BlockSpec((n_batch, block, n_ctx * piece), lambda i: (0, i, 0))],
        out_specs=pl.BlockSpec((block, hidden), lambda i: (i, 0)),
    )(parts)


def weights_kernel(n_batch, n_ctx, qkv_ref, proj_ref, gain_ref, qkv_all, proj_all, gain_all, *sems):
    send_far, recv_far, send_side, recv_side, send_near, recv_near, own_sem = sems
    spot = lax.axis_index("batch")
    me = lax.axis_index("ctx")
    n_chip = n_ctx // 2
    chip, core = me // 2, lax.rem(me, 2)
    near = {"ctx": me + 1 - 2 * core}
    barrier = pltpu.get_barrier_semaphore()

    def far_at(step):
        return {"ctx": 2 * lax.rem(chip + step, n_chip) + core}

    def side_at(step):
        return {"batch": lax.rem(spot + step, n_batch)}

    peers = [near]
    peers += [far_at(step) for step in range(1, n_chip)]
    peers += [side_at(step) for step in range(1, n_batch)]
    for peer in peers:
        pl.semaphore_signal(barrier, inc=1, device_id=peer, device_id_type=MESH)
    pl.semaphore_wait(barrier, len(peers))

    def remote(source, target, send, recv, peer):
        return pltpu.make_async_remote_copy(
            src_ref=source,
            dst_ref=target,
            send_sem=send,
            recv_sem=recv,
            device_id=peer,
            device_id_type=MESH,
        )

    waits = []
    far = []
    for step in range(1, n_chip):
        triple = [
            remote(source, target, send_far.at[step - 1, item], recv_far.at[step - 1, item], far_at(step))
            for item, (source, target) in enumerate(
                (
                    (qkv_ref.at[spot], qkv_all.at[spot, me]),
                    (proj_ref.at[spot], proj_all.at[me, spot]),
                    (gain_ref, gain_all.at[me]),
                )
            )
        ]
        for copy in triple:
            copy.start()
        far.append(triple)
    own = [
        pltpu.make_async_copy(qkv_ref, qkv_all.at[:, me], own_sem.at[0]),
        pltpu.make_async_copy(proj_ref, proj_all.at[me], own_sem.at[1]),
        pltpu.make_async_copy(gain_ref, gain_all.at[me], own_sem.at[2]),
    ]
    for copy in own:
        copy.start()
    first = n_chip - 1
    pairs = [
        remote(source, target, send_near.at[first, 0, item], recv_near.at[first, 0, item], near)
        for item, (source, target) in enumerate(
            (
                (qkv_ref, qkv_all.at[:, me]),
                (proj_ref, proj_all.at[me]),
                (gain_ref, gain_all.at[me]),
            )
        )
    ]
    for copy in pairs:
        copy.start()
    waits += pairs

    def hand_near(step, turn):
        origin = 2 * lax.rem(chip + n_chip - step, n_chip) + core
        quarter = lax.rem(spot + n_batch - turn, n_batch)
        blocks = [qkv_all.at[quarter, origin], proj_all.at[origin, quarter]]
        blocks += [gain_all.at[origin]] if turn == 0 else []
        for item, block in enumerate(blocks):
            copy = remote(
                block,
                block,
                send_near.at[step - 1, turn, item],
                recv_near.at[step - 1, turn, item],
                near,
            )
            copy.start()
            waits.append(copy)

    side = []
    for step in range(1, n_chip):
        for copy in far[step - 1]:
            copy.wait_recv()
        origin = 2 * lax.rem(chip + n_chip - step, n_chip) + core
        for turn in range(1, n_batch):
            pair = [
                remote(
                    block,
                    block,
                    send_side.at[step - 1, turn - 1, item],
                    recv_side.at[step - 1, turn - 1, item],
                    side_at(turn),
                )
                for item, block in enumerate((qkv_all.at[spot, origin], proj_all.at[origin, spot]))
            ]
            for copy in pair:
                copy.start()
            side.append((step, turn, pair))
        hand_near(step, 0)
    for step, turn, pair in side:
        for copy in pair:
            copy.wait_recv()
        hand_near(step, turn)
    for copy in waits:
        copy.wait()
    for copy in own:
        copy.wait()
    for triple in far:
        for copy in triple:
            copy.wait_send()
    for _, _, pair in side:
        for copy in pair:
            copy.wait_send()


def gather_weights(n_batch, n_ctx, qkv, proj, gains):
    n_chip = n_ctx // 2
    dma = pltpu.SemaphoreType.DMA
    vmem = pl.BlockSpec(memory_space=pltpu.VMEM)
    return pl.pallas_call(
        functools.partial(weights_kernel, n_batch, n_ctx),
        name="gather_weights",
        out_shape=(
            jax.ShapeDtypeStruct((n_batch, n_ctx, *qkv.shape[1:]), qkv.dtype),
            jax.ShapeDtypeStruct((n_ctx, *proj.shape), proj.dtype),
            jax.ShapeDtypeStruct((n_ctx, *gains.shape), gains.dtype),
        ),
        in_specs=[vmem] * 3,
        out_specs=[vmem] * 3,
        scratch_shapes=[
            dma((n_chip - 1, 3)),
            dma((n_chip - 1, 3)),
            dma((n_chip - 1, n_batch - 1, 2)),
            dma((n_chip - 1, n_batch - 1, 2)),
            dma((n_chip, n_batch, 3)),
            dma((n_chip, n_batch, 3)),
            dma((3,)),
        ],
        compiler_params=pltpu.CompilerParams(collective_id=12, has_side_effects=True),
    )(qkv, proj, gains)


def gathered(shard):
    return lax.all_gather(shard, "ctx", axis=0, tiled=True)


def scattered(whole):
    return lax.psum_scatter(whole.astype(BF16), "ctx", scatter_dimension=0, tiled=True)


def local(
    n_batch,
    n_ctx,
    block_in,
    positions,
    counts,
    cotangent,
    gain_input,
    w_query,
    w_key,
    w_value,
    gain_query,
    gain_key,
    w_output,
    gain_attn,
    gain_ffn,
    w_gate,
    w_up,
    w_down,
    gain_final,
):
    block_in = block_in[0]
    positions = positions[0]
    cotangent = cotangent[0]
    tok_count, model_width = block_in.shape
    width_shard = w_query.shape[0]
    query_width = w_query.shape[1]
    head_size = w_key.shape[1]
    head_count = query_width // head_size
    hidden_shard = w_down.shape[0]
    piece = hidden_shard // n_batch
    halo_depth = (WINDOW + tok_count - 2) // tok_count
    batch_at = lax.axis_index("batch")
    ctx_at = lax.axis_index("ctx")
    all_tok = n_batch * tok_count

    gains = jnp.concatenate(
        [gain_input, gain_attn, gain_ffn, gain_final, gain_query, gain_key]
    )
    slots_of = query_width + 2 * head_size
    quarter = slots_of // n_batch
    qkv_full, proj_full, gains_all = gather_weights(
        n_batch,
        n_ctx,
        jnp.concatenate([w_query, w_key, w_value], axis=1)
        .reshape(width_shard, n_batch, quarter)
        .transpose(1, 0, 2),
        w_output.reshape(n_batch, -1, model_width),
        gains[None],
    )
    qkv_full = qkv_full.reshape(n_batch, model_width, quarter)
    full_output = proj_full.reshape(query_width, model_width)
    gains_all = gains_all[:, 0].astype(F32)

    def gain_at(start, length):
        return gains_all[:, start : start + length].reshape(1, -1)

    head_shard = gain_query.shape[0]
    full_gain_in = gain_at(0, width_shard)
    full_gain_attn = gain_at(width_shard, width_shard)
    full_gain_ffn = gain_at(2 * width_shard, width_shard)
    full_gain_final = gain_at(3 * width_shard, width_shard)
    full_gain_q = gain_at(4 * width_shard, head_shard)
    full_gain_k = gain_at(4 * width_shard + head_shard, head_shard)

    part_down = gathered(lax.dynamic_slice_in_dim(w_down, batch_at * piece, piece, 0))
    own_gate, own_up = pick_columns(n_batch, n_ctx, piece, w_gate, w_up)
    part_gate = gathered(own_gate)
    part_up = gathered(own_up)

    first_token = ctx_at * tok_count
    token_place = first_token + jnp.arange(tok_count, dtype=jnp.int32)
    valid_mask = (token_place < counts[0]).astype(F32)[:, None]
    resid_in = block_in.astype(F32)
    act_in = normed(resid_in, full_gain_in).astype(BF16)
    qkv_raw = jnp.concatenate([project(act_in, qkv_full[i]) for i in range(n_batch)], axis=1)
    query_raw = qkv_raw[:, :query_width].reshape(tok_count, head_count, head_size)
    key_raw = qkv_raw[:, query_width : query_width + head_size]
    value_low = qkv_raw[:, query_width + head_size :].astype(BF16)
    inv_freq = BASE ** (-jnp.arange(0, head_size, 2, dtype=F32) / head_size)
    angles = positions.astype(F32)[:, None] * inv_freq

    def query_path(raw_query, gain_vec):
        return rotate(normed(raw_query, gain_vec), angles[:, None, :])

    def key_path(raw_key, gain_vec):
        return rotate(normed(raw_key, gain_vec), angles)

    query_rot = query_path(query_raw, full_gain_q).astype(BF16)
    key_rot = key_path(key_raw, full_gain_k).astype(BF16)
    own_pair = jnp.concatenate([key_rot, value_low], axis=-1)
    halo = halo_exchange("halo_out", 1, n_ctx, halo_depth, 1, own_pair)
    context = jnp.concatenate([halo.reshape(halo_depth * tok_count, -1), own_pair], axis=0)
    ctx_keys = context[:, :head_size]
    ctx_values = context[:, head_size:]
    key_total = (halo_depth + 1) * tok_count
    distance = (
        jnp.arange(tok_count, dtype=jnp.int32)[:, None]
        + halo_depth * tok_count
        - jnp.arange(key_total, dtype=jnp.int32)[None, :]
    )
    allowed = (distance >= 0) & (distance < WINDOW) & (distance <= positions[:, None])
    score_scale = head_size ** (-0.5)
    raw_scores = jnp.einsum("thd,kd->htk", query_rot, ctx_keys, preferred_element_type=F32)
    scores = jnp.where(allowed[None], raw_scores * score_scale, MASKED)
    exp_scores = jnp.exp(scores - jnp.max(scores, axis=-1, keepdims=True))
    attn_prob = exp_scores / jnp.sum(exp_scores, axis=-1, keepdims=True)
    prob_low = attn_prob.astype(BF16)
    attended = jnp.einsum("htk,kd->thd", prob_low, ctx_values, preferred_element_type=F32)
    attn_low = attended.reshape(tok_count, query_width).astype(BF16)
    attn_proj = project(attn_low, full_output)
    middle = resid_in + normed(attn_proj, full_gain_attn)
    ffn_in = normed(middle, full_gain_ffn).astype(BF16)

    ffn_in_all, act_in_all, attn_all = batch_exchange(
        "gather_in", 2, n_batch, whole=(ffn_in, act_in, attn_low)
    )
    ffn_in_all = ffn_in_all.reshape(all_tok, model_width)
    act_in_all = act_in_all.reshape(all_tok, model_width)
    attn_all = attn_all.reshape(all_tok, query_width)
    gate_pre = project(ffn_in_all, part_gate)
    up_pre = project(ffn_in_all, part_up)
    mixed_low = gated_gelu(gate_pre, up_pre).astype(BF16)
    proj_part = project(mixed_low, part_down).astype(BF16)
    (proj_parts,) = batch_exchange(
        "sum_out", 3, n_batch, slots=(proj_part.reshape(n_batch, tok_count, model_width),)
    )
    ffn_proj = jnp.sum(proj_parts.astype(F32), axis=0)
    final_sum = middle + normed(ffn_proj, full_gain_final)
    block_out = (final_sum * valid_mask).astype(BF16)

    grad_final = cotangent.astype(F32) * valid_mask
    _, pull_final = jax.vjp(normed, ffn_proj, full_gain_final)
    grad_ffn_proj, grad_gain_final = pull_final(grad_final)
    (grad_ffn_low,) = batch_exchange("gather_grad", 4, n_batch, whole=(grad_ffn_proj.astype(BF16),))
    grad_ffn_low = grad_ffn_low.reshape(all_tok, model_width)
    down_grad = weight_grad(mixed_low, grad_ffn_low).astype(BF16)
    down_grad, grad_ffn_low = lax.optimization_barrier((down_grad, grad_ffn_low))
    grad_w_down = scattered(down_grad)
    grad_mixed = project_back(grad_ffn_low, part_down)
    _, pull_gelu = jax.vjp(gated_gelu, gate_pre, up_pre)
    grad_gate, grad_up = pull_gelu(grad_mixed)
    grad_gate_low = grad_gate.astype(BF16)
    grad_up_low = grad_up.astype(BF16)
    back_part = project_back(grad_gate_low, part_gate) + project_back(grad_up_low, part_up)
    (back_parts,) = batch_exchange(
        "sum_back", 5, n_batch, slots=(back_part.astype(BF16).reshape(n_batch, tok_count, model_width),)
    )
    back_parts, grad_gate_low, grad_up_low = lax.optimization_barrier(
        (back_parts, grad_gate_low, grad_up_low)
    )
    gate_grad = weight_grad(ffn_in_all, grad_gate_low).astype(BF16)
    up_grad = weight_grad(ffn_in_all, grad_up_low).astype(BF16)
    back_parts, gate_grad, up_grad = lax.optimization_barrier((back_parts, gate_grad, up_grad))
    grad_w_gate = scattered(gate_grad)
    grad_w_up = scattered(up_grad)
    grad_ffn_in = jnp.sum(back_parts.astype(F32), axis=0)
    _, pull_ffn_norm = jax.vjp(normed, middle, full_gain_ffn)
    grad_middle_part, grad_gain_ffn = pull_ffn_norm(grad_ffn_in)
    grad_middle = grad_final + grad_middle_part
    _, pull_attn_norm = jax.vjp(normed, attn_proj, full_gain_attn)
    grad_attn_proj, grad_gain_attn = pull_attn_norm(grad_middle)

    grad_proj_low = grad_attn_proj.astype(BF16)
    grad_attended = (
        project_back(grad_proj_low, full_output)
        .astype(BF16)
        .reshape(tok_count, head_count, head_size)
    )
    grad_prob = jnp.einsum("thd,kd->htk", grad_attended, ctx_values, preferred_element_type=F32)
    row_delta = jnp.sum(attn_prob * grad_prob, axis=-1, keepdims=True)
    grad_scores = (attn_prob * (grad_prob - row_delta)).astype(BF16)
    grad_queries = (
        jnp.einsum("htk,kd->thd", grad_scores, ctx_keys, preferred_element_type=F32) * score_scale
    )
    grad_ctx_keys = (
        jnp.einsum("htk,thd->kd", grad_scores, query_rot, preferred_element_type=F32) * score_scale
    )
    grad_ctx_values = jnp.einsum("htk,thd->kd", prob_low, grad_attended, preferred_element_type=F32)
    grad_context = jnp.concatenate([grad_ctx_keys, grad_ctx_values], axis=-1)
    halo_rows = halo_depth * tok_count
    returned = halo_exchange(
        "halo_back",
        6,
        n_ctx,
        halo_depth,
        -1,
        grad_context[:halo_rows].astype(BF16).reshape(halo_depth, tok_count, 2 * head_size),
    )
    own_grad = grad_context[halo_rows:] + jnp.sum(returned.astype(F32), axis=0)
    grad_value_low = own_grad[:, head_size:].astype(BF16)
    _, pull_key = jax.vjp(key_path, key_raw, full_gain_k)
    grad_key_raw, grad_gain_key = pull_key(own_grad[:, :head_size])
    _, pull_query = jax.vjp(query_path, query_raw, full_gain_q)
    grad_query_raw, grad_gain_query = pull_query(grad_queries)
    grad_qkv_low = jnp.concatenate(
        [
            grad_query_raw.astype(BF16).reshape(tok_count, query_width),
            grad_key_raw.astype(BF16),
            grad_value_low,
        ],
        axis=1,
    )
    grad_act_in = sum(
        project_back(grad_qkv_low[:, i * quarter : (i + 1) * quarter], qkv_full[i])
        for i in range(n_batch)
    )
    _, pull_input = jax.vjp(normed, resid_in, full_gain_in)
    grad_in_part, grad_gain_input = pull_input(grad_act_in)
    grad_in = (grad_middle + grad_in_part).astype(BF16)

    def column_slots(upstream):
        return upstream.reshape(tok_count, n_batch, -1).transpose(1, 0, 2)

    gain_rows = jnp.concatenate(
        [
            grad.reshape(n_ctx, -1)
            for grad in (
                grad_gain_input,
                grad_gain_attn,
                grad_gain_ffn,
                grad_gain_final,
                grad_gain_query,
                grad_gain_key,
            )
        ],
        axis=1,
    )
    gain_parts, qkv_slots, proj_slots = batch_exchange(
        "spread_grads",
        7,
        n_batch,
        whole=(gain_rows,),
        slots=(column_slots(grad_qkv_low), column_slots(grad_proj_low)),
    )
    proj_rows = w_output.shape[0]
    gain_count = gain_rows.shape[1]
    gain_lines = -(-gain_count // quarter)
    used = width_shard + proj_rows + gain_lines
    lines = -(-used // 16) * 16
    grad_w_output = weight_grad(attn_all, proj_slots.reshape(all_tok, -1)).astype(BF16)
    grad_w_qkv = weight_grad(act_in_all, qkv_slots.reshape(all_tok, -1)).astype(BF16)
    output_part = model_width // n_batch
    gain_sum = jnp.sum(gain_parts, axis=0).astype(BF16)
    packed = jnp.concatenate(
        [
            grad_w_qkv.reshape(n_ctx, width_shard, quarter),
            jnp.pad(
                grad_w_output.reshape(n_ctx, proj_rows, output_part),
                ((0, 0), (0, 0), (0, quarter - output_part)),
            ),
            jnp.pad(gain_sum, ((0, 0), (0, gain_lines * quarter - gain_count))).reshape(
                n_ctx, gain_lines, quarter
            ),
            jnp.zeros((n_ctx, lines - used, quarter), BF16),
        ],
        axis=1,
    )
    attn_sum = scattered(packed.reshape(n_ctx * lines, quarter))

    (down_all,) = batch_exchange("spread_down", 8, n_batch, whole=(grad_w_down,))
    (gate_all,) = batch_exchange("spread_gate", 9, n_batch, whole=(grad_w_gate,))
    (up_all,) = batch_exchange("spread_up", 10, n_batch, whole=(grad_w_up,))
    (attn_grads,) = batch_exchange("spread_attn", 11, n_batch, whole=(attn_sum,))
    gain_mine = attn_grads[0, width_shard + proj_rows : used].reshape(-1).astype(F32)

    def columns_back(pieces):
        return pieces.astype(F32).transpose(1, 0, 2).reshape(pieces.shape[1], -1)

    grad_qkv_shard = columns_back(attn_grads[:, :width_shard])
    return (
        block_out[None],
        grad_in[None],
        gain_mine[:width_shard],
        grad_qkv_shard[:, :query_width],
        grad_qkv_shard[:, query_width : query_width + head_size],
        grad_qkv_shard[:, query_width + head_size :],
        gain_mine[4 * width_shard : 4 * width_shard + head_shard],
        gain_mine[4 * width_shard + head_shard : gain_count],
        columns_back(attn_grads[:, width_shard : width_shard + proj_rows, :output_part]),
        gain_mine[width_shard : 2 * width_shard],
        gain_mine[2 * width_shard : 3 * width_shard],
        place_columns("place_gate", n_batch, n_ctx, piece, gate_all),
        place_columns("place_up", n_batch, n_ctx, piece, up_all),
        down_all.reshape(hidden_shard, model_width).astype(F32),
        gain_mine[3 * width_shard : 4 * width_shard],
    )


def solution(mesh):
    matrix = P("ctx", None)
    vector = P("ctx")
    tokens = P("batch", "ctx", None)
    return jax.shard_map(
        functools.partial(local, mesh.shape["batch"], mesh.shape["ctx"]),
        mesh=mesh,
        in_specs=(
            tokens,
            P("batch", "ctx"),
            P("batch"),
            tokens,
            vector,
            matrix,
            matrix,
            matrix,
            vector,
            vector,
            matrix,
            vector,
            vector,
            matrix,
            matrix,
            matrix,
            vector,
        ),
        out_specs=(
            tokens,
            tokens,
            vector,
            matrix,
            matrix,
            matrix,
            vector,
            vector,
            matrix,
            vector,
            vector,
            matrix,
            matrix,
            matrix,
            vector,
        ),
        check_vma=False,
    )
```

```python
import functools

import jax
import jax.numpy as jnp
from jax import lax
from jax.experimental import pallas as pl
from jax.experimental.pallas import tpu as pltpu
from jax.sharding import PartitionSpec as P

WINDOW = 512


EPS = 1e-06
BASE = 10000.0
MASKED = -1e30
BF16 = jnp.bfloat16
F32 = jnp.float32
MESH = pl.DeviceIdType.MESH


def normed(vector, gain_vec):
    return vector * lax.rsqrt(jnp.mean(vector * vector, axis=-1, keepdims=True) + EPS) * gain_vec


def rotate(vector, angles):
    half_size = vector.shape[-1] // 2
    cosine = jnp.cos(angles)
    sine_part = jnp.sin(angles)
    first_half = vector[..., :half_size]
    second = vector[..., half_size:]
    return jnp.concatenate(
        [first_half * cosine - second * sine_part, second * cosine + first_half * sine_part],
        axis=-1,
    )


def project(inputs, weight):
    return lax.dot_general(inputs, weight, (((1,), (0,)), ((), ())), preferred_element_type=F32)


def project_back(upstream, weight):
    return lax.dot_general(upstream, weight, (((1,), (1,)), ((), ())), preferred_element_type=F32)


def weight_grad(inputs, upstream):
    return lax.dot_general(inputs, upstream, (((0,), (0,)), ((), ())), preferred_element_type=F32)


def gated_gelu(gate_val, up_val):
    return jax.nn.gelu(gate_val, approximate=True) * up_val


def batch_kernel(size, kinds, *refs):
    count = len(kinds)
    sources, results = refs[:count], refs[count : 2 * count]
    send_sem, recv_sem, own_sem = refs[2 * count :]
    me = lax.axis_index("batch")
    barrier = pltpu.get_barrier_semaphore()
    for step in range(1, size):
        pl.semaphore_signal(
            barrier, inc=1, device_id={"batch": lax.rem(me + step, size)}, device_id_type=MESH
        )
    pl.semaphore_wait(barrier, size - 1)
    copies = []
    for step in range(1, size):
        peer = lax.rem(me + step, size)
        for item in range(count):
            source = sources[item].at[peer] if kinds[item] else sources[item]
            copies.append(
                pltpu.make_async_remote_copy(
                    src_ref=source,
                    dst_ref=results[item].at[me],
                    send_sem=send_sem.at[item, step - 1],
                    recv_sem=recv_sem.at[item, step - 1],
                    device_id={"batch": peer},
                    device_id_type=MESH,
                )
            )
    for copy in copies:
        copy.start()
    own = []
    for item in range(count):
        source = sources[item].at[me] if kinds[item] else sources[item]
        own.append(pltpu.make_async_copy(source, results[item].at[me], own_sem.at[item]))
    for copy in own:
        copy.start()
    for copy in own:
        copy.wait()
    for copy in copies:
        copy.wait()


def batch_exchange(collective_id, size, whole=(), slots=()):
    arrays = list(whole) + list(slots)
    kinds = [0] * len(whole) + [1] * len(slots)
    count = len(arrays)
    shapes = [
        jax.ShapeDtypeStruct(a.shape if k else (size, *a.shape), a.dtype)
        for a, k in zip(arrays, kinds)
    ]
    return pl.pallas_call(
        functools.partial(batch_kernel, size, kinds),
        out_shape=shapes,
        in_specs=[pl.BlockSpec(memory_space=pltpu.VMEM)] * count,
        out_specs=[pl.BlockSpec(memory_space=pltpu.VMEM)] * count,
        scratch_shapes=[
            pltpu.SemaphoreType.DMA((count, size - 1)),
            pltpu.SemaphoreType.DMA((count, size - 1)),
            pltpu.SemaphoreType.DMA((count,)),
        ],
        compiler_params=pltpu.CompilerParams(collective_id=collective_id, has_side_effects=True),
    )(*arrays)


def square_kernel(count, *refs):
    sources, results = refs[:count], refs[count : 2 * count]
    send_sem, recv_sem, own_sem = refs[2 * count :]
    me = lax.axis_index("batch")
    across = me + 1 - 2 * lax.rem(me, 2)
    along = lax.rem(me + 2, 4)
    barrier = pltpu.get_barrier_semaphore()
    for peer in (across, along):
        pl.semaphore_signal(barrier, inc=1, device_id={"batch": peer}, device_id_type=MESH)
    pl.semaphore_wait(barrier, 2)

    def remote(source, target, item, turn, peer):
        copy = pltpu.make_async_remote_copy(
            src_ref=source,
            dst_ref=target,
            send_sem=send_sem.at[item, turn],
            recv_sem=recv_sem.at[item, turn],
            device_id={"batch": peer},
            device_id_type=MESH,
        )
        copy.start()
        return copy

    firsts = [
        [
            remote(sources[item], results[item].at[me], item, turn, peer)
            for turn, peer in enumerate((across, along))
        ]
        for item in range(count)
    ]
    own = [
        pltpu.make_async_copy(sources[item], results[item].at[me], own_sem.at[item])
        for item in range(count)
    ]
    for copy in own:
        copy.start()
    seconds = []
    for item in range(count):
        columns = sources[item].shape[-1]
        cut = columns // 256 * 128
        halves = (pl.ds(0, cut), pl.ds(cut, columns - cut))
        for turn, (giver, taker) in enumerate(((across, along), (along, across))):
            firsts[item][turn].wait_recv()
            block = results[item].at[giver, :, halves[turn]]
            seconds.append(remote(block, block, item, 2 + turn, taker))
    for copy in own:
        copy.wait()
    for copy in seconds:
        copy.wait()
    for pair in firsts:
        for copy in pair:
            copy.wait_send()


def square_gather(collective_id, *arrays):
    count = len(arrays)
    return pl.pallas_call(
        functools.partial(square_kernel, count),
        out_shape=[jax.ShapeDtypeStruct((4, *a.shape), a.dtype) for a in arrays],
        in_specs=[pl.BlockSpec(memory_space=pltpu.VMEM)] * count,
        out_specs=[pl.BlockSpec(memory_space=pltpu.VMEM)] * count,
        scratch_shapes=[
            pltpu.SemaphoreType.DMA((count, 4)),
            pltpu.SemaphoreType.DMA((count, 4)),
            pltpu.SemaphoreType.DMA((count,)),
        ],
        compiler_params=pltpu.CompilerParams(collective_id=collective_id, has_side_effects=True),
    )(*arrays)


def halo_kernel(size, depth, direction, source_ref, result_ref, send_sem, recv_sem):
    me = lax.axis_index("ctx")
    barrier = pltpu.get_barrier_semaphore()
    for step in range(1, depth + 1):
        giver = me - direction * step

        @pl.when((giver >= 0) & (giver < size))
        def _():
            pl.semaphore_signal(barrier, inc=1, device_id={"ctx": giver}, device_id_type=MESH)

    takers = jnp.minimum(depth, size - 1 - me) if direction > 0 else jnp.minimum(depth, me)

    @pl.when(takers > 0)
    def _():
        pl.semaphore_wait(barrier, takers)

    def copy(step):
        slot = depth - step
        source = source_ref if direction > 0 else source_ref.at[slot]
        return pltpu.make_async_remote_copy(
            src_ref=source,
            dst_ref=result_ref.at[slot],
            send_sem=send_sem.at[step - 1],
            recv_sem=recv_sem.at[step - 1],
            device_id={"ctx": jnp.clip(me + direction * step, 0, size - 1)},
            device_id_type=MESH,
        )

    for step in range(depth, 0, -1):
        taker = me + direction * step

        @pl.when((taker >= 0) & (taker < size))
        def _():
            copy(step).start()

    for step in range(1, depth + 1):
        taker = me + direction * step
        giver = me - direction * step

        @pl.when((giver < 0) | (giver >= size))
        def _():
            result_ref[depth - step] = jnp.zeros(result_ref.shape[1:], result_ref.dtype)

        @pl.when((giver >= 0) & (giver < size))
        def _():
            copy(step).wait_recv()

        @pl.when((taker >= 0) & (taker < size))
        def _():
            copy(step).wait_send()


def halo_exchange(collective_id, size, depth, direction, block):
    return pl.pallas_call(
        functools.partial(halo_kernel, size, depth, direction),
        out_shape=jax.ShapeDtypeStruct((depth, *block.shape[-2:]), block.dtype),
        in_specs=[pl.BlockSpec(memory_space=pltpu.VMEM)],
        out_specs=pl.BlockSpec(memory_space=pltpu.VMEM),
        scratch_shapes=[pltpu.SemaphoreType.DMA((depth,)), pltpu.SemaphoreType.DMA((depth,))],
        compiler_params=pltpu.CompilerParams(collective_id=collective_id, has_side_effects=True),
    )(block)


def pick_kernel(n_batch, n_ctx, piece, padded, gate_ref, up_ref, out_ref):
    me = lax.axis_index("batch")
    out_ref[...] = jnp.zeros_like(out_ref)
    for spot in range(n_batch):

        @pl.when(me == spot)
        def _():
            for shard in range(n_ctx):
                start = (shard * n_batch + spot) * piece
                for half, ref in enumerate((gate_ref, up_ref)):
                    place = (half * n_ctx + shard) * padded
                    out_ref[:, place : place + piece] = ref[:, start : start + piece]


def row_block(rows):
    return 48 if rows % 48 == 0 else rows


def pick_columns(n_batch, n_ctx, piece, padded, w_gate, w_up):
    rows, hidden = w_gate.shape
    block = row_block(rows)
    spec = pl.BlockSpec((block, hidden), lambda i: (i, 0))
    return pl.pallas_call(
        functools.partial(pick_kernel, n_batch, n_ctx, piece, padded),
        name="pick_columns",
        grid=(rows // block,),
        out_shape=jax.ShapeDtypeStruct((rows, 2 * n_ctx * padded), w_gate.dtype),
        in_specs=[spec, spec],
        out_specs=pl.BlockSpec((block, 2 * n_ctx * padded), lambda i: (i, 0)),
    )(w_gate, w_up)


def place_kernel(n_batch, n_ctx, piece, padded, parts_ref, gate_ref, up_ref):
    for shard in range(n_ctx):
        for spot in range(n_batch):
            start = (shard * n_batch + spot) * piece
            for half, ref in enumerate((gate_ref, up_ref)):
                place = (half * n_ctx + shard) * padded
                ref[:, start : start + piece] = parts_ref[spot, :, place : place + piece].astype(F32)


def place_columns(n_batch, n_ctx, piece, padded, parts):
    rows = parts.shape[1]
    block = row_block(rows)
    hidden = n_batch * n_ctx * piece
    spec = pl.BlockSpec((block, hidden), lambda i: (i, 0))
    out = jax.ShapeDtypeStruct((rows, hidden), F32)
    return pl.pallas_call(
        functools.partial(place_kernel, n_batch, n_ctx, piece, padded),
        name="place_columns",
        grid=(rows // block,),
        out_shape=(out, out),
        in_specs=[pl.BlockSpec((n_batch, block, 2 * n_ctx * padded), lambda i: (0, i, 0))],
        out_specs=[spec, spec],
    )(parts)


def weights_kernel(n_batch, n_ctx, qkv_ref, proj_ref, gain_ref, qkv_all, proj_all, gain_all, *sems):
    send_far, recv_far, send_side, recv_side, send_near, recv_near, own_sem = sems
    spot = lax.axis_index("batch")
    me = lax.axis_index("ctx")
    n_chip = n_ctx // 2
    chip, core = me // 2, lax.rem(me, 2)
    near = {"ctx": me + 1 - 2 * core}
    barrier = pltpu.get_barrier_semaphore()

    def far_at(step):
        return {"ctx": 2 * lax.rem(chip + step, n_chip) + core}

    def side_at(step):
        return {"batch": lax.rem(spot + step, n_batch)}

    peers = [near]
    peers += [far_at(step) for step in range(1, n_chip)]
    peers += [side_at(step) for step in range(1, n_batch)]
    for peer in peers:
        pl.semaphore_signal(barrier, inc=1, device_id=peer, device_id_type=MESH)
    pl.semaphore_wait(barrier, len(peers))

    def remote(source, target, send, recv, peer):
        return pltpu.make_async_remote_copy(
            src_ref=source,
            dst_ref=target,
            send_sem=send,
            recv_sem=recv,
            device_id=peer,
            device_id_type=MESH,
        )

    waits = []
    far = []
    for step in range(1, n_chip):
        triple = [
            remote(source, target, send_far.at[step - 1, item], recv_far.at[step - 1, item], far_at(step))
            for item, (source, target) in enumerate(
                (
                    (qkv_ref.at[spot], qkv_all.at[spot, me]),
                    (proj_ref.at[spot], proj_all.at[me, spot]),
                    (gain_ref, gain_all.at[me]),
                )
            )
        ]
        for copy in triple:
            copy.start()
        far.append(triple)
    own = [
        pltpu.make_async_copy(qkv_ref, qkv_all.at[:, me], own_sem.at[0]),
        pltpu.make_async_copy(proj_ref, proj_all.at[me], own_sem.at[1]),
        pltpu.make_async_copy(gain_ref, gain_all.at[me], own_sem.at[2]),
    ]
    for copy in own:
        copy.start()
    first = n_chip - 1
    pairs = [
        remote(source, target, send_near.at[first, 0, item], recv_near.at[first, 0, item], near)
        for item, (source, target) in enumerate(
            (
                (qkv_ref, qkv_all.at[:, me]),
                (proj_ref, proj_all.at[me]),
                (gain_ref, gain_all.at[me]),
            )
        )
    ]
    for copy in pairs:
        copy.start()
    waits += pairs

    def hand_near(step, turn):
        origin = 2 * lax.rem(chip + n_chip - step, n_chip) + core
        quarter = lax.rem(spot + n_batch - turn, n_batch)
        blocks = [qkv_all.at[quarter, origin], proj_all.at[origin, quarter]]
        blocks += [gain_all.at[origin]] if turn == 0 else []
        for item, block in enumerate(blocks):
            copy = remote(
                block,
                block,
                send_near.at[step - 1, turn, item],
                recv_near.at[step - 1, turn, item],
                near,
            )
            copy.start()
            waits.append(copy)

    side = []
    for step in range(1, n_chip):
        for copy in far[step - 1]:
            copy.wait_recv()
        origin = 2 * lax.rem(chip + n_chip - step, n_chip) + core
        for turn in range(1, n_batch):
            pair = [
                remote(
                    block,
                    block,
                    send_side.at[step - 1, turn - 1, item],
                    recv_side.at[step - 1, turn - 1, item],
                    side_at(turn),
                )
                for item, block in enumerate((qkv_all.at[spot, origin], proj_all.at[origin, spot]))
            ]
            for copy in pair:
                copy.start()
            side.append((step, turn, pair))
        hand_near(step, 0)
    for step, turn, pair in side:
        for copy in pair:
            copy.wait_recv()
        hand_near(step, turn)
    for copy in waits:
        copy.wait()
    for copy in own:
        copy.wait()
    for triple in far:
        for copy in triple:
            copy.wait_send()
    for _, _, pair in side:
        for copy in pair:
            copy.wait_send()


def gather_weights(n_batch, n_ctx, qkv, proj, gains):
    n_chip = n_ctx // 2
    dma = pltpu.SemaphoreType.DMA
    vmem = pl.BlockSpec(memory_space=pltpu.VMEM)
    return pl.pallas_call(
        functools.partial(weights_kernel, n_batch, n_ctx),
        name="gather_weights",
        out_shape=(
            jax.ShapeDtypeStruct((n_batch, n_ctx, *qkv.shape[1:]), qkv.dtype),
            jax.ShapeDtypeStruct((n_ctx, *proj.shape), proj.dtype),
            jax.ShapeDtypeStruct((n_ctx, *gains.shape), gains.dtype),
        ),
        in_specs=[vmem] * 3,
        out_specs=[vmem] * 3,
        scratch_shapes=[
            dma((n_chip - 1, 3)),
            dma((n_chip - 1, 3)),
            dma((n_chip - 1, n_batch - 1, 2)),
            dma((n_chip - 1, n_batch - 1, 2)),
            dma((n_chip, n_batch, 3)),
            dma((n_chip, n_batch, 3)),
            dma((3,)),
        ],
        compiler_params=pltpu.CompilerParams(collective_id=12, has_side_effects=True),
    )(qkv, proj, gains)


def gathered(shard):
    return lax.all_gather(shard, "ctx", axis=0, tiled=True)


def scattered(whole):
    return lax.psum_scatter(whole, "ctx", scatter_dimension=0, tiled=True)


def local(
    n_batch,
    n_ctx,
    block_in,
    positions,
    counts,
    cotangent,
    gain_input,
    w_query,
    w_key,
    w_value,
    gain_query,
    gain_key,
    w_output,
    gain_attn,
    gain_ffn,
    w_gate,
    w_up,
    w_down,
    gain_final,
):
    block_in = block_in[0]
    positions = positions[0]
    cotangent = cotangent[0]
    tok_count, model_width = block_in.shape
    width_shard = w_query.shape[0]
    query_width = w_query.shape[1]
    head_size = w_key.shape[1]
    head_count = query_width // head_size
    hidden_shard = w_down.shape[0]
    piece = hidden_shard // n_batch
    hidden_part = -(-piece * n_ctx // 128) * 128
    padded = hidden_part // n_ctx
    halo_depth = (WINDOW + tok_count - 2) // tok_count
    batch_at = lax.axis_index("batch")
    ctx_at = lax.axis_index("ctx")
    all_tok = n_batch * tok_count

    gains = jnp.concatenate(
        [gain_input, gain_attn, gain_ffn, gain_final, gain_query, gain_key]
    )
    slots_of = query_width + 2 * head_size
    quarter = slots_of // n_batch
    qkv_full, proj_full, gains_all = gather_weights(
        n_batch,
        n_ctx,
        jnp.concatenate([w_query, w_key, w_value], axis=1)
        .reshape(width_shard, n_batch, quarter)
        .transpose(1, 0, 2),
        w_output.reshape(n_batch, -1, model_width),
        gains[None],
    )
    qkv_full = qkv_full.reshape(n_batch, model_width, quarter)
    full_output = proj_full.reshape(query_width, model_width)
    gains_all = gains_all[:, 0].astype(F32)

    def gain_at(start, length):
        return gains_all[:, start : start + length].reshape(1, -1)

    head_shard = gain_query.shape[0]
    full_gain_in = gain_at(0, width_shard)
    full_gain_attn = gain_at(width_shard, width_shard)
    full_gain_ffn = gain_at(2 * width_shard, width_shard)
    full_gain_final = gain_at(3 * width_shard, width_shard)
    full_gain_q = gain_at(4 * width_shard, head_shard)
    full_gain_k = gain_at(4 * width_shard + head_shard, head_shard)

    part_both = gathered(pick_columns(n_batch, n_ctx, piece, padded, w_gate, w_up))
    own_down = lax.dynamic_slice_in_dim(w_down, batch_at * piece, piece, 0)
    part_down = gathered(jnp.pad(own_down, ((0, padded - piece), (0, 0))))

    first_token = ctx_at * tok_count
    token_place = first_token + jnp.arange(tok_count, dtype=jnp.int32)
    valid_mask = (token_place < counts[0]).astype(F32)[:, None]
    resid_in = block_in.astype(F32)
    act_in = normed(resid_in, full_gain_in).astype(BF16)
    qkv_raw = jnp.concatenate([project(act_in, qkv_full[i]) for i in range(n_batch)], axis=1)
    query_raw = qkv_raw[:, :query_width].reshape(tok_count, head_count, head_size)
    key_raw = qkv_raw[:, query_width : query_width + head_size]
    value_low = qkv_raw[:, query_width + head_size :].astype(BF16)
    inv_freq = BASE ** (-jnp.arange(0, head_size, 2, dtype=F32) / head_size)
    angles = positions.astype(F32)[:, None] * inv_freq

    def query_path(raw_query, gain_vec):
        return rotate(normed(raw_query, gain_vec), angles[:, None, :])

    def key_path(raw_key, gain_vec):
        return rotate(normed(raw_key, gain_vec), angles)

    query_rot = query_path(query_raw, full_gain_q).astype(BF16)
    key_rot = key_path(key_raw, full_gain_k).astype(BF16)
    own_pair = jnp.concatenate([key_rot, value_low], axis=-1)
    halo = halo_exchange(1, n_ctx, halo_depth, 1, own_pair)
    context = jnp.concatenate([halo.reshape(halo_depth * tok_count, -1), own_pair], axis=0)
    ctx_keys = context[:, :head_size]
    ctx_values = context[:, head_size:]
    key_total = (halo_depth + 1) * tok_count
    distance = (
        jnp.arange(tok_count, dtype=jnp.int32)[:, None]
        + halo_depth * tok_count
        - jnp.arange(key_total, dtype=jnp.int32)[None, :]
    )
    allowed = (distance >= 0) & (distance < WINDOW) & (distance <= positions[:, None])
    score_scale = head_size ** (-0.5)
    raw_scores = jnp.einsum("thd,kd->htk", query_rot, ctx_keys, preferred_element_type=F32)
    scores = jnp.where(allowed[None], raw_scores * score_scale, MASKED)
    exp_scores = jnp.exp(scores - jnp.max(scores, axis=-1, keepdims=True))
    attn_prob = exp_scores / jnp.sum(exp_scores, axis=-1, keepdims=True)
    prob_low = attn_prob.astype(BF16)
    attended = jnp.einsum("htk,kd->thd", prob_low, ctx_values, preferred_element_type=F32)
    attn_low = attended.reshape(tok_count, query_width).astype(BF16)
    attn_proj = project(attn_low, full_output)
    middle = resid_in + normed(attn_proj, full_gain_attn)
    ffn_in = normed(middle, full_gain_ffn).astype(BF16)

    (ffn_in_all,) = square_gather(2, ffn_in)
    ffn_in_all = ffn_in_all.reshape(all_tok, model_width)
    both_pre = project(ffn_in_all, part_both)
    gate_pre, up_pre = both_pre[:, :hidden_part], both_pre[:, hidden_part:]
    mixed_low = gated_gelu(gate_pre, up_pre).astype(BF16)
    proj_part = project(mixed_low, part_down).astype(BF16)
    (proj_parts,) = batch_exchange(
        3, n_batch, slots=(proj_part.reshape(n_batch, tok_count, model_width),)
    )
    ffn_proj = jnp.sum(proj_parts.astype(F32), axis=0)
    final_sum = middle + normed(ffn_proj, full_gain_final)
    block_out = (final_sum * valid_mask).astype(BF16)

    grad_final = cotangent.astype(F32) * valid_mask
    _, pull_final = jax.vjp(normed, ffn_proj, full_gain_final)
    grad_ffn_proj, grad_gain_final = pull_final(grad_final)
    (grad_ffn_low,) = square_gather(4, grad_ffn_proj.astype(BF16))
    grad_ffn_low = grad_ffn_low.reshape(all_tok, model_width)
    down_grad = weight_grad(mixed_low, grad_ffn_low).astype(BF16)
    down_grad, grad_ffn_low = lax.optimization_barrier((down_grad, grad_ffn_low))
    grad_w_down = scattered(down_grad)
    grad_mixed = project_back(grad_ffn_low, part_down)
    _, pull_gelu = jax.vjp(gated_gelu, gate_pre, up_pre)
    grad_gate, grad_up = pull_gelu(grad_mixed)
    grad_both_low = jnp.concatenate([grad_gate, grad_up], axis=1).astype(BF16)
    back_part = project_back(grad_both_low, part_both).astype(BF16)
    (back_parts,) = batch_exchange(
        5, n_batch, slots=(back_part.reshape(n_batch, tok_count, model_width),)
    )
    back_parts, grad_both_low = lax.optimization_barrier((back_parts, grad_both_low))
    both_grad = weight_grad(ffn_in_all, grad_both_low).astype(BF16)
    back_parts, both_grad = lax.optimization_barrier((back_parts, both_grad))
    grad_w_both = scattered(both_grad)
    grad_ffn_in = jnp.sum(back_parts.astype(F32), axis=0)
    _, pull_ffn_norm = jax.vjp(normed, middle, full_gain_ffn)
    grad_middle_part, grad_gain_ffn = pull_ffn_norm(grad_ffn_in)
    grad_middle = grad_final + grad_middle_part
    _, pull_attn_norm = jax.vjp(normed, attn_proj, full_gain_attn)
    grad_attn_proj, grad_gain_attn = pull_attn_norm(grad_middle)

    grad_proj_low = grad_attn_proj.astype(BF16)
    grad_attended = (
        project_back(grad_proj_low, full_output)
        .astype(BF16)
        .reshape(tok_count, head_count, head_size)
    )
    grad_prob = jnp.einsum("thd,kd->htk", grad_attended, ctx_values, preferred_element_type=F32)
    row_delta = jnp.sum(attn_prob * grad_prob, axis=-1, keepdims=True)
    grad_scores = (attn_prob * (grad_prob - row_delta)).astype(BF16)
    grad_queries = (
        jnp.einsum("htk,kd->thd", grad_scores, ctx_keys, preferred_element_type=F32) * score_scale
    )
    grad_ctx_keys = (
        jnp.einsum("htk,thd->kd", grad_scores, query_rot, preferred_element_type=F32) * score_scale
    )
    grad_ctx_values = jnp.einsum("htk,thd->kd", prob_low, grad_attended, preferred_element_type=F32)
    grad_context = jnp.concatenate([grad_ctx_keys, grad_ctx_values], axis=-1)
    halo_rows = halo_depth * tok_count
    returned = halo_exchange(
        6,
        n_ctx,
        halo_depth,
        -1,
        grad_context[:halo_rows].astype(BF16).reshape(halo_depth, tok_count, 2 * head_size),
    )
    own_grad = grad_context[halo_rows:] + jnp.sum(returned.astype(F32), axis=0)
    grad_value_low = own_grad[:, head_size:].astype(BF16)
    _, pull_key = jax.vjp(key_path, key_raw, full_gain_k)
    grad_key_raw, grad_gain_key = pull_key(own_grad[:, :head_size])
    _, pull_query = jax.vjp(query_path, query_raw, full_gain_q)
    grad_query_raw, grad_gain_query = pull_query(grad_queries)
    grad_qkv_low = jnp.concatenate(
        [
            grad_query_raw.astype(BF16).reshape(tok_count, query_width),
            grad_key_raw.astype(BF16),
            grad_value_low,
        ],
        axis=1,
    )
    grad_act_in = sum(
        project_back(grad_qkv_low[:, i * quarter : (i + 1) * quarter], qkv_full[i])
        for i in range(n_batch)
    )
    _, pull_input = jax.vjp(normed, resid_in, full_gain_in)
    grad_in_part, grad_gain_input = pull_input(grad_act_in)
    grad_in = (grad_middle + grad_in_part).astype(BF16)

    def column_slots(upstream):
        return upstream.reshape(tok_count, n_batch, -1).transpose(1, 0, 2)

    gain_rows = jnp.concatenate(
        [
            grad.reshape(n_ctx, -1)
            for grad in (
                grad_gain_input,
                grad_gain_attn,
                grad_gain_ffn,
                grad_gain_final,
                grad_gain_query,
                grad_gain_key,
            )
        ],
        axis=1,
    )
    gain_parts, act_in_all, attn_all, qkv_slots, proj_slots = batch_exchange(
        7,
        n_batch,
        whole=(gain_rows, act_in, attn_low),
        slots=(column_slots(grad_qkv_low), column_slots(grad_proj_low)),
    )
    act_in_all = act_in_all.reshape(all_tok, model_width)
    attn_all = attn_all.reshape(all_tok, query_width)
    proj_rows = w_output.shape[0]
    gain_count = gain_rows.shape[1]
    gain_lines = -(-gain_count // quarter)
    used = width_shard + proj_rows + gain_lines
    lines = -(-used // 16) * 16
    grad_w_output = weight_grad(attn_all, proj_slots.reshape(all_tok, -1)).astype(BF16)
    grad_w_qkv = weight_grad(act_in_all, qkv_slots.reshape(all_tok, -1)).astype(BF16)
    output_part = model_width // n_batch
    gain_sum = jnp.sum(gain_parts, axis=0).astype(BF16)
    packed = jnp.concatenate(
        [
            grad_w_qkv.reshape(n_ctx, width_shard, quarter),
            jnp.pad(
                grad_w_output.reshape(n_ctx, proj_rows, output_part),
                ((0, 0), (0, 0), (0, quarter - output_part)),
            ),
            jnp.pad(gain_sum, ((0, 0), (0, gain_lines * quarter - gain_count))).reshape(
                n_ctx, gain_lines, quarter
            ),
            jnp.zeros((n_ctx, lines - used, quarter), BF16),
        ],
        axis=1,
    )
    attn_sum = scattered(packed.reshape(n_ctx * lines, quarter))

    (down_all,) = square_gather(8, grad_w_down)
    (both_all,) = square_gather(9, grad_w_both)
    (attn_grads,) = square_gather(11, attn_sum)
    grad_gate_shard, grad_up_shard = place_columns(n_batch, n_ctx, piece, padded, both_all)
    gain_mine = attn_grads[0, width_shard + proj_rows : used].reshape(-1).astype(F32)

    def columns_back(pieces):
        return pieces.astype(F32).transpose(1, 0, 2).reshape(pieces.shape[1], -1)

    grad_qkv_shard = columns_back(attn_grads[:, :width_shard])
    return (
        block_out[None],
        grad_in[None],
        gain_mine[:width_shard],
        grad_qkv_shard[:, :query_width],
        grad_qkv_shard[:, query_width : query_width + head_size],
        grad_qkv_shard[:, query_width + head_size :],
        gain_mine[4 * width_shard : 4 * width_shard + head_shard],
        gain_mine[4 * width_shard + head_shard : gain_count],
        columns_back(attn_grads[:, width_shard : width_shard + proj_rows, :output_part]),
        gain_mine[width_shard : 2 * width_shard],
        gain_mine[2 * width_shard : 3 * width_shard],
        grad_gate_shard,
        grad_up_shard,
        down_all[:, :piece].reshape(hidden_shard, model_width).astype(F32),
        gain_mine[3 * width_shard : 4 * width_shard],
    )


def solution(mesh):
    matrix = P("ctx", None)
    vector = P("ctx")
    tokens = P("batch", "ctx", None)

    def step(*arrays):
        return local(mesh.shape["batch"], mesh.shape["ctx"], *arrays)

    return jax.shard_map(
        step,
        mesh=mesh,
        in_specs=(
            tokens,
            P("batch", "ctx"),
            P("batch"),
            tokens,
            vector,
            matrix,
            matrix,
            matrix,
            vector,
            vector,
            matrix,
            vector,
            vector,
            matrix,
            matrix,
            matrix,
            vector,
        ),
        out_specs=(
            tokens,
            tokens,
            vector,
            matrix,
            matrix,
            matrix,
            vector,
            vector,
            matrix,
            vector,
            vector,
            matrix,
            matrix,
            matrix,
            vector,
        ),
        check_vma=False,
    )
```

```python
import functools

import jax
import jax.numpy as jnp
from jax import lax
from jax.experimental import pallas as pl
from jax.experimental.pallas import tpu as pltpu
from jax.sharding import PartitionSpec as P

WINDOW = 512


EPS = 1e-06
BASE = 10000.0
MASKED = -1e30
BF16 = jnp.bfloat16
F32 = jnp.float32
MESH = pl.DeviceIdType.MESH


def normed(vector, gain_vec):
    return vector * lax.rsqrt(jnp.mean(vector * vector, axis=-1, keepdims=True) + EPS) * gain_vec


def rotate(vector, angles):
    half_size = vector.shape[-1] // 2
    cosine = jnp.cos(angles)
    sine_part = jnp.sin(angles)
    first_half = vector[..., :half_size]
    second = vector[..., half_size:]
    return jnp.concatenate(
        [first_half * cosine - second * sine_part, second * cosine + first_half * sine_part],
        axis=-1,
    )


def project(inputs, weight):
    return lax.dot_general(inputs, weight, (((1,), (0,)), ((), ())), preferred_element_type=F32)


def project_back(upstream, weight):
    return lax.dot_general(upstream, weight, (((1,), (1,)), ((), ())), preferred_element_type=F32)


def weight_grad(inputs, upstream):
    return lax.dot_general(inputs, upstream, (((0,), (0,)), ((), ())), preferred_element_type=F32)


def gated_gelu(gate_val, up_val):
    return jax.nn.gelu(gate_val, approximate=True) * up_val


def batch_kernel(size, kinds, *refs):
    count = len(kinds)
    sources, results = refs[:count], refs[count : 2 * count]
    send_sem, recv_sem, own_sem = refs[2 * count :]
    me = lax.axis_index("batch")
    barrier = pltpu.get_barrier_semaphore()
    for step in range(1, size):
        pl.semaphore_signal(
            barrier, inc=1, device_id={"batch": lax.rem(me + step, size)}, device_id_type=MESH
        )
    pl.semaphore_wait(barrier, size - 1)
    copies = []
    for step in range(1, size):
        peer = lax.rem(me + step, size)
        for item in range(count):
            source = sources[item].at[peer] if kinds[item] else sources[item]
            copies.append(
                pltpu.make_async_remote_copy(
                    src_ref=source,
                    dst_ref=results[item].at[me],
                    send_sem=send_sem.at[item, step - 1],
                    recv_sem=recv_sem.at[item, step - 1],
                    device_id={"batch": peer},
                    device_id_type=MESH,
                )
            )
    for copy in copies:
        copy.start()
    own = []
    for item in range(count):
        source = sources[item].at[me] if kinds[item] else sources[item]
        own.append(pltpu.make_async_copy(source, results[item].at[me], own_sem.at[item]))
    for copy in own:
        copy.start()
    for copy in own:
        copy.wait()
    for copy in copies:
        copy.wait()


def batch_exchange(collective_id, size, whole=(), slots=()):
    arrays = list(whole) + list(slots)
    kinds = [0] * len(whole) + [1] * len(slots)
    count = len(arrays)
    shapes = [
        jax.ShapeDtypeStruct(a.shape if k else (size, *a.shape), a.dtype)
        for a, k in zip(arrays, kinds)
    ]
    return pl.pallas_call(
        functools.partial(batch_kernel, size, kinds),
        out_shape=shapes,
        in_specs=[pl.BlockSpec(memory_space=pltpu.VMEM)] * count,
        out_specs=[pl.BlockSpec(memory_space=pltpu.VMEM)] * count,
        scratch_shapes=[
            pltpu.SemaphoreType.DMA((count, size - 1)),
            pltpu.SemaphoreType.DMA((count, size - 1)),
            pltpu.SemaphoreType.DMA((count,)),
        ],
        compiler_params=pltpu.CompilerParams(collective_id=collective_id, has_side_effects=True),
    )(*arrays)


def square_kernel(count, *refs):
    sources, results = refs[:count], refs[count : 2 * count]
    send_sem, recv_sem, own_sem = refs[2 * count :]
    me = lax.axis_index("batch")
    across = me + 1 - 2 * lax.rem(me, 2)
    along = lax.rem(me + 2, 4)
    barrier = pltpu.get_barrier_semaphore()
    for peer in (across, along):
        pl.semaphore_signal(barrier, inc=1, device_id={"batch": peer}, device_id_type=MESH)
    pl.semaphore_wait(barrier, 2)

    def remote(source, target, item, turn, peer):
        copy = pltpu.make_async_remote_copy(
            src_ref=source,
            dst_ref=target,
            send_sem=send_sem.at[item, turn],
            recv_sem=recv_sem.at[item, turn],
            device_id={"batch": peer},
            device_id_type=MESH,
        )
        copy.start()
        return copy

    firsts = [
        [
            remote(sources[item], results[item].at[me], item, turn, peer)
            for turn, peer in enumerate((across, along))
        ]
        for item in range(count)
    ]
    own = [
        pltpu.make_async_copy(sources[item], results[item].at[me], own_sem.at[item])
        for item in range(count)
    ]
    for copy in own:
        copy.start()
    seconds = []
    for item in range(count):
        columns = sources[item].shape[-1]
        cut = columns // 256 * 128
        halves = (pl.ds(0, cut), pl.ds(cut, columns - cut))
        for turn, (giver, taker) in enumerate(((across, along), (along, across))):
            firsts[item][turn].wait_recv()
            block = results[item].at[giver, :, halves[turn]]
            seconds.append(remote(block, block, item, 2 + turn, taker))
    for copy in own:
        copy.wait()
    for copy in seconds:
        copy.wait()
    for pair in firsts:
        for copy in pair:
            copy.wait_send()


def square_gather(collective_id, *arrays):
    count = len(arrays)
    return pl.pallas_call(
        functools.partial(square_kernel, count),
        out_shape=[jax.ShapeDtypeStruct((4, *a.shape), a.dtype) for a in arrays],
        in_specs=[pl.BlockSpec(memory_space=pltpu.VMEM)] * count,
        out_specs=[pl.BlockSpec(memory_space=pltpu.VMEM)] * count,
        scratch_shapes=[
            pltpu.SemaphoreType.DMA((count, 4)),
            pltpu.SemaphoreType.DMA((count, 4)),
            pltpu.SemaphoreType.DMA((count,)),
        ],
        compiler_params=pltpu.CompilerParams(collective_id=collective_id, has_side_effects=True),
    )(*arrays)


def halo_kernel(size, depth, direction, source_ref, result_ref, send_sem, recv_sem):
    me = lax.axis_index("ctx")
    barrier = pltpu.get_barrier_semaphore()
    for step in range(1, depth + 1):
        giver = me - direction * step

        @pl.when((giver >= 0) & (giver < size))
        def _():
            pl.semaphore_signal(barrier, inc=1, device_id={"ctx": giver}, device_id_type=MESH)

    takers = jnp.minimum(depth, size - 1 - me) if direction > 0 else jnp.minimum(depth, me)

    @pl.when(takers > 0)
    def _():
        pl.semaphore_wait(barrier, takers)

    def copy(step):
        slot = depth - step
        source = source_ref if direction > 0 else source_ref.at[slot]
        return pltpu.make_async_remote_copy(
            src_ref=source,
            dst_ref=result_ref.at[slot],
            send_sem=send_sem.at[step - 1],
            recv_sem=recv_sem.at[step - 1],
            device_id={"ctx": jnp.clip(me + direction * step, 0, size - 1)},
            device_id_type=MESH,
        )

    for step in range(depth, 0, -1):
        taker = me + direction * step

        @pl.when((taker >= 0) & (taker < size))
        def _():
            copy(step).start()

    for step in range(1, depth + 1):
        taker = me + direction * step
        giver = me - direction * step

        @pl.when((giver < 0) | (giver >= size))
        def _():
            result_ref[depth - step] = jnp.zeros(result_ref.shape[1:], result_ref.dtype)

        @pl.when((giver >= 0) & (giver < size))
        def _():
            copy(step).wait_recv()

        @pl.when((taker >= 0) & (taker < size))
        def _():
            copy(step).wait_send()


def halo_exchange(collective_id, size, depth, direction, block):
    return pl.pallas_call(
        functools.partial(halo_kernel, size, depth, direction),
        out_shape=jax.ShapeDtypeStruct((depth, *block.shape[-2:]), block.dtype),
        in_specs=[pl.BlockSpec(memory_space=pltpu.VMEM)],
        out_specs=pl.BlockSpec(memory_space=pltpu.VMEM),
        scratch_shapes=[pltpu.SemaphoreType.DMA((depth,)), pltpu.SemaphoreType.DMA((depth,))],
        compiler_params=pltpu.CompilerParams(collective_id=collective_id, has_side_effects=True),
    )(block)


def pick_kernel(n_batch, n_ctx, piece, padded, gate_ref, up_ref, out_ref):
    me = lax.axis_index("batch")
    out_ref[...] = jnp.zeros_like(out_ref)
    for spot in range(n_batch):

        @pl.when(me == spot)
        def _():
            for shard in range(n_ctx):
                start = (shard * n_batch + spot) * piece
                for half, ref in enumerate((gate_ref, up_ref)):
                    place = (half * n_ctx + shard) * padded
                    out_ref[:, place : place + piece] = ref[:, start : start + piece]


def row_block(rows):
    return 48 if rows % 48 == 0 else rows


def pick_columns(n_batch, n_ctx, piece, padded, w_gate, w_up):
    rows, hidden = w_gate.shape
    block = row_block(rows)
    spec = pl.BlockSpec((block, hidden), lambda i: (i, 0))
    return pl.pallas_call(
        functools.partial(pick_kernel, n_batch, n_ctx, piece, padded),
        name="pick_columns",
        grid=(rows // block,),
        out_shape=jax.ShapeDtypeStruct((rows, 2 * n_ctx * padded), w_gate.dtype),
        in_specs=[spec, spec],
        out_specs=pl.BlockSpec((block, 2 * n_ctx * padded), lambda i: (i, 0)),
    )(w_gate, w_up)


def place_kernel(n_batch, n_ctx, piece, padded, parts_ref, out_ref):
    for shard in range(n_ctx):
        for spot in range(n_batch):
            start = (shard * n_batch + spot) * piece
            place = shard * padded
            out_ref[:, start : start + piece] = parts_ref[spot, :, place : place + piece].astype(F32)


def place_columns(n_batch, n_ctx, piece, padded, parts):
    rows = parts.shape[1]
    block = row_block(rows)
    hidden = n_batch * n_ctx * piece
    return pl.pallas_call(
        functools.partial(place_kernel, n_batch, n_ctx, piece, padded),
        grid=(rows // block,),
        out_shape=jax.ShapeDtypeStruct((rows, hidden), F32),
        in_specs=[pl.BlockSpec((n_batch, block, n_ctx * padded), lambda i: (0, i, 0))],
        out_specs=pl.BlockSpec((block, hidden), lambda i: (i, 0)),
    )(parts)


def weights_kernel(n_batch, n_ctx, qkv_ref, proj_ref, gain_ref, qkv_all, proj_all, gain_all, *sems):
    send_far, recv_far, send_side, recv_side, send_near, recv_near, own_sem = sems
    spot = lax.axis_index("batch")
    me = lax.axis_index("ctx")
    n_chip = n_ctx // 2
    chip, core = me // 2, lax.rem(me, 2)
    near = {"ctx": me + 1 - 2 * core}
    barrier = pltpu.get_barrier_semaphore()

    def far_at(step):
        return {"ctx": 2 * lax.rem(chip + step, n_chip) + core}

    def side_at(step):
        return {"batch": lax.rem(spot + step, n_batch)}

    peers = [near]
    peers += [far_at(step) for step in range(1, n_chip)]
    peers += [side_at(step) for step in range(1, n_batch)]
    for peer in peers:
        pl.semaphore_signal(barrier, inc=1, device_id=peer, device_id_type=MESH)
    pl.semaphore_wait(barrier, len(peers))

    def remote(source, target, send, recv, peer):
        return pltpu.make_async_remote_copy(
            src_ref=source,
            dst_ref=target,
            send_sem=send,
            recv_sem=recv,
            device_id=peer,
            device_id_type=MESH,
        )

    waits = []
    far = []
    for step in range(1, n_chip):
        triple = [
            remote(source, target, send_far.at[step - 1, item], recv_far.at[step - 1, item], far_at(step))
            for item, (source, target) in enumerate(
                (
                    (qkv_ref.at[spot], qkv_all.at[spot, me]),
                    (proj_ref.at[spot], proj_all.at[me, spot]),
                    (gain_ref, gain_all.at[me]),
                )
            )
        ]
        for copy in triple:
            copy.start()
        far.append(triple)
    own = [
        pltpu.make_async_copy(qkv_ref, qkv_all.at[:, me], own_sem.at[0]),
        pltpu.make_async_copy(proj_ref, proj_all.at[me], own_sem.at[1]),
        pltpu.make_async_copy(gain_ref, gain_all.at[me], own_sem.at[2]),
    ]
    for copy in own:
        copy.start()
    first = n_chip - 1
    pairs = [
        remote(source, target, send_near.at[first, 0, item], recv_near.at[first, 0, item], near)
        for item, (source, target) in enumerate(
            (
                (qkv_ref, qkv_all.at[:, me]),
                (proj_ref, proj_all.at[me]),
                (gain_ref, gain_all.at[me]),
            )
        )
    ]
    for copy in pairs:
        copy.start()
    waits += pairs

    def hand_near(step, turn):
        origin = 2 * lax.rem(chip + n_chip - step, n_chip) + core
        quarter = lax.rem(spot + n_batch - turn, n_batch)
        blocks = [qkv_all.at[quarter, origin], proj_all.at[origin, quarter]]
        blocks += [gain_all.at[origin]] if turn == 0 else []
        for item, block in enumerate(blocks):
            copy = remote(
                block,
                block,
                send_near.at[step - 1, turn, item],
                recv_near.at[step - 1, turn, item],
                near,
            )
            copy.start()
            waits.append(copy)

    side = []
    for step in range(1, n_chip):
        for copy in far[step - 1]:
            copy.wait_recv()
        origin = 2 * lax.rem(chip + n_chip - step, n_chip) + core
        for turn in range(1, n_batch):
            pair = [
                remote(
                    block,
                    block,
                    send_side.at[step - 1, turn - 1, item],
                    recv_side.at[step - 1, turn - 1, item],
                    side_at(turn),
                )
                for item, block in enumerate((qkv_all.at[spot, origin], proj_all.at[origin, spot]))
            ]
            for copy in pair:
                copy.start()
            side.append((step, turn, pair))
        hand_near(step, 0)
    for step, turn, pair in side:
        for copy in pair:
            copy.wait_recv()
        hand_near(step, turn)
    for copy in waits:
        copy.wait()
    for copy in own:
        copy.wait()
    for triple in far:
        for copy in triple:
            copy.wait_send()
    for _, _, pair in side:
        for copy in pair:
            copy.wait_send()


def gather_weights(n_batch, n_ctx, qkv, proj, gains):
    n_chip = n_ctx // 2
    dma = pltpu.SemaphoreType.DMA
    vmem = pl.BlockSpec(memory_space=pltpu.VMEM)
    return pl.pallas_call(
        functools.partial(weights_kernel, n_batch, n_ctx),
        name="gather_weights",
        out_shape=(
            jax.ShapeDtypeStruct((n_batch, n_ctx, *qkv.shape[1:]), qkv.dtype),
            jax.ShapeDtypeStruct((n_ctx, *proj.shape), proj.dtype),
            jax.ShapeDtypeStruct((n_ctx, *gains.shape), gains.dtype),
        ),
        in_specs=[vmem] * 3,
        out_specs=[vmem] * 3,
        scratch_shapes=[
            dma((n_chip - 1, 3)),
            dma((n_chip - 1, 3)),
            dma((n_chip - 1, n_batch - 1, 2)),
            dma((n_chip - 1, n_batch - 1, 2)),
            dma((n_chip, n_batch, 3)),
            dma((n_chip, n_batch, 3)),
            dma((3,)),
        ],
        compiler_params=pltpu.CompilerParams(collective_id=12, has_side_effects=True),
    )(qkv, proj, gains)


def gathered(shard):
    return lax.all_gather(shard, "ctx", axis=0, tiled=True)


def scattered(whole):
    return lax.psum_scatter(whole, "ctx", scatter_dimension=0, tiled=True)


def local(
    n_batch,
    n_ctx,
    block_in,
    positions,
    counts,
    cotangent,
    gain_input,
    w_query,
    w_key,
    w_value,
    gain_query,
    gain_key,
    w_output,
    gain_attn,
    gain_ffn,
    w_gate,
    w_up,
    w_down,
    gain_final,
):
    block_in = block_in[0]
    positions = positions[0]
    cotangent = cotangent[0]
    tok_count, model_width = block_in.shape
    width_shard = w_query.shape[0]
    query_width = w_query.shape[1]
    head_size = w_key.shape[1]
    head_count = query_width // head_size
    hidden_shard = w_down.shape[0]
    piece = hidden_shard // n_batch
    hidden_part = -(-piece * n_ctx // 128) * 128
    padded = hidden_part // n_ctx
    halo_depth = (WINDOW + tok_count - 2) // tok_count
    batch_at = lax.axis_index("batch")
    ctx_at = lax.axis_index("ctx")
    all_tok = n_batch * tok_count

    gains = jnp.concatenate(
        [gain_input, gain_attn, gain_ffn, gain_final, gain_query, gain_key]
    )
    slots_of = query_width + 2 * head_size
    quarter = slots_of // n_batch
    qkv_full, proj_full, gains_all = gather_weights(
        n_batch,
        n_ctx,
        jnp.concatenate([w_query, w_key, w_value], axis=1)
        .reshape(width_shard, n_batch, quarter)
        .transpose(1, 0, 2),
        w_output.reshape(n_batch, -1, model_width),
        gains[None],
    )
    qkv_full = qkv_full.reshape(n_batch, model_width, quarter)
    full_output = proj_full.reshape(query_width, model_width)
    gains_all = gains_all[:, 0].astype(F32)

    def gain_at(start, length):
        return gains_all[:, start : start + length].reshape(1, -1)

    head_shard = gain_query.shape[0]
    full_gain_in = gain_at(0, width_shard)
    full_gain_attn = gain_at(width_shard, width_shard)
    full_gain_ffn = gain_at(2 * width_shard, width_shard)
    full_gain_final = gain_at(3 * width_shard, width_shard)
    full_gain_q = gain_at(4 * width_shard, head_shard)
    full_gain_k = gain_at(4 * width_shard + head_shard, head_shard)

    part_both = gathered(pick_columns(n_batch, n_ctx, piece, padded, w_gate, w_up))
    own_down = lax.dynamic_slice_in_dim(w_down, batch_at * piece, piece, 0)
    part_down = gathered(jnp.pad(own_down, ((0, padded - piece), (0, 0))))

    first_token = ctx_at * tok_count
    token_place = first_token + jnp.arange(tok_count, dtype=jnp.int32)
    valid_mask = (token_place < counts[0]).astype(F32)[:, None]
    resid_in = block_in.astype(F32)
    act_in = normed(resid_in, full_gain_in).astype(BF16)
    qkv_raw = jnp.concatenate([project(act_in, qkv_full[i]) for i in range(n_batch)], axis=1)
    query_raw = qkv_raw[:, :query_width].reshape(tok_count, head_count, head_size)
    key_raw = qkv_raw[:, query_width : query_width + head_size]
    value_low = qkv_raw[:, query_width + head_size :].astype(BF16)
    inv_freq = BASE ** (-jnp.arange(0, head_size, 2, dtype=F32) / head_size)
    angles = positions.astype(F32)[:, None] * inv_freq

    def query_path(raw_query, gain_vec):
        return rotate(normed(raw_query, gain_vec), angles[:, None, :])

    def key_path(raw_key, gain_vec):
        return rotate(normed(raw_key, gain_vec), angles)

    query_rot = query_path(query_raw, full_gain_q).astype(BF16)
    key_rot = key_path(key_raw, full_gain_k).astype(BF16)
    own_pair = jnp.concatenate([key_rot, value_low], axis=-1)
    halo = halo_exchange(1, n_ctx, halo_depth, 1, own_pair)
    context = jnp.concatenate([halo.reshape(halo_depth * tok_count, -1), own_pair], axis=0)
    ctx_keys = context[:, :head_size]
    ctx_values = context[:, head_size:]
    key_total = (halo_depth + 1) * tok_count
    distance = (
        jnp.arange(tok_count, dtype=jnp.int32)[:, None]
        + halo_depth * tok_count
        - jnp.arange(key_total, dtype=jnp.int32)[None, :]
    )
    allowed = (distance >= 0) & (distance < WINDOW) & (distance <= positions[:, None])
    score_scale = head_size ** (-0.5)
    raw_scores = jnp.einsum("thd,kd->htk", query_rot, ctx_keys, preferred_element_type=F32)
    scores = jnp.where(allowed[None], raw_scores * score_scale, MASKED)
    exp_scores = jnp.exp(scores - jnp.max(scores, axis=-1, keepdims=True))
    attn_prob = exp_scores / jnp.sum(exp_scores, axis=-1, keepdims=True)
    prob_low = attn_prob.astype(BF16)
    attended = jnp.einsum("htk,kd->thd", prob_low, ctx_values, preferred_element_type=F32)
    attn_low = attended.reshape(tok_count, query_width).astype(BF16)
    attn_proj = project(attn_low, full_output)
    middle = resid_in + normed(attn_proj, full_gain_attn)
    ffn_in = normed(middle, full_gain_ffn).astype(BF16)

    (ffn_in_all,) = square_gather(2, ffn_in)
    ffn_in_all = ffn_in_all.reshape(all_tok, model_width)
    both_pre = project(ffn_in_all, part_both)
    gate_pre, up_pre = both_pre[:, :hidden_part], both_pre[:, hidden_part:]
    mixed_low = gated_gelu(gate_pre, up_pre).astype(BF16)
    mixed_low, act_in_late, attn_late = lax.optimization_barrier((mixed_low, act_in, attn_low))
    act_in_all, attn_all = square_gather(13, act_in_late, attn_late)
    mixed_low, act_in_all, attn_all = lax.optimization_barrier((mixed_low, act_in_all, attn_all))
    act_in_all = act_in_all.reshape(all_tok, model_width)
    attn_all = attn_all.reshape(all_tok, query_width)
    proj_part = project(mixed_low, part_down).astype(BF16)
    (proj_parts,) = batch_exchange(
        3, n_batch, slots=(proj_part.reshape(n_batch, tok_count, model_width),)
    )
    ffn_proj = jnp.sum(proj_parts.astype(F32), axis=0)
    final_sum = middle + normed(ffn_proj, full_gain_final)
    block_out = (final_sum * valid_mask).astype(BF16)

    grad_final = cotangent.astype(F32) * valid_mask
    _, pull_final = jax.vjp(normed, ffn_proj, full_gain_final)
    grad_ffn_proj, grad_gain_final = pull_final(grad_final)
    (grad_ffn_low,) = square_gather(4, grad_ffn_proj.astype(BF16))
    grad_ffn_low = grad_ffn_low.reshape(all_tok, model_width)
    down_grad = weight_grad(mixed_low, grad_ffn_low).astype(BF16)
    down_grad, grad_ffn_low = lax.optimization_barrier((down_grad, grad_ffn_low))
    grad_w_down = scattered(down_grad)
    grad_mixed = project_back(grad_ffn_low, part_down)
    _, pull_gelu = jax.vjp(gated_gelu, gate_pre, up_pre)
    grad_gate, grad_up = pull_gelu(grad_mixed)
    grad_gate_low = grad_gate.astype(BF16)
    grad_up_low = grad_up.astype(BF16)
    grad_both_low = jnp.concatenate([grad_gate_low, grad_up_low], axis=1)
    back_part = project_back(grad_both_low, part_both).astype(BF16)
    (back_parts,) = batch_exchange(
        5, n_batch, slots=(back_part.reshape(n_batch, tok_count, model_width),)
    )
    back_parts, grad_gate_low, grad_up_low = lax.optimization_barrier(
        (back_parts, grad_gate_low, grad_up_low)
    )
    gate_grad = weight_grad(ffn_in_all, grad_gate_low).astype(BF16)
    up_grad = weight_grad(ffn_in_all, grad_up_low).astype(BF16)
    back_parts, gate_grad, up_grad = lax.optimization_barrier((back_parts, gate_grad, up_grad))
    grad_w_gate = scattered(gate_grad)
    grad_w_up = scattered(up_grad)
    grad_ffn_in = jnp.sum(back_parts.astype(F32), axis=0)
    _, pull_ffn_norm = jax.vjp(normed, middle, full_gain_ffn)
    grad_middle_part, grad_gain_ffn = pull_ffn_norm(grad_ffn_in)
    grad_middle = grad_final + grad_middle_part
    _, pull_attn_norm = jax.vjp(normed, attn_proj, full_gain_attn)
    grad_attn_proj, grad_gain_attn = pull_attn_norm(grad_middle)

    grad_proj_low = grad_attn_proj.astype(BF16)
    grad_attended = (
        project_back(grad_proj_low, full_output)
        .astype(BF16)
        .reshape(tok_count, head_count, head_size)
    )
    grad_prob = jnp.einsum("thd,kd->htk", grad_attended, ctx_values, preferred_element_type=F32)
    row_delta = jnp.sum(attn_prob * grad_prob, axis=-1, keepdims=True)
    grad_scores = (attn_prob * (grad_prob - row_delta)).astype(BF16)
    grad_queries = (
        jnp.einsum("htk,kd->thd", grad_scores, ctx_keys, preferred_element_type=F32) * score_scale
    )
    grad_ctx_keys = (
        jnp.einsum("htk,thd->kd", grad_scores, query_rot, preferred_element_type=F32) * score_scale
    )
    grad_ctx_values = jnp.einsum("htk,thd->kd", prob_low, grad_attended, preferred_element_type=F32)
    grad_context = jnp.concatenate([grad_ctx_keys, grad_ctx_values], axis=-1)
    halo_rows = halo_depth * tok_count
    returned = halo_exchange(
        6,
        n_ctx,
        halo_depth,
        -1,
        grad_context[:halo_rows].astype(BF16).reshape(halo_depth, tok_count, 2 * head_size),
    )
    own_grad = grad_context[halo_rows:] + jnp.sum(returned.astype(F32), axis=0)
    grad_value_low = own_grad[:, head_size:].astype(BF16)
    _, pull_key = jax.vjp(key_path, key_raw, full_gain_k)
    grad_key_raw, grad_gain_key = pull_key(own_grad[:, :head_size])
    _, pull_query = jax.vjp(query_path, query_raw, full_gain_q)
    grad_query_raw, grad_gain_query = pull_query(grad_queries)
    grad_qkv_low = jnp.concatenate(
        [
            grad_query_raw.astype(BF16).reshape(tok_count, query_width),
            grad_key_raw.astype(BF16),
            grad_value_low,
        ],
        axis=1,
    )
    grad_act_in = sum(
        project_back(grad_qkv_low[:, i * quarter : (i + 1) * quarter], qkv_full[i])
        for i in range(n_batch)
    )
    _, pull_input = jax.vjp(normed, resid_in, full_gain_in)
    grad_in_part, grad_gain_input = pull_input(grad_act_in)
    grad_in = (grad_middle + grad_in_part).astype(BF16)

    def column_slots(upstream):
        return upstream.reshape(tok_count, n_batch, -1).transpose(1, 0, 2)

    gain_rows = jnp.concatenate(
        [
            grad.reshape(n_ctx, -1)
            for grad in (
                grad_gain_input,
                grad_gain_attn,
                grad_gain_ffn,
                grad_gain_final,
                grad_gain_query,
                grad_gain_key,
            )
        ],
        axis=1,
    )
    gain_parts, qkv_slots, proj_slots = batch_exchange(
        7,
        n_batch,
        whole=(gain_rows,),
        slots=(column_slots(grad_qkv_low), column_slots(grad_proj_low)),
    )
    proj_rows = w_output.shape[0]
    gain_count = gain_rows.shape[1]
    gain_lines = -(-gain_count // quarter)
    used = width_shard + proj_rows + gain_lines
    lines = -(-used // 16) * 16
    grad_w_output = weight_grad(attn_all, proj_slots.reshape(all_tok, -1)).astype(BF16)
    grad_w_qkv = weight_grad(act_in_all, qkv_slots.reshape(all_tok, -1)).astype(BF16)
    output_part = model_width // n_batch
    gain_sum = jnp.sum(gain_parts, axis=0).astype(BF16)
    packed = jnp.concatenate(
        [
            grad_w_qkv.reshape(n_ctx, width_shard, quarter),
            jnp.pad(
                grad_w_output.reshape(n_ctx, proj_rows, output_part),
                ((0, 0), (0, 0), (0, quarter - output_part)),
            ),
            jnp.pad(gain_sum, ((0, 0), (0, gain_lines * quarter - gain_count))).reshape(
                n_ctx, gain_lines, quarter
            ),
            jnp.zeros((n_ctx, lines - used, quarter), BF16),
        ],
        axis=1,
    )
    attn_sum = scattered(packed.reshape(n_ctx * lines, quarter))

    down_all, gate_all = square_gather(8, grad_w_down, grad_w_gate)
    (up_all,) = square_gather(9, grad_w_up)
    (attn_grads,) = square_gather(11, attn_sum)
    gain_mine = attn_grads[0, width_shard + proj_rows : used].reshape(-1).astype(F32)

    def columns_back(pieces):
        return pieces.astype(F32).transpose(1, 0, 2).reshape(pieces.shape[1], -1)

    grad_qkv_shard = columns_back(attn_grads[:, :width_shard])
    return (
        block_out[None],
        grad_in[None],
        gain_mine[:width_shard],
        grad_qkv_shard[:, :query_width],
        grad_qkv_shard[:, query_width : query_width + head_size],
        grad_qkv_shard[:, query_width + head_size :],
        gain_mine[4 * width_shard : 4 * width_shard + head_shard],
        gain_mine[4 * width_shard + head_shard : gain_count],
        columns_back(attn_grads[:, width_shard : width_shard + proj_rows, :output_part]),
        gain_mine[width_shard : 2 * width_shard],
        gain_mine[2 * width_shard : 3 * width_shard],
        place_columns(n_batch, n_ctx, piece, padded, gate_all),
        place_columns(n_batch, n_ctx, piece, padded, up_all),
        down_all[:, :piece].reshape(hidden_shard, model_width).astype(F32),
        gain_mine[3 * width_shard : 4 * width_shard],
    )


def solution(mesh):
    matrix = P("ctx", None)
    vector = P("ctx")
    tokens = P("batch", "ctx", None)

    def step(*arrays):
        return local(mesh.shape["batch"], mesh.shape["ctx"], *arrays)

    return jax.shard_map(
        step,
        mesh=mesh,
        in_specs=(
            tokens,
            P("batch", "ctx"),
            P("batch"),
            tokens,
            vector,
            matrix,
            matrix,
            matrix,
            vector,
            vector,
            matrix,
            vector,
            vector,
            matrix,
            matrix,
            matrix,
            vector,
        ),
        out_specs=(
            tokens,
            tokens,
            vector,
            matrix,
            matrix,
            matrix,
            vector,
            vector,
            matrix,
            vector,
            vector,
            matrix,
            matrix,
            matrix,
            vector,
        ),
        check_vma=False,
    )
```

```python
import functools

import jax
import jax.numpy as jnp
from jax import lax
from jax.experimental import pallas as pl
from jax.experimental.pallas import tpu as pltpu
from jax.sharding import PartitionSpec as P

WINDOW = 512


EPS = 1e-06
BASE = 10000.0
MASKED = -1e30
BF16 = jnp.bfloat16
F32 = jnp.float32
MESH = pl.DeviceIdType.MESH


def normed(vector, gain_vec):
    return vector * lax.rsqrt(jnp.mean(vector * vector, axis=-1, keepdims=True) + EPS) * gain_vec


def rotate(vector, angles):
    half_size = vector.shape[-1] // 2
    cosine = jnp.cos(angles)
    sine_part = jnp.sin(angles)
    first_half = vector[..., :half_size]
    second = vector[..., half_size:]
    return jnp.concatenate(
        [first_half * cosine - second * sine_part, second * cosine + first_half * sine_part],
        axis=-1,
    )


def project(inputs, weight):
    return lax.dot_general(inputs, weight, (((1,), (0,)), ((), ())), preferred_element_type=F32)


def project_back(upstream, weight):
    return lax.dot_general(upstream, weight, (((1,), (1,)), ((), ())), preferred_element_type=F32)


def weight_grad(inputs, upstream):
    return lax.dot_general(inputs, upstream, (((0,), (0,)), ((), ())), preferred_element_type=F32)


def gated_gelu(gate_val, up_val):
    return jax.nn.gelu(gate_val, approximate=True) * up_val


def batch_kernel(size, kinds, *refs):
    count = len(kinds)
    sources, results = refs[:count], refs[count : 2 * count]
    send_sem, recv_sem, own_sem = refs[2 * count :]
    me = lax.axis_index("batch")
    barrier = pltpu.get_barrier_semaphore()
    for step in range(1, size):
        pl.semaphore_signal(
            barrier, inc=1, device_id={"batch": lax.rem(me + step, size)}, device_id_type=MESH
        )
    pl.semaphore_wait(barrier, size - 1)
    copies = []
    for step in range(1, size):
        peer = lax.rem(me + step, size)
        for item in range(count):
            source = sources[item].at[peer] if kinds[item] else sources[item]
            copies.append(
                pltpu.make_async_remote_copy(
                    src_ref=source,
                    dst_ref=results[item].at[me],
                    send_sem=send_sem.at[item, step - 1],
                    recv_sem=recv_sem.at[item, step - 1],
                    device_id={"batch": peer},
                    device_id_type=MESH,
                )
            )
    for copy in copies:
        copy.start()
    own = []
    for item in range(count):
        source = sources[item].at[me] if kinds[item] else sources[item]
        own.append(pltpu.make_async_copy(source, results[item].at[me], own_sem.at[item]))
    for copy in own:
        copy.start()
    for copy in own:
        copy.wait()
    for copy in copies:
        copy.wait()


def batch_exchange(collective_id, size, whole=(), slots=()):
    arrays = list(whole) + list(slots)
    kinds = [0] * len(whole) + [1] * len(slots)
    count = len(arrays)
    shapes = [
        jax.ShapeDtypeStruct(a.shape if k else (size, *a.shape), a.dtype)
        for a, k in zip(arrays, kinds)
    ]
    return pl.pallas_call(
        functools.partial(batch_kernel, size, kinds),
        out_shape=shapes,
        in_specs=[pl.BlockSpec(memory_space=pltpu.VMEM)] * count,
        out_specs=[pl.BlockSpec(memory_space=pltpu.VMEM)] * count,
        scratch_shapes=[
            pltpu.SemaphoreType.DMA((count, size - 1)),
            pltpu.SemaphoreType.DMA((count, size - 1)),
            pltpu.SemaphoreType.DMA((count,)),
        ],
        compiler_params=pltpu.CompilerParams(collective_id=collective_id, has_side_effects=True),
    )(*arrays)


def square_kernel(count, *refs):
    sources, results = refs[:count], refs[count : 2 * count]
    send_sem, recv_sem, own_sem = refs[2 * count :]
    me = lax.axis_index("batch")
    across = me + 1 - 2 * lax.rem(me, 2)
    along = lax.rem(me + 2, 4)
    barrier = pltpu.get_barrier_semaphore()
    for peer in (across, along):
        pl.semaphore_signal(barrier, inc=1, device_id={"batch": peer}, device_id_type=MESH)
    pl.semaphore_wait(barrier, 2)

    def remote(source, target, item, turn, peer):
        copy = pltpu.make_async_remote_copy(
            src_ref=source,
            dst_ref=target,
            send_sem=send_sem.at[item, turn],
            recv_sem=recv_sem.at[item, turn],
            device_id={"batch": peer},
            device_id_type=MESH,
        )
        copy.start()
        return copy

    firsts = [
        [
            remote(sources[item], results[item].at[me], item, turn, peer)
            for turn, peer in enumerate((across, along))
        ]
        for item in range(count)
    ]
    own = [
        pltpu.make_async_copy(sources[item], results[item].at[me], own_sem.at[item])
        for item in range(count)
    ]
    for copy in own:
        copy.start()
    seconds = []
    for item in range(count):
        columns = sources[item].shape[-1]
        cut = columns // 256 * 128
        halves = (pl.ds(0, cut), pl.ds(cut, columns - cut))
        for turn, (giver, taker) in enumerate(((across, along), (along, across))):
            firsts[item][turn].wait_recv()
            block = results[item].at[giver, :, halves[turn]]
            seconds.append(remote(block, block, item, 2 + turn, taker))
    for copy in own:
        copy.wait()
    for copy in seconds:
        copy.wait()
    for pair in firsts:
        for copy in pair:
            copy.wait_send()


def square_gather(collective_id, *arrays):
    count = len(arrays)
    return pl.pallas_call(
        functools.partial(square_kernel, count),
        out_shape=[jax.ShapeDtypeStruct((4, *a.shape), a.dtype) for a in arrays],
        in_specs=[pl.BlockSpec(memory_space=pltpu.VMEM)] * count,
        out_specs=[pl.BlockSpec(memory_space=pltpu.VMEM)] * count,
        scratch_shapes=[
            pltpu.SemaphoreType.DMA((count, 4)),
            pltpu.SemaphoreType.DMA((count, 4)),
            pltpu.SemaphoreType.DMA((count,)),
        ],
        compiler_params=pltpu.CompilerParams(collective_id=collective_id, has_side_effects=True),
    )(*arrays)


def turn_kernel(
    mixed_ref,
    down_ref,
    middle_ref,
    upstream_ref,
    valid_ref,
    gain_ref,
    out_ref,
    grads_ref,
    gain_grad_ref,
    part_ref,
    taken_ref,
    send_sem,
    recv_sem,
    pass_sem,
    take_sem,
):
    me = lax.axis_index("batch")
    across = me + 1 - 2 * lax.rem(me, 2)
    along = lax.rem(me + 2, 4)
    corner = lax.rem(across + 2, 4)
    order = (corner, across, along)
    tok_count = middle_ref.shape[0]
    barrier = pltpu.get_barrier_semaphore()
    for peer in order:
        pl.semaphore_signal(barrier, inc=1, device_id={"batch": peer}, device_id_type=MESH)
    pl.semaphore_wait(barrier, 3)

    def product(place):
        rows = pl.ds(pl.multiple_of(place * tok_count, tok_count), tok_count)
        return jnp.dot(mixed_ref[rows, :], down_ref[...], preferred_element_type=F32)

    copies = [
        pltpu.make_async_remote_copy(
            src_ref=part_ref.at[turn],
            dst_ref=taken_ref.at[turn],
            send_sem=send_sem.at[turn],
            recv_sem=recv_sem.at[turn],
            device_id={"batch": peer},
            device_id_type=MESH,
        )
        for turn, peer in enumerate(order)
    ]
    for turn, peer in enumerate(order):
        part_ref[turn] = product(peer).astype(BF16)
        if turn > 0:
            copies[turn - 1].start()
    total = product(me)
    copies[2].start()
    for turn in range(3):
        copies[turn].wait_recv()
        total = total + taken_ref[turn].astype(F32)
    gain = gain_ref[...]
    valid = valid_ref[...]
    scale = lax.rsqrt(jnp.mean(total * total, axis=-1, keepdims=True) + EPS)
    upstream = upstream_ref[...].astype(F32) * valid
    gained = upstream * gain
    back = scale * gained - total * (
        scale * scale * scale * jnp.mean(total * gained, axis=-1, keepdims=True)
    )
    grads_ref[me] = back.astype(BF16)
    unit = total * scale
    out_ref[...] = ((middle_ref[...] + unit * gain) * valid).astype(BF16)
    gain_grad_ref[...] = jnp.sum(upstream * unit, axis=0, keepdims=True)

    def remote(block, turn, peer):
        copy = pltpu.make_async_remote_copy(
            src_ref=block,
            dst_ref=block,
            send_sem=pass_sem.at[turn],
            recv_sem=take_sem.at[turn],
            device_id={"batch": peer},
            device_id_type=MESH,
        )
        copy.start()
        return copy

    firsts = [remote(grads_ref.at[me], turn, peer) for turn, peer in enumerate((across, along))]
    columns = grads_ref.shape[-1]
    cut = columns // 256 * 128
    halves = (pl.ds(0, cut), pl.ds(cut, columns - cut))
    seconds = []
    for turn, (giver, taker) in enumerate(((across, along), (along, across))):
        firsts[turn].wait_recv()
        seconds.append(remote(grads_ref.at[giver, :, halves[turn]], 2 + turn, taker))
    for copy in seconds:
        copy.wait()
    for copy in firsts + copies:
        copy.wait_send()


def turn_round(mixed, down, middle, upstream, valid, gain):
    tok_count, width = middle.shape
    dma = pltpu.SemaphoreType.DMA
    vmem = pl.BlockSpec(memory_space=pltpu.VMEM)
    flops = 2 * mixed.shape[0] * mixed.shape[1] * width
    return pl.pallas_call(
        turn_kernel,
        name="turn_round",
        out_shape=(
            jax.ShapeDtypeStruct((tok_count, width), BF16),
            jax.ShapeDtypeStruct((4, tok_count, width), BF16),
            jax.ShapeDtypeStruct((1, width), F32),
        ),
        in_specs=[vmem] * 6,
        out_specs=[vmem] * 3,
        scratch_shapes=[
            pltpu.VMEM((3, tok_count, width), BF16),
            pltpu.VMEM((3, tok_count, width), BF16),
            dma((3,)),
            dma((3,)),
            dma((4,)),
            dma((4,)),
        ],
        cost_estimate=pl.CostEstimate(flops=flops, bytes_accessed=8 << 20, transcendentals=0),
        compiler_params=pltpu.CompilerParams(collective_id=3, has_side_effects=True),
    )(mixed, down, middle, upstream, valid, gain)


def product_kernel(left_ref, right_ref, out_ref):
    out_ref[...] = jnp.dot(left_ref[...], right_ref[...], preferred_element_type=F32).astype(BF16)


def product_low(tile, left, right):
    rows, depth = left.shape
    columns = right.shape[1]
    return pl.pallas_call(
        product_kernel,
        grid=(columns // tile,),
        out_shape=jax.ShapeDtypeStruct((rows, columns), BF16),
        in_specs=[
            pl.BlockSpec((rows, depth), lambda i: (0, 0)),
            pl.BlockSpec((depth, tile), lambda i: (0, i)),
        ],
        out_specs=pl.BlockSpec((rows, tile), lambda i: (0, i)),
        cost_estimate=pl.CostEstimate(
            flops=2 * rows * depth * columns, bytes_accessed=8 << 20, transcendentals=0
        ),
    )(left, right)


def mix_kernel(tokens_ref, w_gate_ref, w_up_ref, gate_ref, up_ref, mixed_ref, turned_ref):
    gate = project(tokens_ref[...], w_gate_ref[...])
    up = project(tokens_ref[...], w_up_ref[...])
    gate_ref[...] = gate
    up_ref[...] = up
    mixed = gated_gelu(gate, up)
    mixed_ref[...] = mixed.astype(BF16)
    turned_ref[...] = mixed.T.astype(BF16)


def hidden_mix(tile, tokens, both_weights):
    count, width = tokens.shape
    hidden = both_weights.shape[1] // 2
    steps = hidden // tile
    wide = jax.ShapeDtypeStruct((count, hidden), F32)
    column = pl.BlockSpec((count, tile), lambda i: (0, i))
    return pl.pallas_call(
        mix_kernel,
        name="hidden_mix",
        grid=(steps,),
        out_shape=(
            wide,
            wide,
            jax.ShapeDtypeStruct((count, hidden), BF16),
            jax.ShapeDtypeStruct((hidden, count), BF16),
        ),
        in_specs=[
            pl.BlockSpec((count, width), lambda i: (0, 0)),
            pl.BlockSpec((width, tile), lambda i: (0, i)),
            pl.BlockSpec((width, tile), lambda i: (0, i + steps)),
        ],
        out_specs=[column, column, column, pl.BlockSpec((tile, count), lambda i: (i, 0))],
        cost_estimate=pl.CostEstimate(
            flops=4 * count * hidden * width, bytes_accessed=24 << 20, transcendentals=0
        ),
    )(tokens, both_weights, both_weights)


def back_kernel(
    upstream_ref, down_ref, gate_ref, up_ref, w_gate_ref, w_up_ref, gate_out, up_out, back_ref, total
):
    step = pl.program_id(0)
    grad_mixed = project_back(upstream_ref[...], down_ref[...])
    _, pull_gelu = jax.vjp(gated_gelu, gate_ref[...], up_ref[...])
    grad_gate, grad_up = pull_gelu(grad_mixed)
    grad_gate, grad_up = grad_gate.astype(BF16), grad_up.astype(BF16)
    gate_out[...] = grad_gate
    up_out[...] = grad_up
    part = project_back(grad_gate, w_gate_ref[...]) + project_back(grad_up, w_up_ref[...])

    @pl.when(step == 0)
    def _():
        total[...] = part

    @pl.when(step > 0)
    def _():
        total[...] += part

    @pl.when(step == pl.num_programs(0) - 1)
    def _():
        back_ref[...] = total[...].astype(BF16)


def hidden_back(tile, upstream, down, gate_pre, up_pre, both_weights):
    tokens, width = upstream.shape
    hidden = down.shape[0]
    count = hidden // tile
    low = jax.ShapeDtypeStruct((tokens, hidden), BF16)
    return pl.pallas_call(
        back_kernel,
        name="hidden_back",
        grid=(count,),
        out_shape=(low, low, jax.ShapeDtypeStruct((tokens, width), BF16)),
        in_specs=[
            pl.BlockSpec((tokens, width), lambda i: (0, 0)),
            pl.BlockSpec((tile, width), lambda i: (i, 0)),
            pl.BlockSpec((tokens, tile), lambda i: (0, i)),
            pl.BlockSpec((tokens, tile), lambda i: (0, i)),
            pl.BlockSpec((width, tile), lambda i: (0, i)),
            pl.BlockSpec((width, tile), lambda i: (0, i + count)),
        ],
        out_specs=[
            pl.BlockSpec((tokens, tile), lambda i: (0, i)),
            pl.BlockSpec((tokens, tile), lambda i: (0, i)),
            pl.BlockSpec((tokens, width), lambda i: (0, 0)),
        ],
        scratch_shapes=[pltpu.VMEM((tokens, width), F32)],
        cost_estimate=pl.CostEstimate(
            flops=6 * tokens * hidden * width, bytes_accessed=24 << 20, transcendentals=0
        ),
    )(upstream, down, gate_pre, up_pre, both_weights, both_weights)


def halo_kernel(size, depth, direction, source_ref, result_ref, send_sem, recv_sem):
    me = lax.axis_index("ctx")
    barrier = pltpu.get_barrier_semaphore()
    for step in range(1, depth + 1):
        giver = me - direction * step

        @pl.when((giver >= 0) & (giver < size))
        def _():
            pl.semaphore_signal(barrier, inc=1, device_id={"ctx": giver}, device_id_type=MESH)

    takers = jnp.minimum(depth, size - 1 - me) if direction > 0 else jnp.minimum(depth, me)

    @pl.when(takers > 0)
    def _():
        pl.semaphore_wait(barrier, takers)

    def copy(step):
        slot = depth - step
        source = source_ref if direction > 0 else source_ref.at[slot]
        return pltpu.make_async_remote_copy(
            src_ref=source,
            dst_ref=result_ref.at[slot],
            send_sem=send_sem.at[step - 1],
            recv_sem=recv_sem.at[step - 1],
            device_id={"ctx": jnp.clip(me + direction * step, 0, size - 1)},
            device_id_type=MESH,
        )

    for step in range(depth, 0, -1):
        taker = me + direction * step

        @pl.when((taker >= 0) & (taker < size))
        def _():
            copy(step).start()

    for step in range(1, depth + 1):
        taker = me + direction * step
        giver = me - direction * step

        @pl.when((giver < 0) | (giver >= size))
        def _():
            result_ref[depth - step] = jnp.zeros(result_ref.shape[1:], result_ref.dtype)

        @pl.when((giver >= 0) & (giver < size))
        def _():
            copy(step).wait_recv()

        @pl.when((taker >= 0) & (taker < size))
        def _():
            copy(step).wait_send()


def halo_exchange(collective_id, size, depth, direction, block):
    return pl.pallas_call(
        functools.partial(halo_kernel, size, depth, direction),
        out_shape=jax.ShapeDtypeStruct((depth, *block.shape[-2:]), block.dtype),
        in_specs=[pl.BlockSpec(memory_space=pltpu.VMEM)],
        out_specs=pl.BlockSpec(memory_space=pltpu.VMEM),
        scratch_shapes=[pltpu.SemaphoreType.DMA((depth,)), pltpu.SemaphoreType.DMA((depth,))],
        compiler_params=pltpu.CompilerParams(collective_id=collective_id, has_side_effects=True),
    )(block)


def pick_kernel(n_batch, n_ctx, piece, padded, gate_ref, up_ref, out_ref):
    me = lax.axis_index("batch")
    out_ref[...] = jnp.zeros_like(out_ref)
    for spot in range(n_batch):

        @pl.when(me == spot)
        def _():
            for shard in range(n_ctx):
                start = (shard * n_batch + spot) * piece
                for half, ref in enumerate((gate_ref, up_ref)):
                    place = (half * n_ctx + shard) * padded
                    out_ref[:, place : place + piece] = ref[:, start : start + piece]


def row_block(rows):
    return 16 if rows % 16 == 0 else rows


def pick_columns(n_batch, n_ctx, piece, padded, w_gate, w_up):
    rows, hidden = w_gate.shape
    block = row_block(rows)
    spec = pl.BlockSpec((block, hidden), lambda i: (i, 0))
    return pl.pallas_call(
        functools.partial(pick_kernel, n_batch, n_ctx, piece, padded),
        name="pick_columns",
        grid=(rows // block,),
        out_shape=jax.ShapeDtypeStruct((rows, 2 * n_ctx * padded), w_gate.dtype),
        in_specs=[spec, spec],
        out_specs=pl.BlockSpec((block, 2 * n_ctx * padded), lambda i: (i, 0)),
    )(w_gate, w_up)


def place_kernel(n_batch, n_ctx, piece, padded, parts_ref, out_ref):
    for shard in range(n_ctx):
        for spot in range(n_batch):
            start = (shard * n_batch + spot) * piece
            place = shard * padded
            out_ref[:, start : start + piece] = parts_ref[spot, :, place : place + piece].astype(F32)


def place_columns(n_batch, n_ctx, piece, padded, parts):
    rows = parts.shape[1]
    block = row_block(rows)
    hidden = n_batch * n_ctx * piece
    return pl.pallas_call(
        functools.partial(place_kernel, n_batch, n_ctx, piece, padded),
        grid=(rows // block,),
        out_shape=jax.ShapeDtypeStruct((rows, hidden), F32),
        in_specs=[pl.BlockSpec((n_batch, block, n_ctx * padded), lambda i: (0, i, 0))],
        out_specs=pl.BlockSpec((block, hidden), lambda i: (i, 0)),
    )(parts)


def weights_kernel(n_batch, n_ctx, qkv_ref, proj_ref, gain_ref, qkv_all, proj_all, gain_all, *sems):
    send_far, recv_far, send_side, recv_side, send_near, recv_near, own_sem = sems
    spot = lax.axis_index("batch")
    me = lax.axis_index("ctx")
    n_chip = n_ctx // 2
    chip, core = me // 2, lax.rem(me, 2)
    near = {"ctx": me + 1 - 2 * core}
    barrier = pltpu.get_barrier_semaphore()

    def far_at(step):
        return {"ctx": 2 * lax.rem(chip + step, n_chip) + core}

    def side_at(step):
        return {"batch": lax.rem(spot + step, n_batch)}

    peers = [near]
    peers += [far_at(step) for step in range(1, n_chip)]
    peers += [side_at(step) for step in range(1, n_batch)]
    for peer in peers:
        pl.semaphore_signal(barrier, inc=1, device_id=peer, device_id_type=MESH)
    pl.semaphore_wait(barrier, len(peers))

    def remote(source, target, send, recv, peer):
        return pltpu.make_async_remote_copy(
            src_ref=source,
            dst_ref=target,
            send_sem=send,
            recv_sem=recv,
            device_id=peer,
            device_id_type=MESH,
        )

    waits = []
    far = []
    for step in range(1, n_chip):
        triple = [
            remote(source, target, send_far.at[step - 1, item], recv_far.at[step - 1, item], far_at(step))
            for item, (source, target) in enumerate(
                (
                    (qkv_ref.at[spot], qkv_all.at[spot, me]),
                    (proj_ref.at[spot], proj_all.at[me, spot]),
                    (gain_ref, gain_all.at[me]),
                )
            )
        ]
        for copy in triple:
            copy.start()
        far.append(triple)
    own = [
        pltpu.make_async_copy(qkv_ref, qkv_all.at[:, me], own_sem.at[0]),
        pltpu.make_async_copy(proj_ref, proj_all.at[me], own_sem.at[1]),
        pltpu.make_async_copy(gain_ref, gain_all.at[me], own_sem.at[2]),
    ]
    for copy in own:
        copy.start()
    first = n_chip - 1
    pairs = [
        remote(source, target, send_near.at[first, 0, item], recv_near.at[first, 0, item], near)
        for item, (source, target) in enumerate(
            (
                (qkv_ref, qkv_all.at[:, me]),
                (proj_ref, proj_all.at[me]),
                (gain_ref, gain_all.at[me]),
            )
        )
    ]
    for copy in pairs:
        copy.start()
    waits += pairs

    def hand_near(step, turn):
        origin = 2 * lax.rem(chip + n_chip - step, n_chip) + core
        quarter = lax.rem(spot + n_batch - turn, n_batch)
        blocks = [qkv_all.at[quarter, origin], proj_all.at[origin, quarter]]
        blocks += [gain_all.at[origin]] if turn == 0 else []
        for item, block in enumerate(blocks):
            copy = remote(
                block,
                block,
                send_near.at[step - 1, turn, item],
                recv_near.at[step - 1, turn, item],
                near,
            )
            copy.start()
            waits.append(copy)

    side = []
    for step in range(1, n_chip):
        for copy in far[step - 1]:
            copy.wait_recv()
        origin = 2 * lax.rem(chip + n_chip - step, n_chip) + core
        for turn in range(1, n_batch):
            pair = [
                remote(
                    block,
                    block,
                    send_side.at[step - 1, turn - 1, item],
                    recv_side.at[step - 1, turn - 1, item],
                    side_at(turn),
                )
                for item, block in enumerate((qkv_all.at[spot, origin], proj_all.at[origin, spot]))
            ]
            for copy in pair:
                copy.start()
            side.append((step, turn, pair))
        hand_near(step, 0)
    for step, turn, pair in side:
        for copy in pair:
            copy.wait_recv()
        hand_near(step, turn)
    for copy in waits:
        copy.wait()
    for copy in own:
        copy.wait()
    for triple in far:
        for copy in triple:
            copy.wait_send()
    for _, _, pair in side:
        for copy in pair:
            copy.wait_send()


def gather_weights(n_batch, n_ctx, qkv, proj, gains):
    n_chip = n_ctx // 2
    dma = pltpu.SemaphoreType.DMA
    vmem = pl.BlockSpec(memory_space=pltpu.VMEM)
    return pl.pallas_call(
        functools.partial(weights_kernel, n_batch, n_ctx),
        name="gather_weights",
        out_shape=(
            jax.ShapeDtypeStruct((n_batch, n_ctx, *qkv.shape[1:]), qkv.dtype),
            jax.ShapeDtypeStruct((n_ctx, *proj.shape), proj.dtype),
            jax.ShapeDtypeStruct((n_ctx, *gains.shape), gains.dtype),
        ),
        in_specs=[vmem] * 3,
        out_specs=[vmem] * 3,
        scratch_shapes=[
            dma((n_chip - 1, 3)),
            dma((n_chip - 1, 3)),
            dma((n_chip - 1, n_batch - 1, 2)),
            dma((n_chip - 1, n_batch - 1, 2)),
            dma((n_chip, n_batch, 3)),
            dma((n_chip, n_batch, 3)),
            dma((3,)),
        ],
        compiler_params=pltpu.CompilerParams(collective_id=12, has_side_effects=True),
    )(qkv, proj, gains)


def gathered(shard):
    return lax.all_gather(shard, "ctx", axis=0, tiled=True)


def scattered(whole):
    return lax.psum_scatter(whole, "ctx", scatter_dimension=0, tiled=True)


def local(
    n_batch,
    n_ctx,
    block_in,
    positions,
    counts,
    cotangent,
    gain_input,
    w_query,
    w_key,
    w_value,
    gain_query,
    gain_key,
    w_output,
    gain_attn,
    gain_ffn,
    w_gate,
    w_up,
    w_down,
    gain_final,
):
    block_in = block_in[0]
    positions = positions[0]
    cotangent = cotangent[0]
    tok_count, model_width = block_in.shape
    width_shard = w_query.shape[0]
    query_width = w_query.shape[1]
    head_size = w_key.shape[1]
    head_count = query_width // head_size
    hidden_shard = w_down.shape[0]
    piece = hidden_shard // n_batch
    hidden_part = -(-piece * n_ctx // 128) * 128
    padded = hidden_part // n_ctx
    halo_depth = (WINDOW + tok_count - 2) // tok_count
    batch_at = lax.axis_index("batch")
    ctx_at = lax.axis_index("ctx")
    all_tok = n_batch * tok_count

    gains = jnp.concatenate(
        [gain_input, gain_attn, gain_ffn, gain_final, gain_query, gain_key]
    )
    slots_of = query_width + 2 * head_size
    quarter = slots_of // n_batch
    qkv_full, proj_full, gains_all = gather_weights(
        n_batch,
        n_ctx,
        jnp.concatenate([w_query, w_key, w_value], axis=1)
        .reshape(width_shard, n_batch, quarter)
        .transpose(1, 0, 2),
        w_output.reshape(n_batch, -1, model_width),
        gains[None],
    )
    qkv_full = qkv_full.reshape(n_batch, model_width, quarter)
    full_output = proj_full.reshape(query_width, model_width)
    gains_all = gains_all[:, 0].astype(F32)

    def gain_at(start, length):
        return gains_all[:, start : start + length].reshape(1, -1)

    head_shard = gain_query.shape[0]
    full_gain_in = gain_at(0, width_shard)
    full_gain_attn = gain_at(width_shard, width_shard)
    full_gain_ffn = gain_at(2 * width_shard, width_shard)
    full_gain_final = gain_at(3 * width_shard, width_shard)
    full_gain_q = gain_at(4 * width_shard, head_shard)
    full_gain_k = gain_at(4 * width_shard + head_shard, head_shard)

    part_both = gathered(pick_columns(n_batch, n_ctx, piece, padded, w_gate, w_up))
    own_down = lax.dynamic_slice_in_dim(w_down, batch_at * piece, piece, 0)
    part_down = gathered(jnp.pad(own_down, ((0, padded - piece), (0, 0))))

    first_token = ctx_at * tok_count
    token_place = first_token + jnp.arange(tok_count, dtype=jnp.int32)
    valid_mask = (token_place < counts[0]).astype(F32)[:, None]
    resid_in = block_in.astype(F32)
    act_in = normed(resid_in, full_gain_in).astype(BF16)
    qkv_raw = jnp.concatenate([project(act_in, qkv_full[i]) for i in range(n_batch)], axis=1)
    query_raw = qkv_raw[:, :query_width].reshape(tok_count, head_count, head_size)
    key_raw = qkv_raw[:, query_width : query_width + head_size]
    value_low = qkv_raw[:, query_width + head_size :].astype(BF16)
    inv_freq = BASE ** (-jnp.arange(0, head_size, 2, dtype=F32) / head_size)
    angles = positions.astype(F32)[:, None] * inv_freq

    def query_path(raw_query, gain_vec):
        return rotate(normed(raw_query, gain_vec), angles[:, None, :])

    def key_path(raw_key, gain_vec):
        return rotate(normed(raw_key, gain_vec), angles)

    query_rot = query_path(query_raw, full_gain_q).astype(BF16)
    key_rot = key_path(key_raw, full_gain_k).astype(BF16)
    own_pair = jnp.concatenate([key_rot, value_low], axis=-1)
    halo = halo_exchange(1, n_ctx, halo_depth, 1, own_pair)
    context = jnp.concatenate([halo.reshape(halo_depth * tok_count, -1), own_pair], axis=0)
    ctx_keys = context[:, :head_size]
    ctx_values = context[:, head_size:]
    key_total = (halo_depth + 1) * tok_count
    distance = (
        jnp.arange(tok_count, dtype=jnp.int32)[:, None]
        + halo_depth * tok_count
        - jnp.arange(key_total, dtype=jnp.int32)[None, :]
    )
    allowed = (distance >= 0) & (distance < WINDOW) & (distance <= positions[:, None])
    score_scale = head_size ** (-0.5)
    raw_scores = jnp.einsum("thd,kd->htk", query_rot, ctx_keys, preferred_element_type=F32)
    scores = jnp.where(allowed[None], raw_scores * score_scale, MASKED)
    exp_scores = jnp.exp(scores - jnp.max(scores, axis=-1, keepdims=True))
    attn_prob = exp_scores / jnp.sum(exp_scores, axis=-1, keepdims=True)
    prob_low = attn_prob.astype(BF16)
    attended = jnp.einsum("htk,kd->thd", prob_low, ctx_values, preferred_element_type=F32)
    attn_low = attended.reshape(tok_count, query_width).astype(BF16)
    attn_proj = project(attn_low, full_output)
    middle = resid_in + normed(attn_proj, full_gain_attn)
    ffn_in = normed(middle, full_gain_ffn).astype(BF16)

    (ffn_in_all,) = square_gather(2, ffn_in)
    ffn_in_all = ffn_in_all.reshape(all_tok, model_width)
    gate_pre, up_pre, mixed_low, mixed_turned = hidden_mix(256, ffn_in_all, part_both)
    mixed_low, act_in_late, attn_late = lax.optimization_barrier((mixed_low, act_in, attn_low))
    act_in_all, attn_all = square_gather(13, act_in_late, attn_late)
    ffn_in_turned = ffn_in_all.T
    mixed_low, act_in_all, attn_all, mixed_turned, ffn_in_turned = lax.optimization_barrier(
        (mixed_low, act_in_all, attn_all, mixed_turned, ffn_in_turned)
    )
    act_in_all = act_in_all.reshape(all_tok, model_width)
    attn_all = attn_all.reshape(all_tok, query_width)
    block_out, grad_ffn_low, grad_gain_final = turn_round(
        mixed_low, part_down, middle, cotangent, valid_mask, full_gain_final
    )

    grad_final = cotangent.astype(F32) * valid_mask
    grad_ffn_low = grad_ffn_low.reshape(all_tok, model_width)
    down_grad = product_low(384, mixed_turned, grad_ffn_low)
    down_grad, grad_ffn_low = lax.optimization_barrier((down_grad, grad_ffn_low))
    grad_w_down = scattered(down_grad)
    grad_gate_low, grad_up_low, back_part = hidden_back(
        256, grad_ffn_low, part_down, gate_pre, up_pre, part_both
    )
    (back_parts,) = batch_exchange(
        5, n_batch, slots=(back_part.reshape(n_batch, tok_count, model_width),)
    )
    back_parts, grad_gate_low, grad_up_low = lax.optimization_barrier(
        (back_parts, grad_gate_low, grad_up_low)
    )
    gate_grad = product_low(256, ffn_in_turned, grad_gate_low)
    up_grad = product_low(256, ffn_in_turned, grad_up_low)
    back_parts, gate_grad, up_grad = lax.optimization_barrier((back_parts, gate_grad, up_grad))
    grad_w_gate = scattered(gate_grad)
    grad_w_up = scattered(up_grad)
    grad_ffn_in = jnp.sum(back_parts.astype(F32), axis=0)
    _, pull_ffn_norm = jax.vjp(normed, middle, full_gain_ffn)
    grad_middle_part, grad_gain_ffn = pull_ffn_norm(grad_ffn_in)
    grad_middle = grad_final + grad_middle_part
    _, pull_attn_norm = jax.vjp(normed, attn_proj, full_gain_attn)
    grad_attn_proj, grad_gain_attn = pull_attn_norm(grad_middle)

    grad_proj_low = grad_attn_proj.astype(BF16)
    grad_attended = (
        project_back(grad_proj_low, full_output)
        .astype(BF16)
        .reshape(tok_count, head_count, head_size)
    )
    grad_prob = jnp.einsum("thd,kd->htk", grad_attended, ctx_values, preferred_element_type=F32)
    row_delta = jnp.sum(attn_prob * grad_prob, axis=-1, keepdims=True)
    grad_scores = (attn_prob * (grad_prob - row_delta)).astype(BF16)
    grad_queries = (
        jnp.einsum("htk,kd->thd", grad_scores, ctx_keys, preferred_element_type=F32) * score_scale
    )
    grad_ctx_keys = (
        jnp.einsum("htk,thd->kd", grad_scores, query_rot, preferred_element_type=F32) * score_scale
    )
    grad_ctx_values = jnp.einsum("htk,thd->kd", prob_low, grad_attended, preferred_element_type=F32)
    grad_context = jnp.concatenate([grad_ctx_keys, grad_ctx_values], axis=-1)
    halo_rows = halo_depth * tok_count
    returned = halo_exchange(
        6,
        n_ctx,
        halo_depth,
        -1,
        grad_context[:halo_rows].astype(BF16).reshape(halo_depth, tok_count, 2 * head_size),
    )
    own_grad = grad_context[halo_rows:] + jnp.sum(returned.astype(F32), axis=0)
    grad_value_low = own_grad[:, head_size:].astype(BF16)
    _, pull_key = jax.vjp(key_path, key_raw, full_gain_k)
    grad_key_raw, grad_gain_key = pull_key(own_grad[:, :head_size])
    _, pull_query = jax.vjp(query_path, query_raw, full_gain_q)
    grad_query_raw, grad_gain_query = pull_query(grad_queries)
    grad_qkv_low = jnp.concatenate(
        [
            grad_query_raw.astype(BF16).reshape(tok_count, query_width),
            grad_key_raw.astype(BF16),
            grad_value_low,
        ],
        axis=1,
    )
    grad_act_in = sum(
        project_back(grad_qkv_low[:, i * quarter : (i + 1) * quarter], qkv_full[i])
        for i in range(n_batch)
    )
    _, pull_input = jax.vjp(normed, resid_in, full_gain_in)
    grad_in_part, grad_gain_input = pull_input(grad_act_in)
    grad_in = (grad_middle + grad_in_part).astype(BF16)

    def column_slots(upstream):
        return upstream.reshape(tok_count, n_batch, -1).transpose(1, 0, 2)

    gain_rows = jnp.concatenate(
        [
            grad.reshape(n_ctx, -1)
            for grad in (
                grad_gain_input,
                grad_gain_attn,
                grad_gain_ffn,
                grad_gain_final,
                grad_gain_query,
                grad_gain_key,
            )
        ],
        axis=1,
    )
    gain_parts, qkv_slots, proj_slots = batch_exchange(
        7,
        n_batch,
        whole=(gain_rows,),
        slots=(column_slots(grad_qkv_low), column_slots(grad_proj_low)),
    )
    proj_rows = w_output.shape[0]
    gain_count = gain_rows.shape[1]
    gain_lines = -(-gain_count // quarter)
    used = width_shard + proj_rows + gain_lines
    lines = -(-used // 16) * 16
    grad_w_output = weight_grad(attn_all, proj_slots.reshape(all_tok, -1)).astype(BF16)
    grad_w_qkv = weight_grad(act_in_all, qkv_slots.reshape(all_tok, -1)).astype(BF16)
    output_part = model_width // n_batch
    gain_sum = jnp.sum(gain_parts, axis=0).astype(BF16)
    packed = jnp.concatenate(
        [
            grad_w_qkv.reshape(n_ctx, width_shard, quarter),
            jnp.pad(
                grad_w_output.reshape(n_ctx, proj_rows, output_part),
                ((0, 0), (0, 0), (0, quarter - output_part)),
            ),
            jnp.pad(gain_sum, ((0, 0), (0, gain_lines * quarter - gain_count))).reshape(
                n_ctx, gain_lines, quarter
            ),
            jnp.zeros((n_ctx, lines - used, quarter), BF16),
        ],
        axis=1,
    )
    attn_sum = scattered(packed.reshape(n_ctx * lines, quarter))

    down_all, gate_all = square_gather(8, grad_w_down, grad_w_gate)
    (up_all,) = square_gather(9, grad_w_up)
    (attn_grads,) = square_gather(11, attn_sum)
    gain_mine = attn_grads[0, width_shard + proj_rows : used].reshape(-1).astype(F32)

    def columns_back(pieces):
        return pieces.astype(F32).transpose(1, 0, 2).reshape(pieces.shape[1], -1)

    grad_qkv_shard = columns_back(attn_grads[:, :width_shard])
    return (
        block_out[None],
        grad_in[None],
        gain_mine[:width_shard],
        grad_qkv_shard[:, :query_width],
        grad_qkv_shard[:, query_width : query_width + head_size],
        grad_qkv_shard[:, query_width + head_size :],
        gain_mine[4 * width_shard : 4 * width_shard + head_shard],
        gain_mine[4 * width_shard + head_shard : gain_count],
        columns_back(attn_grads[:, width_shard : width_shard + proj_rows, :output_part]),
        gain_mine[width_shard : 2 * width_shard],
        gain_mine[2 * width_shard : 3 * width_shard],
        place_columns(n_batch, n_ctx, piece, padded, gate_all),
        place_columns(n_batch, n_ctx, piece, padded, up_all),
        down_all[:, :piece].reshape(hidden_shard, model_width).astype(F32),
        gain_mine[3 * width_shard : 4 * width_shard],
    )


def solution(mesh):
    matrix = P("ctx", None)
    vector = P("ctx")
    tokens = P("batch", "ctx", None)

    def step(*arrays):
        return local(mesh.shape["batch"], mesh.shape["ctx"], *arrays)

    return jax.shard_map(
        step,
        mesh=mesh,
        in_specs=(
            tokens,
            P("batch", "ctx"),
            P("batch"),
            tokens,
            vector,
            matrix,
            matrix,
            matrix,
            vector,
            vector,
            matrix,
            vector,
            vector,
            matrix,
            matrix,
            matrix,
            vector,
        ),
        out_specs=(
            tokens,
            tokens,
            vector,
            matrix,
            matrix,
            matrix,
            vector,
            vector,
            matrix,
            vector,
            vector,
            matrix,
            matrix,
            matrix,
            vector,
        ),
        check_vma=False,
    )
```

```python
import functools

import jax
import jax.numpy as jnp
from jax import lax
from jax.experimental import pallas as pl
from jax.experimental.pallas import tpu as pltpu
from jax.sharding import PartitionSpec as P

WINDOW = 512


EPS = 1e-06
BASE = 10000.0
MASKED = -1e30
BF16 = jnp.bfloat16
F32 = jnp.float32
MESH = pl.DeviceIdType.MESH


def normed(vector, gain_vec):
    return vector * lax.rsqrt(jnp.mean(vector * vector, axis=-1, keepdims=True) + EPS) * gain_vec


def rotate(vector, angles):
    half_size = vector.shape[-1] // 2
    cosine = jnp.cos(angles)
    sine_part = jnp.sin(angles)
    first_half = vector[..., :half_size]
    second = vector[..., half_size:]
    return jnp.concatenate(
        [first_half * cosine - second * sine_part, second * cosine + first_half * sine_part],
        axis=-1,
    )


def project(inputs, weight):
    return lax.dot_general(inputs, weight, (((1,), (0,)), ((), ())), preferred_element_type=F32)


def project_back(upstream, weight):
    return lax.dot_general(upstream, weight, (((1,), (1,)), ((), ())), preferred_element_type=F32)


def weight_grad(inputs, upstream):
    return lax.dot_general(inputs, upstream, (((0,), (0,)), ((), ())), preferred_element_type=F32)


def gated_gelu(gate_val, up_val):
    return jax.nn.gelu(gate_val, approximate=True) * up_val


def batch_kernel(size, kinds, *refs):
    count = len(kinds)
    sources, results = refs[:count], refs[count : 2 * count]
    send_sem, recv_sem, own_sem = refs[2 * count :]
    me = lax.axis_index("batch")
    barrier = pltpu.get_barrier_semaphore()
    for step in range(1, size):
        pl.semaphore_signal(
            barrier, inc=1, device_id={"batch": lax.rem(me + step, size)}, device_id_type=MESH
        )
    pl.semaphore_wait(barrier, size - 1)
    copies = []
    for step in range(1, size):
        peer = lax.rem(me + step, size)
        for item in range(count):
            source = sources[item].at[peer] if kinds[item] else sources[item]
            copies.append(
                pltpu.make_async_remote_copy(
                    src_ref=source,
                    dst_ref=results[item].at[me],
                    send_sem=send_sem.at[item, step - 1],
                    recv_sem=recv_sem.at[item, step - 1],
                    device_id={"batch": peer},
                    device_id_type=MESH,
                )
            )
    for copy in copies:
        copy.start()
    own = []
    for item in range(count):
        source = sources[item].at[me] if kinds[item] else sources[item]
        own.append(pltpu.make_async_copy(source, results[item].at[me], own_sem.at[item]))
    for copy in own:
        copy.start()
    for copy in own:
        copy.wait()
    for copy in copies:
        copy.wait()


def batch_exchange(collective_id, size, whole=(), slots=()):
    arrays = list(whole) + list(slots)
    kinds = [0] * len(whole) + [1] * len(slots)
    count = len(arrays)
    shapes = [
        jax.ShapeDtypeStruct(a.shape if k else (size, *a.shape), a.dtype)
        for a, k in zip(arrays, kinds)
    ]
    return pl.pallas_call(
        functools.partial(batch_kernel, size, kinds),
        out_shape=shapes,
        in_specs=[pl.BlockSpec(memory_space=pltpu.VMEM)] * count,
        out_specs=[pl.BlockSpec(memory_space=pltpu.VMEM)] * count,
        scratch_shapes=[
            pltpu.SemaphoreType.DMA((count, size - 1)),
            pltpu.SemaphoreType.DMA((count, size - 1)),
            pltpu.SemaphoreType.DMA((count,)),
        ],
        compiler_params=pltpu.CompilerParams(collective_id=collective_id, has_side_effects=True),
    )(*arrays)


def square_kernel(count, *refs):
    sources, results = refs[:count], refs[count : 2 * count]
    send_sem, recv_sem, own_sem = refs[2 * count :]
    me = lax.axis_index("batch")
    across = me + 1 - 2 * lax.rem(me, 2)
    along = lax.rem(me + 2, 4)
    barrier = pltpu.get_barrier_semaphore()
    for peer in (across, along):
        pl.semaphore_signal(barrier, inc=1, device_id={"batch": peer}, device_id_type=MESH)
    pl.semaphore_wait(barrier, 2)

    def remote(source, target, item, turn, peer):
        copy = pltpu.make_async_remote_copy(
            src_ref=source,
            dst_ref=target,
            send_sem=send_sem.at[item, turn],
            recv_sem=recv_sem.at[item, turn],
            device_id={"batch": peer},
            device_id_type=MESH,
        )
        copy.start()
        return copy

    firsts = [
        [
            remote(sources[item], results[item].at[me], item, turn, peer)
            for turn, peer in enumerate((across, along))
        ]
        for item in range(count)
    ]
    own = [
        pltpu.make_async_copy(sources[item], results[item].at[me], own_sem.at[item])
        for item in range(count)
    ]
    for copy in own:
        copy.start()
    seconds = []
    for item in range(count):
        columns = sources[item].shape[-1]
        cut = columns // 256 * 128
        halves = (pl.ds(0, cut), pl.ds(cut, columns - cut))
        for turn, (giver, taker) in enumerate(((across, along), (along, across))):
            firsts[item][turn].wait_recv()
            block = results[item].at[giver, :, halves[turn]]
            seconds.append(remote(block, block, item, 2 + turn, taker))
    for copy in own:
        copy.wait()
    for copy in seconds:
        copy.wait()
    for pair in firsts:
        for copy in pair:
            copy.wait_send()


def square_gather(collective_id, *arrays):
    count = len(arrays)
    return pl.pallas_call(
        functools.partial(square_kernel, count),
        out_shape=[jax.ShapeDtypeStruct((4, *a.shape), a.dtype) for a in arrays],
        in_specs=[pl.BlockSpec(memory_space=pltpu.VMEM)] * count,
        out_specs=[pl.BlockSpec(memory_space=pltpu.VMEM)] * count,
        scratch_shapes=[
            pltpu.SemaphoreType.DMA((count, 4)),
            pltpu.SemaphoreType.DMA((count, 4)),
            pltpu.SemaphoreType.DMA((count,)),
        ],
        compiler_params=pltpu.CompilerParams(collective_id=collective_id, has_side_effects=True),
    )(*arrays)


def turn_kernel(
    mixed_ref,
    down_ref,
    middle_ref,
    upstream_ref,
    valid_ref,
    gain_ref,
    out_ref,
    grads_ref,
    gain_grad_ref,
    part_ref,
    taken_ref,
    send_sem,
    recv_sem,
    pass_sem,
    take_sem,
):
    me = lax.axis_index("batch")
    across = me + 1 - 2 * lax.rem(me, 2)
    along = lax.rem(me + 2, 4)
    corner = lax.rem(across + 2, 4)
    order = (corner, across, along)
    tok_count = middle_ref.shape[0]
    barrier = pltpu.get_barrier_semaphore()
    for peer in order:
        pl.semaphore_signal(barrier, inc=1, device_id={"batch": peer}, device_id_type=MESH)
    pl.semaphore_wait(barrier, 3)

    def product(place):
        rows = pl.ds(pl.multiple_of(place * tok_count, tok_count), tok_count)
        return jnp.dot(mixed_ref[rows, :], down_ref[...], preferred_element_type=F32)

    copies = [
        pltpu.make_async_remote_copy(
            src_ref=part_ref.at[turn],
            dst_ref=taken_ref.at[turn],
            send_sem=send_sem.at[turn],
            recv_sem=recv_sem.at[turn],
            device_id={"batch": peer},
            device_id_type=MESH,
        )
        for turn, peer in enumerate(order)
    ]
    for turn, peer in enumerate(order):
        part_ref[turn] = product(peer).astype(BF16)
        if turn > 0:
            copies[turn - 1].start()
    total = product(me)
    copies[2].start()
    for turn in range(3):
        copies[turn].wait_recv()
        total = total + taken_ref[turn].astype(F32)
    gain = gain_ref[...]
    valid = valid_ref[...]
    scale = lax.rsqrt(jnp.mean(total * total, axis=-1, keepdims=True) + EPS)
    upstream = upstream_ref[...].astype(F32) * valid
    gained = upstream * gain
    back = scale * gained - total * (
        scale * scale * scale * jnp.mean(total * gained, axis=-1, keepdims=True)
    )
    grads_ref[me] = back.astype(BF16)
    unit = total * scale
    out_ref[...] = ((middle_ref[...] + unit * gain) * valid).astype(BF16)
    gain_grad_ref[...] = jnp.sum(upstream * unit, axis=0, keepdims=True)

    def remote(block, turn, peer):
        copy = pltpu.make_async_remote_copy(
            src_ref=block,
            dst_ref=block,
            send_sem=pass_sem.at[turn],
            recv_sem=take_sem.at[turn],
            device_id={"batch": peer},
            device_id_type=MESH,
        )
        copy.start()
        return copy

    firsts = [remote(grads_ref.at[me], turn, peer) for turn, peer in enumerate((across, along))]
    columns = grads_ref.shape[-1]
    cut = columns // 256 * 128
    halves = (pl.ds(0, cut), pl.ds(cut, columns - cut))
    seconds = []
    for turn, (giver, taker) in enumerate(((across, along), (along, across))):
        firsts[turn].wait_recv()
        seconds.append(remote(grads_ref.at[giver, :, halves[turn]], 2 + turn, taker))
    for copy in seconds:
        copy.wait()
    for copy in firsts + copies:
        copy.wait_send()


def turn_round(mixed, down, middle, upstream, valid, gain):
    tok_count, width = middle.shape
    dma = pltpu.SemaphoreType.DMA
    vmem = pl.BlockSpec(memory_space=pltpu.VMEM)
    flops = 2 * mixed.shape[0] * mixed.shape[1] * width
    return pl.pallas_call(
        turn_kernel,
        name="turn_round",
        out_shape=(
            jax.ShapeDtypeStruct((tok_count, width), BF16),
            jax.ShapeDtypeStruct((4, tok_count, width), BF16),
            jax.ShapeDtypeStruct((1, width), F32),
        ),
        in_specs=[vmem] * 6,
        out_specs=[vmem] * 3,
        scratch_shapes=[
            pltpu.VMEM((3, tok_count, width), BF16),
            pltpu.VMEM((3, tok_count, width), BF16),
            dma((3,)),
            dma((3,)),
            dma((4,)),
            dma((4,)),
        ],
        cost_estimate=pl.CostEstimate(flops=flops, bytes_accessed=8 << 20, transcendentals=0),
        compiler_params=pltpu.CompilerParams(collective_id=3, has_side_effects=True),
    )(mixed, down, middle, upstream, valid, gain)


def product_kernel(left_ref, right_ref, out_ref):
    out_ref[...] = jnp.dot(left_ref[...], right_ref[...], preferred_element_type=F32).astype(BF16)


def product_low(tile, left, right):
    rows, depth = left.shape
    columns = right.shape[1]
    return pl.pallas_call(
        product_kernel,
        grid=(columns // tile,),
        out_shape=jax.ShapeDtypeStruct((rows, columns), BF16),
        in_specs=[
            pl.BlockSpec((rows, depth), lambda i: (0, 0)),
            pl.BlockSpec((depth, tile), lambda i: (0, i)),
        ],
        out_specs=pl.BlockSpec((rows, tile), lambda i: (0, i)),
        cost_estimate=pl.CostEstimate(
            flops=2 * rows * depth * columns, bytes_accessed=8 << 20, transcendentals=0
        ),
    )(left, right)


def mix_kernel(tokens_ref, w_gate_ref, w_up_ref, gate_ref, up_ref, mixed_ref, turned_ref):
    gate = project(tokens_ref[...], w_gate_ref[...])
    up = project(tokens_ref[...], w_up_ref[...])
    gate_ref[...] = gate
    up_ref[...] = up
    mixed = gated_gelu(gate, up)
    mixed_ref[...] = mixed.astype(BF16)
    turned_ref[...] = mixed.T.astype(BF16)


def hidden_mix(tile, tokens, both_weights):
    count, width = tokens.shape
    hidden = both_weights.shape[1] // 2
    steps = hidden // tile
    wide = jax.ShapeDtypeStruct((count, hidden), F32)
    column = pl.BlockSpec((count, tile), lambda i: (0, i))
    return pl.pallas_call(
        mix_kernel,
        name="hidden_mix",
        grid=(steps,),
        out_shape=(
            wide,
            wide,
            jax.ShapeDtypeStruct((count, hidden), BF16),
            jax.ShapeDtypeStruct((hidden, count), BF16),
        ),
        in_specs=[
            pl.BlockSpec((count, width), lambda i: (0, 0)),
            pl.BlockSpec((width, tile), lambda i: (0, i)),
            pl.BlockSpec((width, tile), lambda i: (0, i + steps)),
        ],
        out_specs=[column, column, column, pl.BlockSpec((tile, count), lambda i: (i, 0))],
        cost_estimate=pl.CostEstimate(
            flops=4 * count * hidden * width, bytes_accessed=24 << 20, transcendentals=0
        ),
    )(tokens, both_weights, both_weights)


def back_kernel(
    upstream_ref, down_ref, gate_ref, up_ref, w_gate_ref, w_up_ref, gate_out, up_out, back_ref, total
):
    step = pl.program_id(0)
    grad_mixed = project_back(upstream_ref[...], down_ref[...])
    _, pull_gelu = jax.vjp(gated_gelu, gate_ref[...], up_ref[...])
    grad_gate, grad_up = pull_gelu(grad_mixed)
    grad_gate, grad_up = grad_gate.astype(BF16), grad_up.astype(BF16)
    gate_out[...] = grad_gate
    up_out[...] = grad_up
    part = project_back(grad_gate, w_gate_ref[...]) + project_back(grad_up, w_up_ref[...])

    @pl.when(step == 0)
    def _():
        total[...] = part

    @pl.when(step > 0)
    def _():
        total[...] += part

    @pl.when(step == pl.num_programs(0) - 1)
    def _():
        back_ref[...] = total[...].astype(BF16)


def hidden_back(tile, upstream, down, gate_pre, up_pre, both_weights):
    tokens, width = upstream.shape
    hidden = down.shape[0]
    count = hidden // tile
    low = jax.ShapeDtypeStruct((tokens, hidden), BF16)
    return pl.pallas_call(
        back_kernel,
        name="hidden_back",
        grid=(count,),
        out_shape=(low, low, jax.ShapeDtypeStruct((tokens, width), BF16)),
        in_specs=[
            pl.BlockSpec((tokens, width), lambda i: (0, 0)),
            pl.BlockSpec((tile, width), lambda i: (i, 0)),
            pl.BlockSpec((tokens, tile), lambda i: (0, i)),
            pl.BlockSpec((tokens, tile), lambda i: (0, i)),
            pl.BlockSpec((width, tile), lambda i: (0, i)),
            pl.BlockSpec((width, tile), lambda i: (0, i + count)),
        ],
        out_specs=[
            pl.BlockSpec((tokens, tile), lambda i: (0, i)),
            pl.BlockSpec((tokens, tile), lambda i: (0, i)),
            pl.BlockSpec((tokens, width), lambda i: (0, 0)),
        ],
        scratch_shapes=[pltpu.VMEM((tokens, width), F32)],
        cost_estimate=pl.CostEstimate(
            flops=6 * tokens * hidden * width, bytes_accessed=24 << 20, transcendentals=0
        ),
    )(upstream, down, gate_pre, up_pre, both_weights, both_weights)


def halo_kernel(size, depth, direction, source_ref, result_ref, send_sem, recv_sem):
    me = lax.axis_index("ctx")
    barrier = pltpu.get_barrier_semaphore()
    for step in range(1, depth + 1):
        giver = me - direction * step

        @pl.when((giver >= 0) & (giver < size))
        def _():
            pl.semaphore_signal(barrier, inc=1, device_id={"ctx": giver}, device_id_type=MESH)

    takers = jnp.minimum(depth, size - 1 - me) if direction > 0 else jnp.minimum(depth, me)

    @pl.when(takers > 0)
    def _():
        pl.semaphore_wait(barrier, takers)

    def copy(step):
        slot = depth - step
        source = source_ref if direction > 0 else source_ref.at[slot]
        return pltpu.make_async_remote_copy(
            src_ref=source,
            dst_ref=result_ref.at[slot],
            send_sem=send_sem.at[step - 1],
            recv_sem=recv_sem.at[step - 1],
            device_id={"ctx": jnp.clip(me + direction * step, 0, size - 1)},
            device_id_type=MESH,
        )

    for step in range(depth, 0, -1):
        taker = me + direction * step

        @pl.when((taker >= 0) & (taker < size))
        def _():
            copy(step).start()

    for step in range(1, depth + 1):
        taker = me + direction * step
        giver = me - direction * step

        @pl.when((giver < 0) | (giver >= size))
        def _():
            result_ref[depth - step] = jnp.zeros(result_ref.shape[1:], result_ref.dtype)

        @pl.when((giver >= 0) & (giver < size))
        def _():
            copy(step).wait_recv()

        @pl.when((taker >= 0) & (taker < size))
        def _():
            copy(step).wait_send()


def halo_exchange(collective_id, size, depth, direction, block):
    return pl.pallas_call(
        functools.partial(halo_kernel, size, depth, direction),
        out_shape=jax.ShapeDtypeStruct((depth, *block.shape[-2:]), block.dtype),
        in_specs=[pl.BlockSpec(memory_space=pltpu.VMEM)],
        out_specs=pl.BlockSpec(memory_space=pltpu.VMEM),
        scratch_shapes=[pltpu.SemaphoreType.DMA((depth,)), pltpu.SemaphoreType.DMA((depth,))],
        compiler_params=pltpu.CompilerParams(collective_id=collective_id, has_side_effects=True),
    )(block)


def pick_kernel(n_batch, n_ctx, piece, padded, gate_ref, up_ref, out_ref):
    me = lax.axis_index("batch")
    out_ref[...] = jnp.zeros_like(out_ref)
    for spot in range(n_batch):

        @pl.when(me == spot)
        def _():
            for shard in range(n_ctx):
                start = (shard * n_batch + spot) * piece
                for half, ref in enumerate((gate_ref, up_ref)):
                    place = (half * n_ctx + shard) * padded
                    out_ref[:, place : place + piece] = ref[:, start : start + piece]


def row_block(rows):
    return 48 if rows % 48 == 0 else rows


def pick_columns(n_batch, n_ctx, piece, padded, w_gate, w_up):
    rows, hidden = w_gate.shape
    block = row_block(rows)
    spec = pl.BlockSpec((block, hidden), lambda i: (i, 0))
    return pl.pallas_call(
        functools.partial(pick_kernel, n_batch, n_ctx, piece, padded),
        name="pick_columns",
        grid=(rows // block,),
        out_shape=jax.ShapeDtypeStruct((rows, 2 * n_ctx * padded), w_gate.dtype),
        in_specs=[spec, spec],
        out_specs=pl.BlockSpec((block, 2 * n_ctx * padded), lambda i: (i, 0)),
    )(w_gate, w_up)


def place_kernel(n_batch, n_ctx, piece, padded, parts_ref, out_ref):
    for shard in range(n_ctx):
        for spot in range(n_batch):
            start = (shard * n_batch + spot) * piece
            place = shard * padded
            out_ref[:, start : start + piece] = parts_ref[spot, :, place : place + piece].astype(F32)


def place_columns(n_batch, n_ctx, piece, padded, parts):
    rows = parts.shape[1]
    block = row_block(rows)
    hidden = n_batch * n_ctx * piece
    return pl.pallas_call(
        functools.partial(place_kernel, n_batch, n_ctx, piece, padded),
        grid=(rows // block,),
        out_shape=jax.ShapeDtypeStruct((rows, hidden), F32),
        in_specs=[pl.BlockSpec((n_batch, block, n_ctx * padded), lambda i: (0, i, 0))],
        out_specs=pl.BlockSpec((block, hidden), lambda i: (i, 0)),
    )(parts)


def weights_kernel(n_batch, n_ctx, qkv_ref, proj_ref, gain_ref, qkv_all, proj_all, gain_all, *sems):
    send_far, recv_far, send_side, recv_side, send_near, recv_near, own_sem = sems
    spot = lax.axis_index("batch")
    me = lax.axis_index("ctx")
    n_chip = n_ctx // 2
    chip, core = me // 2, lax.rem(me, 2)
    near = {"ctx": me + 1 - 2 * core}
    barrier = pltpu.get_barrier_semaphore()

    def far_at(step):
        return {"ctx": 2 * lax.rem(chip + step, n_chip) + core}

    def side_at(step):
        return {"batch": lax.rem(spot + step, n_batch)}

    peers = [near]
    peers += [far_at(step) for step in range(1, n_chip)]
    peers += [side_at(step) for step in range(1, n_batch)]
    for peer in peers:
        pl.semaphore_signal(barrier, inc=1, device_id=peer, device_id_type=MESH)
    pl.semaphore_wait(barrier, len(peers))

    def remote(source, target, send, recv, peer):
        return pltpu.make_async_remote_copy(
            src_ref=source,
            dst_ref=target,
            send_sem=send,
            recv_sem=recv,
            device_id=peer,
            device_id_type=MESH,
        )

    waits = []
    far = []
    for step in range(1, n_chip):
        triple = [
            remote(source, target, send_far.at[step - 1, item], recv_far.at[step - 1, item], far_at(step))
            for item, (source, target) in enumerate(
                (
                    (qkv_ref.at[spot], qkv_all.at[spot, me]),
                    (proj_ref.at[spot], proj_all.at[me, spot]),
                    (gain_ref, gain_all.at[me]),
                )
            )
        ]
        for copy in triple:
            copy.start()
        far.append(triple)
    own = [
        pltpu.make_async_copy(qkv_ref, qkv_all.at[:, me], own_sem.at[0]),
        pltpu.make_async_copy(proj_ref, proj_all.at[me], own_sem.at[1]),
        pltpu.make_async_copy(gain_ref, gain_all.at[me], own_sem.at[2]),
    ]
    for copy in own:
        copy.start()
    first = n_chip - 1
    pairs = [
        remote(source, target, send_near.at[first, 0, item], recv_near.at[first, 0, item], near)
        for item, (source, target) in enumerate(
            (
                (qkv_ref, qkv_all.at[:, me]),
                (proj_ref, proj_all.at[me]),
                (gain_ref, gain_all.at[me]),
            )
        )
    ]
    for copy in pairs:
        copy.start()
    waits += pairs

    def hand_near(step, turn):
        origin = 2 * lax.rem(chip + n_chip - step, n_chip) + core
        quarter = lax.rem(spot + n_batch - turn, n_batch)
        blocks = [qkv_all.at[quarter, origin], proj_all.at[origin, quarter]]
        blocks += [gain_all.at[origin]] if turn == 0 else []
        for item, block in enumerate(blocks):
            copy = remote(
                block,
                block,
                send_near.at[step - 1, turn, item],
                recv_near.at[step - 1, turn, item],
                near,
            )
            copy.start()
            waits.append(copy)

    side = []
    for step in range(1, n_chip):
        for copy in far[step - 1]:
            copy.wait_recv()
        origin = 2 * lax.rem(chip + n_chip - step, n_chip) + core
        for turn in range(1, n_batch):
            pair = [
                remote(
                    block,
                    block,
                    send_side.at[step - 1, turn - 1, item],
                    recv_side.at[step - 1, turn - 1, item],
                    side_at(turn),
                )
                for item, block in enumerate((qkv_all.at[spot, origin], proj_all.at[origin, spot]))
            ]
            for copy in pair:
                copy.start()
            side.append((step, turn, pair))
        hand_near(step, 0)
    for step, turn, pair in side:
        for copy in pair:
            copy.wait_recv()
        hand_near(step, turn)
    for copy in waits:
        copy.wait()
    for copy in own:
        copy.wait()
    for triple in far:
        for copy in triple:
            copy.wait_send()
    for _, _, pair in side:
        for copy in pair:
            copy.wait_send()


def gather_weights(n_batch, n_ctx, qkv, proj, gains):
    n_chip = n_ctx // 2
    dma = pltpu.SemaphoreType.DMA
    vmem = pl.BlockSpec(memory_space=pltpu.VMEM)
    return pl.pallas_call(
        functools.partial(weights_kernel, n_batch, n_ctx),
        name="gather_weights",
        out_shape=(
            jax.ShapeDtypeStruct((n_batch, n_ctx, *qkv.shape[1:]), qkv.dtype),
            jax.ShapeDtypeStruct((n_ctx, *proj.shape), proj.dtype),
            jax.ShapeDtypeStruct((n_ctx, *gains.shape), gains.dtype),
        ),
        in_specs=[vmem] * 3,
        out_specs=[vmem] * 3,
        scratch_shapes=[
            dma((n_chip - 1, 3)),
            dma((n_chip - 1, 3)),
            dma((n_chip - 1, n_batch - 1, 2)),
            dma((n_chip - 1, n_batch - 1, 2)),
            dma((n_chip, n_batch, 3)),
            dma((n_chip, n_batch, 3)),
            dma((3,)),
        ],
        compiler_params=pltpu.CompilerParams(collective_id=12, has_side_effects=True),
    )(qkv, proj, gains)


def tail_kernel(
    n_ctx,
    gate_ref,
    down_ref,
    up_ref,
    attn_ref,
    gate_all,
    down_all,
    up_all,
    attn_all,
    pair_up,
    pair_attn,
    way_up,
    way_attn,
    pair_send,
    pair_recv,
    way_send,
    way_recv,
    side_send,
    side_recv,
    own_sem,
):
    n_chip = n_ctx // 2
    spot = lax.axis_index("batch")
    me = lax.axis_index("ctx")
    chip, core = me // 2, lax.rem(me, 2)
    across = {"batch": spot + 1 - 2 * lax.rem(spot, 2)}
    along = {"batch": lax.rem(spot + 2, 4)}
    near = {"ctx": me + 1 - 2 * core}
    beyond = ({"ctx": jnp.minimum(me + 2, n_ctx - 1)}, {"ctx": jnp.maximum(me - 2, 0)})
    inner = (chip > 0, chip < n_chip - 1)
    barrier = pltpu.get_barrier_semaphore()
    for peer in (near, across, along):
        pl.semaphore_signal(barrier, inc=1, device_id=peer, device_id_type=MESH)
    for has_giver, giver in zip(inner, (beyond[1], beyond[0])):

        @pl.when(has_giver)
        def _():
            pl.semaphore_signal(barrier, inc=1, device_id=giver, device_id_type=MESH)

    pl.semaphore_wait(barrier, 3 + jnp.minimum(chip, 1) + jnp.minimum(n_chip - 1 - chip, 1))

    def remote(source, target, send, recv, peer):
        return pltpu.make_async_remote_copy(
            src_ref=source,
            dst_ref=target,
            send_sem=send,
            recv_sem=recv,
            device_id=peer,
            device_id_type=MESH,
        )

    width = up_ref.shape[-1]
    cut = width // 256 * 128
    chains = (
        (up_ref, pair_up, way_up, up_all, pl.ds(0, cut)),
        (up_ref, pair_up, way_up, up_all, pl.ds(cut, width - cut)),
        (attn_ref, pair_attn, way_attn, attn_all, pl.ds(0, attn_ref.shape[-1])),
    )
    numbers = range(len(chains))

    def pair_copy(number, place):
        source, pair, _, _, columns = chains[number]
        return remote(
            source.at[2 * place + 1 - core, :, columns],
            pair.at[place, :, columns],
            pair_send.at[number, place],
            pair_recv.at[number, place],
            near,
        )

    def way_copy(number, direction, step, source):
        _, _, way, _, columns = chains[number]
        return remote(
            source,
            way.at[direction, step - 1, :, columns],
            way_send.at[number, direction, step - 1],
            way_recv.at[number, direction, step - 1],
            beyond[direction],
        )

    def passes(direction, step):
        return chip <= step - 1 if direction == 0 else chip >= n_chip - step

    def bound_for(direction, step):
        place = chip + n_chip - step if direction == 0 else chip - n_chip + step
        return jnp.clip(place, 0, n_chip - 1)

    def side_pair(item, sources, target, columns):
        return [
            remote(
                sources,
                target.at[spot, :, columns],
                side_send.at[item, turn],
                side_recv.at[item, turn],
                peer,
            )
            for turn, peer in enumerate((across, along))
        ]

    def side_pass(item, firsts, target, start, length):
        half = length // 256 * 128
        halves = (pl.ds(start, half), pl.ds(start + half, length - half))
        copies = []
        for turn, (giver, taker) in enumerate(((across, along), (along, across))):
            firsts[turn].wait_recv()
            block = target.at[giver["batch"], :, halves[turn]]
            copies.append(
                remote(block, block, side_send.at[item, 2 + turn], side_recv.at[item, 2 + turn], taker)
            )
            copies[-1].start()
        return copies

    for number in numbers:
        for place in range(n_chip):
            pair_copy(number, place).start()
    early = ((gate_ref, gate_all), (down_ref, down_all))
    side_firsts = []
    for item, (source, target) in enumerate(early):
        side_firsts.append(side_pair(item, source, target, pl.ds(0, source.shape[-1])))
        for copy in side_firsts[-1]:
            copy.start()
    own = [
        pltpu.make_async_copy(source, target.at[spot], own_sem.at[item])
        for item, (source, target) in enumerate(early)
    ]
    for copy in own:
        copy.start()
    for _, _, way, _, columns in chains:
        for direction in range(2):

            @pl.when(jnp.logical_not(inner[direction]))
            def _():
                way[direction, n_chip - 2, :, columns] = jnp.zeros(
                    (way.shape[2], columns.size), way.dtype
                )

    for number in numbers:
        source, pair, _, _, columns = chains[number]
        for place in range(n_chip):
            pair_copy(number, place).wait_recv()
            pair[place, :, columns] = (
                pair[place, :, columns].astype(F32)
                + source[2 * place + core, :, columns].astype(F32)
            ).astype(BF16)
        for direction in range(2):

            @pl.when(passes(direction, 1))
            def _():
                place = bound_for(direction, 1)
                way_copy(number, direction, 1, pair.at[place, :, columns]).start()

    side_seconds = []
    for step in range(2, n_chip + 1):
        if step <= 3:
            item = step - 2
            target = early[item][1]
            side_seconds += side_pass(item, side_firsts[item], target, 0, target.shape[-1])
        if step == n_chip:
            break
        for number in numbers:
            _, pair, way, _, columns = chains[number]
            for direction in range(2):
                place = bound_for(direction, step)

                @pl.when(passes(direction, step) & inner[direction])
                def _():
                    way_copy(number, direction, step - 1, pair.at[place, :, columns]).wait_recv()
                    way[direction, step - 2, :, columns] = (
                        way[direction, step - 2, :, columns].astype(F32)
                        + pair[place, :, columns].astype(F32)
                    ).astype(BF16)

            for direction in range(2):
                place = bound_for(direction, step)

                @pl.when(passes(direction, step) & inner[direction])
                def _():
                    way_copy(number, direction, step, way.at[direction, step - 2, :, columns]).start()

                @pl.when(passes(direction, step) & jnp.logical_not(inner[direction]))
                def _():
                    way_copy(number, direction, step, pair.at[place, :, columns]).start()

    chain_firsts = []
    for number in numbers:
        _, pair, way, target, columns = chains[number]
        for direction in range(2):

            @pl.when(inner[direction])
            def _():
                way_copy(number, direction, n_chip - 1, pair.at[0, :, columns]).wait_recv()

        target[spot, :, columns] = (
            pair[chip, :, columns].astype(F32)
            + way[0, n_chip - 2, :, columns].astype(F32)
            + way[1, n_chip - 2, :, columns].astype(F32)
        ).astype(BF16)
        firsts = side_pair(2 + number, target.at[spot, :, columns], target, columns)
        for copy in firsts:
            copy.start()
        chain_firsts.append(firsts)
    for number in numbers:
        _, _, _, target, columns = chains[number]
        side_seconds += side_pass(
            2 + number, chain_firsts[number], target, columns.start, columns.size
        )
    for copy in own:
        copy.wait()
    for copy in side_seconds:
        copy.wait()
    for firsts in side_firsts + chain_firsts:
        for copy in firsts:
            copy.wait_send()
    for number in numbers:
        _, pair, _, _, columns = chains[number]
        for place in range(n_chip):
            pair_copy(number, place).wait_send()
        for direction in range(2):
            for step in range(1, n_chip):

                @pl.when(passes(direction, step))
                def _():
                    way_copy(number, direction, step, pair.at[0, :, columns]).wait_send()


def tail_round(n_ctx, gate, down, up, attn):
    n_chip = n_ctx // 2
    dma = pltpu.SemaphoreType.DMA
    vmem = pl.BlockSpec(memory_space=pltpu.VMEM)
    shapes = (gate.shape, down.shape, up.shape[1:], attn.shape[1:])
    return pl.pallas_call(
        functools.partial(tail_kernel, n_ctx),
        name="tail_round",
        out_shape=[jax.ShapeDtypeStruct((4, *shape), BF16) for shape in shapes],
        in_specs=[vmem] * 4,
        out_specs=[vmem] * 4,
        scratch_shapes=[
            pltpu.VMEM((n_chip, *up.shape[1:]), BF16),
            pltpu.VMEM((n_chip, *attn.shape[1:]), BF16),
            pltpu.VMEM((2, n_chip - 1, *up.shape[1:]), BF16),
            pltpu.VMEM((2, n_chip - 1, *attn.shape[1:]), BF16),
            dma((3, n_chip)),
            dma((3, n_chip)),
            dma((3, 2, n_chip - 1)),
            dma((3, 2, n_chip - 1)),
            dma((5, 4)),
            dma((5, 4)),
            dma((2,)),
        ],
        compiler_params=pltpu.CompilerParams(collective_id=8, has_side_effects=True),
    )(gate, down, up, attn)


def gathered(shard):
    return lax.all_gather(shard, "ctx", axis=0, tiled=True)


def scattered(whole):
    return lax.psum_scatter(whole, "ctx", scatter_dimension=0, tiled=True)


def local(
    n_batch,
    n_ctx,
    block_in,
    positions,
    counts,
    cotangent,
    gain_input,
    w_query,
    w_key,
    w_value,
    gain_query,
    gain_key,
    w_output,
    gain_attn,
    gain_ffn,
    w_gate,
    w_up,
    w_down,
    gain_final,
):
    block_in = block_in[0]
    positions = positions[0]
    cotangent = cotangent[0]
    tok_count, model_width = block_in.shape
    width_shard = w_query.shape[0]
    query_width = w_query.shape[1]
    head_size = w_key.shape[1]
    head_count = query_width // head_size
    hidden_shard = w_down.shape[0]
    piece = hidden_shard // n_batch
    hidden_part = -(-piece * n_ctx // 128) * 128
    padded = hidden_part // n_ctx
    halo_depth = (WINDOW + tok_count - 2) // tok_count
    batch_at = lax.axis_index("batch")
    ctx_at = lax.axis_index("ctx")
    all_tok = n_batch * tok_count

    gains = jnp.concatenate(
        [gain_input, gain_attn, gain_ffn, gain_final, gain_query, gain_key]
    )
    slots_of = query_width + 2 * head_size
    quarter = slots_of // n_batch
    qkv_full, proj_full, gains_all = gather_weights(
        n_batch,
        n_ctx,
        jnp.concatenate([w_query, w_key, w_value], axis=1)
        .reshape(width_shard, n_batch, quarter)
        .transpose(1, 0, 2),
        w_output.reshape(n_batch, -1, model_width),
        gains[None],
    )
    qkv_full = qkv_full.reshape(n_batch, model_width, quarter)
    full_output = proj_full.reshape(query_width, model_width)
    gains_all = gains_all[:, 0].astype(F32)

    def gain_at(start, length):
        return gains_all[:, start : start + length].reshape(1, -1)

    head_shard = gain_query.shape[0]
    full_gain_in = gain_at(0, width_shard)
    full_gain_attn = gain_at(width_shard, width_shard)
    full_gain_ffn = gain_at(2 * width_shard, width_shard)
    full_gain_final = gain_at(3 * width_shard, width_shard)
    full_gain_q = gain_at(4 * width_shard, head_shard)
    full_gain_k = gain_at(4 * width_shard + head_shard, head_shard)

    part_both = gathered(pick_columns(n_batch, n_ctx, piece, padded, w_gate, w_up))
    own_down = lax.dynamic_slice_in_dim(w_down, batch_at * piece, piece, 0)
    part_down = gathered(jnp.pad(own_down, ((0, padded - piece), (0, 0))))

    first_token = ctx_at * tok_count
    token_place = first_token + jnp.arange(tok_count, dtype=jnp.int32)
    valid_mask = (token_place < counts[0]).astype(F32)[:, None]
    resid_in = block_in.astype(F32)
    act_in = normed(resid_in, full_gain_in).astype(BF16)
    qkv_raw = jnp.concatenate([project(act_in, qkv_full[i]) for i in range(n_batch)], axis=1)
    query_raw = qkv_raw[:, :query_width].reshape(tok_count, head_count, head_size)
    key_raw = qkv_raw[:, query_width : query_width + head_size]
    value_low = qkv_raw[:, query_width + head_size :].astype(BF16)
    inv_freq = BASE ** (-jnp.arange(0, head_size, 2, dtype=F32) / head_size)
    angles = positions.astype(F32)[:, None] * inv_freq

    def query_path(raw_query, gain_vec):
        return rotate(normed(raw_query, gain_vec), angles[:, None, :])

    def key_path(raw_key, gain_vec):
        return rotate(normed(raw_key, gain_vec), angles)

    query_rot = query_path(query_raw, full_gain_q).astype(BF16)
    key_rot = key_path(key_raw, full_gain_k).astype(BF16)
    own_pair = jnp.concatenate([key_rot, value_low], axis=-1)
    halo = halo_exchange(1, n_ctx, halo_depth, 1, own_pair)
    context = jnp.concatenate([halo.reshape(halo_depth * tok_count, -1), own_pair], axis=0)
    ctx_keys = context[:, :head_size]
    ctx_values = context[:, head_size:]
    key_total = (halo_depth + 1) * tok_count
    distance = (
        jnp.arange(tok_count, dtype=jnp.int32)[:, None]
        + halo_depth * tok_count
        - jnp.arange(key_total, dtype=jnp.int32)[None, :]
    )
    allowed = (distance >= 0) & (distance < WINDOW) & (distance <= positions[:, None])
    score_scale = head_size ** (-0.5)
    raw_scores = jnp.einsum("thd,kd->htk", query_rot, ctx_keys, preferred_element_type=F32)
    scores = jnp.where(allowed[None], raw_scores * score_scale, MASKED)
    exp_scores = jnp.exp(scores - jnp.max(scores, axis=-1, keepdims=True))
    attn_prob = exp_scores / jnp.sum(exp_scores, axis=-1, keepdims=True)
    prob_low = attn_prob.astype(BF16)
    attended = jnp.einsum("htk,kd->thd", prob_low, ctx_values, preferred_element_type=F32)
    attn_low = attended.reshape(tok_count, query_width).astype(BF16)
    attn_proj = project(attn_low, full_output)
    middle = resid_in + normed(attn_proj, full_gain_attn)
    ffn_in = normed(middle, full_gain_ffn).astype(BF16)

    (ffn_in_all,) = square_gather(2, ffn_in)
    ffn_in_all = ffn_in_all.reshape(all_tok, model_width)
    gate_pre, up_pre, mixed_low, mixed_turned = hidden_mix(256, ffn_in_all, part_both)
    mixed_low, act_in_late, attn_late = lax.optimization_barrier((mixed_low, act_in, attn_low))
    act_in_all, attn_all = square_gather(13, act_in_late, attn_late)
    ffn_in_turned = ffn_in_all.T
    mixed_low, act_in_all, attn_all, mixed_turned, ffn_in_turned = lax.optimization_barrier(
        (mixed_low, act_in_all, attn_all, mixed_turned, ffn_in_turned)
    )
    act_in_all = act_in_all.reshape(all_tok, model_width)
    attn_all = attn_all.reshape(all_tok, query_width)
    block_out, grad_ffn_low, grad_gain_final = turn_round(
        mixed_low, part_down, middle, cotangent, valid_mask, full_gain_final
    )

    grad_final = cotangent.astype(F32) * valid_mask
    grad_ffn_low = grad_ffn_low.reshape(all_tok, model_width)
    down_grad = product_low(384, mixed_turned, grad_ffn_low)
    down_grad, grad_ffn_low = lax.optimization_barrier((down_grad, grad_ffn_low))
    grad_w_down = scattered(down_grad)
    grad_gate_low, grad_up_low, back_part = hidden_back(
        256, grad_ffn_low, part_down, gate_pre, up_pre, part_both
    )
    (back_parts,) = batch_exchange(
        5, n_batch, slots=(back_part.reshape(n_batch, tok_count, model_width),)
    )
    back_parts, grad_gate_low, grad_up_low = lax.optimization_barrier(
        (back_parts, grad_gate_low, grad_up_low)
    )
    gate_grad = product_low(256, ffn_in_turned, grad_gate_low)
    up_grad = product_low(256, ffn_in_turned, grad_up_low)
    back_parts, gate_grad, up_grad = lax.optimization_barrier((back_parts, gate_grad, up_grad))
    grad_w_gate = scattered(gate_grad)
    grad_ffn_in = jnp.sum(back_parts.astype(F32), axis=0)
    _, pull_ffn_norm = jax.vjp(normed, middle, full_gain_ffn)
    grad_middle_part, grad_gain_ffn = pull_ffn_norm(grad_ffn_in)
    grad_middle = grad_final + grad_middle_part
    _, pull_attn_norm = jax.vjp(normed, attn_proj, full_gain_attn)
    grad_attn_proj, grad_gain_attn = pull_attn_norm(grad_middle)

    grad_proj_low = grad_attn_proj.astype(BF16)
    grad_attended = (
        project_back(grad_proj_low, full_output)
        .astype(BF16)
        .reshape(tok_count, head_count, head_size)
    )
    grad_prob = jnp.einsum("thd,kd->htk", grad_attended, ctx_values, preferred_element_type=F32)
    row_delta = jnp.sum(attn_prob * grad_prob, axis=-1, keepdims=True)
    grad_scores = (attn_prob * (grad_prob - row_delta)).astype(BF16)
    grad_queries = (
        jnp.einsum("htk,kd->thd", grad_scores, ctx_keys, preferred_element_type=F32) * score_scale
    )
    grad_ctx_keys = (
        jnp.einsum("htk,thd->kd", grad_scores, query_rot, preferred_element_type=F32) * score_scale
    )
    grad_ctx_values = jnp.einsum("htk,thd->kd", prob_low, grad_attended, preferred_element_type=F32)
    grad_context = jnp.concatenate([grad_ctx_keys, grad_ctx_values], axis=-1)
    halo_rows = halo_depth * tok_count
    returned = halo_exchange(
        6,
        n_ctx,
        halo_depth,
        -1,
        grad_context[:halo_rows].astype(BF16).reshape(halo_depth, tok_count, 2 * head_size),
    )
    own_grad = grad_context[halo_rows:] + jnp.sum(returned.astype(F32), axis=0)
    grad_value_low = own_grad[:, head_size:].astype(BF16)
    _, pull_key = jax.vjp(key_path, key_raw, full_gain_k)
    grad_key_raw, grad_gain_key = pull_key(own_grad[:, :head_size])
    _, pull_query = jax.vjp(query_path, query_raw, full_gain_q)
    grad_query_raw, grad_gain_query = pull_query(grad_queries)
    grad_qkv_low = jnp.concatenate(
        [
            grad_query_raw.astype(BF16).reshape(tok_count, query_width),
            grad_key_raw.astype(BF16),
            grad_value_low,
        ],
        axis=1,
    )
    grad_act_in = sum(
        project_back(grad_qkv_low[:, i * quarter : (i + 1) * quarter], qkv_full[i])
        for i in range(n_batch)
    )
    _, pull_input = jax.vjp(normed, resid_in, full_gain_in)
    grad_in_part, grad_gain_input = pull_input(grad_act_in)
    grad_in = (grad_middle + grad_in_part).astype(BF16)

    def column_slots(upstream):
        return upstream.reshape(tok_count, n_batch, -1).transpose(1, 0, 2)

    gain_rows = jnp.concatenate(
        [
            grad.reshape(n_ctx, -1)
            for grad in (
                grad_gain_input,
                grad_gain_attn,
                grad_gain_ffn,
                grad_gain_final,
                grad_gain_query,
                grad_gain_key,
            )
        ],
        axis=1,
    )
    gain_parts, qkv_slots, proj_slots = batch_exchange(
        7,
        n_batch,
        whole=(gain_rows,),
        slots=(column_slots(grad_qkv_low), column_slots(grad_proj_low)),
    )
    proj_rows = w_output.shape[0]
    gain_count = gain_rows.shape[1]
    gain_lines = -(-gain_count // quarter)
    used = width_shard + proj_rows + gain_lines
    lines = -(-used // 16) * 16
    grad_w_output = weight_grad(attn_all, proj_slots.reshape(all_tok, -1)).astype(BF16)
    grad_w_qkv = weight_grad(act_in_all, qkv_slots.reshape(all_tok, -1)).astype(BF16)
    output_part = model_width // n_batch
    gain_sum = jnp.sum(gain_parts, axis=0).astype(BF16)
    packed = jnp.concatenate(
        [
            grad_w_qkv.reshape(n_ctx, width_shard, quarter),
            jnp.pad(
                grad_w_output.reshape(n_ctx, proj_rows, output_part),
                ((0, 0), (0, 0), (0, quarter - output_part)),
            ),
            jnp.pad(gain_sum, ((0, 0), (0, gain_lines * quarter - gain_count))).reshape(
                n_ctx, gain_lines, quarter
            ),
            jnp.zeros((n_ctx, lines - used, quarter), BF16),
        ],
        axis=1,
    )
    gate_all, down_all, up_all, attn_grads = tail_round(
        n_ctx,
        grad_w_gate,
        grad_w_down,
        up_grad.reshape(n_ctx, width_shard, hidden_part),
        packed,
    )
    gain_mine = attn_grads[0, width_shard + proj_rows : used].reshape(-1).astype(F32)

    def columns_back(pieces):
        return pieces.astype(F32).transpose(1, 0, 2).reshape(pieces.shape[1], -1)

    grad_qkv_shard = columns_back(attn_grads[:, :width_shard])
    return (
        block_out[None],
        grad_in[None],
        gain_mine[:width_shard],
        grad_qkv_shard[:, :query_width],
        grad_qkv_shard[:, query_width : query_width + head_size],
        grad_qkv_shard[:, query_width + head_size :],
        gain_mine[4 * width_shard : 4 * width_shard + head_shard],
        gain_mine[4 * width_shard + head_shard : gain_count],
        columns_back(attn_grads[:, width_shard : width_shard + proj_rows, :output_part]),
        gain_mine[width_shard : 2 * width_shard],
        gain_mine[2 * width_shard : 3 * width_shard],
        place_columns(n_batch, n_ctx, piece, padded, gate_all),
        place_columns(n_batch, n_ctx, piece, padded, up_all),
        down_all[:, :piece].reshape(hidden_shard, model_width).astype(F32),
        gain_mine[3 * width_shard : 4 * width_shard],
    )


def solution(mesh):
    matrix = P("ctx", None)
    vector = P("ctx")
    tokens = P("batch", "ctx", None)

    def step(*arrays):
        return local(mesh.shape["batch"], mesh.shape["ctx"], *arrays)

    return jax.shard_map(
        step,
        mesh=mesh,
        in_specs=(
            tokens,
            P("batch", "ctx"),
            P("batch"),
            tokens,
            vector,
            matrix,
            matrix,
            matrix,
            vector,
            vector,
            matrix,
            vector,
            vector,
            matrix,
            matrix,
            matrix,
            vector,
        ),
        out_specs=(
            tokens,
            tokens,
            vector,
            matrix,
            matrix,
            matrix,
            vector,
            vector,
            matrix,
            vector,
            vector,
            matrix,
            matrix,
            matrix,
            vector,
        ),
        check_vma=False,
    )
```

```python
import functools

import jax
import jax.numpy as jnp
from jax import lax
from jax.experimental import pallas as pl
from jax.experimental.pallas import tpu as pltpu
from jax.sharding import PartitionSpec as P

WINDOW = 512


EPS = 1e-06
BASE = 10000.0
MASKED = -1e30
BF16 = jnp.bfloat16
F32 = jnp.float32
MESH = pl.DeviceIdType.MESH


def normed(vector, gain_vec):
    return vector * lax.rsqrt(jnp.mean(vector * vector, axis=-1, keepdims=True) + EPS) * gain_vec


def rotate(vector, angles):
    half_size = vector.shape[-1] // 2
    cosine = jnp.cos(angles)
    sine_part = jnp.sin(angles)
    first_half = vector[..., :half_size]
    second = vector[..., half_size:]
    return jnp.concatenate(
        [first_half * cosine - second * sine_part, second * cosine + first_half * sine_part],
        axis=-1,
    )


def project(inputs, weight):
    return lax.dot_general(inputs, weight, (((1,), (0,)), ((), ())), preferred_element_type=F32)


def project_back(upstream, weight):
    return lax.dot_general(upstream, weight, (((1,), (1,)), ((), ())), preferred_element_type=F32)


def weight_grad(inputs, upstream):
    return lax.dot_general(inputs, upstream, (((0,), (0,)), ((), ())), preferred_element_type=F32)


def gated_gelu(gate_val, up_val):
    return jax.nn.gelu(gate_val, approximate=True) * up_val


def batch_kernel(size, kinds, *refs):
    count = len(kinds)
    sources, results = refs[:count], refs[count : 2 * count]
    send_sem, recv_sem, own_sem = refs[2 * count :]
    me = lax.axis_index("batch")
    barrier = pltpu.get_barrier_semaphore()
    for step in range(1, size):
        pl.semaphore_signal(
            barrier, inc=1, device_id={"batch": lax.rem(me + step, size)}, device_id_type=MESH
        )
    pl.semaphore_wait(barrier, size - 1)
    copies = []
    for step in range(1, size):
        peer = lax.rem(me + step, size)
        for item in range(count):
            source = sources[item].at[peer] if kinds[item] else sources[item]
            copies.append(
                pltpu.make_async_remote_copy(
                    src_ref=source,
                    dst_ref=results[item].at[me],
                    send_sem=send_sem.at[item, step - 1],
                    recv_sem=recv_sem.at[item, step - 1],
                    device_id={"batch": peer},
                    device_id_type=MESH,
                )
            )
    for copy in copies:
        copy.start()
    own = []
    for item in range(count):
        source = sources[item].at[me] if kinds[item] else sources[item]
        own.append(pltpu.make_async_copy(source, results[item].at[me], own_sem.at[item]))
    for copy in own:
        copy.start()
    for copy in own:
        copy.wait()
    for copy in copies:
        copy.wait()


def batch_exchange(collective_id, size, whole=(), slots=()):
    arrays = list(whole) + list(slots)
    kinds = [0] * len(whole) + [1] * len(slots)
    count = len(arrays)
    shapes = [
        jax.ShapeDtypeStruct(a.shape if k else (size, *a.shape), a.dtype)
        for a, k in zip(arrays, kinds)
    ]
    return pl.pallas_call(
        functools.partial(batch_kernel, size, kinds),
        out_shape=shapes,
        in_specs=[pl.BlockSpec(memory_space=pltpu.VMEM)] * count,
        out_specs=[pl.BlockSpec(memory_space=pltpu.VMEM)] * count,
        scratch_shapes=[
            pltpu.SemaphoreType.DMA((count, size - 1)),
            pltpu.SemaphoreType.DMA((count, size - 1)),
            pltpu.SemaphoreType.DMA((count,)),
        ],
        compiler_params=pltpu.CompilerParams(collective_id=collective_id, has_side_effects=True),
    )(*arrays)


def square_kernel(count, *refs):
    sources, results = refs[:count], refs[count : 2 * count]
    send_sem, recv_sem, own_sem = refs[2 * count :]
    me = lax.axis_index("batch")
    across = me + 1 - 2 * lax.rem(me, 2)
    along = lax.rem(me + 2, 4)
    barrier = pltpu.get_barrier_semaphore()
    for peer in (across, along):
        pl.semaphore_signal(barrier, inc=1, device_id={"batch": peer}, device_id_type=MESH)
    pl.semaphore_wait(barrier, 2)

    def remote(source, target, item, turn, peer):
        copy = pltpu.make_async_remote_copy(
            src_ref=source,
            dst_ref=target,
            send_sem=send_sem.at[item, turn],
            recv_sem=recv_sem.at[item, turn],
            device_id={"batch": peer},
            device_id_type=MESH,
        )
        copy.start()
        return copy

    firsts = [
        [
            remote(sources[item], results[item].at[me], item, turn, peer)
            for turn, peer in enumerate((across, along))
        ]
        for item in range(count)
    ]
    own = [
        pltpu.make_async_copy(sources[item], results[item].at[me], own_sem.at[item])
        for item in range(count)
    ]
    for copy in own:
        copy.start()
    seconds = []
    for item in range(count):
        columns = sources[item].shape[-1]
        cut = columns // 256 * 128
        halves = (pl.ds(0, cut), pl.ds(cut, columns - cut))
        for turn, (giver, taker) in enumerate(((across, along), (along, across))):
            firsts[item][turn].wait_recv()
            block = results[item].at[giver, :, halves[turn]]
            seconds.append(remote(block, block, item, 2 + turn, taker))
    for copy in own:
        copy.wait()
    for copy in seconds:
        copy.wait()
    for pair in firsts:
        for copy in pair:
            copy.wait_send()


def square_gather(collective_id, *arrays):
    count = len(arrays)
    return pl.pallas_call(
        functools.partial(square_kernel, count),
        out_shape=[jax.ShapeDtypeStruct((4, *a.shape), a.dtype) for a in arrays],
        in_specs=[pl.BlockSpec(memory_space=pltpu.VMEM)] * count,
        out_specs=[pl.BlockSpec(memory_space=pltpu.VMEM)] * count,
        scratch_shapes=[
            pltpu.SemaphoreType.DMA((count, 4)),
            pltpu.SemaphoreType.DMA((count, 4)),
            pltpu.SemaphoreType.DMA((count,)),
        ],
        compiler_params=pltpu.CompilerParams(collective_id=collective_id, has_side_effects=True),
    )(*arrays)


def turn_kernel(
    mixed_ref,
    down_ref,
    middle_ref,
    upstream_ref,
    valid_ref,
    gain_ref,
    out_ref,
    grads_ref,
    gain_grad_ref,
    part_ref,
    taken_ref,
    send_sem,
    recv_sem,
    pass_sem,
    take_sem,
):
    me = lax.axis_index("batch")
    across = me + 1 - 2 * lax.rem(me, 2)
    along = lax.rem(me + 2, 4)
    corner = lax.rem(across + 2, 4)
    order = (corner, across, along)
    tok_count = middle_ref.shape[0]
    barrier = pltpu.get_barrier_semaphore()
    for peer in order:
        pl.semaphore_signal(barrier, inc=1, device_id={"batch": peer}, device_id_type=MESH)
    pl.semaphore_wait(barrier, 3)

    def product(place):
        rows = pl.ds(pl.multiple_of(place * tok_count, tok_count), tok_count)
        return jnp.dot(mixed_ref[rows, :], down_ref[...], preferred_element_type=F32)

    copies = [
        pltpu.make_async_remote_copy(
            src_ref=part_ref.at[turn],
            dst_ref=taken_ref.at[turn],
            send_sem=send_sem.at[turn],
            recv_sem=recv_sem.at[turn],
            device_id={"batch": peer},
            device_id_type=MESH,
        )
        for turn, peer in enumerate(order)
    ]
    for turn, peer in enumerate(order):
        part_ref[turn] = product(peer).astype(BF16)
        if turn > 0:
            copies[turn - 1].start()
    total = product(me)
    copies[2].start()
    for turn in range(3):
        copies[turn].wait_recv()
        total = total + taken_ref[turn].astype(F32)
    gain = gain_ref[...]
    valid = valid_ref[...]
    scale = lax.rsqrt(jnp.mean(total * total, axis=-1, keepdims=True) + EPS)
    upstream = upstream_ref[...].astype(F32) * valid
    gained = upstream * gain
    back = scale * gained - total * (
        scale * scale * scale * jnp.mean(total * gained, axis=-1, keepdims=True)
    )
    grads_ref[me] = back.astype(BF16)
    unit = total * scale
    out_ref[...] = ((middle_ref[...] + unit * gain) * valid).astype(BF16)
    gain_grad_ref[...] = jnp.sum(upstream * unit, axis=0, keepdims=True)

    def remote(block, turn, peer):
        copy = pltpu.make_async_remote_copy(
            src_ref=block,
            dst_ref=block,
            send_sem=pass_sem.at[turn],
            recv_sem=take_sem.at[turn],
            device_id={"batch": peer},
            device_id_type=MESH,
        )
        copy.start()
        return copy

    firsts = [remote(grads_ref.at[me], turn, peer) for turn, peer in enumerate((across, along))]
    columns = grads_ref.shape[-1]
    cut = columns // 256 * 128
    halves = (pl.ds(0, cut), pl.ds(cut, columns - cut))
    seconds = []
    for turn, (giver, taker) in enumerate(((across, along), (along, across))):
        firsts[turn].wait_recv()
        seconds.append(remote(grads_ref.at[giver, :, halves[turn]], 2 + turn, taker))
    for copy in seconds:
        copy.wait()
    for copy in firsts + copies:
        copy.wait_send()


def turn_round(mixed, down, middle, upstream, valid, gain):
    tok_count, width = middle.shape
    dma = pltpu.SemaphoreType.DMA
    vmem = pl.BlockSpec(memory_space=pltpu.VMEM)
    flops = 2 * mixed.shape[0] * mixed.shape[1] * width
    return pl.pallas_call(
        turn_kernel,
        name="turn_round",
        out_shape=(
            jax.ShapeDtypeStruct((tok_count, width), BF16),
            jax.ShapeDtypeStruct((4, tok_count, width), BF16),
            jax.ShapeDtypeStruct((1, width), F32),
        ),
        in_specs=[vmem] * 6,
        out_specs=[vmem] * 3,
        scratch_shapes=[
            pltpu.VMEM((3, tok_count, width), BF16),
            pltpu.VMEM((3, tok_count, width), BF16),
            dma((3,)),
            dma((3,)),
            dma((4,)),
            dma((4,)),
        ],
        cost_estimate=pl.CostEstimate(flops=flops, bytes_accessed=8 << 20, transcendentals=0),
        compiler_params=pltpu.CompilerParams(collective_id=3, has_side_effects=True),
    )(mixed, down, middle, upstream, valid, gain)


def product_kernel(left_ref, right_ref, out_ref):
    out_ref[...] = jnp.dot(left_ref[...], right_ref[...], preferred_element_type=F32).astype(BF16)


def product_low(tile, left, right):
    rows, depth = left.shape
    columns = right.shape[1]
    return pl.pallas_call(
        product_kernel,
        grid=(columns // tile,),
        out_shape=jax.ShapeDtypeStruct((rows, columns), BF16),
        in_specs=[
            pl.BlockSpec((rows, depth), lambda i: (0, 0)),
            pl.BlockSpec((depth, tile), lambda i: (0, i)),
        ],
        out_specs=pl.BlockSpec((rows, tile), lambda i: (0, i)),
        cost_estimate=pl.CostEstimate(
            flops=2 * rows * depth * columns, bytes_accessed=8 << 20, transcendentals=0
        ),
    )(left, right)


def mix_kernel(tokens_ref, w_gate_ref, w_up_ref, gate_ref, up_ref, mixed_ref, turned_ref):
    gate = project(tokens_ref[...], w_gate_ref[...])
    up = project(tokens_ref[...], w_up_ref[...])
    gate_ref[...] = gate
    up_ref[...] = up
    mixed = gated_gelu(gate, up)
    mixed_ref[...] = mixed.astype(BF16)
    turned_ref[...] = mixed.T.astype(BF16)


def hidden_mix(tile, tokens, both_weights):
    count, width = tokens.shape
    hidden = both_weights.shape[1] // 2
    steps = hidden // tile
    wide = jax.ShapeDtypeStruct((count, hidden), F32)
    column = pl.BlockSpec((count, tile), lambda i: (0, i))
    return pl.pallas_call(
        mix_kernel,
        name="hidden_mix",
        grid=(steps,),
        out_shape=(
            wide,
            wide,
            jax.ShapeDtypeStruct((count, hidden), BF16),
            jax.ShapeDtypeStruct((hidden, count), BF16),
        ),
        in_specs=[
            pl.BlockSpec((count, width), lambda i: (0, 0)),
            pl.BlockSpec((width, tile), lambda i: (0, i)),
            pl.BlockSpec((width, tile), lambda i: (0, i + steps)),
        ],
        out_specs=[column, column, column, pl.BlockSpec((tile, count), lambda i: (i, 0))],
        cost_estimate=pl.CostEstimate(
            flops=4 * count * hidden * width, bytes_accessed=24 << 20, transcendentals=0
        ),
    )(tokens, both_weights, both_weights)


def back_kernel(
    upstream_ref, down_ref, gate_ref, up_ref, w_gate_ref, w_up_ref, gate_out, up_out, back_ref, total
):
    step = pl.program_id(0)
    grad_mixed = project_back(upstream_ref[...], down_ref[...])
    _, pull_gelu = jax.vjp(gated_gelu, gate_ref[...], up_ref[...])
    grad_gate, grad_up = pull_gelu(grad_mixed)
    grad_gate, grad_up = grad_gate.astype(BF16), grad_up.astype(BF16)
    gate_out[...] = grad_gate
    up_out[...] = grad_up
    part = project_back(grad_gate, w_gate_ref[...]) + project_back(grad_up, w_up_ref[...])

    @pl.when(step == 0)
    def _():
        total[...] = part

    @pl.when(step > 0)
    def _():
        total[...] += part

    @pl.when(step == pl.num_programs(0) - 1)
    def _():
        back_ref[...] = total[...].astype(BF16)


def hidden_back(tile, upstream, down, gate_pre, up_pre, both_weights):
    tokens, width = upstream.shape
    hidden = down.shape[0]
    count = hidden // tile
    low = jax.ShapeDtypeStruct((tokens, hidden), BF16)
    return pl.pallas_call(
        back_kernel,
        name="hidden_back",
        grid=(count,),
        out_shape=(low, low, jax.ShapeDtypeStruct((tokens, width), BF16)),
        in_specs=[
            pl.BlockSpec((tokens, width), lambda i: (0, 0)),
            pl.BlockSpec((tile, width), lambda i: (i, 0)),
            pl.BlockSpec((tokens, tile), lambda i: (0, i)),
            pl.BlockSpec((tokens, tile), lambda i: (0, i)),
            pl.BlockSpec((width, tile), lambda i: (0, i)),
            pl.BlockSpec((width, tile), lambda i: (0, i + count)),
        ],
        out_specs=[
            pl.BlockSpec((tokens, tile), lambda i: (0, i)),
            pl.BlockSpec((tokens, tile), lambda i: (0, i)),
            pl.BlockSpec((tokens, width), lambda i: (0, 0)),
        ],
        scratch_shapes=[pltpu.VMEM((tokens, width), F32)],
        cost_estimate=pl.CostEstimate(
            flops=6 * tokens * hidden * width, bytes_accessed=24 << 20, transcendentals=0
        ),
    )(upstream, down, gate_pre, up_pre, both_weights, both_weights)


def halo_out_kernel(n_chip, source_ref, result_ref, send_sem, recv_sem):
    me = lax.axis_index("ctx")
    chip, core = me // 2, lax.rem(me, 2)
    near = {"ctx": me + 1 - 2 * core}
    after = {"ctx": jnp.minimum(me + 2, 2 * n_chip - 1)}
    has_after = chip < n_chip - 1
    barrier = pltpu.get_barrier_semaphore()
    pl.semaphore_signal(barrier, inc=1, device_id=near, device_id_type=MESH)

    @pl.when(chip > 0)
    def _():
        before = {"ctx": jnp.maximum(me - 2, 0)}
        pl.semaphore_signal(barrier, inc=1, device_id=before, device_id_type=MESH)

    pl.semaphore_wait(barrier, 1 + jnp.minimum(n_chip - 1 - chip, 1))

    def remote(source, slot, turn, peer):
        return pltpu.make_async_remote_copy(
            src_ref=source,
            dst_ref=result_ref.at[slot],
            send_sem=send_sem.at[turn],
            recv_sem=recv_sem.at[turn],
            device_id=peer,
            device_id_type=MESH,
        )

    one_on = remote(source_ref, 2, 0, after)
    two_on = remote(result_ref.at[2], 0, 1, after)
    own_near = remote(source_ref, 3, 2, near)
    before_near = remote(result_ref.at[2], 3 - 2 * (1 - core), 3, near)
    far_near = remote(result_ref.at[0], 1, 4, near)

    @pl.when(has_after)
    def _():
        one_on.start()

    @pl.when(core == 0)
    def _():
        own_near.start()

    def blank(slot):
        result_ref[slot] = jnp.zeros(result_ref.shape[1:], result_ref.dtype)

    @pl.when(chip == 0)
    def _():
        blank(2)
        blank(0)
        blank(1)

    @pl.when((chip == 0) & (core == 0))
    def _():
        blank(3)

    @pl.when(chip == 1)
    def _():
        blank(0)

    @pl.when((chip == 1) & (core == 0))
    def _():
        blank(1)

    @pl.when(chip > 0)
    def _():
        one_on.wait_recv()

    @pl.when((chip > 0) & has_after)
    def _():
        two_on.start()

    @pl.when(chip > 0)
    def _():
        before_near.start()

    @pl.when(chip > 1)
    def _():
        two_on.wait_recv()

    @pl.when((chip > 1) & (core == 1))
    def _():
        far_near.start()

    @pl.when(core == 1)
    def _():
        own_near.wait_recv()

    @pl.when(core == 0)
    def _():
        own_near.wait_send()

    @pl.when(chip > 0)
    def _():
        before_near.wait()

    @pl.when((chip > 1) & (core == 0))
    def _():
        far_near.wait_recv()

    @pl.when((chip > 1) & (core == 1))
    def _():
        far_near.wait_send()

    @pl.when(has_after)
    def _():
        one_on.wait_send()

    @pl.when((chip > 0) & has_after)
    def _():
        two_on.wait_send()


def halo_back_kernel(
    n_chip, source_ref, result_ref, near_ref, far_ref, way_ref, send_sem, recv_sem
):
    me = lax.axis_index("ctx")
    chip, core = me // 2, lax.rem(me, 2)
    near = {"ctx": me + 1 - 2 * core}
    before = {"ctx": jnp.maximum(me - 2, 0)}
    has_after = chip < n_chip - 1
    barrier = pltpu.get_barrier_semaphore()
    pl.semaphore_signal(barrier, inc=1, device_id=near, device_id_type=MESH)

    @pl.when(has_after)
    def _():
        after = {"ctx": jnp.minimum(me + 2, 2 * n_chip - 1)}
        pl.semaphore_signal(barrier, inc=1, device_id=after, device_id_type=MESH)

    pl.semaphore_wait(barrier, 1 + jnp.minimum(chip, 1))

    def remote(source, target, turn, peer):
        return pltpu.make_async_remote_copy(
            src_ref=source,
            dst_ref=target,
            send_sem=send_sem.at[turn],
            recv_sem=recv_sem.at[turn],
            device_id=peer,
            device_id_type=MESH,
        )

    to_before = remote(source_ref.at[3 - 2 * core], near_ref.at[0], 0, near)
    to_other = remote(source_ref.at[1 + 2 * core], near_ref.at[1], 1, near)
    to_before.start()
    to_other.start()

    @pl.when((chip == 0) | jnp.logical_not(has_after))
    def _():
        way_ref[0] = jnp.zeros(way_ref.shape[1:], way_ref.dtype)

    @pl.when(jnp.logical_not(has_after))
    def _():
        way_ref[1] = jnp.zeros(way_ref.shape[1:], way_ref.dtype)

    to_other.wait_recv()
    theirs = near_ref[1].astype(F32)
    far_ref[0] = (source_ref[0].astype(F32) + jnp.where(core == 1, theirs, 0.0)).astype(BF16)
    two_back = remote(far_ref.at[0], way_ref.at[0], 2, before)
    one_back = remote(far_ref.at[1], way_ref.at[1], 3, before)

    @pl.when(chip > 1)
    def _():
        two_back.start()

    to_before.wait_recv()
    due = source_ref[2].astype(F32) + near_ref[0].astype(F32)

    @pl.when((chip > 0) & has_after)
    def _():
        two_back.wait_recv()

    far_ref[1] = (due + way_ref[0].astype(F32)).astype(BF16)

    @pl.when(chip > 0)
    def _():
        one_back.start()

    @pl.when(has_after)
    def _():
        one_back.wait_recv()

    result_ref[...] = way_ref[1].astype(F32) + jnp.where(core == 0, theirs, 0.0)
    to_before.wait_send()
    to_other.wait_send()

    @pl.when(chip > 1)
    def _():
        two_back.wait_send()

    @pl.when(chip > 0)
    def _():
        one_back.wait_send()


def halo_call(collective_id, kernel, n_ctx, block, out_shape, buffers, copies):
    dma = pltpu.SemaphoreType.DMA
    return pl.pallas_call(
        functools.partial(kernel, n_ctx // 2),
        out_shape=out_shape,
        in_specs=[pl.BlockSpec(memory_space=pltpu.VMEM)],
        out_specs=pl.BlockSpec(memory_space=pltpu.VMEM),
        scratch_shapes=[*buffers, dma((copies,)), dma((copies,))],
        compiler_params=pltpu.CompilerParams(collective_id=collective_id, has_side_effects=True),
    )(block)


def halo_out(n_ctx, block):
    out_shape = jax.ShapeDtypeStruct((4, *block.shape), block.dtype)
    return halo_call(1, halo_out_kernel, n_ctx, block, out_shape, (), 5)


def halo_back(n_ctx, blocks):
    shape = blocks.shape[1:]
    buffers = [pltpu.VMEM((2, *shape), blocks.dtype)] * 3
    out_shape = jax.ShapeDtypeStruct(shape, F32)
    return halo_call(6, halo_back_kernel, n_ctx, blocks, out_shape, buffers, 4)


def pick_kernel(n_batch, n_ctx, piece, padded, gate_ref, up_ref, out_ref):
    me = lax.axis_index("batch")
    out_ref[...] = jnp.zeros_like(out_ref)
    for spot in range(n_batch):

        @pl.when(me == spot)
        def _():
            for shard in range(n_ctx):
                start = (shard * n_batch + spot) * piece
                for half, ref in enumerate((gate_ref, up_ref)):
                    place = (half * n_ctx + shard) * padded
                    out_ref[:, place : place + piece] = ref[:, start : start + piece]


def row_block(rows):
    return 48 if rows % 48 == 0 else rows


def pick_columns(n_batch, n_ctx, piece, padded, w_gate, w_up):
    rows, hidden = w_gate.shape
    block = row_block(rows)
    spec = pl.BlockSpec((block, hidden), lambda i: (i, 0))
    return pl.pallas_call(
        functools.partial(pick_kernel, n_batch, n_ctx, piece, padded),
        name="pick_columns",
        grid=(rows // block,),
        out_shape=jax.ShapeDtypeStruct((rows, 2 * n_ctx * padded), w_gate.dtype),
        in_specs=[spec, spec],
        out_specs=pl.BlockSpec((block, 2 * n_ctx * padded), lambda i: (i, 0)),
    )(w_gate, w_up)


def place_kernel(n_batch, n_ctx, piece, padded, parts_ref, out_ref):
    for shard in range(n_ctx):
        for spot in range(n_batch):
            start = (shard * n_batch + spot) * piece
            place = shard * padded
            out_ref[:, start : start + piece] = parts_ref[spot, :, place : place + piece].astype(F32)


def place_columns(n_batch, n_ctx, piece, padded, parts):
    rows = parts.shape[1]
    block = row_block(rows)
    hidden = n_batch * n_ctx * piece
    return pl.pallas_call(
        functools.partial(place_kernel, n_batch, n_ctx, piece, padded),
        grid=(rows // block,),
        out_shape=jax.ShapeDtypeStruct((rows, hidden), F32),
        in_specs=[pl.BlockSpec((n_batch, block, n_ctx * padded), lambda i: (0, i, 0))],
        out_specs=pl.BlockSpec((block, hidden), lambda i: (i, 0)),
    )(parts)


def weights_kernel(n_batch, n_ctx, qkv_ref, proj_ref, gain_ref, qkv_all, proj_all, gain_all, *sems):
    send_far, recv_far, send_side, recv_side, send_near, recv_near, own_sem = sems
    spot = lax.axis_index("batch")
    me = lax.axis_index("ctx")
    n_chip = n_ctx // 2
    chip, core = me // 2, lax.rem(me, 2)
    near = {"ctx": me + 1 - 2 * core}
    barrier = pltpu.get_barrier_semaphore()

    def far_at(step):
        return {"ctx": 2 * lax.rem(chip + step, n_chip) + core}

    def side_at(step):
        return {"batch": lax.rem(spot + step, n_batch)}

    peers = [near]
    peers += [far_at(step) for step in range(1, n_chip)]
    peers += [side_at(step) for step in range(1, n_batch)]
    for peer in peers:
        pl.semaphore_signal(barrier, inc=1, device_id=peer, device_id_type=MESH)
    pl.semaphore_wait(barrier, len(peers))

    def remote(source, target, send, recv, peer):
        return pltpu.make_async_remote_copy(
            src_ref=source,
            dst_ref=target,
            send_sem=send,
            recv_sem=recv,
            device_id=peer,
            device_id_type=MESH,
        )

    waits = []
    far = []
    for step in range(1, n_chip):
        triple = [
            remote(source, target, send_far.at[step - 1, item], recv_far.at[step - 1, item], far_at(step))
            for item, (source, target) in enumerate(
                (
                    (qkv_ref.at[spot], qkv_all.at[spot, me]),
                    (proj_ref.at[spot], proj_all.at[me, spot]),
                    (gain_ref, gain_all.at[me]),
                )
            )
        ]
        for copy in triple:
            copy.start()
        far.append(triple)
    own = [
        pltpu.make_async_copy(qkv_ref, qkv_all.at[:, me], own_sem.at[0]),
        pltpu.make_async_copy(proj_ref, proj_all.at[me], own_sem.at[1]),
        pltpu.make_async_copy(gain_ref, gain_all.at[me], own_sem.at[2]),
    ]
    for copy in own:
        copy.start()
    first = n_chip - 1
    pairs = [
        remote(source, target, send_near.at[first, 0, item], recv_near.at[first, 0, item], near)
        for item, (source, target) in enumerate(
            (
                (qkv_ref, qkv_all.at[:, me]),
                (proj_ref, proj_all.at[me]),
                (gain_ref, gain_all.at[me]),
            )
        )
    ]
    for copy in pairs:
        copy.start()
    waits += pairs

    def hand_near(step, turn):
        origin = 2 * lax.rem(chip + n_chip - step, n_chip) + core
        quarter = lax.rem(spot + n_batch - turn, n_batch)
        blocks = [qkv_all.at[quarter, origin], proj_all.at[origin, quarter]]
        blocks += [gain_all.at[origin]] if turn == 0 else []
        for item, block in enumerate(blocks):
            copy = remote(
                block,
                block,
                send_near.at[step - 1, turn, item],
                recv_near.at[step - 1, turn, item],
                near,
            )
            copy.start()
            waits.append(copy)

    side = []
    for step in range(1, n_chip):
        for copy in far[step - 1]:
            copy.wait_recv()
        origin = 2 * lax.rem(chip + n_chip - step, n_chip) + core
        for turn in range(1, n_batch):
            pair = [
                remote(
                    block,
                    block,
                    send_side.at[step - 1, turn - 1, item],
                    recv_side.at[step - 1, turn - 1, item],
                    side_at(turn),
                )
                for item, block in enumerate((qkv_all.at[spot, origin], proj_all.at[origin, spot]))
            ]
            for copy in pair:
                copy.start()
            side.append((step, turn, pair))
        hand_near(step, 0)
    for step, turn, pair in side:
        for copy in pair:
            copy.wait_recv()
        hand_near(step, turn)
    for copy in waits:
        copy.wait()
    for copy in own:
        copy.wait()
    for triple in far:
        for copy in triple:
            copy.wait_send()
    for _, _, pair in side:
        for copy in pair:
            copy.wait_send()


def gather_weights(n_batch, n_ctx, qkv, proj, gains):
    n_chip = n_ctx // 2
    dma = pltpu.SemaphoreType.DMA
    vmem = pl.BlockSpec(memory_space=pltpu.VMEM)
    return pl.pallas_call(
        functools.partial(weights_kernel, n_batch, n_ctx),
        name="gather_weights",
        out_shape=(
            jax.ShapeDtypeStruct((n_batch, n_ctx, *qkv.shape[1:]), qkv.dtype),
            jax.ShapeDtypeStruct((n_ctx, *proj.shape), proj.dtype),
            jax.ShapeDtypeStruct((n_ctx, *gains.shape), gains.dtype),
        ),
        in_specs=[vmem] * 3,
        out_specs=[vmem] * 3,
        scratch_shapes=[
            dma((n_chip - 1, 3)),
            dma((n_chip - 1, 3)),
            dma((n_chip - 1, n_batch - 1, 2)),
            dma((n_chip - 1, n_batch - 1, 2)),
            dma((n_chip, n_batch, 3)),
            dma((n_chip, n_batch, 3)),
            dma((3,)),
        ],
        compiler_params=pltpu.CompilerParams(collective_id=12, has_side_effects=True),
    )(qkv, proj, gains)


def tail_kernel(
    n_ctx,
    gate_ref,
    down_ref,
    up_ref,
    attn_ref,
    gate_all,
    down_all,
    up_all,
    attn_all,
    pair_up,
    pair_attn,
    way_up,
    way_attn,
    pair_send,
    pair_recv,
    way_send,
    way_recv,
    side_send,
    side_recv,
    own_sem,
):
    n_chip = n_ctx // 2
    spot = lax.axis_index("batch")
    me = lax.axis_index("ctx")
    chip, core = me // 2, lax.rem(me, 2)
    across = {"batch": spot + 1 - 2 * lax.rem(spot, 2)}
    along = {"batch": lax.rem(spot + 2, 4)}
    near = {"ctx": me + 1 - 2 * core}
    beyond = ({"ctx": jnp.minimum(me + 2, n_ctx - 1)}, {"ctx": jnp.maximum(me - 2, 0)})
    inner = (chip > 0, chip < n_chip - 1)
    barrier = pltpu.get_barrier_semaphore()
    for peer in (near, across, along):
        pl.semaphore_signal(barrier, inc=1, device_id=peer, device_id_type=MESH)
    for has_giver, giver in zip(inner, (beyond[1], beyond[0])):

        @pl.when(has_giver)
        def _():
            pl.semaphore_signal(barrier, inc=1, device_id=giver, device_id_type=MESH)

    pl.semaphore_wait(barrier, 3 + jnp.minimum(chip, 1) + jnp.minimum(n_chip - 1 - chip, 1))

    def remote(source, target, send, recv, peer):
        return pltpu.make_async_remote_copy(
            src_ref=source,
            dst_ref=target,
            send_sem=send,
            recv_sem=recv,
            device_id=peer,
            device_id_type=MESH,
        )

    width = up_ref.shape[-1]
    cut = width // 256 * 128
    chains = (
        (up_ref, pair_up, way_up, up_all, pl.ds(0, cut)),
        (up_ref, pair_up, way_up, up_all, pl.ds(cut, width - cut)),
        (attn_ref, pair_attn, way_attn, attn_all, pl.ds(0, attn_ref.shape[-1])),
    )
    numbers = range(len(chains))

    def pair_copy(number, place):
        source, pair, _, _, columns = chains[number]
        return remote(
            source.at[2 * place + 1 - core, :, columns],
            pair.at[place, :, columns],
            pair_send.at[number, place],
            pair_recv.at[number, place],
            near,
        )

    def way_copy(number, direction, step, source):
        _, _, way, _, columns = chains[number]
        return remote(
            source,
            way.at[direction, step - 1, :, columns],
            way_send.at[number, direction, step - 1],
            way_recv.at[number, direction, step - 1],
            beyond[direction],
        )

    def passes(direction, step):
        return chip <= step - 1 if direction == 0 else chip >= n_chip - step

    def bound_for(direction, step):
        place = chip + n_chip - step if direction == 0 else chip - n_chip + step
        return jnp.clip(place, 0, n_chip - 1)

    def side_pair(item, sources, target, columns):
        return [
            remote(
                sources,
                target.at[spot, :, columns],
                side_send.at[item, turn],
                side_recv.at[item, turn],
                peer,
            )
            for turn, peer in enumerate((across, along))
        ]

    def side_pass(item, firsts, target, start, length):
        half = length // 256 * 128
        halves = (pl.ds(start, half), pl.ds(start + half, length - half))
        copies = []
        for turn, (giver, taker) in enumerate(((across, along), (along, across))):
            firsts[turn].wait_recv()
            block = target.at[giver["batch"], :, halves[turn]]
            copies.append(
                remote(block, block, side_send.at[item, 2 + turn], side_recv.at[item, 2 + turn], taker)
            )
            copies[-1].start()
        return copies

    for number in numbers:
        for place in range(n_chip):
            pair_copy(number, place).start()
    early = ((gate_ref, gate_all), (down_ref, down_all))
    side_firsts = []
    for item, (source, target) in enumerate(early):
        side_firsts.append(side_pair(item, source, target, pl.ds(0, source.shape[-1])))
        for copy in side_firsts[-1]:
            copy.start()
    own = [
        pltpu.make_async_copy(source, target.at[spot], own_sem.at[item])
        for item, (source, target) in enumerate(early)
    ]
    for copy in own:
        copy.start()
    for _, _, way, _, columns in chains:
        for direction in range(2):

            @pl.when(jnp.logical_not(inner[direction]))
            def _():
                way[direction, n_chip - 2, :, columns] = jnp.zeros(
                    (way.shape[2], columns.size), way.dtype
                )

    for number in numbers:
        source, pair, _, _, columns = chains[number]
        for place in range(n_chip):
            pair_copy(number, place).wait_recv()
            pair[place, :, columns] = (
                pair[place, :, columns].astype(F32)
                + source[2 * place + core, :, columns].astype(F32)
            ).astype(BF16)
        for direction in range(2):

            @pl.when(passes(direction, 1))
            def _():
                place = bound_for(direction, 1)
                way_copy(number, direction, 1, pair.at[place, :, columns]).start()

    side_seconds = []
    for step in range(2, n_chip + 1):
        if step <= 3:
            item = step - 2
            target = early[item][1]
            side_seconds += side_pass(item, side_firsts[item], target, 0, target.shape[-1])
        if step == n_chip:
            break
        for number in numbers:
            _, pair, way, _, columns = chains[number]
            for direction in range(2):
                place = bound_for(direction, step)

                @pl.when(passes(direction, step) & inner[direction])
                def _():
                    way_copy(number, direction, step - 1, pair.at[place, :, columns]).wait_recv()
                    way[direction, step - 2, :, columns] = (
                        way[direction, step - 2, :, columns].astype(F32)
                        + pair[place, :, columns].astype(F32)
                    ).astype(BF16)

            for direction in range(2):
                place = bound_for(direction, step)

                @pl.when(passes(direction, step) & inner[direction])
                def _():
                    way_copy(number, direction, step, way.at[direction, step - 2, :, columns]).start()

                @pl.when(passes(direction, step) & jnp.logical_not(inner[direction]))
                def _():
                    way_copy(number, direction, step, pair.at[place, :, columns]).start()

    chain_firsts = []
    for number in numbers:
        _, pair, way, target, columns = chains[number]
        for direction in range(2):

            @pl.when(inner[direction])
            def _():
                way_copy(number, direction, n_chip - 1, pair.at[0, :, columns]).wait_recv()

        target[spot, :, columns] = (
            pair[chip, :, columns].astype(F32)
            + way[0, n_chip - 2, :, columns].astype(F32)
            + way[1, n_chip - 2, :, columns].astype(F32)
        ).astype(BF16)
        firsts = side_pair(2 + number, target.at[spot, :, columns], target, columns)
        for copy in firsts:
            copy.start()
        chain_firsts.append(firsts)
    for number in numbers:
        _, _, _, target, columns = chains[number]
        side_seconds += side_pass(
            2 + number, chain_firsts[number], target, columns.start, columns.size
        )
    for copy in own:
        copy.wait()
    for copy in side_seconds:
        copy.wait()
    for firsts in side_firsts + chain_firsts:
        for copy in firsts:
            copy.wait_send()
    for number in numbers:
        _, pair, _, _, columns = chains[number]
        for place in range(n_chip):
            pair_copy(number, place).wait_send()
        for direction in range(2):
            for step in range(1, n_chip):

                @pl.when(passes(direction, step))
                def _():
                    way_copy(number, direction, step, pair.at[0, :, columns]).wait_send()


def tail_round(n_ctx, gate, down, up, attn):
    n_chip = n_ctx // 2
    dma = pltpu.SemaphoreType.DMA
    vmem = pl.BlockSpec(memory_space=pltpu.VMEM)
    shapes = (gate.shape, down.shape, up.shape[1:], attn.shape[1:])
    return pl.pallas_call(
        functools.partial(tail_kernel, n_ctx),
        name="tail_round",
        out_shape=[jax.ShapeDtypeStruct((4, *shape), BF16) for shape in shapes],
        in_specs=[vmem] * 4,
        out_specs=[vmem] * 4,
        scratch_shapes=[
            pltpu.VMEM((n_chip, *up.shape[1:]), BF16),
            pltpu.VMEM((n_chip, *attn.shape[1:]), BF16),
            pltpu.VMEM((2, n_chip - 1, *up.shape[1:]), BF16),
            pltpu.VMEM((2, n_chip - 1, *attn.shape[1:]), BF16),
            dma((3, n_chip)),
            dma((3, n_chip)),
            dma((3, 2, n_chip - 1)),
            dma((3, 2, n_chip - 1)),
            dma((5, 4)),
            dma((5, 4)),
            dma((2,)),
        ],
        compiler_params=pltpu.CompilerParams(collective_id=8, has_side_effects=True),
    )(gate, down, up, attn)


def gathered(shard):
    return lax.all_gather(shard, "ctx", axis=0, tiled=True)


def scattered(whole):
    return lax.psum_scatter(whole, "ctx", scatter_dimension=0, tiled=True)


def local(
    n_batch,
    n_ctx,
    block_in,
    positions,
    counts,
    cotangent,
    gain_input,
    w_query,
    w_key,
    w_value,
    gain_query,
    gain_key,
    w_output,
    gain_attn,
    gain_ffn,
    w_gate,
    w_up,
    w_down,
    gain_final,
):
    block_in = block_in[0]
    positions = positions[0]
    cotangent = cotangent[0]
    tok_count, model_width = block_in.shape
    width_shard = w_query.shape[0]
    query_width = w_query.shape[1]
    head_size = w_key.shape[1]
    head_count = query_width // head_size
    hidden_shard = w_down.shape[0]
    piece = hidden_shard // n_batch
    hidden_part = -(-piece * n_ctx // 128) * 128
    padded = hidden_part // n_ctx
    halo_depth = (WINDOW + tok_count - 2) // tok_count
    assert halo_depth == 4
    batch_at = lax.axis_index("batch")
    ctx_at = lax.axis_index("ctx")
    all_tok = n_batch * tok_count

    gains = jnp.concatenate(
        [gain_input, gain_attn, gain_ffn, gain_final, gain_query, gain_key]
    )
    slots_of = query_width + 2 * head_size
    quarter = slots_of // n_batch
    qkv_full, proj_full, gains_all = gather_weights(
        n_batch,
        n_ctx,
        jnp.concatenate([w_query, w_key, w_value], axis=1)
        .reshape(width_shard, n_batch, quarter)
        .transpose(1, 0, 2),
        w_output.reshape(n_batch, -1, model_width),
        gains[None],
    )
    qkv_full = qkv_full.reshape(n_batch, model_width, quarter)
    full_output = proj_full.reshape(query_width, model_width)
    gains_all = gains_all[:, 0].astype(F32)

    def gain_at(start, length):
        return gains_all[:, start : start + length].reshape(1, -1)

    head_shard = gain_query.shape[0]
    full_gain_in = gain_at(0, width_shard)
    full_gain_attn = gain_at(width_shard, width_shard)
    full_gain_ffn = gain_at(2 * width_shard, width_shard)
    full_gain_final = gain_at(3 * width_shard, width_shard)
    full_gain_q = gain_at(4 * width_shard, head_shard)
    full_gain_k = gain_at(4 * width_shard + head_shard, head_shard)

    part_both = gathered(pick_columns(n_batch, n_ctx, piece, padded, w_gate, w_up))
    own_down = lax.dynamic_slice_in_dim(w_down, batch_at * piece, piece, 0)
    part_down = gathered(jnp.pad(own_down, ((0, padded - piece), (0, 0))))

    first_token = ctx_at * tok_count
    token_place = first_token + jnp.arange(tok_count, dtype=jnp.int32)
    valid_mask = (token_place < counts[0]).astype(F32)[:, None]
    resid_in = block_in.astype(F32)
    act_in = normed(resid_in, full_gain_in).astype(BF16)
    qkv_raw = jnp.concatenate([project(act_in, qkv_full[i]) for i in range(n_batch)], axis=1)
    query_raw = qkv_raw[:, :query_width].reshape(tok_count, head_count, head_size)
    key_raw = qkv_raw[:, query_width : query_width + head_size]
    value_low = qkv_raw[:, query_width + head_size :].astype(BF16)
    inv_freq = BASE ** (-jnp.arange(0, head_size, 2, dtype=F32) / head_size)
    angles = positions.astype(F32)[:, None] * inv_freq

    def query_path(raw_query, gain_vec):
        return rotate(normed(raw_query, gain_vec), angles[:, None, :])

    def key_path(raw_key, gain_vec):
        return rotate(normed(raw_key, gain_vec), angles)

    query_rot = query_path(query_raw, full_gain_q).astype(BF16)
    key_rot = key_path(key_raw, full_gain_k).astype(BF16)
    own_pair = jnp.concatenate([key_rot, value_low], axis=-1)
    halo = halo_out(n_ctx, own_pair)
    context = jnp.concatenate([halo.reshape(halo_depth * tok_count, -1), own_pair], axis=0)
    ctx_keys = context[:, :head_size]
    ctx_values = context[:, head_size:]
    key_total = (halo_depth + 1) * tok_count
    distance = (
        jnp.arange(tok_count, dtype=jnp.int32)[:, None]
        + halo_depth * tok_count
        - jnp.arange(key_total, dtype=jnp.int32)[None, :]
    )
    allowed = (distance >= 0) & (distance < WINDOW) & (distance <= positions[:, None])
    score_scale = head_size ** (-0.5)
    raw_scores = jnp.einsum("thd,kd->htk", query_rot, ctx_keys, preferred_element_type=F32)
    scores = jnp.where(allowed[None], raw_scores * score_scale, MASKED)
    exp_scores = jnp.exp(scores - jnp.max(scores, axis=-1, keepdims=True))
    attn_prob = exp_scores / jnp.sum(exp_scores, axis=-1, keepdims=True)
    prob_low = attn_prob.astype(BF16)
    attended = jnp.einsum("htk,kd->thd", prob_low, ctx_values, preferred_element_type=F32)
    attn_low = attended.reshape(tok_count, query_width).astype(BF16)
    attn_proj = project(attn_low, full_output)
    middle = resid_in + normed(attn_proj, full_gain_attn)
    ffn_in = normed(middle, full_gain_ffn).astype(BF16)

    (ffn_in_all,) = square_gather(2, ffn_in)
    ffn_in_all = ffn_in_all.reshape(all_tok, model_width)
    gate_pre, up_pre, mixed_low, mixed_turned = hidden_mix(256, ffn_in_all, part_both)
    mixed_low, act_in_late, attn_late = lax.optimization_barrier((mixed_low, act_in, attn_low))
    act_in_all, attn_all = square_gather(13, act_in_late, attn_late)
    ffn_in_turned = ffn_in_all.T
    mixed_low, act_in_all, attn_all, mixed_turned, ffn_in_turned = lax.optimization_barrier(
        (mixed_low, act_in_all, attn_all, mixed_turned, ffn_in_turned)
    )
    act_in_all = act_in_all.reshape(all_tok, model_width)
    attn_all = attn_all.reshape(all_tok, query_width)
    block_out, grad_ffn_low, grad_gain_final = turn_round(
        mixed_low, part_down, middle, cotangent, valid_mask, full_gain_final
    )

    grad_final = cotangent.astype(F32) * valid_mask
    grad_ffn_low = grad_ffn_low.reshape(all_tok, model_width)
    down_grad = product_low(384, mixed_turned, grad_ffn_low)
    down_grad, grad_ffn_low = lax.optimization_barrier((down_grad, grad_ffn_low))
    grad_w_down = scattered(down_grad)
    grad_gate_low, grad_up_low, back_part = hidden_back(
        256, grad_ffn_low, part_down, gate_pre, up_pre, part_both
    )
    (back_parts,) = batch_exchange(
        5, n_batch, slots=(back_part.reshape(n_batch, tok_count, model_width),)
    )
    back_parts, grad_gate_low, grad_up_low = lax.optimization_barrier(
        (back_parts, grad_gate_low, grad_up_low)
    )
    gate_grad = product_low(256, ffn_in_turned, grad_gate_low)
    up_grad = product_low(256, ffn_in_turned, grad_up_low)
    back_parts, gate_grad, up_grad = lax.optimization_barrier((back_parts, gate_grad, up_grad))
    grad_w_gate = scattered(gate_grad)
    grad_ffn_in = jnp.sum(back_parts.astype(F32), axis=0)
    _, pull_ffn_norm = jax.vjp(normed, middle, full_gain_ffn)
    grad_middle_part, grad_gain_ffn = pull_ffn_norm(grad_ffn_in)
    grad_middle = grad_final + grad_middle_part
    _, pull_attn_norm = jax.vjp(normed, attn_proj, full_gain_attn)
    grad_attn_proj, grad_gain_attn = pull_attn_norm(grad_middle)

    grad_proj_low = grad_attn_proj.astype(BF16)
    grad_attended = (
        project_back(grad_proj_low, full_output)
        .astype(BF16)
        .reshape(tok_count, head_count, head_size)
    )
    grad_prob = jnp.einsum("thd,kd->htk", grad_attended, ctx_values, preferred_element_type=F32)
    row_delta = jnp.sum(attn_prob * grad_prob, axis=-1, keepdims=True)
    grad_scores = (attn_prob * (grad_prob - row_delta)).astype(BF16)
    grad_queries = (
        jnp.einsum("htk,kd->thd", grad_scores, ctx_keys, preferred_element_type=F32) * score_scale
    )
    grad_ctx_keys = (
        jnp.einsum("htk,thd->kd", grad_scores, query_rot, preferred_element_type=F32) * score_scale
    )
    grad_ctx_values = jnp.einsum("htk,thd->kd", prob_low, grad_attended, preferred_element_type=F32)
    grad_context = jnp.concatenate([grad_ctx_keys, grad_ctx_values], axis=-1)
    halo_rows = halo_depth * tok_count
    returned = halo_back(
        n_ctx,
        grad_context[:halo_rows].astype(BF16).reshape(halo_depth, tok_count, 2 * head_size),
    )
    own_grad = grad_context[halo_rows:] + returned
    grad_value_low = own_grad[:, head_size:].astype(BF16)
    _, pull_key = jax.vjp(key_path, key_raw, full_gain_k)
    grad_key_raw, grad_gain_key = pull_key(own_grad[:, :head_size])
    _, pull_query = jax.vjp(query_path, query_raw, full_gain_q)
    grad_query_raw, grad_gain_query = pull_query(grad_queries)
    grad_qkv_low = jnp.concatenate(
        [
            grad_query_raw.astype(BF16).reshape(tok_count, query_width),
            grad_key_raw.astype(BF16),
            grad_value_low,
        ],
        axis=1,
    )
    grad_act_in = sum(
        project_back(grad_qkv_low[:, i * quarter : (i + 1) * quarter], qkv_full[i])
        for i in range(n_batch)
    )
    _, pull_input = jax.vjp(normed, resid_in, full_gain_in)
    grad_in_part, grad_gain_input = pull_input(grad_act_in)
    grad_in = (grad_middle + grad_in_part).astype(BF16)

    def column_slots(upstream):
        return upstream.reshape(tok_count, n_batch, -1).transpose(1, 0, 2)

    gain_rows = jnp.concatenate(
        [
            grad.reshape(n_ctx, -1)
            for grad in (
                grad_gain_input,
                grad_gain_attn,
                grad_gain_ffn,
                grad_gain_final,
                grad_gain_query,
                grad_gain_key,
            )
        ],
        axis=1,
    )
    gain_parts, qkv_slots, proj_slots = batch_exchange(
        7,
        n_batch,
        whole=(gain_rows,),
        slots=(column_slots(grad_qkv_low), column_slots(grad_proj_low)),
    )
    proj_rows = w_output.shape[0]
    gain_count = gain_rows.shape[1]
    gain_lines = -(-gain_count // quarter)
    used = width_shard + proj_rows + gain_lines
    lines = -(-used // 16) * 16
    grad_w_output = weight_grad(attn_all, proj_slots.reshape(all_tok, -1)).astype(BF16)
    grad_w_qkv = weight_grad(act_in_all, qkv_slots.reshape(all_tok, -1)).astype(BF16)
    output_part = model_width // n_batch
    gain_sum = jnp.sum(gain_parts, axis=0).astype(BF16)
    packed = jnp.concatenate(
        [
            grad_w_qkv.reshape(n_ctx, width_shard, quarter),
            jnp.pad(
                grad_w_output.reshape(n_ctx, proj_rows, output_part),
                ((0, 0), (0, 0), (0, quarter - output_part)),
            ),
            jnp.pad(gain_sum, ((0, 0), (0, gain_lines * quarter - gain_count))).reshape(
                n_ctx, gain_lines, quarter
            ),
            jnp.zeros((n_ctx, lines - used, quarter), BF16),
        ],
        axis=1,
    )
    gate_all, down_all, up_all, attn_grads = tail_round(
        n_ctx,
        grad_w_gate,
        grad_w_down,
        up_grad.reshape(n_ctx, width_shard, hidden_part),
        packed,
    )
    gain_mine = attn_grads[0, width_shard + proj_rows : used].reshape(-1).astype(F32)

    def columns_back(pieces):
        return pieces.astype(F32).transpose(1, 0, 2).reshape(pieces.shape[1], -1)

    grad_qkv_shard = columns_back(attn_grads[:, :width_shard])
    return (
        block_out[None],
        grad_in[None],
        gain_mine[:width_shard],
        grad_qkv_shard[:, :query_width],
        grad_qkv_shard[:, query_width : query_width + head_size],
        grad_qkv_shard[:, query_width + head_size :],
        gain_mine[4 * width_shard : 4 * width_shard + head_shard],
        gain_mine[4 * width_shard + head_shard : gain_count],
        columns_back(attn_grads[:, width_shard : width_shard + proj_rows, :output_part]),
        gain_mine[width_shard : 2 * width_shard],
        gain_mine[2 * width_shard : 3 * width_shard],
        place_columns(n_batch, n_ctx, piece, padded, gate_all),
        place_columns(n_batch, n_ctx, piece, padded, up_all),
        down_all[:, :piece].reshape(hidden_shard, model_width).astype(F32),
        gain_mine[3 * width_shard : 4 * width_shard],
    )


def solution(mesh):
    matrix = P("ctx", None)
    vector = P("ctx")
    tokens = P("batch", "ctx", None)

    def step(*arrays):
        return local(mesh.shape["batch"], mesh.shape["ctx"], *arrays)

    return jax.shard_map(
        step,
        mesh=mesh,
        in_specs=(
            tokens,
            P("batch", "ctx"),
            P("batch"),
            tokens,
            vector,
            matrix,
            matrix,
            matrix,
            vector,
            vector,
            matrix,
            vector,
            vector,
            matrix,
            matrix,
            matrix,
            vector,
        ),
        out_specs=(
            tokens,
            tokens,
            vector,
            matrix,
            matrix,
            matrix,
            vector,
            vector,
            matrix,
            vector,
            vector,
            matrix,
            matrix,
            matrix,
            vector,
        ),
        check_vma=False,
    )
```

```python
import functools

import jax
import jax.numpy as jnp
from jax import lax
from jax.experimental import pallas as pl
from jax.experimental.pallas import tpu as pltpu
from jax.sharding import PartitionSpec as P

WINDOW = 512


EPS = 1e-06
BASE = 10000.0
MASKED = -1e30
BF16 = jnp.bfloat16
F32 = jnp.float32
MESH = pl.DeviceIdType.MESH


def normed(vector, gain_vec):
    return vector * lax.rsqrt(jnp.mean(vector * vector, axis=-1, keepdims=True) + EPS) * gain_vec


def rotate(vector, angles):
    half_size = vector.shape[-1] // 2
    cosine = jnp.cos(angles)
    sine_part = jnp.sin(angles)
    first_half = vector[..., :half_size]
    second = vector[..., half_size:]
    return jnp.concatenate(
        [first_half * cosine - second * sine_part, second * cosine + first_half * sine_part],
        axis=-1,
    )


def project(inputs, weight):
    return lax.dot_general(inputs, weight, (((1,), (0,)), ((), ())), preferred_element_type=F32)


def project_back(upstream, weight):
    return lax.dot_general(upstream, weight, (((1,), (1,)), ((), ())), preferred_element_type=F32)


def weight_grad(inputs, upstream):
    return lax.dot_general(inputs, upstream, (((0,), (0,)), ((), ())), preferred_element_type=F32)


def gated_gelu(gate_val, up_val):
    return jax.nn.gelu(gate_val, approximate=True) * up_val


def batch_kernel(size, kinds, *refs):
    count = len(kinds)
    sources, results = refs[:count], refs[count : 2 * count]
    send_sem, recv_sem, own_sem = refs[2 * count :]
    me = lax.axis_index("batch")
    barrier = pltpu.get_barrier_semaphore()
    for step in range(1, size):
        pl.semaphore_signal(
            barrier, inc=1, device_id={"batch": lax.rem(me + step, size)}, device_id_type=MESH
        )
    pl.semaphore_wait(barrier, size - 1)
    copies = []
    for step in range(1, size):
        peer = lax.rem(me + step, size)
        for item in range(count):
            source = sources[item].at[peer] if kinds[item] else sources[item]
            copies.append(
                pltpu.make_async_remote_copy(
                    src_ref=source,
                    dst_ref=results[item].at[me],
                    send_sem=send_sem.at[item, step - 1],
                    recv_sem=recv_sem.at[item, step - 1],
                    device_id={"batch": peer},
                    device_id_type=MESH,
                )
            )
    for copy in copies:
        copy.start()
    own = []
    for item in range(count):
        source = sources[item].at[me] if kinds[item] else sources[item]
        own.append(pltpu.make_async_copy(source, results[item].at[me], own_sem.at[item]))
    for copy in own:
        copy.start()
    for copy in own:
        copy.wait()
    for copy in copies:
        copy.wait()


def batch_exchange(collective_id, size, whole=(), slots=()):
    arrays = list(whole) + list(slots)
    kinds = [0] * len(whole) + [1] * len(slots)
    count = len(arrays)
    shapes = [
        jax.ShapeDtypeStruct(a.shape if k else (size, *a.shape), a.dtype)
        for a, k in zip(arrays, kinds)
    ]
    return pl.pallas_call(
        functools.partial(batch_kernel, size, kinds),
        out_shape=shapes,
        in_specs=[pl.BlockSpec(memory_space=pltpu.VMEM)] * count,
        out_specs=[pl.BlockSpec(memory_space=pltpu.VMEM)] * count,
        scratch_shapes=[
            pltpu.SemaphoreType.DMA((count, size - 1)),
            pltpu.SemaphoreType.DMA((count, size - 1)),
            pltpu.SemaphoreType.DMA((count,)),
        ],
        compiler_params=pltpu.CompilerParams(collective_id=collective_id, has_side_effects=True),
    )(*arrays)


def square_kernel(count, *refs):
    sources, results = refs[:count], refs[count : 2 * count]
    send_sem, recv_sem, own_sem = refs[2 * count :]
    me = lax.axis_index("batch")
    across = me + 1 - 2 * lax.rem(me, 2)
    along = lax.rem(me + 2, 4)
    barrier = pltpu.get_barrier_semaphore()
    for peer in (across, along):
        pl.semaphore_signal(barrier, inc=1, device_id={"batch": peer}, device_id_type=MESH)
    pl.semaphore_wait(barrier, 2)

    def remote(source, target, item, turn, peer):
        copy = pltpu.make_async_remote_copy(
            src_ref=source,
            dst_ref=target,
            send_sem=send_sem.at[item, turn],
            recv_sem=recv_sem.at[item, turn],
            device_id={"batch": peer},
            device_id_type=MESH,
        )
        copy.start()
        return copy

    firsts = [
        [
            remote(sources[item], results[item].at[me], item, turn, peer)
            for turn, peer in enumerate((across, along))
        ]
        for item in range(count)
    ]
    own = [
        pltpu.make_async_copy(sources[item], results[item].at[me], own_sem.at[item])
        for item in range(count)
    ]
    for copy in own:
        copy.start()
    seconds = []
    for item in range(count):
        columns = sources[item].shape[-1]
        cut = columns // 256 * 128
        halves = (pl.ds(0, cut), pl.ds(cut, columns - cut))
        for turn, (giver, taker) in enumerate(((across, along), (along, across))):
            firsts[item][turn].wait_recv()
            block = results[item].at[giver, :, halves[turn]]
            seconds.append(remote(block, block, item, 2 + turn, taker))
    for copy in own:
        copy.wait()
    for copy in seconds:
        copy.wait()
    for pair in firsts:
        for copy in pair:
            copy.wait_send()


def square_gather(collective_id, *arrays):
    count = len(arrays)
    return pl.pallas_call(
        functools.partial(square_kernel, count),
        out_shape=[jax.ShapeDtypeStruct((4, *a.shape), a.dtype) for a in arrays],
        in_specs=[pl.BlockSpec(memory_space=pltpu.VMEM)] * count,
        out_specs=[pl.BlockSpec(memory_space=pltpu.VMEM)] * count,
        scratch_shapes=[
            pltpu.SemaphoreType.DMA((count, 4)),
            pltpu.SemaphoreType.DMA((count, 4)),
            pltpu.SemaphoreType.DMA((count,)),
        ],
        compiler_params=pltpu.CompilerParams(collective_id=collective_id, has_side_effects=True),
    )(*arrays)


def turn_kernel(
    mixed_ref,
    down_ref,
    middle_ref,
    upstream_ref,
    valid_ref,
    gain_ref,
    out_ref,
    grads_ref,
    gain_grad_ref,
    part_ref,
    taken_ref,
    send_sem,
    recv_sem,
    pass_sem,
    take_sem,
):
    me = lax.axis_index("batch")
    across = me + 1 - 2 * lax.rem(me, 2)
    along = lax.rem(me + 2, 4)
    corner = lax.rem(across + 2, 4)
    order = (corner, across, along)
    tok_count = middle_ref.shape[0]
    barrier = pltpu.get_barrier_semaphore()
    for peer in order:
        pl.semaphore_signal(barrier, inc=1, device_id={"batch": peer}, device_id_type=MESH)
    pl.semaphore_wait(barrier, 3)

    def product(place):
        rows = pl.ds(pl.multiple_of(place * tok_count, tok_count), tok_count)
        return jnp.dot(mixed_ref[rows, :], down_ref[...], preferred_element_type=F32)

    copies = [
        pltpu.make_async_remote_copy(
            src_ref=part_ref.at[turn],
            dst_ref=taken_ref.at[turn],
            send_sem=send_sem.at[turn],
            recv_sem=recv_sem.at[turn],
            device_id={"batch": peer},
            device_id_type=MESH,
        )
        for turn, peer in enumerate(order)
    ]
    for turn, peer in enumerate(order):
        part_ref[turn] = product(peer).astype(BF16)
        if turn > 0:
            copies[turn - 1].start()
    total = product(me)
    copies[2].start()
    for turn in range(3):
        copies[turn].wait_recv()
        total = total + taken_ref[turn].astype(F32)
    gain = gain_ref[...]
    valid = valid_ref[...]
    scale = lax.rsqrt(jnp.mean(total * total, axis=-1, keepdims=True) + EPS)
    upstream = upstream_ref[...].astype(F32) * valid
    gained = upstream * gain
    back = scale * gained - total * (
        scale * scale * scale * jnp.mean(total * gained, axis=-1, keepdims=True)
    )
    grads_ref[me] = back.astype(BF16)
    unit = total * scale
    out_ref[...] = ((middle_ref[...] + unit * gain) * valid).astype(BF16)
    gain_grad_ref[...] = jnp.sum(upstream * unit, axis=0, keepdims=True)

    def remote(block, turn, peer):
        copy = pltpu.make_async_remote_copy(
            src_ref=block,
            dst_ref=block,
            send_sem=pass_sem.at[turn],
            recv_sem=take_sem.at[turn],
            device_id={"batch": peer},
            device_id_type=MESH,
        )
        copy.start()
        return copy

    firsts = [remote(grads_ref.at[me], turn, peer) for turn, peer in enumerate((across, along))]
    columns = grads_ref.shape[-1]
    cut = columns // 256 * 128
    halves = (pl.ds(0, cut), pl.ds(cut, columns - cut))
    seconds = []
    for turn, (giver, taker) in enumerate(((across, along), (along, across))):
        firsts[turn].wait_recv()
        seconds.append(remote(grads_ref.at[giver, :, halves[turn]], 2 + turn, taker))
    for copy in seconds:
        copy.wait()
    for copy in firsts + copies:
        copy.wait_send()


def turn_round(mixed, down, middle, upstream, valid, gain):
    tok_count, width = middle.shape
    dma = pltpu.SemaphoreType.DMA
    vmem = pl.BlockSpec(memory_space=pltpu.VMEM)
    flops = 2 * mixed.shape[0] * mixed.shape[1] * width
    return pl.pallas_call(
        turn_kernel,
        name="turn_round",
        out_shape=(
            jax.ShapeDtypeStruct((tok_count, width), BF16),
            jax.ShapeDtypeStruct((4, tok_count, width), BF16),
            jax.ShapeDtypeStruct((1, width), F32),
        ),
        in_specs=[vmem] * 6,
        out_specs=[vmem] * 3,
        scratch_shapes=[
            pltpu.VMEM((3, tok_count, width), BF16),
            pltpu.VMEM((3, tok_count, width), BF16),
            dma((3,)),
            dma((3,)),
            dma((4,)),
            dma((4,)),
        ],
        cost_estimate=pl.CostEstimate(flops=flops, bytes_accessed=8 << 20, transcendentals=0),
        compiler_params=pltpu.CompilerParams(collective_id=3, has_side_effects=True),
    )(mixed, down, middle, upstream, valid, gain)


def product_kernel(left_ref, right_ref, out_ref):
    out_ref[...] = jnp.dot(left_ref[...], right_ref[...], preferred_element_type=F32).astype(BF16)


def product_low(tile, left, right):
    rows, depth = left.shape
    columns = right.shape[1]
    return pl.pallas_call(
        product_kernel,
        grid=(columns // tile,),
        out_shape=jax.ShapeDtypeStruct((rows, columns), BF16),
        in_specs=[
            pl.BlockSpec((rows, depth), lambda i: (0, 0)),
            pl.BlockSpec((depth, tile), lambda i: (0, i)),
        ],
        out_specs=pl.BlockSpec((rows, tile), lambda i: (0, i)),
        cost_estimate=pl.CostEstimate(
            flops=2 * rows * depth * columns, bytes_accessed=8 << 20, transcendentals=0
        ),
    )(left, right)


def mix_kernel(tokens_ref, w_gate_ref, w_up_ref, gate_ref, up_ref, mixed_ref, turned_ref):
    gate = project(tokens_ref[...], w_gate_ref[...])
    up = project(tokens_ref[...], w_up_ref[...])
    gate_ref[...] = gate
    up_ref[...] = up
    mixed = gated_gelu(gate, up)
    mixed_ref[...] = mixed.astype(BF16)
    turned_ref[...] = mixed.T.astype(BF16)


def hidden_mix(tile, tokens, both_weights):
    count, width = tokens.shape
    hidden = both_weights.shape[1] // 2
    steps = hidden // tile
    wide = jax.ShapeDtypeStruct((count, hidden), F32)
    column = pl.BlockSpec((count, tile), lambda i: (0, i))
    return pl.pallas_call(
        mix_kernel,
        name="hidden_mix",
        grid=(steps,),
        out_shape=(
            wide,
            wide,
            jax.ShapeDtypeStruct((count, hidden), BF16),
            jax.ShapeDtypeStruct((hidden, count), BF16),
        ),
        in_specs=[
            pl.BlockSpec((count, width), lambda i: (0, 0)),
            pl.BlockSpec((width, tile), lambda i: (0, i)),
            pl.BlockSpec((width, tile), lambda i: (0, i + steps)),
        ],
        out_specs=[column, column, column, pl.BlockSpec((tile, count), lambda i: (i, 0))],
        cost_estimate=pl.CostEstimate(
            flops=4 * count * hidden * width, bytes_accessed=24 << 20, transcendentals=0
        ),
    )(tokens, both_weights, both_weights)


def back_kernel(
    upstream_ref, down_ref, gate_ref, up_ref, w_gate_ref, w_up_ref, gate_out, up_out, back_ref, total
):
    step = pl.program_id(0)
    grad_mixed = project_back(upstream_ref[...], down_ref[...])
    _, pull_gelu = jax.vjp(gated_gelu, gate_ref[...], up_ref[...])
    grad_gate, grad_up = pull_gelu(grad_mixed)
    grad_gate, grad_up = grad_gate.astype(BF16), grad_up.astype(BF16)
    gate_out[...] = grad_gate
    up_out[...] = grad_up
    part = project_back(grad_gate, w_gate_ref[...]) + project_back(grad_up, w_up_ref[...])

    @pl.when(step == 0)
    def _():
        total[...] = part

    @pl.when(step > 0)
    def _():
        total[...] += part

    @pl.when(step == pl.num_programs(0) - 1)
    def _():
        back_ref[...] = total[...].astype(BF16)


def hidden_back(tile, upstream, down, gate_pre, up_pre, both_weights):
    tokens, width = upstream.shape
    hidden = down.shape[0]
    count = hidden // tile
    low = jax.ShapeDtypeStruct((tokens, hidden), BF16)
    return pl.pallas_call(
        back_kernel,
        name="hidden_back",
        grid=(count,),
        out_shape=(low, low, jax.ShapeDtypeStruct((tokens, width), BF16)),
        in_specs=[
            pl.BlockSpec((tokens, width), lambda i: (0, 0)),
            pl.BlockSpec((tile, width), lambda i: (i, 0)),
            pl.BlockSpec((tokens, tile), lambda i: (0, i)),
            pl.BlockSpec((tokens, tile), lambda i: (0, i)),
            pl.BlockSpec((width, tile), lambda i: (0, i)),
            pl.BlockSpec((width, tile), lambda i: (0, i + count)),
        ],
        out_specs=[
            pl.BlockSpec((tokens, tile), lambda i: (0, i)),
            pl.BlockSpec((tokens, tile), lambda i: (0, i)),
            pl.BlockSpec((tokens, width), lambda i: (0, 0)),
        ],
        scratch_shapes=[pltpu.VMEM((tokens, width), F32)],
        cost_estimate=pl.CostEstimate(
            flops=6 * tokens * hidden * width, bytes_accessed=24 << 20, transcendentals=0
        ),
    )(upstream, down, gate_pre, up_pre, both_weights, both_weights)


def halo_out_kernel(n_chip, source_ref, result_ref, send_sem, recv_sem):
    me = lax.axis_index("ctx")
    chip, core = me // 2, lax.rem(me, 2)
    near = {"ctx": me + 1 - 2 * core}
    after = {"ctx": jnp.minimum(me + 2, 2 * n_chip - 1)}
    has_after = chip < n_chip - 1
    barrier = pltpu.get_barrier_semaphore()
    pl.semaphore_signal(barrier, inc=1, device_id=near, device_id_type=MESH)

    @pl.when(chip > 0)
    def _():
        before = {"ctx": jnp.maximum(me - 2, 0)}
        pl.semaphore_signal(barrier, inc=1, device_id=before, device_id_type=MESH)

    pl.semaphore_wait(barrier, 1 + jnp.minimum(n_chip - 1 - chip, 1))

    def remote(source, slot, turn, peer):
        return pltpu.make_async_remote_copy(
            src_ref=source,
            dst_ref=result_ref.at[slot],
            send_sem=send_sem.at[turn],
            recv_sem=recv_sem.at[turn],
            device_id=peer,
            device_id_type=MESH,
        )

    one_on = remote(source_ref, 2, 0, after)
    two_on = remote(result_ref.at[2], 0, 1, after)
    own_near = remote(source_ref, 3, 2, near)
    before_near = remote(result_ref.at[2], 3 - 2 * (1 - core), 3, near)
    far_near = remote(result_ref.at[0], 1, 4, near)

    @pl.when(has_after)
    def _():
        one_on.start()

    @pl.when(core == 0)
    def _():
        own_near.start()

    def blank(slot):
        result_ref[slot] = jnp.zeros(result_ref.shape[1:], result_ref.dtype)

    @pl.when(chip == 0)
    def _():
        blank(2)
        blank(0)
        blank(1)

    @pl.when((chip == 0) & (core == 0))
    def _():
        blank(3)

    @pl.when(chip == 1)
    def _():
        blank(0)

    @pl.when((chip == 1) & (core == 0))
    def _():
        blank(1)

    @pl.when(chip > 0)
    def _():
        one_on.wait_recv()

    @pl.when((chip > 0) & has_after)
    def _():
        two_on.start()

    @pl.when(chip > 0)
    def _():
        before_near.start()

    @pl.when(chip > 1)
    def _():
        two_on.wait_recv()

    @pl.when((chip > 1) & (core == 1))
    def _():
        far_near.start()

    @pl.when(core == 1)
    def _():
        own_near.wait_recv()

    @pl.when(core == 0)
    def _():
        own_near.wait_send()

    @pl.when(chip > 0)
    def _():
        before_near.wait()

    @pl.when((chip > 1) & (core == 0))
    def _():
        far_near.wait_recv()

    @pl.when((chip > 1) & (core == 1))
    def _():
        far_near.wait_send()

    @pl.when(has_after)
    def _():
        one_on.wait_send()

    @pl.when((chip > 0) & has_after)
    def _():
        two_on.wait_send()


def halo_back_kernel(
    n_chip, source_ref, result_ref, near_ref, far_ref, way_ref, send_sem, recv_sem
):
    me = lax.axis_index("ctx")
    chip, core = me // 2, lax.rem(me, 2)
    near = {"ctx": me + 1 - 2 * core}
    before = {"ctx": jnp.maximum(me - 2, 0)}
    has_after = chip < n_chip - 1
    barrier = pltpu.get_barrier_semaphore()
    pl.semaphore_signal(barrier, inc=1, device_id=near, device_id_type=MESH)

    @pl.when(has_after)
    def _():
        after = {"ctx": jnp.minimum(me + 2, 2 * n_chip - 1)}
        pl.semaphore_signal(barrier, inc=1, device_id=after, device_id_type=MESH)

    pl.semaphore_wait(barrier, 1 + jnp.minimum(chip, 1))

    def remote(source, target, turn, peer):
        return pltpu.make_async_remote_copy(
            src_ref=source,
            dst_ref=target,
            send_sem=send_sem.at[turn],
            recv_sem=recv_sem.at[turn],
            device_id=peer,
            device_id_type=MESH,
        )

    to_before = remote(source_ref.at[3 - 2 * core], near_ref.at[0], 0, near)
    to_other = remote(source_ref.at[1 + 2 * core], near_ref.at[1], 1, near)
    to_before.start()
    to_other.start()

    @pl.when((chip == 0) | jnp.logical_not(has_after))
    def _():
        way_ref[0] = jnp.zeros(way_ref.shape[1:], way_ref.dtype)

    @pl.when(jnp.logical_not(has_after))
    def _():
        way_ref[1] = jnp.zeros(way_ref.shape[1:], way_ref.dtype)

    to_other.wait_recv()
    theirs = near_ref[1].astype(F32)
    far_ref[0] = (source_ref[0].astype(F32) + jnp.where(core == 1, theirs, 0.0)).astype(BF16)
    two_back = remote(far_ref.at[0], way_ref.at[0], 2, before)
    one_back = remote(far_ref.at[1], way_ref.at[1], 3, before)

    @pl.when(chip > 1)
    def _():
        two_back.start()

    to_before.wait_recv()
    due = source_ref[2].astype(F32) + near_ref[0].astype(F32)

    @pl.when((chip > 0) & has_after)
    def _():
        two_back.wait_recv()

    far_ref[1] = (due + way_ref[0].astype(F32)).astype(BF16)

    @pl.when(chip > 0)
    def _():
        one_back.start()

    @pl.when(has_after)
    def _():
        one_back.wait_recv()

    result_ref[...] = way_ref[1].astype(F32) + jnp.where(core == 0, theirs, 0.0)
    to_before.wait_send()
    to_other.wait_send()

    @pl.when(chip > 1)
    def _():
        two_back.wait_send()

    @pl.when(chip > 0)
    def _():
        one_back.wait_send()


def halo_call(collective_id, kernel, n_ctx, block, out_shape, buffers, copies):
    dma = pltpu.SemaphoreType.DMA
    return pl.pallas_call(
        functools.partial(kernel, n_ctx // 2),
        out_shape=out_shape,
        in_specs=[pl.BlockSpec(memory_space=pltpu.VMEM)],
        out_specs=pl.BlockSpec(memory_space=pltpu.VMEM),
        scratch_shapes=[*buffers, dma((copies,)), dma((copies,))],
        compiler_params=pltpu.CompilerParams(collective_id=collective_id, has_side_effects=True),
    )(block)


def halo_out(n_ctx, block):
    out_shape = jax.ShapeDtypeStruct((4, *block.shape), block.dtype)
    return halo_call(1, halo_out_kernel, n_ctx, block, out_shape, (), 5)


def halo_back(n_ctx, blocks):
    shape = blocks.shape[1:]
    buffers = [pltpu.VMEM((2, *shape), blocks.dtype)] * 3
    out_shape = jax.ShapeDtypeStruct(shape, F32)
    return halo_call(6, halo_back_kernel, n_ctx, blocks, out_shape, buffers, 4)


def pick_kernel(n_batch, n_ctx, piece, padded, gate_ref, up_ref, out_ref):
    me = lax.axis_index("batch")
    out_ref[...] = jnp.zeros_like(out_ref)
    for spot in range(n_batch):

        @pl.when(me == spot)
        def _():
            for shard in range(n_ctx):
                start = (shard * n_batch + spot) * piece
                for half, ref in enumerate((gate_ref, up_ref)):
                    place = (half * n_ctx + shard) * padded
                    out_ref[:, place : place + piece] = ref[:, start : start + piece]


def row_block(rows):
    return 48 if rows % 48 == 0 else rows


def pick_columns(n_batch, n_ctx, piece, padded, w_gate, w_up):
    rows, hidden = w_gate.shape
    block = row_block(rows)
    spec = pl.BlockSpec((block, hidden), lambda i: (i, 0))
    return pl.pallas_call(
        functools.partial(pick_kernel, n_batch, n_ctx, piece, padded),
        name="pick_columns",
        grid=(rows // block,),
        out_shape=jax.ShapeDtypeStruct((rows, 2 * n_ctx * padded), w_gate.dtype),
        in_specs=[spec, spec],
        out_specs=pl.BlockSpec((block, 2 * n_ctx * padded), lambda i: (i, 0)),
    )(w_gate, w_up)


def finish_kernel(n_batch, n_ctx, piece, padded, proj_part, gate_ref, up_ref, down_ref, attn_ref, *refs):
    outs, bufs, sems = refs[:8], refs[8:16], refs[16]
    gate_buf, up_buf, down_buf, query_buf, key_buf, value_buf, proj_buf, gain_buf = bufs
    copies = [pltpu.make_async_copy(bufs[i], outs[i], sems.at[i]) for i in range(8)]
    rows = gate_ref.shape[1]
    block = row_block(rows)

    for ref, buf, copy in ((gate_ref, gate_buf, copies[0]), (up_ref, up_buf, copies[1])):

        def place_rows(step, carry):
            lines = pl.ds(pl.multiple_of(step * block, block), block)
            for shard in range(n_ctx):
                for spot in range(n_batch):
                    start = (shard * n_batch + spot) * piece
                    place = shard * padded
                    buf[lines, start : start + piece] = ref[
                        spot, lines, place : place + piece
                    ].astype(F32)
            return carry

        lax.fori_loop(0, rows // block, place_rows, 0)
        copy.start()
    for spot in range(n_batch):
        down_buf[spot * piece : (spot + 1) * piece, :] = down_ref[spot, :piece, :].astype(F32)
    copies[2].start()
    quarter = attn_ref.shape[-1]
    proj_rows = proj_buf.shape[0]
    for spot in range(n_batch):
        for tile in range(0, quarter, 128):
            column = spot * quarter + tile
            for buf in (query_buf, key_buf, value_buf):
                if 0 <= column < buf.shape[-1]:
                    buf[:, column : column + 128] = attn_ref[
                        spot, :rows, tile : tile + 128
                    ].astype(F32)
                column -= buf.shape[-1]
        proj_buf[:, spot * proj_part : (spot + 1) * proj_part] = attn_ref[
            spot, rows : rows + proj_rows, :proj_part
        ].astype(F32)
    gain_buf[...] = attn_ref[0, rows + proj_rows : rows + proj_rows + gain_buf.shape[0], :].astype(F32)
    for copy in copies[3:]:
        copy.start()
    for copy in copies:
        copy.wait()


def finish_round(n_batch, n_ctx, piece, padded, proj_part, gate, up, down, attn, shapes):
    outs = [jax.ShapeDtypeStruct(shape, F32) for shape in shapes]
    return pl.pallas_call(
        functools.partial(finish_kernel, n_batch, n_ctx, piece, padded, proj_part),
        name="finish_round",
        out_shape=outs,
        in_specs=[pl.BlockSpec(memory_space=pltpu.VMEM)] * 4,
        out_specs=[pl.BlockSpec(memory_space=pl.ANY)] * 8,
        scratch_shapes=[pltpu.VMEM(shape, F32) for shape in shapes] + [pltpu.SemaphoreType.DMA((8,))],
    )(gate, up, down, attn)


def weights_kernel(n_batch, n_ctx, qkv_ref, proj_ref, gain_ref, qkv_all, proj_all, gain_all, *sems):
    send_far, recv_far, send_side, recv_side, send_near, recv_near, own_sem = sems
    spot = lax.axis_index("batch")
    me = lax.axis_index("ctx")
    n_chip = n_ctx // 2
    chip, core = me // 2, lax.rem(me, 2)
    near = {"ctx": me + 1 - 2 * core}
    barrier = pltpu.get_barrier_semaphore()

    def far_at(step):
        return {"ctx": 2 * lax.rem(chip + step, n_chip) + core}

    def side_at(step):
        return {"batch": lax.rem(spot + step, n_batch)}

    peers = [near]
    peers += [far_at(step) for step in range(1, n_chip)]
    peers += [side_at(step) for step in range(1, n_batch)]
    for peer in peers:
        pl.semaphore_signal(barrier, inc=1, device_id=peer, device_id_type=MESH)
    pl.semaphore_wait(barrier, len(peers))

    def remote(source, target, send, recv, peer):
        return pltpu.make_async_remote_copy(
            src_ref=source,
            dst_ref=target,
            send_sem=send,
            recv_sem=recv,
            device_id=peer,
            device_id_type=MESH,
        )

    waits = []
    far = []
    for step in range(1, n_chip):
        triple = [
            remote(source, target, send_far.at[step - 1, item], recv_far.at[step - 1, item], far_at(step))
            for item, (source, target) in enumerate(
                (
                    (qkv_ref.at[spot], qkv_all.at[spot, me]),
                    (proj_ref.at[spot], proj_all.at[me, spot]),
                    (gain_ref, gain_all.at[me]),
                )
            )
        ]
        for copy in triple:
            copy.start()
        far.append(triple)
    own = [
        pltpu.make_async_copy(qkv_ref, qkv_all.at[:, me], own_sem.at[0]),
        pltpu.make_async_copy(proj_ref, proj_all.at[me], own_sem.at[1]),
        pltpu.make_async_copy(gain_ref, gain_all.at[me], own_sem.at[2]),
    ]
    for copy in own:
        copy.start()
    first = n_chip - 1
    pairs = [
        remote(source, target, send_near.at[first, 0, item], recv_near.at[first, 0, item], near)
        for item, (source, target) in enumerate(
            (
                (qkv_ref, qkv_all.at[:, me]),
                (proj_ref, proj_all.at[me]),
                (gain_ref, gain_all.at[me]),
            )
        )
    ]
    for copy in pairs:
        copy.start()
    waits += pairs

    def hand_near(step, turn):
        origin = 2 * lax.rem(chip + n_chip - step, n_chip) + core
        quarter = lax.rem(spot + n_batch - turn, n_batch)
        blocks = [qkv_all.at[quarter, origin], proj_all.at[origin, quarter]]
        blocks += [gain_all.at[origin]] if turn == 0 else []
        for item, block in enumerate(blocks):
            copy = remote(
                block,
                block,
                send_near.at[step - 1, turn, item],
                recv_near.at[step - 1, turn, item],
                near,
            )
            copy.start()
            waits.append(copy)

    side = []
    for step in range(1, n_chip):
        for copy in far[step - 1]:
            copy.wait_recv()
        origin = 2 * lax.rem(chip + n_chip - step, n_chip) + core
        for turn in range(1, n_batch):
            pair = [
                remote(
                    block,
                    block,
                    send_side.at[step - 1, turn - 1, item],
                    recv_side.at[step - 1, turn - 1, item],
                    side_at(turn),
                )
                for item, block in enumerate((qkv_all.at[spot, origin], proj_all.at[origin, spot]))
            ]
            for copy in pair:
                copy.start()
            side.append((step, turn, pair))
        hand_near(step, 0)
    for step, turn, pair in side:
        for copy in pair:
            copy.wait_recv()
        hand_near(step, turn)
    for copy in waits:
        copy.wait()
    for copy in own:
        copy.wait()
    for triple in far:
        for copy in triple:
            copy.wait_send()
    for _, _, pair in side:
        for copy in pair:
            copy.wait_send()


def gather_weights(n_batch, n_ctx, qkv, proj, gains):
    n_chip = n_ctx // 2
    dma = pltpu.SemaphoreType.DMA
    vmem = pl.BlockSpec(memory_space=pltpu.VMEM)
    return pl.pallas_call(
        functools.partial(weights_kernel, n_batch, n_ctx),
        name="gather_weights",
        out_shape=(
            jax.ShapeDtypeStruct((n_batch, n_ctx, *qkv.shape[1:]), qkv.dtype),
            jax.ShapeDtypeStruct((n_ctx, *proj.shape), proj.dtype),
            jax.ShapeDtypeStruct((n_ctx, *gains.shape), gains.dtype),
        ),
        in_specs=[vmem] * 3,
        out_specs=[vmem] * 3,
        scratch_shapes=[
            dma((n_chip - 1, 3)),
            dma((n_chip - 1, 3)),
            dma((n_chip - 1, n_batch - 1, 2)),
            dma((n_chip - 1, n_batch - 1, 2)),
            dma((n_chip, n_batch, 3)),
            dma((n_chip, n_batch, 3)),
            dma((3,)),
        ],
        compiler_params=pltpu.CompilerParams(collective_id=12, has_side_effects=True),
    )(qkv, proj, gains)


def tail_kernel(
    n_ctx,
    gate_ref,
    down_ref,
    up_ref,
    attn_ref,
    gate_all,
    down_all,
    up_all,
    attn_all,
    pair_up,
    pair_attn,
    way_up,
    way_attn,
    pair_send,
    pair_recv,
    way_send,
    way_recv,
    side_send,
    side_recv,
    own_sem,
):
    n_chip = n_ctx // 2
    spot = lax.axis_index("batch")
    me = lax.axis_index("ctx")
    chip, core = me // 2, lax.rem(me, 2)
    across = {"batch": spot + 1 - 2 * lax.rem(spot, 2)}
    along = {"batch": lax.rem(spot + 2, 4)}
    near = {"ctx": me + 1 - 2 * core}
    beyond = ({"ctx": jnp.minimum(me + 2, n_ctx - 1)}, {"ctx": jnp.maximum(me - 2, 0)})
    inner = (chip > 0, chip < n_chip - 1)
    barrier = pltpu.get_barrier_semaphore()
    for peer in (near, across, along):
        pl.semaphore_signal(barrier, inc=1, device_id=peer, device_id_type=MESH)
    for has_giver, giver in zip(inner, (beyond[1], beyond[0])):

        @pl.when(has_giver)
        def _():
            pl.semaphore_signal(barrier, inc=1, device_id=giver, device_id_type=MESH)

    pl.semaphore_wait(barrier, 3 + jnp.minimum(chip, 1) + jnp.minimum(n_chip - 1 - chip, 1))

    def remote(source, target, send, recv, peer):
        return pltpu.make_async_remote_copy(
            src_ref=source,
            dst_ref=target,
            send_sem=send,
            recv_sem=recv,
            device_id=peer,
            device_id_type=MESH,
        )

    width = up_ref.shape[-1]
    cut = width // 256 * 128
    chains = (
        (up_ref, pair_up, way_up, up_all, pl.ds(0, cut)),
        (up_ref, pair_up, way_up, up_all, pl.ds(cut, width - cut)),
        (attn_ref, pair_attn, way_attn, attn_all, pl.ds(0, attn_ref.shape[-1])),
    )
    numbers = range(len(chains))

    def pair_copy(number, place):
        source, pair, _, _, columns = chains[number]
        return remote(
            source.at[2 * place + 1 - core, :, columns],
            pair.at[place, :, columns],
            pair_send.at[number, place],
            pair_recv.at[number, place],
            near,
        )

    def way_copy(number, direction, step, source):
        _, _, way, _, columns = chains[number]
        return remote(
            source,
            way.at[direction, step - 1, :, columns],
            way_send.at[number, direction, step - 1],
            way_recv.at[number, direction, step - 1],
            beyond[direction],
        )

    def passes(direction, step):
        return chip <= step - 1 if direction == 0 else chip >= n_chip - step

    def bound_for(direction, step):
        place = chip + n_chip - step if direction == 0 else chip - n_chip + step
        return jnp.clip(place, 0, n_chip - 1)

    def side_pair(item, sources, target, columns):
        return [
            remote(
                sources,
                target.at[spot, :, columns],
                side_send.at[item, turn],
                side_recv.at[item, turn],
                peer,
            )
            for turn, peer in enumerate((across, along))
        ]

    def side_pass(item, firsts, target, start, length):
        half = length // 256 * 128
        halves = (pl.ds(start, half), pl.ds(start + half, length - half))
        copies = []
        for turn, (giver, taker) in enumerate(((across, along), (along, across))):
            firsts[turn].wait_recv()
            block = target.at[giver["batch"], :, halves[turn]]
            copies.append(
                remote(block, block, side_send.at[item, 2 + turn], side_recv.at[item, 2 + turn], taker)
            )
            copies[-1].start()
        return copies

    for number in numbers:
        for place in range(n_chip):
            pair_copy(number, place).start()
    early = ((gate_ref, gate_all), (down_ref, down_all))
    side_firsts = []
    for item, (source, target) in enumerate(early):
        side_firsts.append(side_pair(item, source, target, pl.ds(0, source.shape[-1])))
        for copy in side_firsts[-1]:
            copy.start()
    own = [
        pltpu.make_async_copy(source, target.at[spot], own_sem.at[item])
        for item, (source, target) in enumerate(early)
    ]
    for copy in own:
        copy.start()
    for _, _, way, _, columns in chains:
        for direction in range(2):

            @pl.when(jnp.logical_not(inner[direction]))
            def _():
                way[direction, n_chip - 2, :, columns] = jnp.zeros(
                    (way.shape[2], columns.size), way.dtype
                )

    for number in numbers:
        source, pair, _, _, columns = chains[number]
        for place in range(n_chip):
            pair_copy(number, place).wait_recv()
            pair[place, :, columns] = (
                pair[place, :, columns].astype(F32)
                + source[2 * place + core, :, columns].astype(F32)
            ).astype(BF16)
        for direction in range(2):

            @pl.when(passes(direction, 1))
            def _():
                place = bound_for(direction, 1)
                way_copy(number, direction, 1, pair.at[place, :, columns]).start()

    side_seconds = []
    for step in range(2, n_chip + 1):
        if step <= 3:
            item = step - 2
            target = early[item][1]
            side_seconds += side_pass(item, side_firsts[item], target, 0, target.shape[-1])
        if step == n_chip:
            break
        for number in numbers:
            _, pair, way, _, columns = chains[number]
            for direction in range(2):
                place = bound_for(direction, step)

                @pl.when(passes(direction, step) & inner[direction])
                def _():
                    way_copy(number, direction, step - 1, pair.at[place, :, columns]).wait_recv()
                    way[direction, step - 2, :, columns] = (
                        way[direction, step - 2, :, columns].astype(F32)
                        + pair[place, :, columns].astype(F32)
                    ).astype(BF16)

            for direction in range(2):
                place = bound_for(direction, step)

                @pl.when(passes(direction, step) & inner[direction])
                def _():
                    way_copy(number, direction, step, way.at[direction, step - 2, :, columns]).start()

                @pl.when(passes(direction, step) & jnp.logical_not(inner[direction]))
                def _():
                    way_copy(number, direction, step, pair.at[place, :, columns]).start()

    chain_firsts = []
    for number in numbers:
        _, pair, way, target, columns = chains[number]
        for direction in range(2):

            @pl.when(inner[direction])
            def _():
                way_copy(number, direction, n_chip - 1, pair.at[0, :, columns]).wait_recv()

        target[spot, :, columns] = (
            pair[chip, :, columns].astype(F32)
            + way[0, n_chip - 2, :, columns].astype(F32)
            + way[1, n_chip - 2, :, columns].astype(F32)
        ).astype(BF16)
        firsts = side_pair(2 + number, target.at[spot, :, columns], target, columns)
        for copy in firsts:
            copy.start()
        chain_firsts.append(firsts)
    for number in numbers:
        _, _, _, target, columns = chains[number]
        side_seconds += side_pass(
            2 + number, chain_firsts[number], target, columns.start, columns.size
        )
    for copy in own:
        copy.wait()
    for copy in side_seconds:
        copy.wait()
    for firsts in side_firsts + chain_firsts:
        for copy in firsts:
            copy.wait_send()
    for number in numbers:
        _, pair, _, _, columns = chains[number]
        for place in range(n_chip):
            pair_copy(number, place).wait_send()
        for direction in range(2):
            for step in range(1, n_chip):

                @pl.when(passes(direction, step))
                def _():
                    way_copy(number, direction, step, pair.at[0, :, columns]).wait_send()


def tail_round(n_ctx, gate, down, up, attn):
    n_chip = n_ctx // 2
    dma = pltpu.SemaphoreType.DMA
    vmem = pl.BlockSpec(memory_space=pltpu.VMEM)
    shapes = (gate.shape, down.shape, up.shape[1:], attn.shape[1:])
    return pl.pallas_call(
        functools.partial(tail_kernel, n_ctx),
        name="tail_round",
        out_shape=[jax.ShapeDtypeStruct((4, *shape), BF16) for shape in shapes],
        in_specs=[vmem] * 4,
        out_specs=[vmem] * 4,
        scratch_shapes=[
            pltpu.VMEM((n_chip, *up.shape[1:]), BF16),
            pltpu.VMEM((n_chip, *attn.shape[1:]), BF16),
            pltpu.VMEM((2, n_chip - 1, *up.shape[1:]), BF16),
            pltpu.VMEM((2, n_chip - 1, *attn.shape[1:]), BF16),
            dma((3, n_chip)),
            dma((3, n_chip)),
            dma((3, 2, n_chip - 1)),
            dma((3, 2, n_chip - 1)),
            dma((5, 4)),
            dma((5, 4)),
            dma((2,)),
        ],
        compiler_params=pltpu.CompilerParams(collective_id=8, has_side_effects=True),
    )(gate, down, up, attn)


def gathered(shard):
    return lax.all_gather(shard, "ctx", axis=0, tiled=True)


def scattered(whole):
    return lax.psum_scatter(whole, "ctx", scatter_dimension=0, tiled=True)


def local(
    n_batch,
    n_ctx,
    block_in,
    positions,
    counts,
    cotangent,
    gain_input,
    w_query,
    w_key,
    w_value,
    gain_query,
    gain_key,
    w_output,
    gain_attn,
    gain_ffn,
    w_gate,
    w_up,
    w_down,
    gain_final,
):
    block_in = block_in[0]
    positions = positions[0]
    cotangent = cotangent[0]
    tok_count, model_width = block_in.shape
    width_shard = w_query.shape[0]
    query_width = w_query.shape[1]
    head_size = w_key.shape[1]
    head_count = query_width // head_size
    hidden_shard = w_down.shape[0]
    piece = hidden_shard // n_batch
    hidden_part = -(-piece * n_ctx // 128) * 128
    padded = hidden_part // n_ctx
    halo_depth = (WINDOW + tok_count - 2) // tok_count
    assert halo_depth == 4
    batch_at = lax.axis_index("batch")
    ctx_at = lax.axis_index("ctx")
    all_tok = n_batch * tok_count

    gains = jnp.concatenate(
        [gain_input, gain_attn, gain_ffn, gain_final, gain_query, gain_key]
    )
    slots_of = query_width + 2 * head_size
    quarter = slots_of // n_batch
    qkv_full, proj_full, gains_all = gather_weights(
        n_batch,
        n_ctx,
        jnp.concatenate([w_query, w_key, w_value], axis=1)
        .reshape(width_shard, n_batch, quarter)
        .transpose(1, 0, 2),
        w_output.reshape(n_batch, -1, model_width),
        gains[None],
    )
    qkv_full = qkv_full.reshape(n_batch, model_width, quarter)
    full_output = proj_full.reshape(query_width, model_width)
    gains_all = gains_all[:, 0].astype(F32)

    def gain_at(start, length):
        return gains_all[:, start : start + length].reshape(1, -1)

    head_shard = gain_query.shape[0]
    full_gain_in = gain_at(0, width_shard)
    full_gain_attn = gain_at(width_shard, width_shard)
    full_gain_ffn = gain_at(2 * width_shard, width_shard)
    full_gain_final = gain_at(3 * width_shard, width_shard)
    full_gain_q = gain_at(4 * width_shard, head_shard)
    full_gain_k = gain_at(4 * width_shard + head_shard, head_shard)

    part_both = gathered(pick_columns(n_batch, n_ctx, piece, padded, w_gate, w_up))
    own_down = lax.dynamic_slice_in_dim(w_down, batch_at * piece, piece, 0)
    part_down = gathered(jnp.pad(own_down, ((0, padded - piece), (0, 0))))

    first_token = ctx_at * tok_count
    token_place = first_token + jnp.arange(tok_count, dtype=jnp.int32)
    valid_mask = (token_place < counts[0]).astype(F32)[:, None]
    resid_in = block_in.astype(F32)
    act_in = normed(resid_in, full_gain_in).astype(BF16)
    qkv_raw = jnp.concatenate([project(act_in, qkv_full[i]) for i in range(n_batch)], axis=1)
    query_raw = qkv_raw[:, :query_width].reshape(tok_count, head_count, head_size)
    key_raw = qkv_raw[:, query_width : query_width + head_size]
    value_low = qkv_raw[:, query_width + head_size :].astype(BF16)
    inv_freq = BASE ** (-jnp.arange(0, head_size, 2, dtype=F32) / head_size)
    angles = positions.astype(F32)[:, None] * inv_freq

    def query_path(raw_query, gain_vec):
        return rotate(normed(raw_query, gain_vec), angles[:, None, :])

    def key_path(raw_key, gain_vec):
        return rotate(normed(raw_key, gain_vec), angles)

    query_rot = query_path(query_raw, full_gain_q).astype(BF16)
    key_rot = key_path(key_raw, full_gain_k).astype(BF16)
    own_pair = jnp.concatenate([key_rot, value_low], axis=-1)
    halo = halo_out(n_ctx, own_pair)
    context = jnp.concatenate([halo.reshape(halo_depth * tok_count, -1), own_pair], axis=0)
    ctx_keys = context[:, :head_size]
    ctx_values = context[:, head_size:]
    key_total = (halo_depth + 1) * tok_count
    distance = (
        jnp.arange(tok_count, dtype=jnp.int32)[:, None]
        + halo_depth * tok_count
        - jnp.arange(key_total, dtype=jnp.int32)[None, :]
    )
    allowed = (distance >= 0) & (distance < WINDOW) & (distance <= positions[:, None])
    score_scale = head_size ** (-0.5)
    raw_scores = jnp.einsum("thd,kd->htk", query_rot, ctx_keys, preferred_element_type=F32)
    scores = jnp.where(allowed[None], raw_scores * score_scale, MASKED)
    exp_scores = jnp.exp(scores - jnp.max(scores, axis=-1, keepdims=True))
    attn_prob = exp_scores / jnp.sum(exp_scores, axis=-1, keepdims=True)
    prob_low = attn_prob.astype(BF16)
    attended = jnp.einsum("htk,kd->thd", prob_low, ctx_values, preferred_element_type=F32)
    attn_low = attended.reshape(tok_count, query_width).astype(BF16)
    attn_proj = project(attn_low, full_output)
    middle = resid_in + normed(attn_proj, full_gain_attn)
    ffn_in = normed(middle, full_gain_ffn).astype(BF16)

    (ffn_in_all,) = square_gather(2, ffn_in)
    ffn_in_all = ffn_in_all.reshape(all_tok, model_width)
    gate_pre, up_pre, mixed_low, mixed_turned = hidden_mix(256, ffn_in_all, part_both)
    mixed_low, act_in_late, attn_late = lax.optimization_barrier((mixed_low, act_in, attn_low))
    act_in_all, attn_all = square_gather(13, act_in_late, attn_late)
    ffn_in_turned = ffn_in_all.T
    mixed_low, act_in_all, attn_all, mixed_turned, ffn_in_turned = lax.optimization_barrier(
        (mixed_low, act_in_all, attn_all, mixed_turned, ffn_in_turned)
    )
    act_in_all = act_in_all.reshape(all_tok, model_width)
    attn_all = attn_all.reshape(all_tok, query_width)
    block_out, grad_ffn_low, grad_gain_final = turn_round(
        mixed_low, part_down, middle, cotangent, valid_mask, full_gain_final
    )

    grad_final = cotangent.astype(F32) * valid_mask
    grad_ffn_low = grad_ffn_low.reshape(all_tok, model_width)
    down_grad = product_low(384, mixed_turned, grad_ffn_low)
    down_grad, grad_ffn_low = lax.optimization_barrier((down_grad, grad_ffn_low))
    grad_w_down = scattered(down_grad)
    grad_gate_low, grad_up_low, back_part = hidden_back(
        256, grad_ffn_low, part_down, gate_pre, up_pre, part_both
    )
    (back_parts,) = batch_exchange(
        5, n_batch, slots=(back_part.reshape(n_batch, tok_count, model_width),)
    )
    back_parts, grad_gate_low, grad_up_low = lax.optimization_barrier(
        (back_parts, grad_gate_low, grad_up_low)
    )
    gate_grad = product_low(256, ffn_in_turned, grad_gate_low)
    up_grad = product_low(256, ffn_in_turned, grad_up_low)
    back_parts, gate_grad, up_grad = lax.optimization_barrier((back_parts, gate_grad, up_grad))
    grad_w_gate = scattered(gate_grad)
    grad_ffn_in = jnp.sum(back_parts.astype(F32), axis=0)
    _, pull_ffn_norm = jax.vjp(normed, middle, full_gain_ffn)
    grad_middle_part, grad_gain_ffn = pull_ffn_norm(grad_ffn_in)
    grad_middle = grad_final + grad_middle_part
    _, pull_attn_norm = jax.vjp(normed, attn_proj, full_gain_attn)
    grad_attn_proj, grad_gain_attn = pull_attn_norm(grad_middle)

    grad_proj_low = grad_attn_proj.astype(BF16)
    grad_attended = (
        project_back(grad_proj_low, full_output)
        .astype(BF16)
        .reshape(tok_count, head_count, head_size)
    )
    grad_prob = jnp.einsum("thd,kd->htk", grad_attended, ctx_values, preferred_element_type=F32)
    row_delta = jnp.sum(attn_prob * grad_prob, axis=-1, keepdims=True)
    grad_scores = (attn_prob * (grad_prob - row_delta)).astype(BF16)
    grad_queries = (
        jnp.einsum("htk,kd->thd", grad_scores, ctx_keys, preferred_element_type=F32) * score_scale
    )
    grad_ctx_keys = (
        jnp.einsum("htk,thd->kd", grad_scores, query_rot, preferred_element_type=F32) * score_scale
    )
    grad_ctx_values = jnp.einsum("htk,thd->kd", prob_low, grad_attended, preferred_element_type=F32)
    grad_context = jnp.concatenate([grad_ctx_keys, grad_ctx_values], axis=-1)
    halo_rows = halo_depth * tok_count
    returned = halo_back(
        n_ctx,
        grad_context[:halo_rows].astype(BF16).reshape(halo_depth, tok_count, 2 * head_size),
    )
    own_grad = grad_context[halo_rows:] + returned
    grad_value_low = own_grad[:, head_size:].astype(BF16)
    _, pull_key = jax.vjp(key_path, key_raw, full_gain_k)
    grad_key_raw, grad_gain_key = pull_key(own_grad[:, :head_size])
    _, pull_query = jax.vjp(query_path, query_raw, full_gain_q)
    grad_query_raw, grad_gain_query = pull_query(grad_queries)
    grad_qkv_low = jnp.concatenate(
        [
            grad_query_raw.astype(BF16).reshape(tok_count, query_width),
            grad_key_raw.astype(BF16),
            grad_value_low,
        ],
        axis=1,
    )
    grad_act_in = sum(
        project_back(grad_qkv_low[:, i * quarter : (i + 1) * quarter], qkv_full[i])
        for i in range(n_batch)
    )
    _, pull_input = jax.vjp(normed, resid_in, full_gain_in)
    grad_in_part, grad_gain_input = pull_input(grad_act_in)
    grad_in = (grad_middle + grad_in_part).astype(BF16)

    def column_slots(upstream):
        return upstream.reshape(tok_count, n_batch, -1).transpose(1, 0, 2)

    gain_rows = jnp.concatenate(
        [
            grad.reshape(n_ctx, -1)
            for grad in (
                grad_gain_input,
                grad_gain_attn,
                grad_gain_ffn,
                grad_gain_final,
                grad_gain_query,
                grad_gain_key,
            )
        ],
        axis=1,
    )
    gain_parts, qkv_slots, proj_slots = batch_exchange(
        7,
        n_batch,
        whole=(gain_rows,),
        slots=(column_slots(grad_qkv_low), column_slots(grad_proj_low)),
    )
    proj_rows = w_output.shape[0]
    gain_count = gain_rows.shape[1]
    gain_lines = -(-gain_count // quarter)
    used = width_shard + proj_rows + gain_lines
    lines = -(-used // 16) * 16
    grad_w_output = weight_grad(attn_all, proj_slots.reshape(all_tok, -1)).astype(BF16)
    grad_w_qkv = weight_grad(act_in_all, qkv_slots.reshape(all_tok, -1)).astype(BF16)
    output_part = model_width // n_batch
    gain_sum = jnp.sum(gain_parts, axis=0).astype(BF16)
    packed = jnp.concatenate(
        [
            grad_w_qkv.reshape(n_ctx, width_shard, quarter),
            jnp.pad(
                grad_w_output.reshape(n_ctx, proj_rows, output_part),
                ((0, 0), (0, 0), (0, quarter - output_part)),
            ),
            jnp.pad(gain_sum, ((0, 0), (0, gain_lines * quarter - gain_count))).reshape(
                n_ctx, gain_lines, quarter
            ),
            jnp.zeros((n_ctx, lines - used, quarter), BF16),
        ],
        axis=1,
    )
    gate_all, down_all, up_all, attn_grads = tail_round(
        n_ctx,
        grad_w_gate,
        grad_w_down,
        up_grad.reshape(n_ctx, width_shard, hidden_part),
        packed,
    )
    shapes = (
        (width_shard, w_gate.shape[1]),
        (width_shard, w_gate.shape[1]),
        (hidden_shard, model_width),
        (width_shard, query_width),
        (width_shard, head_size),
        (width_shard, head_size),
        (proj_rows, model_width),
        (gain_lines, quarter),
    )
    (
        grad_gate_shard,
        grad_up_shard,
        grad_down_shard,
        grad_query_shard,
        grad_key_shard,
        grad_value_shard,
        grad_output_shard,
        gain_block,
    ) = finish_round(
        n_batch, n_ctx, piece, padded, output_part, gate_all, up_all, down_all, attn_grads, shapes
    )
    gain_mine = gain_block.reshape(-1)

    return (
        block_out[None],
        grad_in[None],
        gain_mine[:width_shard],
        grad_query_shard,
        grad_key_shard,
        grad_value_shard,
        gain_mine[4 * width_shard : 4 * width_shard + head_shard],
        gain_mine[4 * width_shard + head_shard : gain_count],
        grad_output_shard,
        gain_mine[width_shard : 2 * width_shard],
        gain_mine[2 * width_shard : 3 * width_shard],
        grad_gate_shard,
        grad_up_shard,
        grad_down_shard,
        gain_mine[3 * width_shard : 4 * width_shard],
    )


def solution(mesh):
    matrix = P("ctx", None)
    vector = P("ctx")
    tokens = P("batch", "ctx", None)

    def step(*arrays):
        return local(mesh.shape["batch"], mesh.shape["ctx"], *arrays)

    return jax.shard_map(
        step,
        mesh=mesh,
        in_specs=(
            tokens,
            P("batch", "ctx"),
            P("batch"),
            tokens,
            vector,
            matrix,
            matrix,
            matrix,
            vector,
            vector,
            matrix,
            vector,
            vector,
            matrix,
            matrix,
            matrix,
            vector,
        ),
        out_specs=(
            tokens,
            tokens,
            vector,
            matrix,
            matrix,
            matrix,
            vector,
            vector,
            matrix,
            vector,
            vector,
            matrix,
            matrix,
            matrix,
            vector,
        ),
        check_vma=False,
    )
```

```python
import functools

import jax
import jax.numpy as jnp
from jax import lax
from jax.experimental import pallas as pl
from jax.experimental.pallas import tpu as pltpu
from jax.sharding import PartitionSpec as P

WINDOW = 512
UP_FIRST = 512


EPS = 1e-06
BASE = 10000.0
MASKED = -1e30
BF16 = jnp.bfloat16
F32 = jnp.float32
MESH = pl.DeviceIdType.MESH


def normed(vector, gain_vec):
    return vector * lax.rsqrt(jnp.mean(vector * vector, axis=-1, keepdims=True) + EPS) * gain_vec


def rotate(vector, angles):
    half_size = vector.shape[-1] // 2
    cosine = jnp.cos(angles)
    sine_part = jnp.sin(angles)
    first_half = vector[..., :half_size]
    second = vector[..., half_size:]
    return jnp.concatenate(
        [first_half * cosine - second * sine_part, second * cosine + first_half * sine_part],
        axis=-1,
    )


def project(inputs, weight):
    return lax.dot_general(inputs, weight, (((1,), (0,)), ((), ())), preferred_element_type=F32)


def project_back(upstream, weight):
    return lax.dot_general(upstream, weight, (((1,), (1,)), ((), ())), preferred_element_type=F32)


def weight_grad(inputs, upstream):
    return lax.dot_general(inputs, upstream, (((0,), (0,)), ((), ())), preferred_element_type=F32)


def gated_gelu(gate_val, up_val):
    return jax.nn.gelu(gate_val, approximate=True) * up_val


def batch_kernel(size, kinds, *refs):
    count = len(kinds)
    sources, results = refs[:count], refs[count : 2 * count]
    send_sem, recv_sem, own_sem = refs[2 * count :]
    me = lax.axis_index("batch")
    barrier = pltpu.get_barrier_semaphore()
    for step in range(1, size):
        pl.semaphore_signal(
            barrier, inc=1, device_id={"batch": lax.rem(me + step, size)}, device_id_type=MESH
        )
    pl.semaphore_wait(barrier, size - 1)
    copies = []
    for step in range(1, size):
        peer = lax.rem(me + step, size)
        for item in range(count):
            source = sources[item].at[peer] if kinds[item] else sources[item]
            copies.append(
                pltpu.make_async_remote_copy(
                    src_ref=source,
                    dst_ref=results[item].at[me],
                    send_sem=send_sem.at[item, step - 1],
                    recv_sem=recv_sem.at[item, step - 1],
                    device_id={"batch": peer},
                    device_id_type=MESH,
                )
            )
    for copy in copies:
        copy.start()
    own = []
    for item in range(count):
        source = sources[item].at[me] if kinds[item] else sources[item]
        own.append(pltpu.make_async_copy(source, results[item].at[me], own_sem.at[item]))
    for copy in own:
        copy.start()
    for copy in own:
        copy.wait()
    for copy in copies:
        copy.wait()


def batch_exchange(collective_id, size, whole=(), slots=()):
    arrays = list(whole) + list(slots)
    kinds = [0] * len(whole) + [1] * len(slots)
    count = len(arrays)
    shapes = [
        jax.ShapeDtypeStruct(a.shape if k else (size, *a.shape), a.dtype)
        for a, k in zip(arrays, kinds)
    ]
    return pl.pallas_call(
        functools.partial(batch_kernel, size, kinds),
        out_shape=shapes,
        in_specs=[pl.BlockSpec(memory_space=pltpu.VMEM)] * count,
        out_specs=[pl.BlockSpec(memory_space=pltpu.VMEM)] * count,
        scratch_shapes=[
            pltpu.SemaphoreType.DMA((count, size - 1)),
            pltpu.SemaphoreType.DMA((count, size - 1)),
            pltpu.SemaphoreType.DMA((count,)),
        ],
        compiler_params=pltpu.CompilerParams(collective_id=collective_id, has_side_effects=True),
    )(*arrays)


def square_kernel(count, *refs):
    sources, results = refs[:count], refs[count : 2 * count]
    send_sem, recv_sem, own_sem = refs[2 * count :]
    me = lax.axis_index("batch")
    across = me + 1 - 2 * lax.rem(me, 2)
    along = lax.rem(me + 2, 4)
    barrier = pltpu.get_barrier_semaphore()
    for peer in (across, along):
        pl.semaphore_signal(barrier, inc=1, device_id={"batch": peer}, device_id_type=MESH)
    pl.semaphore_wait(barrier, 2)

    def remote(source, target, item, turn, peer):
        copy = pltpu.make_async_remote_copy(
            src_ref=source,
            dst_ref=target,
            send_sem=send_sem.at[item, turn],
            recv_sem=recv_sem.at[item, turn],
            device_id={"batch": peer},
            device_id_type=MESH,
        )
        copy.start()
        return copy

    firsts = [
        [
            remote(sources[item], results[item].at[me], item, turn, peer)
            for turn, peer in enumerate((across, along))
        ]
        for item in range(count)
    ]
    own = [
        pltpu.make_async_copy(sources[item], results[item].at[me], own_sem.at[item])
        for item in range(count)
    ]
    for copy in own:
        copy.start()
    seconds = []
    for item in range(count):
        columns = sources[item].shape[-1]
        cut = columns // 256 * 128
        halves = (pl.ds(0, cut), pl.ds(cut, columns - cut))
        for turn, (giver, taker) in enumerate(((across, along), (along, across))):
            firsts[item][turn].wait_recv()
            block = results[item].at[giver, :, halves[turn]]
            seconds.append(remote(block, block, item, 2 + turn, taker))
    for copy in own:
        copy.wait()
    for copy in seconds:
        copy.wait()
    for pair in firsts:
        for copy in pair:
            copy.wait_send()


def square_gather(collective_id, *arrays):
    count = len(arrays)
    return pl.pallas_call(
        functools.partial(square_kernel, count),
        out_shape=[jax.ShapeDtypeStruct((4, *a.shape), a.dtype) for a in arrays],
        in_specs=[pl.BlockSpec(memory_space=pltpu.VMEM)] * count,
        out_specs=[pl.BlockSpec(memory_space=pltpu.VMEM)] * count,
        scratch_shapes=[
            pltpu.SemaphoreType.DMA((count, 4)),
            pltpu.SemaphoreType.DMA((count, 4)),
            pltpu.SemaphoreType.DMA((count,)),
        ],
        compiler_params=pltpu.CompilerParams(collective_id=collective_id, has_side_effects=True),
    )(*arrays)


def turn_kernel(
    mixed_ref,
    down_ref,
    middle_ref,
    upstream_ref,
    valid_ref,
    gain_ref,
    out_ref,
    grads_ref,
    gain_grad_ref,
    part_ref,
    taken_ref,
    send_sem,
    recv_sem,
    pass_sem,
    take_sem,
):
    me = lax.axis_index("batch")
    across = me + 1 - 2 * lax.rem(me, 2)
    along = lax.rem(me + 2, 4)
    corner = lax.rem(across + 2, 4)
    order = (corner, across, along)
    tok_count = middle_ref.shape[0]
    barrier = pltpu.get_barrier_semaphore()
    for peer in order:
        pl.semaphore_signal(barrier, inc=1, device_id={"batch": peer}, device_id_type=MESH)
    pl.semaphore_wait(barrier, 3)

    def product(place):
        rows = pl.ds(pl.multiple_of(place * tok_count, tok_count), tok_count)
        return jnp.dot(mixed_ref[rows, :], down_ref[...], preferred_element_type=F32)

    copies = [
        pltpu.make_async_remote_copy(
            src_ref=part_ref.at[turn],
            dst_ref=taken_ref.at[turn],
            send_sem=send_sem.at[turn],
            recv_sem=recv_sem.at[turn],
            device_id={"batch": peer},
            device_id_type=MESH,
        )
        for turn, peer in enumerate(order)
    ]
    for turn, peer in enumerate(order):
        part_ref[turn] = product(peer).astype(BF16)
        if turn > 0:
            copies[turn - 1].start()
    total = product(me)
    copies[2].start()
    for turn in range(3):
        copies[turn].wait_recv()
        total = total + taken_ref[turn].astype(F32)
    gain = gain_ref[...]
    valid = valid_ref[...]
    scale = lax.rsqrt(jnp.mean(total * total, axis=-1, keepdims=True) + EPS)
    upstream = upstream_ref[...].astype(F32) * valid
    gained = upstream * gain
    back = scale * gained - total * (
        scale * scale * scale * jnp.mean(total * gained, axis=-1, keepdims=True)
    )
    grads_ref[me] = back.astype(BF16)
    unit = total * scale
    out_ref[...] = ((middle_ref[...] + unit * gain) * valid).astype(BF16)
    gain_grad_ref[...] = jnp.sum(upstream * unit, axis=0, keepdims=True)

    def remote(block, turn, peer):
        copy = pltpu.make_async_remote_copy(
            src_ref=block,
            dst_ref=block,
            send_sem=pass_sem.at[turn],
            recv_sem=take_sem.at[turn],
            device_id={"batch": peer},
            device_id_type=MESH,
        )
        copy.start()
        return copy

    firsts = [remote(grads_ref.at[me], turn, peer) for turn, peer in enumerate((across, along))]
    columns = grads_ref.shape[-1]
    cut = columns // 256 * 128
    halves = (pl.ds(0, cut), pl.ds(cut, columns - cut))
    seconds = []
    for turn, (giver, taker) in enumerate(((across, along), (along, across))):
        firsts[turn].wait_recv()
        seconds.append(remote(grads_ref.at[giver, :, halves[turn]], 2 + turn, taker))
    for copy in seconds:
        copy.wait()
    for copy in firsts + copies:
        copy.wait_send()


def turn_round(mixed, down, middle, upstream, valid, gain):
    tok_count, width = middle.shape
    dma = pltpu.SemaphoreType.DMA
    vmem = pl.BlockSpec(memory_space=pltpu.VMEM)
    flops = 2 * mixed.shape[0] * mixed.shape[1] * width
    return pl.pallas_call(
        turn_kernel,
        name="turn_round",
        out_shape=(
            jax.ShapeDtypeStruct((tok_count, width), BF16),
            jax.ShapeDtypeStruct((4, tok_count, width), BF16),
            jax.ShapeDtypeStruct((1, width), F32),
        ),
        in_specs=[vmem] * 6,
        out_specs=[vmem] * 3,
        scratch_shapes=[
            pltpu.VMEM((3, tok_count, width), BF16),
            pltpu.VMEM((3, tok_count, width), BF16),
            dma((3,)),
            dma((3,)),
            dma((4,)),
            dma((4,)),
        ],
        cost_estimate=pl.CostEstimate(flops=flops, bytes_accessed=8 << 20, transcendentals=0),
        compiler_params=pltpu.CompilerParams(collective_id=3, has_side_effects=True),
    )(mixed, down, middle, upstream, valid, gain)


def product_kernel(left_ref, right_ref, out_ref):
    out_ref[...] = jnp.dot(left_ref[...], right_ref[...], preferred_element_type=F32).astype(BF16)


def product_low(tile, left, right, start=0, columns=None):
    rows, depth = left.shape
    columns = columns or right.shape[1]
    skip = start // tile
    return pl.pallas_call(
        product_kernel,
        grid=(columns // tile,),
        out_shape=jax.ShapeDtypeStruct((rows, columns), BF16),
        in_specs=[
            pl.BlockSpec((rows, depth), lambda i: (0, 0)),
            pl.BlockSpec((depth, tile), lambda i: (0, i + skip)),
        ],
        out_specs=pl.BlockSpec((rows, tile), lambda i: (0, i)),
        cost_estimate=pl.CostEstimate(
            flops=2 * rows * depth * columns, bytes_accessed=8 << 20, transcendentals=0
        ),
    )(left, right)


def mix_kernel(tokens_ref, w_gate_ref, w_up_ref, gate_ref, up_ref, mixed_ref, turned_ref):
    gate = project(tokens_ref[...], w_gate_ref[...])
    up = project(tokens_ref[...], w_up_ref[...])
    gate_ref[...] = gate
    up_ref[...] = up
    mixed = gated_gelu(gate, up)
    mixed_ref[...] = mixed.astype(BF16)
    turned_ref[...] = mixed.T.astype(BF16)


def hidden_mix(tile, tokens, both_weights):
    count, width = tokens.shape
    hidden = both_weights.shape[1] // 2
    steps = hidden // tile
    wide = jax.ShapeDtypeStruct((count, hidden), F32)
    column = pl.BlockSpec((count, tile), lambda i: (0, i))
    return pl.pallas_call(
        mix_kernel,
        name="hidden_mix",
        grid=(steps,),
        out_shape=(
            wide,
            wide,
            jax.ShapeDtypeStruct((count, hidden), BF16),
            jax.ShapeDtypeStruct((hidden, count), BF16),
        ),
        in_specs=[
            pl.BlockSpec((count, width), lambda i: (0, 0)),
            pl.BlockSpec((width, tile), lambda i: (0, i)),
            pl.BlockSpec((width, tile), lambda i: (0, i + steps)),
        ],
        out_specs=[column, column, column, pl.BlockSpec((tile, count), lambda i: (i, 0))],
        cost_estimate=pl.CostEstimate(
            flops=4 * count * hidden * width, bytes_accessed=24 << 20, transcendentals=0
        ),
    )(tokens, both_weights, both_weights)


def back_kernel(
    upstream_ref, down_ref, gate_ref, up_ref, w_gate_ref, w_up_ref, gate_out, up_out, back_ref, total
):
    step = pl.program_id(0)
    grad_mixed = project_back(upstream_ref[...], down_ref[...])
    _, pull_gelu = jax.vjp(gated_gelu, gate_ref[...], up_ref[...])
    grad_gate, grad_up = pull_gelu(grad_mixed)
    grad_gate, grad_up = grad_gate.astype(BF16), grad_up.astype(BF16)
    gate_out[...] = grad_gate
    up_out[...] = grad_up
    part = project_back(grad_gate, w_gate_ref[...]) + project_back(grad_up, w_up_ref[...])

    @pl.when(step == 0)
    def _():
        total[...] = part

    @pl.when(step > 0)
    def _():
        total[...] += part

    @pl.when(step == pl.num_programs(0) - 1)
    def _():
        back_ref[...] = total[...].astype(BF16)


def hidden_back(tile, upstream, down, gate_pre, up_pre, both_weights):
    tokens, width = upstream.shape
    hidden = down.shape[0]
    count = hidden // tile
    low = jax.ShapeDtypeStruct((tokens, hidden), BF16)
    return pl.pallas_call(
        back_kernel,
        name="hidden_back",
        grid=(count,),
        out_shape=(low, low, jax.ShapeDtypeStruct((tokens, width), BF16)),
        in_specs=[
            pl.BlockSpec((tokens, width), lambda i: (0, 0)),
            pl.BlockSpec((tile, width), lambda i: (i, 0)),
            pl.BlockSpec((tokens, tile), lambda i: (0, i)),
            pl.BlockSpec((tokens, tile), lambda i: (0, i)),
            pl.BlockSpec((width, tile), lambda i: (0, i)),
            pl.BlockSpec((width, tile), lambda i: (0, i + count)),
        ],
        out_specs=[
            pl.BlockSpec((tokens, tile), lambda i: (0, i)),
            pl.BlockSpec((tokens, tile), lambda i: (0, i)),
            pl.BlockSpec((tokens, width), lambda i: (0, 0)),
        ],
        scratch_shapes=[pltpu.VMEM((tokens, width), F32)],
        cost_estimate=pl.CostEstimate(
            flops=6 * tokens * hidden * width, bytes_accessed=24 << 20, transcendentals=0
        ),
    )(upstream, down, gate_pre, up_pre, both_weights, both_weights)


def halo_out_kernel(n_chip, source_ref, result_ref, send_sem, recv_sem):
    me = lax.axis_index("ctx")
    chip, core = me // 2, lax.rem(me, 2)
    near = {"ctx": me + 1 - 2 * core}
    after = {"ctx": jnp.minimum(me + 2, 2 * n_chip - 1)}
    has_after = chip < n_chip - 1
    barrier = pltpu.get_barrier_semaphore()
    pl.semaphore_signal(barrier, inc=1, device_id=near, device_id_type=MESH)

    @pl.when(chip > 0)
    def _():
        before = {"ctx": jnp.maximum(me - 2, 0)}
        pl.semaphore_signal(barrier, inc=1, device_id=before, device_id_type=MESH)

    pl.semaphore_wait(barrier, 1 + jnp.minimum(n_chip - 1 - chip, 1))

    def remote(source, slot, turn, peer):
        return pltpu.make_async_remote_copy(
            src_ref=source,
            dst_ref=result_ref.at[slot],
            send_sem=send_sem.at[turn],
            recv_sem=recv_sem.at[turn],
            device_id=peer,
            device_id_type=MESH,
        )

    one_on = remote(source_ref, 2, 0, after)
    two_on = remote(result_ref.at[2], 0, 1, after)
    own_near = remote(source_ref, 3, 2, near)
    before_near = remote(result_ref.at[2], 3 - 2 * (1 - core), 3, near)
    far_near = remote(result_ref.at[0], 1, 4, near)

    @pl.when(has_after)
    def _():
        one_on.start()

    @pl.when(core == 0)
    def _():
        own_near.start()

    def blank(slot):
        result_ref[slot] = jnp.zeros(result_ref.shape[1:], result_ref.dtype)

    @pl.when(chip == 0)
    def _():
        blank(2)
        blank(0)
        blank(1)

    @pl.when((chip == 0) & (core == 0))
    def _():
        blank(3)

    @pl.when(chip == 1)
    def _():
        blank(0)

    @pl.when((chip == 1) & (core == 0))
    def _():
        blank(1)

    @pl.when(chip > 0)
    def _():
        one_on.wait_recv()

    @pl.when((chip > 0) & has_after)
    def _():
        two_on.start()

    @pl.when(chip > 0)
    def _():
        before_near.start()

    @pl.when(chip > 1)
    def _():
        two_on.wait_recv()

    @pl.when((chip > 1) & (core == 1))
    def _():
        far_near.start()

    @pl.when(core == 1)
    def _():
        own_near.wait_recv()

    @pl.when(core == 0)
    def _():
        own_near.wait_send()

    @pl.when(chip > 0)
    def _():
        before_near.wait()

    @pl.when((chip > 1) & (core == 0))
    def _():
        far_near.wait_recv()

    @pl.when((chip > 1) & (core == 1))
    def _():
        far_near.wait_send()

    @pl.when(has_after)
    def _():
        one_on.wait_send()

    @pl.when((chip > 0) & has_after)
    def _():
        two_on.wait_send()


def halo_back_kernel(
    n_chip,
    source_ref,
    shard_ref,
    result_ref,
    shards_ref,
    near_ref,
    far_ref,
    way_ref,
    send_sem,
    recv_sem,
    pass_sem,
    take_sem,
    own_sem,
):
    me = lax.axis_index("ctx")
    spot = lax.axis_index("batch")
    across = spot + 1 - 2 * lax.rem(spot, 2)
    along = lax.rem(spot + 2, 4)
    chip, core = me // 2, lax.rem(me, 2)
    near = {"ctx": me + 1 - 2 * core}
    before = {"ctx": jnp.maximum(me - 2, 0)}
    has_after = chip < n_chip - 1
    barrier = pltpu.get_barrier_semaphore()
    pl.semaphore_signal(barrier, inc=1, device_id=near, device_id_type=MESH)

    @pl.when(has_after)
    def _():
        after = {"ctx": jnp.minimum(me + 2, 2 * n_chip - 1)}
        pl.semaphore_signal(barrier, inc=1, device_id=after, device_id_type=MESH)

    for peer in (across, along):
        pl.semaphore_signal(barrier, inc=1, device_id={"batch": peer}, device_id_type=MESH)
    pl.semaphore_wait(barrier, 3 + jnp.minimum(chip, 1))

    def beside(source, target, turn, peer):
        copy = pltpu.make_async_remote_copy(
            src_ref=source,
            dst_ref=target,
            send_sem=pass_sem.at[turn],
            recv_sem=take_sem.at[turn],
            device_id={"batch": peer},
            device_id_type=MESH,
        )
        copy.start()
        return copy

    def remote(source, target, turn, peer):
        return pltpu.make_async_remote_copy(
            src_ref=source,
            dst_ref=target,
            send_sem=send_sem.at[turn],
            recv_sem=recv_sem.at[turn],
            device_id=peer,
            device_id_type=MESH,
        )

    to_before = remote(source_ref.at[3 - 2 * core], near_ref.at[0], 0, near)
    to_other = remote(source_ref.at[1 + 2 * core], near_ref.at[1], 1, near)
    to_before.start()
    to_other.start()
    firsts = [
        beside(shard_ref, shards_ref.at[spot], turn, peer)
        for turn, peer in enumerate((across, along))
    ]
    own = pltpu.make_async_copy(shard_ref, shards_ref.at[spot], own_sem.at[0])
    own.start()

    @pl.when((chip == 0) | jnp.logical_not(has_after))
    def _():
        way_ref[0] = jnp.zeros(way_ref.shape[1:], way_ref.dtype)

    @pl.when(jnp.logical_not(has_after))
    def _():
        way_ref[1] = jnp.zeros(way_ref.shape[1:], way_ref.dtype)

    to_other.wait_recv()
    theirs = near_ref[1].astype(F32)
    far_ref[0] = (source_ref[0].astype(F32) + jnp.where(core == 1, theirs, 0.0)).astype(BF16)
    two_back = remote(far_ref.at[0], way_ref.at[0], 2, before)
    one_back = remote(far_ref.at[1], way_ref.at[1], 3, before)

    @pl.when(chip > 1)
    def _():
        two_back.start()

    to_before.wait_recv()
    due = source_ref[2].astype(F32) + near_ref[0].astype(F32)

    @pl.when((chip > 0) & has_after)
    def _():
        two_back.wait_recv()

    far_ref[1] = (due + way_ref[0].astype(F32)).astype(BF16)

    @pl.when(chip > 0)
    def _():
        one_back.start()

    columns = shard_ref.shape[-1]
    cut = columns // 256 * 128
    halves = (pl.ds(0, cut), pl.ds(cut, columns - cut))
    seconds = []
    for turn, (giver, taker) in enumerate(((across, along), (along, across))):
        firsts[turn].wait_recv()
        block = shards_ref.at[giver, :, halves[turn]]
        seconds.append(beside(block, block, 2 + turn, taker))

    @pl.when(has_after)
    def _():
        one_back.wait_recv()

    result_ref[...] = way_ref[1].astype(F32) + jnp.where(core == 0, theirs, 0.0)
    own.wait()
    for copy in seconds:
        copy.wait()
    for copy in firsts + [to_before, to_other]:
        copy.wait_send()

    @pl.when(chip > 1)
    def _():
        two_back.wait_send()

    @pl.when(chip > 0)
    def _():
        one_back.wait_send()


def halo_call(collective_id, kernel, n_ctx, arrays, out_shape, buffers, counts):
    dma = pltpu.SemaphoreType.DMA
    vmem = pl.BlockSpec(memory_space=pltpu.VMEM)
    return pl.pallas_call(
        functools.partial(kernel, n_ctx // 2),
        out_shape=out_shape,
        in_specs=[vmem] * len(arrays),
        out_specs=[vmem] * len(out_shape),
        scratch_shapes=[*buffers, *(dma((count,)) for count in counts)],
        compiler_params=pltpu.CompilerParams(collective_id=collective_id, has_side_effects=True),
    )(*arrays)


def halo_out(n_ctx, block):
    out_shape = [jax.ShapeDtypeStruct((4, *block.shape), block.dtype)]
    return halo_call(1, halo_out_kernel, n_ctx, (block,), out_shape, (), (5, 5))[0]


def halo_back(n_ctx, blocks, shard):
    shape = blocks.shape[1:]
    buffers = [pltpu.VMEM((2, *shape), blocks.dtype)] * 3
    out_shape = [
        jax.ShapeDtypeStruct(shape, F32),
        jax.ShapeDtypeStruct((4, *shard.shape), shard.dtype),
    ]
    counts = (4, 4, 4, 4, 1)
    return halo_call(6, halo_back_kernel, n_ctx, (blocks, shard), out_shape, buffers, counts)


def pick_kernel(n_batch, n_ctx, piece, padded, gate_ref, up_ref, out_ref):
    me = lax.axis_index("batch")
    out_ref[...] = jnp.zeros_like(out_ref)
    for spot in range(n_batch):

        @pl.when(me == spot)
        def _():
            for shard in range(n_ctx):
                start = (shard * n_batch + spot) * piece
                for half, ref in enumerate((gate_ref, up_ref)):
                    place = (half * n_ctx + shard) * padded
                    out_ref[:, place : place + piece] = ref[:, start : start + piece]


def row_block(rows):
    return 48 if rows % 48 == 0 else rows


def pick_columns(n_batch, n_ctx, piece, padded, w_gate, w_up):
    rows, hidden = w_gate.shape
    block = row_block(rows)
    spec = pl.BlockSpec((block, hidden), lambda i: (i, 0))
    return pl.pallas_call(
        functools.partial(pick_kernel, n_batch, n_ctx, piece, padded),
        name="pick_columns",
        grid=(rows // block,),
        out_shape=jax.ShapeDtypeStruct((rows, 2 * n_ctx * padded), w_gate.dtype),
        in_specs=[spec, spec],
        out_specs=pl.BlockSpec((block, 2 * n_ctx * padded), lambda i: (i, 0)),
    )(w_gate, w_up)


def finish_kernel(n_batch, n_ctx, piece, padded, proj_part, gate_ref, up_ref, down_ref, attn_ref, *refs):
    outs, bufs, sems = refs[:8], refs[8:16], refs[16]
    gate_buf, up_buf, down_buf, query_buf, key_buf, value_buf, proj_buf, gain_buf = bufs
    copies = [pltpu.make_async_copy(bufs[i], outs[i], sems.at[i]) for i in range(8)]
    rows = gate_ref.shape[1]
    block = row_block(rows)

    for ref, buf, copy in ((gate_ref, gate_buf, copies[0]), (up_ref, up_buf, copies[1])):

        def place_rows(step, carry):
            lines = pl.ds(pl.multiple_of(step * block, block), block)
            for shard in range(n_ctx):
                for spot in range(n_batch):
                    start = (shard * n_batch + spot) * piece
                    place = shard * padded
                    buf[lines, start : start + piece] = ref[
                        spot, lines, place : place + piece
                    ].astype(F32)
            return carry

        lax.fori_loop(0, rows // block, place_rows, 0)
        copy.start()
    for spot in range(n_batch):
        down_buf[spot * piece : (spot + 1) * piece, :] = down_ref[spot, :piece, :].astype(F32)
    copies[2].start()
    quarter = attn_ref.shape[-1]
    proj_rows = proj_buf.shape[0]
    for spot in range(n_batch):
        for tile in range(0, quarter, 128):
            column = spot * quarter + tile
            for buf in (query_buf, key_buf, value_buf):
                if 0 <= column < buf.shape[-1]:
                    buf[:, column : column + 128] = attn_ref[
                        spot, :rows, tile : tile + 128
                    ].astype(F32)
                column -= buf.shape[-1]
        proj_buf[:, spot * proj_part : (spot + 1) * proj_part] = attn_ref[
            spot, rows : rows + proj_rows, :proj_part
        ].astype(F32)
    gain_buf[...] = attn_ref[0, rows + proj_rows : rows + proj_rows + gain_buf.shape[0], :].astype(F32)
    for copy in copies[3:]:
        copy.start()
    for copy in copies:
        copy.wait()


def finish_round(n_batch, n_ctx, piece, padded, proj_part, gate, up, down, attn, shapes):
    outs = [jax.ShapeDtypeStruct(shape, F32) for shape in shapes]
    return pl.pallas_call(
        functools.partial(finish_kernel, n_batch, n_ctx, piece, padded, proj_part),
        name="finish_round",
        out_shape=outs,
        in_specs=[pl.BlockSpec(memory_space=pltpu.VMEM)] * 4,
        out_specs=[pl.BlockSpec(memory_space=pl.ANY)] * 8,
        scratch_shapes=[pltpu.VMEM(shape, F32) for shape in shapes] + [pltpu.SemaphoreType.DMA((8,))],
    )(gate, up, down, attn)


def weights_kernel(n_batch, n_ctx, qkv_ref, proj_ref, gain_ref, qkv_all, proj_all, gain_all, *sems):
    send_far, recv_far, send_side, recv_side, send_near, recv_near, own_sem = sems
    spot = lax.axis_index("batch")
    me = lax.axis_index("ctx")
    n_chip = n_ctx // 2
    chip, core = me // 2, lax.rem(me, 2)
    near = {"ctx": me + 1 - 2 * core}
    barrier = pltpu.get_barrier_semaphore()

    def far_at(step):
        return {"ctx": 2 * lax.rem(chip + step, n_chip) + core}

    def side_at(step):
        return {"batch": lax.rem(spot + step, n_batch)}

    peers = [near]
    peers += [far_at(step) for step in range(1, n_chip)]
    peers += [side_at(step) for step in range(1, n_batch)]
    for peer in peers:
        pl.semaphore_signal(barrier, inc=1, device_id=peer, device_id_type=MESH)
    pl.semaphore_wait(barrier, len(peers))

    def remote(source, target, send, recv, peer):
        return pltpu.make_async_remote_copy(
            src_ref=source,
            dst_ref=target,
            send_sem=send,
            recv_sem=recv,
            device_id=peer,
            device_id_type=MESH,
        )

    waits = []
    far = []
    for step in range(1, n_chip):
        triple = [
            remote(source, target, send_far.at[step - 1, item], recv_far.at[step - 1, item], far_at(step))
            for item, (source, target) in enumerate(
                (
                    (qkv_ref.at[spot], qkv_all.at[spot, me]),
                    (proj_ref.at[spot], proj_all.at[me, spot]),
                    (gain_ref, gain_all.at[me]),
                )
            )
        ]
        for copy in triple:
            copy.start()
        far.append(triple)
    own = [
        pltpu.make_async_copy(qkv_ref, qkv_all.at[:, me], own_sem.at[0]),
        pltpu.make_async_copy(proj_ref, proj_all.at[me], own_sem.at[1]),
        pltpu.make_async_copy(gain_ref, gain_all.at[me], own_sem.at[2]),
    ]
    for copy in own:
        copy.start()
    first = n_chip - 1
    pairs = [
        remote(source, target, send_near.at[first, 0, item], recv_near.at[first, 0, item], near)
        for item, (source, target) in enumerate(
            (
                (qkv_ref, qkv_all.at[:, me]),
                (proj_ref, proj_all.at[me]),
                (gain_ref, gain_all.at[me]),
            )
        )
    ]
    for copy in pairs:
        copy.start()
    waits += pairs

    def hand_near(step, turn):
        origin = 2 * lax.rem(chip + n_chip - step, n_chip) + core
        quarter = lax.rem(spot + n_batch - turn, n_batch)
        blocks = [qkv_all.at[quarter, origin], proj_all.at[origin, quarter]]
        blocks += [gain_all.at[origin]] if turn == 0 else []
        for item, block in enumerate(blocks):
            copy = remote(
                block,
                block,
                send_near.at[step - 1, turn, item],
                recv_near.at[step - 1, turn, item],
                near,
            )
            copy.start()
            waits.append(copy)

    side = []
    for step in range(1, n_chip):
        for copy in far[step - 1]:
            copy.wait_recv()
        origin = 2 * lax.rem(chip + n_chip - step, n_chip) + core
        for turn in range(1, n_batch):
            pair = [
                remote(
                    block,
                    block,
                    send_side.at[step - 1, turn - 1, item],
                    recv_side.at[step - 1, turn - 1, item],
                    side_at(turn),
                )
                for item, block in enumerate((qkv_all.at[spot, origin], proj_all.at[origin, spot]))
            ]
            for copy in pair:
                copy.start()
            side.append((step, turn, pair))
        hand_near(step, 0)
    for step, turn, pair in side:
        for copy in pair:
            copy.wait_recv()
        hand_near(step, turn)
    for copy in waits:
        copy.wait()
    for copy in own:
        copy.wait()
    for triple in far:
        for copy in triple:
            copy.wait_send()
    for _, _, pair in side:
        for copy in pair:
            copy.wait_send()


def gather_weights(n_batch, n_ctx, qkv, proj, gains):
    n_chip = n_ctx // 2
    dma = pltpu.SemaphoreType.DMA
    vmem = pl.BlockSpec(memory_space=pltpu.VMEM)
    return pl.pallas_call(
        functools.partial(weights_kernel, n_batch, n_ctx),
        name="gather_weights",
        out_shape=(
            jax.ShapeDtypeStruct((n_batch, n_ctx, *qkv.shape[1:]), qkv.dtype),
            jax.ShapeDtypeStruct((n_ctx, *proj.shape), proj.dtype),
            jax.ShapeDtypeStruct((n_ctx, *gains.shape), gains.dtype),
        ),
        in_specs=[vmem] * 3,
        out_specs=[vmem] * 3,
        scratch_shapes=[
            dma((n_chip - 1, 3)),
            dma((n_chip - 1, 3)),
            dma((n_chip - 1, n_batch - 1, 2)),
            dma((n_chip - 1, n_batch - 1, 2)),
            dma((n_chip, n_batch, 3)),
            dma((n_chip, n_batch, 3)),
            dma((3,)),
        ],
        compiler_params=pltpu.CompilerParams(collective_id=12, has_side_effects=True),
    )(qkv, proj, gains)


def tail_kernel(
    n_ctx,
    gate_ref,
    first_ref,
    up_ref,
    attn_ref,
    gate_all,
    up_all,
    attn_all,
    pair_up,
    pair_attn,
    way_up,
    way_attn,
    pair_send,
    pair_recv,
    way_send,
    way_recv,
    side_send,
    side_recv,
    own_sem,
):
    n_chip = n_ctx // 2
    spot = lax.axis_index("batch")
    me = lax.axis_index("ctx")
    chip, core = me // 2, lax.rem(me, 2)
    across = {"batch": spot + 1 - 2 * lax.rem(spot, 2)}
    along = {"batch": lax.rem(spot + 2, 4)}
    near = {"ctx": me + 1 - 2 * core}
    beyond = ({"ctx": jnp.minimum(me + 2, n_ctx - 1)}, {"ctx": jnp.maximum(me - 2, 0)})
    inner = (chip > 0, chip < n_chip - 1)
    barrier = pltpu.get_barrier_semaphore()
    for peer in (near, across, along):
        pl.semaphore_signal(barrier, inc=1, device_id=peer, device_id_type=MESH)
    for has_giver, giver in zip(inner, (beyond[1], beyond[0])):

        @pl.when(has_giver)
        def _():
            pl.semaphore_signal(barrier, inc=1, device_id=giver, device_id_type=MESH)

    pl.semaphore_wait(barrier, 3 + jnp.minimum(chip, 1) + jnp.minimum(n_chip - 1 - chip, 1))

    def remote(source, target, send, recv, peer):
        return pltpu.make_async_remote_copy(
            src_ref=source,
            dst_ref=target,
            send_sem=send,
            recv_sem=recv,
            device_id=peer,
            device_id_type=MESH,
        )

    width = up_ref.shape[-1]
    cut = width // 256 * 128
    chains = (
        (up_ref, pair_up, way_up, up_all, pl.ds(0, cut)),
        (up_ref, pair_up, way_up, up_all, pl.ds(cut, width - cut)),
        (attn_ref, pair_attn, way_attn, attn_all, pl.ds(0, attn_ref.shape[-1])),
    )
    offset = first_ref.shape[-1]
    spread_columns = (pl.ds(offset, cut), pl.ds(offset + cut, width - cut), chains[2][4])
    numbers = range(len(chains))

    def pair_copy(number, place):
        source, pair, _, _, columns = chains[number]
        return remote(
            source.at[2 * place + 1 - core, :, columns],
            pair.at[place, :, columns],
            pair_send.at[number, place],
            pair_recv.at[number, place],
            near,
        )

    def way_copy(number, direction, step, source):
        _, _, way, _, columns = chains[number]
        return remote(
            source,
            way.at[direction, step - 1, :, columns],
            way_send.at[number, direction, step - 1],
            way_recv.at[number, direction, step - 1],
            beyond[direction],
        )

    def passes(direction, step):
        return chip <= step - 1 if direction == 0 else chip >= n_chip - step

    def bound_for(direction, step):
        place = chip + n_chip - step if direction == 0 else chip - n_chip + step
        return jnp.clip(place, 0, n_chip - 1)

    def side_pair(item, sources, target, columns):
        return [
            remote(
                sources,
                target.at[spot, :, columns],
                side_send.at[item, turn],
                side_recv.at[item, turn],
                peer,
            )
            for turn, peer in enumerate((across, along))
        ]

    def side_pass(item, firsts, target, start, length):
        half = length // 256 * 128
        halves = (pl.ds(start, half), pl.ds(start + half, length - half))
        copies = []
        for turn, (giver, taker) in enumerate(((across, along), (along, across))):
            firsts[turn].wait_recv()
            block = target.at[giver["batch"], :, halves[turn]]
            copies.append(
                remote(block, block, side_send.at[item, 2 + turn], side_recv.at[item, 2 + turn], taker)
            )
            copies[-1].start()
        return copies

    for number in numbers:
        for place in range(n_chip):
            pair_copy(number, place).start()
    early = ((gate_ref, gate_all), (first_ref, up_all))
    side_firsts = []
    for item, (source, target) in enumerate(early):
        side_firsts.append(side_pair(item, source, target, pl.ds(0, source.shape[-1])))
        for copy in side_firsts[-1]:
            copy.start()
    own = [
        pltpu.make_async_copy(
            source, target.at[spot, :, pl.ds(0, source.shape[-1])], own_sem.at[item]
        )
        for item, (source, target) in enumerate(early)
    ]
    for copy in own:
        copy.start()
    for _, _, way, _, columns in chains:
        for direction in range(2):

            @pl.when(jnp.logical_not(inner[direction]))
            def _():
                way[direction, n_chip - 2, :, columns] = jnp.zeros(
                    (way.shape[2], columns.size), way.dtype
                )

    for number in numbers:
        source, pair, _, _, columns = chains[number]
        for place in range(n_chip):
            pair_copy(number, place).wait_recv()
            pair[place, :, columns] = (
                pair[place, :, columns].astype(F32)
                + source[2 * place + core, :, columns].astype(F32)
            ).astype(BF16)
        for direction in range(2):

            @pl.when(passes(direction, 1))
            def _():
                place = bound_for(direction, 1)
                way_copy(number, direction, 1, pair.at[place, :, columns]).start()

    side_seconds = []
    for step in range(2, n_chip + 1):
        if step <= 3:
            item = step - 2
            source, target = early[item]
            side_seconds += side_pass(item, side_firsts[item], target, 0, source.shape[-1])
        if step == n_chip:
            break
        for number in numbers:
            _, pair, way, _, columns = chains[number]
            for direction in range(2):
                place = bound_for(direction, step)

                @pl.when(passes(direction, step) & inner[direction])
                def _():
                    way_copy(number, direction, step - 1, pair.at[place, :, columns]).wait_recv()
                    way[direction, step - 2, :, columns] = (
                        way[direction, step - 2, :, columns].astype(F32)
                        + pair[place, :, columns].astype(F32)
                    ).astype(BF16)

            for direction in range(2):
                place = bound_for(direction, step)

                @pl.when(passes(direction, step) & inner[direction])
                def _():
                    way_copy(number, direction, step, way.at[direction, step - 2, :, columns]).start()

                @pl.when(passes(direction, step) & jnp.logical_not(inner[direction]))
                def _():
                    way_copy(number, direction, step, pair.at[place, :, columns]).start()

    chain_firsts = []
    for number in numbers:
        _, pair, way, target, columns = chains[number]
        for direction in range(2):

            @pl.when(inner[direction])
            def _():
                way_copy(number, direction, n_chip - 1, pair.at[0, :, columns]).wait_recv()

        spread = spread_columns[number]
        target[spot, :, spread] = (
            pair[chip, :, columns].astype(F32)
            + way[0, n_chip - 2, :, columns].astype(F32)
            + way[1, n_chip - 2, :, columns].astype(F32)
        ).astype(BF16)
        firsts = side_pair(2 + number, target.at[spot, :, spread], target, spread)
        for copy in firsts:
            copy.start()
        chain_firsts.append(firsts)
    for number in numbers:
        target, spread = chains[number][3], spread_columns[number]
        side_seconds += side_pass(
            2 + number, chain_firsts[number], target, spread.start, spread.size
        )
    for copy in own:
        copy.wait()
    for copy in side_seconds:
        copy.wait()
    for firsts in side_firsts + chain_firsts:
        for copy in firsts:
            copy.wait_send()
    for number in numbers:
        _, pair, _, _, columns = chains[number]
        for place in range(n_chip):
            pair_copy(number, place).wait_send()
        for direction in range(2):
            for step in range(1, n_chip):

                @pl.when(passes(direction, step))
                def _():
                    way_copy(number, direction, step, pair.at[0, :, columns]).wait_send()


def tail_round(n_ctx, gate, first, up, attn):
    n_chip = n_ctx // 2
    dma = pltpu.SemaphoreType.DMA
    vmem = pl.BlockSpec(memory_space=pltpu.VMEM)
    up_shape = (up.shape[1], first.shape[1] + up.shape[2])
    shapes = (gate.shape, up_shape, attn.shape[1:])
    return pl.pallas_call(
        functools.partial(tail_kernel, n_ctx),
        name="tail_round",
        out_shape=[jax.ShapeDtypeStruct((4, *shape), BF16) for shape in shapes],
        in_specs=[vmem] * 4,
        out_specs=[vmem] * 3,
        scratch_shapes=[
            pltpu.VMEM((n_chip, *up.shape[1:]), BF16),
            pltpu.VMEM((n_chip, *attn.shape[1:]), BF16),
            pltpu.VMEM((2, n_chip - 1, *up.shape[1:]), BF16),
            pltpu.VMEM((2, n_chip - 1, *attn.shape[1:]), BF16),
            dma((3, n_chip)),
            dma((3, n_chip)),
            dma((3, 2, n_chip - 1)),
            dma((3, 2, n_chip - 1)),
            dma((5, 4)),
            dma((5, 4)),
            dma((2,)),
        ],
        compiler_params=pltpu.CompilerParams(collective_id=8, has_side_effects=True),
    )(gate, first, up, attn)


def gathered(shard):
    return lax.all_gather(shard, "ctx", axis=0, tiled=True)


def scattered(whole):
    return lax.psum_scatter(whole, "ctx", scatter_dimension=0, tiled=True)


def local(
    n_batch,
    n_ctx,
    block_in,
    positions,
    counts,
    cotangent,
    gain_input,
    w_query,
    w_key,
    w_value,
    gain_query,
    gain_key,
    w_output,
    gain_attn,
    gain_ffn,
    w_gate,
    w_up,
    w_down,
    gain_final,
):
    block_in = block_in[0]
    positions = positions[0]
    cotangent = cotangent[0]
    tok_count, model_width = block_in.shape
    width_shard = w_query.shape[0]
    query_width = w_query.shape[1]
    head_size = w_key.shape[1]
    head_count = query_width // head_size
    hidden_shard = w_down.shape[0]
    piece = hidden_shard // n_batch
    hidden_part = -(-piece * n_ctx // 128) * 128
    padded = hidden_part // n_ctx
    halo_depth = (WINDOW + tok_count - 2) // tok_count
    assert halo_depth == 4
    batch_at = lax.axis_index("batch")
    ctx_at = lax.axis_index("ctx")
    all_tok = n_batch * tok_count

    gains = jnp.concatenate(
        [gain_input, gain_attn, gain_ffn, gain_final, gain_query, gain_key]
    )
    slots_of = query_width + 2 * head_size
    quarter = slots_of // n_batch
    qkv_full, proj_full, gains_all = gather_weights(
        n_batch,
        n_ctx,
        jnp.concatenate([w_query, w_key, w_value], axis=1)
        .reshape(width_shard, n_batch, quarter)
        .transpose(1, 0, 2),
        w_output.reshape(n_batch, -1, model_width),
        gains[None],
    )
    qkv_full = qkv_full.reshape(n_batch, model_width, quarter)
    full_output = proj_full.reshape(query_width, model_width)
    gains_all = gains_all[:, 0].astype(F32)

    def gain_at(start, length):
        return gains_all[:, start : start + length].reshape(1, -1)

    head_shard = gain_query.shape[0]
    full_gain_in = gain_at(0, width_shard)
    full_gain_attn = gain_at(width_shard, width_shard)
    full_gain_ffn = gain_at(2 * width_shard, width_shard)
    full_gain_final = gain_at(3 * width_shard, width_shard)
    full_gain_q = gain_at(4 * width_shard, head_shard)
    full_gain_k = gain_at(4 * width_shard + head_shard, head_shard)

    part_both = gathered(pick_columns(n_batch, n_ctx, piece, padded, w_gate, w_up))
    own_down = lax.dynamic_slice_in_dim(w_down, batch_at * piece, piece, 0)
    part_down = gathered(jnp.pad(own_down, ((0, padded - piece), (0, 0))))

    first_token = ctx_at * tok_count
    token_place = first_token + jnp.arange(tok_count, dtype=jnp.int32)
    valid_mask = (token_place < counts[0]).astype(F32)[:, None]
    resid_in = block_in.astype(F32)
    act_in = normed(resid_in, full_gain_in).astype(BF16)
    qkv_raw = jnp.concatenate([project(act_in, qkv_full[i]) for i in range(n_batch)], axis=1)
    query_raw = qkv_raw[:, :query_width].reshape(tok_count, head_count, head_size)
    key_raw = qkv_raw[:, query_width : query_width + head_size]
    value_low = qkv_raw[:, query_width + head_size :].astype(BF16)
    inv_freq = BASE ** (-jnp.arange(0, head_size, 2, dtype=F32) / head_size)
    angles = positions.astype(F32)[:, None] * inv_freq

    def query_path(raw_query, gain_vec):
        return rotate(normed(raw_query, gain_vec), angles[:, None, :])

    def key_path(raw_key, gain_vec):
        return rotate(normed(raw_key, gain_vec), angles)

    query_rot = query_path(query_raw, full_gain_q).astype(BF16)
    key_rot = key_path(key_raw, full_gain_k).astype(BF16)
    own_pair = jnp.concatenate([key_rot, value_low], axis=-1)
    halo = halo_out(n_ctx, own_pair)
    context = jnp.concatenate([halo.reshape(halo_depth * tok_count, -1), own_pair], axis=0)
    ctx_keys = context[:, :head_size]
    ctx_values = context[:, head_size:]
    key_total = (halo_depth + 1) * tok_count
    distance = (
        jnp.arange(tok_count, dtype=jnp.int32)[:, None]
        + halo_depth * tok_count
        - jnp.arange(key_total, dtype=jnp.int32)[None, :]
    )
    allowed = (distance >= 0) & (distance < WINDOW) & (distance <= positions[:, None])
    score_scale = head_size ** (-0.5)
    raw_scores = jnp.einsum("thd,kd->htk", query_rot, ctx_keys, preferred_element_type=F32)
    scores = jnp.where(allowed[None], raw_scores * score_scale, MASKED)
    exp_scores = jnp.exp(scores - jnp.max(scores, axis=-1, keepdims=True))
    attn_prob = exp_scores / jnp.sum(exp_scores, axis=-1, keepdims=True)
    prob_low = attn_prob.astype(BF16)
    attended = jnp.einsum("htk,kd->thd", prob_low, ctx_values, preferred_element_type=F32)
    attn_low = attended.reshape(tok_count, query_width).astype(BF16)
    attn_proj = project(attn_low, full_output)
    middle = resid_in + normed(attn_proj, full_gain_attn)
    ffn_in = normed(middle, full_gain_ffn).astype(BF16)

    (ffn_in_all,) = square_gather(2, ffn_in)
    ffn_in_all = ffn_in_all.reshape(all_tok, model_width)
    gate_pre, up_pre, mixed_low, mixed_turned = hidden_mix(256, ffn_in_all, part_both)
    mixed_low, act_in_late, attn_late = lax.optimization_barrier((mixed_low, act_in, attn_low))
    act_in_all, attn_all = square_gather(13, act_in_late, attn_late)
    ffn_in_turned = ffn_in_all.T
    mixed_low, act_in_all, attn_all, mixed_turned, ffn_in_turned = lax.optimization_barrier(
        (mixed_low, act_in_all, attn_all, mixed_turned, ffn_in_turned)
    )
    act_in_all = act_in_all.reshape(all_tok, model_width)
    attn_all = attn_all.reshape(all_tok, query_width)
    block_out, grad_ffn_low, grad_gain_final = turn_round(
        mixed_low, part_down, middle, cotangent, valid_mask, full_gain_final
    )

    grad_final = cotangent.astype(F32) * valid_mask
    grad_ffn_low = grad_ffn_low.reshape(all_tok, model_width)
    down_grad = product_low(384, mixed_turned, grad_ffn_low)
    down_grad, grad_ffn_low = lax.optimization_barrier((down_grad, grad_ffn_low))
    grad_w_down = scattered(down_grad)
    grad_gate_low, grad_up_low, back_part = hidden_back(
        256, grad_ffn_low, part_down, gate_pre, up_pre, part_both
    )
    (back_parts,) = batch_exchange(
        5, n_batch, slots=(back_part.reshape(n_batch, tok_count, model_width),)
    )
    back_parts, grad_gate_low, grad_up_low = lax.optimization_barrier(
        (back_parts, grad_gate_low, grad_up_low)
    )
    gate_grad = product_low(256, ffn_in_turned, grad_gate_low)
    up_first = product_low(256, ffn_in_turned, grad_up_low, 0, UP_FIRST)
    up_grad = product_low(256, ffn_in_turned, grad_up_low, UP_FIRST, hidden_part - UP_FIRST)
    back_parts, gate_grad, up_first, up_grad = lax.optimization_barrier(
        (back_parts, gate_grad, up_first, up_grad)
    )
    grad_up_first = scattered(up_first)
    grad_w_gate = scattered(gate_grad)
    grad_ffn_in = jnp.sum(back_parts.astype(F32), axis=0)
    _, pull_ffn_norm = jax.vjp(normed, middle, full_gain_ffn)
    grad_middle_part, grad_gain_ffn = pull_ffn_norm(grad_ffn_in)
    grad_middle = grad_final + grad_middle_part
    _, pull_attn_norm = jax.vjp(normed, attn_proj, full_gain_attn)
    grad_attn_proj, grad_gain_attn = pull_attn_norm(grad_middle)

    grad_proj_low = grad_attn_proj.astype(BF16)
    grad_attended = (
        project_back(grad_proj_low, full_output)
        .astype(BF16)
        .reshape(tok_count, head_count, head_size)
    )
    grad_prob = jnp.einsum("thd,kd->htk", grad_attended, ctx_values, preferred_element_type=F32)
    row_delta = jnp.sum(attn_prob * grad_prob, axis=-1, keepdims=True)
    grad_scores = (attn_prob * (grad_prob - row_delta)).astype(BF16)
    grad_queries = (
        jnp.einsum("htk,kd->thd", grad_scores, ctx_keys, preferred_element_type=F32) * score_scale
    )
    grad_ctx_keys = (
        jnp.einsum("htk,thd->kd", grad_scores, query_rot, preferred_element_type=F32) * score_scale
    )
    grad_ctx_values = jnp.einsum("htk,thd->kd", prob_low, grad_attended, preferred_element_type=F32)
    grad_context = jnp.concatenate([grad_ctx_keys, grad_ctx_values], axis=-1)
    halo_rows = halo_depth * tok_count
    returned, down_all = halo_back(
        n_ctx,
        grad_context[:halo_rows].astype(BF16).reshape(halo_depth, tok_count, 2 * head_size),
        grad_w_down,
    )
    own_grad = grad_context[halo_rows:] + returned
    grad_value_low = own_grad[:, head_size:].astype(BF16)
    _, pull_key = jax.vjp(key_path, key_raw, full_gain_k)
    grad_key_raw, grad_gain_key = pull_key(own_grad[:, :head_size])
    _, pull_query = jax.vjp(query_path, query_raw, full_gain_q)
    grad_query_raw, grad_gain_query = pull_query(grad_queries)
    grad_qkv_low = jnp.concatenate(
        [
            grad_query_raw.astype(BF16).reshape(tok_count, query_width),
            grad_key_raw.astype(BF16),
            grad_value_low,
        ],
        axis=1,
    )
    grad_act_in = sum(
        project_back(grad_qkv_low[:, i * quarter : (i + 1) * quarter], qkv_full[i])
        for i in range(n_batch)
    )
    _, pull_input = jax.vjp(normed, resid_in, full_gain_in)
    grad_in_part, grad_gain_input = pull_input(grad_act_in)
    grad_in = (grad_middle + grad_in_part).astype(BF16)

    def column_slots(upstream):
        return upstream.reshape(tok_count, n_batch, -1).transpose(1, 0, 2)

    gain_rows = jnp.concatenate(
        [
            grad.reshape(n_ctx, -1)
            for grad in (
                grad_gain_input,
                grad_gain_attn,
                grad_gain_ffn,
                grad_gain_final,
                grad_gain_query,
                grad_gain_key,
            )
        ],
        axis=1,
    )
    gain_parts, qkv_slots, proj_slots = batch_exchange(
        7,
        n_batch,
        whole=(gain_rows,),
        slots=(column_slots(grad_qkv_low), column_slots(grad_proj_low)),
    )
    proj_rows = w_output.shape[0]
    gain_count = gain_rows.shape[1]
    gain_lines = -(-gain_count // quarter)
    used = width_shard + proj_rows + gain_lines
    lines = -(-used // 16) * 16
    grad_w_output = weight_grad(attn_all, proj_slots.reshape(all_tok, -1)).astype(BF16)
    grad_w_qkv = weight_grad(act_in_all, qkv_slots.reshape(all_tok, -1)).astype(BF16)
    output_part = model_width // n_batch
    gain_sum = jnp.sum(gain_parts, axis=0).astype(BF16)
    packed = jnp.concatenate(
        [
            grad_w_qkv.reshape(n_ctx, width_shard, quarter),
            jnp.pad(
                grad_w_output.reshape(n_ctx, proj_rows, output_part),
                ((0, 0), (0, 0), (0, quarter - output_part)),
            ),
            jnp.pad(gain_sum, ((0, 0), (0, gain_lines * quarter - gain_count))).reshape(
                n_ctx, gain_lines, quarter
            ),
            jnp.zeros((n_ctx, lines - used, quarter), BF16),
        ],
        axis=1,
    )
    gate_all, up_all, attn_grads = tail_round(
        n_ctx,
        grad_w_gate,
        grad_up_first,
        up_grad.reshape(n_ctx, width_shard, hidden_part - UP_FIRST),
        packed,
    )
    shapes = (
        (width_shard, w_gate.shape[1]),
        (width_shard, w_gate.shape[1]),
        (hidden_shard, model_width),
        (width_shard, query_width),
        (width_shard, head_size),
        (width_shard, head_size),
        (proj_rows, model_width),
        (gain_lines, quarter),
    )
    (
        grad_gate_shard,
        grad_up_shard,
        grad_down_shard,
        grad_query_shard,
        grad_key_shard,
        grad_value_shard,
        grad_output_shard,
        gain_block,
    ) = finish_round(
        n_batch, n_ctx, piece, padded, output_part, gate_all, up_all, down_all, attn_grads, shapes
    )
    gain_mine = gain_block.reshape(-1)

    return (
        block_out[None],
        grad_in[None],
        gain_mine[:width_shard],
        grad_query_shard,
        grad_key_shard,
        grad_value_shard,
        gain_mine[4 * width_shard : 4 * width_shard + head_shard],
        gain_mine[4 * width_shard + head_shard : gain_count],
        grad_output_shard,
        gain_mine[width_shard : 2 * width_shard],
        gain_mine[2 * width_shard : 3 * width_shard],
        grad_gate_shard,
        grad_up_shard,
        grad_down_shard,
        gain_mine[3 * width_shard : 4 * width_shard],
    )


def solution(mesh):
    matrix = P("ctx", None)
    vector = P("ctx")
    tokens = P("batch", "ctx", None)

    def step(*arrays):
        return local(mesh.shape["batch"], mesh.shape["ctx"], *arrays)

    return jax.shard_map(
        step,
        mesh=mesh,
        in_specs=(
            tokens,
            P("batch", "ctx"),
            P("batch"),
            tokens,
            vector,
            matrix,
            matrix,
            matrix,
            vector,
            vector,
            matrix,
            vector,
            vector,
            matrix,
            matrix,
            matrix,
            vector,
        ),
        out_specs=(
            tokens,
            tokens,
            vector,
            matrix,
            matrix,
            matrix,
            vector,
            vector,
            matrix,
            vector,
            vector,
            matrix,
            matrix,
            matrix,
            vector,
        ),
        check_vma=False,
    )
```

```python
import functools

import jax
import jax.numpy as jnp
from jax import lax
from jax.experimental import pallas as pl
from jax.experimental.pallas import tpu as pltpu
from jax.sharding import PartitionSpec as P

WINDOW = 512
UP_FIRST = 512


EPS = 1e-06
BASE = 10000.0
MASKED = -1e30
BF16 = jnp.bfloat16
F32 = jnp.float32
MESH = pl.DeviceIdType.MESH


def normed(vector, gain_vec):
    return vector * lax.rsqrt(jnp.mean(vector * vector, axis=-1, keepdims=True) + EPS) * gain_vec


def rotate(vector, angles):
    half_size = vector.shape[-1] // 2
    cosine = jnp.cos(angles)
    sine_part = jnp.sin(angles)
    first_half = vector[..., :half_size]
    second = vector[..., half_size:]
    return jnp.concatenate(
        [first_half * cosine - second * sine_part, second * cosine + first_half * sine_part],
        axis=-1,
    )


def project(inputs, weight):
    return lax.dot_general(inputs, weight, (((1,), (0,)), ((), ())), preferred_element_type=F32)


def project_back(upstream, weight):
    return lax.dot_general(upstream, weight, (((1,), (1,)), ((), ())), preferred_element_type=F32)


def weight_grad(inputs, upstream):
    return lax.dot_general(inputs, upstream, (((0,), (0,)), ((), ())), preferred_element_type=F32)


def gated_gelu(gate_val, up_val):
    return jax.nn.gelu(gate_val, approximate=True) * up_val


def batch_kernel(size, kinds, *refs):
    count = len(kinds)
    sources, results = refs[:count], refs[count : 2 * count]
    send_sem, recv_sem, own_sem = refs[2 * count :]
    me = lax.axis_index("batch")
    barrier = pltpu.get_barrier_semaphore()
    for step in range(1, size):
        pl.semaphore_signal(
            barrier, inc=1, device_id={"batch": lax.rem(me + step, size)}, device_id_type=MESH
        )
    pl.semaphore_wait(barrier, size - 1)
    copies = []
    for step in range(1, size):
        peer = lax.rem(me + step, size)
        for item in range(count):
            source = sources[item].at[peer] if kinds[item] else sources[item]
            copies.append(
                pltpu.make_async_remote_copy(
                    src_ref=source,
                    dst_ref=results[item].at[me],
                    send_sem=send_sem.at[item, step - 1],
                    recv_sem=recv_sem.at[item, step - 1],
                    device_id={"batch": peer},
                    device_id_type=MESH,
                )
            )
    for copy in copies:
        copy.start()
    own = []
    for item in range(count):
        source = sources[item].at[me] if kinds[item] else sources[item]
        own.append(pltpu.make_async_copy(source, results[item].at[me], own_sem.at[item]))
    for copy in own:
        copy.start()
    for copy in own:
        copy.wait()
    for copy in copies:
        copy.wait()


def batch_exchange(collective_id, size, whole=(), slots=()):
    arrays = list(whole) + list(slots)
    kinds = [0] * len(whole) + [1] * len(slots)
    count = len(arrays)
    shapes = [
        jax.ShapeDtypeStruct(a.shape if k else (size, *a.shape), a.dtype)
        for a, k in zip(arrays, kinds)
    ]
    return pl.pallas_call(
        functools.partial(batch_kernel, size, kinds),
        out_shape=shapes,
        in_specs=[pl.BlockSpec(memory_space=pltpu.VMEM)] * count,
        out_specs=[pl.BlockSpec(memory_space=pltpu.VMEM)] * count,
        scratch_shapes=[
            pltpu.SemaphoreType.DMA((count, size - 1)),
            pltpu.SemaphoreType.DMA((count, size - 1)),
            pltpu.SemaphoreType.DMA((count,)),
        ],
        compiler_params=pltpu.CompilerParams(collective_id=collective_id, has_side_effects=True),
    )(*arrays)


def square_kernel(count, *refs):
    sources, results = refs[:count], refs[count : 2 * count]
    send_sem, recv_sem, own_sem = refs[2 * count :]
    me = lax.axis_index("batch")
    across = me + 1 - 2 * lax.rem(me, 2)
    along = lax.rem(me + 2, 4)
    barrier = pltpu.get_barrier_semaphore()
    for peer in (across, along):
        pl.semaphore_signal(barrier, inc=1, device_id={"batch": peer}, device_id_type=MESH)
    pl.semaphore_wait(barrier, 2)

    def remote(source, target, item, turn, peer):
        copy = pltpu.make_async_remote_copy(
            src_ref=source,
            dst_ref=target,
            send_sem=send_sem.at[item, turn],
            recv_sem=recv_sem.at[item, turn],
            device_id={"batch": peer},
            device_id_type=MESH,
        )
        copy.start()
        return copy

    firsts = [
        [
            remote(sources[item], results[item].at[me], item, turn, peer)
            for turn, peer in enumerate((across, along))
        ]
        for item in range(count)
    ]
    own = [
        pltpu.make_async_copy(sources[item], results[item].at[me], own_sem.at[item])
        for item in range(count)
    ]
    for copy in own:
        copy.start()
    seconds = []
    for item in range(count):
        columns = sources[item].shape[-1]
        cut = columns // 256 * 128
        halves = (pl.ds(0, cut), pl.ds(cut, columns - cut))
        for turn, (giver, taker) in enumerate(((across, along), (along, across))):
            firsts[item][turn].wait_recv()
            block = results[item].at[giver, :, halves[turn]]
            seconds.append(remote(block, block, item, 2 + turn, taker))
    for copy in own:
        copy.wait()
    for copy in seconds:
        copy.wait()
    for pair in firsts:
        for copy in pair:
            copy.wait_send()


def square_gather(collective_id, *arrays):
    count = len(arrays)
    return pl.pallas_call(
        functools.partial(square_kernel, count),
        out_shape=[jax.ShapeDtypeStruct((4, *a.shape), a.dtype) for a in arrays],
        in_specs=[pl.BlockSpec(memory_space=pltpu.VMEM)] * count,
        out_specs=[pl.BlockSpec(memory_space=pltpu.VMEM)] * count,
        scratch_shapes=[
            pltpu.SemaphoreType.DMA((count, 4)),
            pltpu.SemaphoreType.DMA((count, 4)),
            pltpu.SemaphoreType.DMA((count,)),
        ],
        compiler_params=pltpu.CompilerParams(collective_id=collective_id, has_side_effects=True),
    )(*arrays)


def turn_kernel(
    mixed_ref,
    down_ref,
    middle_ref,
    upstream_ref,
    valid_ref,
    gain_ref,
    out_ref,
    grads_ref,
    gain_grad_ref,
    part_ref,
    taken_ref,
    send_sem,
    recv_sem,
    pass_sem,
    take_sem,
):
    me = lax.axis_index("batch")
    across = me + 1 - 2 * lax.rem(me, 2)
    along = lax.rem(me + 2, 4)
    corner = lax.rem(across + 2, 4)
    order = (corner, across, along)
    tok_count = middle_ref.shape[0]
    barrier = pltpu.get_barrier_semaphore()
    for peer in order:
        pl.semaphore_signal(barrier, inc=1, device_id={"batch": peer}, device_id_type=MESH)
    pl.semaphore_wait(barrier, 3)

    def product(place):
        rows = pl.ds(pl.multiple_of(place * tok_count, tok_count), tok_count)
        return jnp.dot(mixed_ref[rows, :], down_ref[...], preferred_element_type=F32)

    copies = [
        pltpu.make_async_remote_copy(
            src_ref=part_ref.at[turn],
            dst_ref=taken_ref.at[turn],
            send_sem=send_sem.at[turn],
            recv_sem=recv_sem.at[turn],
            device_id={"batch": peer},
            device_id_type=MESH,
        )
        for turn, peer in enumerate(order)
    ]
    for turn, peer in enumerate(order):
        part_ref[turn] = product(peer).astype(BF16)
        if turn > 0:
            copies[turn - 1].start()
    total = product(me)
    copies[2].start()
    for turn in range(3):
        copies[turn].wait_recv()
        total = total + taken_ref[turn].astype(F32)
    gain = gain_ref[...]
    valid = valid_ref[...]
    scale = lax.rsqrt(jnp.mean(total * total, axis=-1, keepdims=True) + EPS)
    upstream = upstream_ref[...].astype(F32) * valid
    gained = upstream * gain
    back = scale * gained - total * (
        scale * scale * scale * jnp.mean(total * gained, axis=-1, keepdims=True)
    )
    grads_ref[me] = back.astype(BF16)
    unit = total * scale
    out_ref[...] = ((middle_ref[...] + unit * gain) * valid).astype(BF16)
    gain_grad_ref[...] = jnp.sum(upstream * unit, axis=0, keepdims=True)

    def remote(block, turn, peer):
        copy = pltpu.make_async_remote_copy(
            src_ref=block,
            dst_ref=block,
            send_sem=pass_sem.at[turn],
            recv_sem=take_sem.at[turn],
            device_id={"batch": peer},
            device_id_type=MESH,
        )
        copy.start()
        return copy

    firsts = [remote(grads_ref.at[me], turn, peer) for turn, peer in enumerate((across, along))]
    columns = grads_ref.shape[-1]
    cut = columns // 256 * 128
    halves = (pl.ds(0, cut), pl.ds(cut, columns - cut))
    seconds = []
    for turn, (giver, taker) in enumerate(((across, along), (along, across))):
        firsts[turn].wait_recv()
        seconds.append(remote(grads_ref.at[giver, :, halves[turn]], 2 + turn, taker))
    for copy in seconds:
        copy.wait()
    for copy in firsts + copies:
        copy.wait_send()


def turn_round(mixed, down, middle, upstream, valid, gain):
    tok_count, width = middle.shape
    dma = pltpu.SemaphoreType.DMA
    vmem = pl.BlockSpec(memory_space=pltpu.VMEM)
    flops = 2 * mixed.shape[0] * mixed.shape[1] * width
    return pl.pallas_call(
        turn_kernel,
        name="turn_round",
        out_shape=(
            jax.ShapeDtypeStruct((tok_count, width), BF16),
            jax.ShapeDtypeStruct((4, tok_count, width), BF16),
            jax.ShapeDtypeStruct((1, width), F32),
        ),
        in_specs=[vmem] * 6,
        out_specs=[vmem] * 3,
        scratch_shapes=[
            pltpu.VMEM((3, tok_count, width), BF16),
            pltpu.VMEM((3, tok_count, width), BF16),
            dma((3,)),
            dma((3,)),
            dma((4,)),
            dma((4,)),
        ],
        cost_estimate=pl.CostEstimate(flops=flops, bytes_accessed=8 << 20, transcendentals=0),
        compiler_params=pltpu.CompilerParams(collective_id=3, has_side_effects=True),
    )(mixed, down, middle, upstream, valid, gain)


def product_kernel(left_ref, right_ref, out_ref):
    out_ref[...] = jnp.dot(left_ref[...], right_ref[...], preferred_element_type=F32).astype(BF16)


def product_low(tile, left, right, start=0, columns=None):
    rows, depth = left.shape
    columns = columns or right.shape[1]
    skip = start // tile
    return pl.pallas_call(
        product_kernel,
        grid=(columns // tile,),
        out_shape=jax.ShapeDtypeStruct((rows, columns), BF16),
        in_specs=[
            pl.BlockSpec((rows, depth), lambda i: (0, 0)),
            pl.BlockSpec((depth, tile), lambda i: (0, i + skip)),
        ],
        out_specs=pl.BlockSpec((rows, tile), lambda i: (0, i)),
        cost_estimate=pl.CostEstimate(
            flops=2 * rows * depth * columns, bytes_accessed=8 << 20, transcendentals=0
        ),
    )(left, right)


def mix_kernel(tokens_ref, w_gate_ref, w_up_ref, gate_ref, up_ref, mixed_ref, turned_ref):
    gate = project(tokens_ref[...], w_gate_ref[...])
    up = project(tokens_ref[...], w_up_ref[...])
    gate_ref[...] = gate
    up_ref[...] = up
    mixed = gated_gelu(gate, up)
    mixed_ref[...] = mixed.astype(BF16)
    turned_ref[...] = mixed.T.astype(BF16)


def hidden_mix(tile, tokens, both_weights):
    count, width = tokens.shape
    hidden = both_weights.shape[1] // 2
    steps = hidden // tile
    wide = jax.ShapeDtypeStruct((count, hidden), F32)
    column = pl.BlockSpec((count, tile), lambda i: (0, i))
    return pl.pallas_call(
        mix_kernel,
        name="hidden_mix",
        grid=(steps,),
        out_shape=(
            wide,
            wide,
            jax.ShapeDtypeStruct((count, hidden), BF16),
            jax.ShapeDtypeStruct((hidden, count), BF16),
        ),
        in_specs=[
            pl.BlockSpec((count, width), lambda i: (0, 0)),
            pl.BlockSpec((width, tile), lambda i: (0, i)),
            pl.BlockSpec((width, tile), lambda i: (0, i + steps)),
        ],
        out_specs=[column, column, column, pl.BlockSpec((tile, count), lambda i: (i, 0))],
        cost_estimate=pl.CostEstimate(
            flops=4 * count * hidden * width, bytes_accessed=24 << 20, transcendentals=0
        ),
    )(tokens, both_weights, both_weights)


def back_kernel(
    upstream_ref, down_ref, gate_ref, up_ref, w_gate_ref, w_up_ref, gate_out, up_out, back_ref, total
):
    step = pl.program_id(0)
    grad_mixed = project_back(upstream_ref[...], down_ref[...])
    _, pull_gelu = jax.vjp(gated_gelu, gate_ref[...], up_ref[...])
    grad_gate, grad_up = pull_gelu(grad_mixed)
    grad_gate, grad_up = grad_gate.astype(BF16), grad_up.astype(BF16)
    gate_out[...] = grad_gate
    up_out[...] = grad_up
    part = project_back(grad_gate, w_gate_ref[...]) + project_back(grad_up, w_up_ref[...])

    @pl.when(step == 0)
    def _():
        total[...] = part

    @pl.when(step > 0)
    def _():
        total[...] += part

    @pl.when(step == pl.num_programs(0) - 1)
    def _():
        back_ref[...] = total[...].astype(BF16)


def hidden_back(tile, upstream, down, gate_pre, up_pre, both_weights):
    tokens, width = upstream.shape
    hidden = down.shape[0]
    count = hidden // tile
    low = jax.ShapeDtypeStruct((tokens, hidden), BF16)
    return pl.pallas_call(
        back_kernel,
        name="hidden_back",
        grid=(count,),
        out_shape=(low, low, jax.ShapeDtypeStruct((tokens, width), BF16)),
        in_specs=[
            pl.BlockSpec((tokens, width), lambda i: (0, 0)),
            pl.BlockSpec((tile, width), lambda i: (i, 0)),
            pl.BlockSpec((tokens, tile), lambda i: (0, i)),
            pl.BlockSpec((tokens, tile), lambda i: (0, i)),
            pl.BlockSpec((width, tile), lambda i: (0, i)),
            pl.BlockSpec((width, tile), lambda i: (0, i + count)),
        ],
        out_specs=[
            pl.BlockSpec((tokens, tile), lambda i: (0, i)),
            pl.BlockSpec((tokens, tile), lambda i: (0, i)),
            pl.BlockSpec((tokens, width), lambda i: (0, 0)),
        ],
        scratch_shapes=[pltpu.VMEM((tokens, width), F32)],
        cost_estimate=pl.CostEstimate(
            flops=6 * tokens * hidden * width, bytes_accessed=24 << 20, transcendentals=0
        ),
    )(upstream, down, gate_pre, up_pre, both_weights, both_weights)


def product_pair_kernel(split, left_ref, first_ref, second_ref, out_ref):
    right = jnp.where(pl.program_id(0) < split, first_ref[...], second_ref[...])
    out_ref[...] = jnp.dot(left_ref[...], right, preferred_element_type=F32).astype(BF16)


def product_pair(tile, left, first, second, columns):
    rows, depth = left.shape
    split = first.shape[1] // tile
    steps = split + columns // tile
    return pl.pallas_call(
        functools.partial(product_pair_kernel, split),
        grid=(steps,),
        out_shape=jax.ShapeDtypeStruct((rows, steps * tile), BF16),
        in_specs=[
            pl.BlockSpec((rows, depth), lambda i: (0, 0)),
            pl.BlockSpec((depth, tile), lambda i: (0, jnp.minimum(i, split - 1))),
            pl.BlockSpec((depth, tile), lambda i: (0, jnp.maximum(i - split, 0))),
        ],
        out_specs=pl.BlockSpec((rows, tile), lambda i: (0, i)),
        cost_estimate=pl.CostEstimate(
            flops=2 * rows * depth * steps * tile, bytes_accessed=10 << 20, transcendentals=0
        ),
    )(left, first, second)


def halo_out_kernel(n_chip, source_ref, result_ref, send_sem, recv_sem):
    me = lax.axis_index("ctx")
    chip, core = me // 2, lax.rem(me, 2)
    near = {"ctx": me + 1 - 2 * core}
    after = {"ctx": jnp.minimum(me + 2, 2 * n_chip - 1)}
    has_after = chip < n_chip - 1
    barrier = pltpu.get_barrier_semaphore()
    pl.semaphore_signal(barrier, inc=1, device_id=near, device_id_type=MESH)

    @pl.when(chip > 0)
    def _():
        before = {"ctx": jnp.maximum(me - 2, 0)}
        pl.semaphore_signal(barrier, inc=1, device_id=before, device_id_type=MESH)

    pl.semaphore_wait(barrier, 1 + jnp.minimum(n_chip - 1 - chip, 1))

    def remote(source, slot, turn, peer):
        return pltpu.make_async_remote_copy(
            src_ref=source,
            dst_ref=result_ref.at[slot],
            send_sem=send_sem.at[turn],
            recv_sem=recv_sem.at[turn],
            device_id=peer,
            device_id_type=MESH,
        )

    one_on = remote(source_ref, 2, 0, after)
    two_on = remote(result_ref.at[2], 0, 1, after)
    own_near = remote(source_ref, 3, 2, near)
    before_near = remote(result_ref.at[2], 3 - 2 * (1 - core), 3, near)
    far_near = remote(result_ref.at[0], 1, 4, near)

    @pl.when(has_after)
    def _():
        one_on.start()

    @pl.when(core == 0)
    def _():
        own_near.start()

    def blank(slot):
        result_ref[slot] = jnp.zeros(result_ref.shape[1:], result_ref.dtype)

    @pl.when(chip == 0)
    def _():
        blank(2)
        blank(0)
        blank(1)

    @pl.when((chip == 0) & (core == 0))
    def _():
        blank(3)

    @pl.when(chip == 1)
    def _():
        blank(0)

    @pl.when((chip == 1) & (core == 0))
    def _():
        blank(1)

    @pl.when(chip > 0)
    def _():
        one_on.wait_recv()

    @pl.when((chip > 0) & has_after)
    def _():
        two_on.start()

    @pl.when(chip > 0)
    def _():
        before_near.start()

    @pl.when(chip > 1)
    def _():
        two_on.wait_recv()

    @pl.when((chip > 1) & (core == 1))
    def _():
        far_near.start()

    @pl.when(core == 1)
    def _():
        own_near.wait_recv()

    @pl.when(core == 0)
    def _():
        own_near.wait_send()

    @pl.when(chip > 0)
    def _():
        before_near.wait()

    @pl.when((chip > 1) & (core == 0))
    def _():
        far_near.wait_recv()

    @pl.when((chip > 1) & (core == 1))
    def _():
        far_near.wait_send()

    @pl.when(has_after)
    def _():
        one_on.wait_send()

    @pl.when((chip > 0) & has_after)
    def _():
        two_on.wait_send()


def halo_back_kernel(
    n_chip,
    source_ref,
    shard_ref,
    result_ref,
    shards_ref,
    near_ref,
    far_ref,
    way_ref,
    send_sem,
    recv_sem,
    pass_sem,
    take_sem,
    own_sem,
):
    me = lax.axis_index("ctx")
    spot = lax.axis_index("batch")
    across = spot + 1 - 2 * lax.rem(spot, 2)
    along = lax.rem(spot + 2, 4)
    chip, core = me // 2, lax.rem(me, 2)
    near = {"ctx": me + 1 - 2 * core}
    before = {"ctx": jnp.maximum(me - 2, 0)}
    has_after = chip < n_chip - 1
    barrier = pltpu.get_barrier_semaphore()
    pl.semaphore_signal(barrier, inc=1, device_id=near, device_id_type=MESH)

    @pl.when(has_after)
    def _():
        after = {"ctx": jnp.minimum(me + 2, 2 * n_chip - 1)}
        pl.semaphore_signal(barrier, inc=1, device_id=after, device_id_type=MESH)

    for peer in (across, along):
        pl.semaphore_signal(barrier, inc=1, device_id={"batch": peer}, device_id_type=MESH)
    pl.semaphore_wait(barrier, 3 + jnp.minimum(chip, 1))

    def beside(source, target, turn, peer):
        copy = pltpu.make_async_remote_copy(
            src_ref=source,
            dst_ref=target,
            send_sem=pass_sem.at[turn],
            recv_sem=take_sem.at[turn],
            device_id={"batch": peer},
            device_id_type=MESH,
        )
        copy.start()
        return copy

    def remote(source, target, turn, peer):
        return pltpu.make_async_remote_copy(
            src_ref=source,
            dst_ref=target,
            send_sem=send_sem.at[turn],
            recv_sem=recv_sem.at[turn],
            device_id=peer,
            device_id_type=MESH,
        )

    to_before = remote(source_ref.at[3 - 2 * core], near_ref.at[0], 0, near)
    to_other = remote(source_ref.at[1 + 2 * core], near_ref.at[1], 1, near)
    to_before.start()
    to_other.start()
    firsts = [
        beside(shard_ref, shards_ref.at[spot], turn, peer)
        for turn, peer in enumerate((across, along))
    ]
    own = pltpu.make_async_copy(shard_ref, shards_ref.at[spot], own_sem.at[0])
    own.start()

    @pl.when((chip == 0) | jnp.logical_not(has_after))
    def _():
        way_ref[0] = jnp.zeros(way_ref.shape[1:], way_ref.dtype)

    @pl.when(jnp.logical_not(has_after))
    def _():
        way_ref[1] = jnp.zeros(way_ref.shape[1:], way_ref.dtype)

    to_other.wait_recv()
    theirs = near_ref[1].astype(F32)
    far_ref[0] = (source_ref[0].astype(F32) + jnp.where(core == 1, theirs, 0.0)).astype(BF16)
    two_back = remote(far_ref.at[0], way_ref.at[0], 2, before)
    one_back = remote(far_ref.at[1], way_ref.at[1], 3, before)

    @pl.when(chip > 1)
    def _():
        two_back.start()

    to_before.wait_recv()
    due = source_ref[2].astype(F32) + near_ref[0].astype(F32)

    @pl.when((chip > 0) & has_after)
    def _():
        two_back.wait_recv()

    far_ref[1] = (due + way_ref[0].astype(F32)).astype(BF16)

    @pl.when(chip > 0)
    def _():
        one_back.start()

    columns = shard_ref.shape[-1]
    cut = columns // 256 * 128
    halves = (pl.ds(0, cut), pl.ds(cut, columns - cut))
    seconds = []
    for turn, (giver, taker) in enumerate(((across, along), (along, across))):
        firsts[turn].wait_recv()
        block = shards_ref.at[giver, :, halves[turn]]
        seconds.append(beside(block, block, 2 + turn, taker))

    @pl.when(has_after)
    def _():
        one_back.wait_recv()

    result_ref[...] = way_ref[1].astype(F32) + jnp.where(core == 0, theirs, 0.0)
    own.wait()
    for copy in seconds:
        copy.wait()
    for copy in firsts + [to_before, to_other]:
        copy.wait_send()

    @pl.when(chip > 1)
    def _():
        two_back.wait_send()

    @pl.when(chip > 0)
    def _():
        one_back.wait_send()


def halo_call(collective_id, kernel, n_ctx, arrays, out_shape, buffers, counts):
    dma = pltpu.SemaphoreType.DMA
    vmem = pl.BlockSpec(memory_space=pltpu.VMEM)
    return pl.pallas_call(
        functools.partial(kernel, n_ctx // 2),
        out_shape=out_shape,
        in_specs=[vmem] * len(arrays),
        out_specs=[vmem] * len(out_shape),
        scratch_shapes=[*buffers, *(dma((count,)) for count in counts)],
        compiler_params=pltpu.CompilerParams(collective_id=collective_id, has_side_effects=True),
    )(*arrays)


def halo_out(n_ctx, block):
    out_shape = [jax.ShapeDtypeStruct((4, *block.shape), block.dtype)]
    return halo_call(1, halo_out_kernel, n_ctx, (block,), out_shape, (), (5, 5))[0]


def halo_back(n_ctx, blocks, shard):
    shape = blocks.shape[1:]
    buffers = [pltpu.VMEM((2, *shape), blocks.dtype)] * 3
    out_shape = [
        jax.ShapeDtypeStruct(shape, F32),
        jax.ShapeDtypeStruct((4, *shard.shape), shard.dtype),
    ]
    counts = (4, 4, 4, 4, 1)
    return halo_call(6, halo_back_kernel, n_ctx, (blocks, shard), out_shape, buffers, counts)


def pick_kernel(n_batch, n_ctx, piece, padded, gate_ref, up_ref, out_ref):
    me = lax.axis_index("batch")
    out_ref[...] = jnp.zeros_like(out_ref)
    for spot in range(n_batch):

        @pl.when(me == spot)
        def _():
            for shard in range(n_ctx):
                start = (shard * n_batch + spot) * piece
                for half, ref in enumerate((gate_ref, up_ref)):
                    place = (half * n_ctx + shard) * padded
                    out_ref[:, place : place + piece] = ref[:, start : start + piece]


def row_block(rows):
    return 48 if rows % 48 == 0 else rows


def pick_columns(n_batch, n_ctx, piece, padded, w_gate, w_up):
    rows, hidden = w_gate.shape
    block = row_block(rows)
    spec = pl.BlockSpec((block, hidden), lambda i: (i, 0))
    return pl.pallas_call(
        functools.partial(pick_kernel, n_batch, n_ctx, piece, padded),
        name="pick_columns",
        grid=(rows // block,),
        out_shape=jax.ShapeDtypeStruct((rows, 2 * n_ctx * padded), w_gate.dtype),
        in_specs=[spec, spec],
        out_specs=pl.BlockSpec((block, 2 * n_ctx * padded), lambda i: (i, 0)),
    )(w_gate, w_up)


def finish_kernel(n_batch, n_ctx, piece, padded, proj_part, gate_ref, up_ref, down_ref, attn_ref, *refs):
    outs, bufs, sems = refs[:8], refs[8:16], refs[16]
    gate_buf, up_buf, down_buf, query_buf, key_buf, value_buf, proj_buf, gain_buf = bufs
    copies = [pltpu.make_async_copy(bufs[i], outs[i], sems.at[i]) for i in range(8)]
    rows = gate_ref.shape[1]
    block = row_block(rows)

    for ref, buf, copy in ((gate_ref, gate_buf, copies[0]), (up_ref, up_buf, copies[1])):

        def place_rows(step, carry):
            lines = pl.ds(pl.multiple_of(step * block, block), block)
            for shard in range(n_ctx):
                for spot in range(n_batch):
                    start = (shard * n_batch + spot) * piece
                    place = shard * padded
                    buf[lines, start : start + piece] = ref[
                        spot, lines, place : place + piece
                    ].astype(F32)
            return carry

        lax.fori_loop(0, rows // block, place_rows, 0)
        copy.start()
    for spot in range(n_batch):
        down_buf[spot * piece : (spot + 1) * piece, :] = down_ref[spot, :piece, :].astype(F32)
    copies[2].start()
    quarter = attn_ref.shape[-1]
    proj_rows = proj_buf.shape[0]
    for spot in range(n_batch):
        for tile in range(0, quarter, 128):
            column = spot * quarter + tile
            for buf in (query_buf, key_buf, value_buf):
                if 0 <= column < buf.shape[-1]:
                    buf[:, column : column + 128] = attn_ref[
                        spot, :rows, tile : tile + 128
                    ].astype(F32)
                column -= buf.shape[-1]
        proj_buf[:, spot * proj_part : (spot + 1) * proj_part] = attn_ref[
            spot, rows : rows + proj_rows, :proj_part
        ].astype(F32)
    gain_buf[...] = attn_ref[0, rows + proj_rows : rows + proj_rows + gain_buf.shape[0], :].astype(F32)
    for copy in copies[3:]:
        copy.start()
    for copy in copies:
        copy.wait()


def finish_round(n_batch, n_ctx, piece, padded, proj_part, gate, up, down, attn, shapes):
    outs = [jax.ShapeDtypeStruct(shape, F32) for shape in shapes]
    return pl.pallas_call(
        functools.partial(finish_kernel, n_batch, n_ctx, piece, padded, proj_part),
        name="finish_round",
        out_shape=outs,
        in_specs=[pl.BlockSpec(memory_space=pltpu.VMEM)] * 4,
        out_specs=[pl.BlockSpec(memory_space=pl.ANY)] * 8,
        scratch_shapes=[pltpu.VMEM(shape, F32) for shape in shapes] + [pltpu.SemaphoreType.DMA((8,))],
    )(gate, up, down, attn)


def weights_kernel(n_batch, n_ctx, qkv_ref, proj_ref, gain_ref, qkv_all, proj_all, gain_all, *sems):
    send_far, recv_far, send_side, recv_side, send_near, recv_near, own_sem = sems
    spot = lax.axis_index("batch")
    me = lax.axis_index("ctx")
    n_chip = n_ctx // 2
    chip, core = me // 2, lax.rem(me, 2)
    near = {"ctx": me + 1 - 2 * core}
    barrier = pltpu.get_barrier_semaphore()

    def far_at(step):
        return {"ctx": 2 * lax.rem(chip + step, n_chip) + core}

    def side_at(step):
        return {"batch": lax.rem(spot + step, n_batch)}

    peers = [near]
    peers += [far_at(step) for step in range(1, n_chip)]
    peers += [side_at(step) for step in range(1, n_batch)]
    for peer in peers:
        pl.semaphore_signal(barrier, inc=1, device_id=peer, device_id_type=MESH)
    pl.semaphore_wait(barrier, len(peers))

    def remote(source, target, send, recv, peer):
        return pltpu.make_async_remote_copy(
            src_ref=source,
            dst_ref=target,
            send_sem=send,
            recv_sem=recv,
            device_id=peer,
            device_id_type=MESH,
        )

    waits = []
    far = []
    for step in range(1, n_chip):
        triple = [
            remote(source, target, send_far.at[step - 1, item], recv_far.at[step - 1, item], far_at(step))
            for item, (source, target) in enumerate(
                (
                    (qkv_ref.at[spot], qkv_all.at[spot, me]),
                    (proj_ref.at[spot], proj_all.at[me, spot]),
                    (gain_ref, gain_all.at[me]),
                )
            )
        ]
        for copy in triple:
            copy.start()
        far.append(triple)
    own = [
        pltpu.make_async_copy(qkv_ref, qkv_all.at[:, me], own_sem.at[0]),
        pltpu.make_async_copy(proj_ref, proj_all.at[me], own_sem.at[1]),
        pltpu.make_async_copy(gain_ref, gain_all.at[me], own_sem.at[2]),
    ]
    for copy in own:
        copy.start()
    first = n_chip - 1
    pairs = [
        remote(source, target, send_near.at[first, 0, item], recv_near.at[first, 0, item], near)
        for item, (source, target) in enumerate(
            (
                (qkv_ref, qkv_all.at[:, me]),
                (proj_ref, proj_all.at[me]),
                (gain_ref, gain_all.at[me]),
            )
        )
    ]
    for copy in pairs:
        copy.start()
    waits += pairs

    def hand_near(step, turn):
        origin = 2 * lax.rem(chip + n_chip - step, n_chip) + core
        quarter = lax.rem(spot + n_batch - turn, n_batch)
        blocks = [qkv_all.at[quarter, origin], proj_all.at[origin, quarter]]
        blocks += [gain_all.at[origin]] if turn == 0 else []
        for item, block in enumerate(blocks):
            copy = remote(
                block,
                block,
                send_near.at[step - 1, turn, item],
                recv_near.at[step - 1, turn, item],
                near,
            )
            copy.start()
            waits.append(copy)

    side = []
    for step in range(1, n_chip):
        for copy in far[step - 1]:
            copy.wait_recv()
        origin = 2 * lax.rem(chip + n_chip - step, n_chip) + core
        for turn in range(1, n_batch):
            pair = [
                remote(
                    block,
                    block,
                    send_side.at[step - 1, turn - 1, item],
                    recv_side.at[step - 1, turn - 1, item],
                    side_at(turn),
                )
                for item, block in enumerate((qkv_all.at[spot, origin], proj_all.at[origin, spot]))
            ]
            for copy in pair:
                copy.start()
            side.append((step, turn, pair))
        hand_near(step, 0)
    for step, turn, pair in side:
        for copy in pair:
            copy.wait_recv()
        hand_near(step, turn)
    for copy in waits:
        copy.wait()
    for copy in own:
        copy.wait()
    for triple in far:
        for copy in triple:
            copy.wait_send()
    for _, _, pair in side:
        for copy in pair:
            copy.wait_send()


def gather_weights(n_batch, n_ctx, qkv, proj, gains):
    n_chip = n_ctx // 2
    dma = pltpu.SemaphoreType.DMA
    vmem = pl.BlockSpec(memory_space=pltpu.VMEM)
    return pl.pallas_call(
        functools.partial(weights_kernel, n_batch, n_ctx),
        name="gather_weights",
        out_shape=(
            jax.ShapeDtypeStruct((n_batch, n_ctx, *qkv.shape[1:]), qkv.dtype),
            jax.ShapeDtypeStruct((n_ctx, *proj.shape), proj.dtype),
            jax.ShapeDtypeStruct((n_ctx, *gains.shape), gains.dtype),
        ),
        in_specs=[vmem] * 3,
        out_specs=[vmem] * 3,
        scratch_shapes=[
            dma((n_chip - 1, 3)),
            dma((n_chip - 1, 3)),
            dma((n_chip - 1, n_batch - 1, 2)),
            dma((n_chip - 1, n_batch - 1, 2)),
            dma((n_chip, n_batch, 3)),
            dma((n_chip, n_batch, 3)),
            dma((3,)),
        ],
        compiler_params=pltpu.CompilerParams(collective_id=12, has_side_effects=True),
    )(qkv, proj, gains)


def tail_kernel(
    n_ctx,
    both_ref,
    up_ref,
    attn_ref,
    gate_all,
    up_all,
    attn_all,
    pair_up,
    pair_attn,
    way_up,
    way_attn,
    pair_send,
    pair_recv,
    way_send,
    way_recv,
    side_send,
    side_recv,
    own_sem,
):
    n_chip = n_ctx // 2
    spot = lax.axis_index("batch")
    me = lax.axis_index("ctx")
    chip, core = me // 2, lax.rem(me, 2)
    across = {"batch": spot + 1 - 2 * lax.rem(spot, 2)}
    along = {"batch": lax.rem(spot + 2, 4)}
    near = {"ctx": me + 1 - 2 * core}
    beyond = ({"ctx": jnp.minimum(me + 2, n_ctx - 1)}, {"ctx": jnp.maximum(me - 2, 0)})
    inner = (chip > 0, chip < n_chip - 1)
    barrier = pltpu.get_barrier_semaphore()
    for peer in (near, across, along):
        pl.semaphore_signal(barrier, inc=1, device_id=peer, device_id_type=MESH)
    for has_giver, giver in zip(inner, (beyond[1], beyond[0])):

        @pl.when(has_giver)
        def _():
            pl.semaphore_signal(barrier, inc=1, device_id=giver, device_id_type=MESH)

    pl.semaphore_wait(barrier, 3 + jnp.minimum(chip, 1) + jnp.minimum(n_chip - 1 - chip, 1))

    def remote(source, target, send, recv, peer):
        return pltpu.make_async_remote_copy(
            src_ref=source,
            dst_ref=target,
            send_sem=send,
            recv_sem=recv,
            device_id=peer,
            device_id_type=MESH,
        )

    width = up_ref.shape[-1]
    cut = width // 256 * 128
    chains = (
        (up_ref, pair_up, way_up, up_all, pl.ds(0, cut)),
        (up_ref, pair_up, way_up, up_all, pl.ds(cut, width - cut)),
        (attn_ref, pair_attn, way_attn, attn_all, pl.ds(0, attn_ref.shape[-1])),
    )
    gate_width = gate_all.shape[-1]
    offset = both_ref.shape[-1] - gate_width
    spread_columns = (pl.ds(offset, cut), pl.ds(offset + cut, width - cut), chains[2][4])
    numbers = range(len(chains))

    def pair_copy(number, place):
        source, pair, _, _, columns = chains[number]
        return remote(
            source.at[2 * place + 1 - core, :, columns],
            pair.at[place, :, columns],
            pair_send.at[number, place],
            pair_recv.at[number, place],
            near,
        )

    def way_copy(number, direction, step, source):
        _, _, way, _, columns = chains[number]
        return remote(
            source,
            way.at[direction, step - 1, :, columns],
            way_send.at[number, direction, step - 1],
            way_recv.at[number, direction, step - 1],
            beyond[direction],
        )

    def passes(direction, step):
        return chip <= step - 1 if direction == 0 else chip >= n_chip - step

    def bound_for(direction, step):
        place = chip + n_chip - step if direction == 0 else chip - n_chip + step
        return jnp.clip(place, 0, n_chip - 1)

    def side_pair(item, sources, target, columns):
        return [
            remote(
                sources,
                target.at[spot, :, columns],
                side_send.at[item, turn],
                side_recv.at[item, turn],
                peer,
            )
            for turn, peer in enumerate((across, along))
        ]

    def side_pass(item, firsts, target, start, length):
        half = length // 256 * 128
        halves = (pl.ds(start, half), pl.ds(start + half, length - half))
        copies = []
        for turn, (giver, taker) in enumerate(((across, along), (along, across))):
            firsts[turn].wait_recv()
            block = target.at[giver["batch"], :, halves[turn]]
            copies.append(
                remote(block, block, side_send.at[item, 2 + turn], side_recv.at[item, 2 + turn], taker)
            )
            copies[-1].start()
        return copies

    for number in numbers:
        for place in range(n_chip):
            pair_copy(number, place).start()
    early = (
        (both_ref.at[:, pl.ds(0, gate_width)], gate_all),
        (both_ref.at[:, pl.ds(gate_width, offset)], up_all),
    )
    side_firsts = []
    for item, (source, target) in enumerate(early):
        side_firsts.append(side_pair(item, source, target, pl.ds(0, source.shape[-1])))
        for copy in side_firsts[-1]:
            copy.start()
    own = [
        pltpu.make_async_copy(
            source, target.at[spot, :, pl.ds(0, source.shape[-1])], own_sem.at[item]
        )
        for item, (source, target) in enumerate(early)
    ]
    for copy in own:
        copy.start()
    for _, _, way, _, columns in chains:
        for direction in range(2):

            @pl.when(jnp.logical_not(inner[direction]))
            def _():
                way[direction, n_chip - 2, :, columns] = jnp.zeros(
                    (way.shape[2], columns.size), way.dtype
                )

    for number in numbers:
        source, pair, _, _, columns = chains[number]
        for place in range(n_chip):
            pair_copy(number, place).wait_recv()
            pair[place, :, columns] = (
                pair[place, :, columns].astype(F32)
                + source[2 * place + core, :, columns].astype(F32)
            ).astype(BF16)
        for direction in range(2):

            @pl.when(passes(direction, 1))
            def _():
                place = bound_for(direction, 1)
                way_copy(number, direction, 1, pair.at[place, :, columns]).start()

    side_seconds = []
    for step in range(2, n_chip + 1):
        if step <= 3:
            item = step - 2
            source, target = early[item]
            side_seconds += side_pass(item, side_firsts[item], target, 0, source.shape[-1])
        if step == n_chip:
            break
        for number in numbers:
            _, pair, way, _, columns = chains[number]
            for direction in range(2):
                place = bound_for(direction, step)

                @pl.when(passes(direction, step) & inner[direction])
                def _():
                    way_copy(number, direction, step - 1, pair.at[place, :, columns]).wait_recv()
                    way[direction, step - 2, :, columns] = (
                        way[direction, step - 2, :, columns].astype(F32)
                        + pair[place, :, columns].astype(F32)
                    ).astype(BF16)

            for direction in range(2):
                place = bound_for(direction, step)

                @pl.when(passes(direction, step) & inner[direction])
                def _():
                    way_copy(number, direction, step, way.at[direction, step - 2, :, columns]).start()

                @pl.when(passes(direction, step) & jnp.logical_not(inner[direction]))
                def _():
                    way_copy(number, direction, step, pair.at[place, :, columns]).start()

    chain_firsts = []
    for number in numbers:
        _, pair, way, target, columns = chains[number]
        for direction in range(2):

            @pl.when(inner[direction])
            def _():
                way_copy(number, direction, n_chip - 1, pair.at[0, :, columns]).wait_recv()

        spread = spread_columns[number]
        target[spot, :, spread] = (
            pair[chip, :, columns].astype(F32)
            + way[0, n_chip - 2, :, columns].astype(F32)
            + way[1, n_chip - 2, :, columns].astype(F32)
        ).astype(BF16)
        firsts = side_pair(2 + number, target.at[spot, :, spread], target, spread)
        for copy in firsts:
            copy.start()
        chain_firsts.append(firsts)
    for number in numbers:
        target, spread = chains[number][3], spread_columns[number]
        side_seconds += side_pass(
            2 + number, chain_firsts[number], target, spread.start, spread.size
        )
    for copy in own:
        copy.wait()
    for copy in side_seconds:
        copy.wait()
    for firsts in side_firsts + chain_firsts:
        for copy in firsts:
            copy.wait_send()
    for number in numbers:
        _, pair, _, _, columns = chains[number]
        for place in range(n_chip):
            pair_copy(number, place).wait_send()
        for direction in range(2):
            for step in range(1, n_chip):

                @pl.when(passes(direction, step))
                def _():
                    way_copy(number, direction, step, pair.at[0, :, columns]).wait_send()


def tail_round(n_ctx, hidden, both, up, attn):
    n_chip = n_ctx // 2
    dma = pltpu.SemaphoreType.DMA
    vmem = pl.BlockSpec(memory_space=pltpu.VMEM)
    wide = (up.shape[1], hidden)
    shapes = (wide, wide, attn.shape[1:])
    return pl.pallas_call(
        functools.partial(tail_kernel, n_ctx),
        name="tail_round",
        out_shape=[jax.ShapeDtypeStruct((4, *shape), BF16) for shape in shapes],
        in_specs=[vmem] * 3,
        out_specs=[vmem] * 3,
        scratch_shapes=[
            pltpu.VMEM((n_chip, *up.shape[1:]), BF16),
            pltpu.VMEM((n_chip, *attn.shape[1:]), BF16),
            pltpu.VMEM((2, n_chip - 1, *up.shape[1:]), BF16),
            pltpu.VMEM((2, n_chip - 1, *attn.shape[1:]), BF16),
            dma((3, n_chip)),
            dma((3, n_chip)),
            dma((3, 2, n_chip - 1)),
            dma((3, 2, n_chip - 1)),
            dma((5, 4)),
            dma((5, 4)),
            dma((2,)),
        ],
        compiler_params=pltpu.CompilerParams(collective_id=8, has_side_effects=True),
    )(both, up, attn)


def gathered(shard):
    return lax.all_gather(shard, "ctx", axis=0, tiled=True)


def scattered(whole):
    return lax.psum_scatter(whole, "ctx", scatter_dimension=0, tiled=True)


def local(
    n_batch,
    n_ctx,
    block_in,
    positions,
    counts,
    cotangent,
    gain_input,
    w_query,
    w_key,
    w_value,
    gain_query,
    gain_key,
    w_output,
    gain_attn,
    gain_ffn,
    w_gate,
    w_up,
    w_down,
    gain_final,
):
    block_in = block_in[0]
    positions = positions[0]
    cotangent = cotangent[0]
    tok_count, model_width = block_in.shape
    width_shard = w_query.shape[0]
    query_width = w_query.shape[1]
    head_size = w_key.shape[1]
    head_count = query_width // head_size
    hidden_shard = w_down.shape[0]
    piece = hidden_shard // n_batch
    hidden_part = -(-piece * n_ctx // 128) * 128
    padded = hidden_part // n_ctx
    halo_depth = (WINDOW + tok_count - 2) // tok_count
    assert halo_depth == 4
    batch_at = lax.axis_index("batch")
    ctx_at = lax.axis_index("ctx")
    all_tok = n_batch * tok_count

    gains = jnp.concatenate(
        [gain_input, gain_attn, gain_ffn, gain_final, gain_query, gain_key]
    )
    slots_of = query_width + 2 * head_size
    quarter = slots_of // n_batch
    qkv_full, proj_full, gains_all = gather_weights(
        n_batch,
        n_ctx,
        jnp.concatenate([w_query, w_key, w_value], axis=1)
        .reshape(width_shard, n_batch, quarter)
        .transpose(1, 0, 2),
        w_output.reshape(n_batch, -1, model_width),
        gains[None],
    )
    qkv_full = qkv_full.reshape(n_batch, model_width, quarter)
    full_output = proj_full.reshape(query_width, model_width)
    gains_all = gains_all[:, 0].astype(F32)

    def gain_at(start, length):
        return gains_all[:, start : start + length].reshape(1, -1)

    head_shard = gain_query.shape[0]
    full_gain_in = gain_at(0, width_shard)
    full_gain_attn = gain_at(width_shard, width_shard)
    full_gain_ffn = gain_at(2 * width_shard, width_shard)
    full_gain_final = gain_at(3 * width_shard, width_shard)
    full_gain_q = gain_at(4 * width_shard, head_shard)
    full_gain_k = gain_at(4 * width_shard + head_shard, head_shard)

    part_both = gathered(pick_columns(n_batch, n_ctx, piece, padded, w_gate, w_up))
    own_down = lax.dynamic_slice_in_dim(w_down, batch_at * piece, piece, 0)
    part_down = gathered(jnp.pad(own_down, ((0, padded - piece), (0, 0))))

    first_token = ctx_at * tok_count
    token_place = first_token + jnp.arange(tok_count, dtype=jnp.int32)
    valid_mask = (token_place < counts[0]).astype(F32)[:, None]
    resid_in = block_in.astype(F32)
    act_in = normed(resid_in, full_gain_in).astype(BF16)
    qkv_raw = jnp.concatenate([project(act_in, qkv_full[i]) for i in range(n_batch)], axis=1)
    query_raw = qkv_raw[:, :query_width].reshape(tok_count, head_count, head_size)
    key_raw = qkv_raw[:, query_width : query_width + head_size]
    value_low = qkv_raw[:, query_width + head_size :].astype(BF16)
    inv_freq = BASE ** (-jnp.arange(0, head_size, 2, dtype=F32) / head_size)
    angles = positions.astype(F32)[:, None] * inv_freq

    def query_path(raw_query, gain_vec):
        return rotate(normed(raw_query, gain_vec), angles[:, None, :])

    def key_path(raw_key, gain_vec):
        return rotate(normed(raw_key, gain_vec), angles)

    query_rot = query_path(query_raw, full_gain_q).astype(BF16)
    key_rot = key_path(key_raw, full_gain_k).astype(BF16)
    own_pair = jnp.concatenate([key_rot, value_low], axis=-1)
    halo = halo_out(n_ctx, own_pair)
    context = jnp.concatenate([halo.reshape(halo_depth * tok_count, -1), own_pair], axis=0)
    ctx_keys = context[:, :head_size]
    ctx_values = context[:, head_size:]
    key_total = (halo_depth + 1) * tok_count
    distance = (
        jnp.arange(tok_count, dtype=jnp.int32)[:, None]
        + halo_depth * tok_count
        - jnp.arange(key_total, dtype=jnp.int32)[None, :]
    )
    allowed = (distance >= 0) & (distance < WINDOW) & (distance <= positions[:, None])
    score_scale = head_size ** (-0.5)
    raw_scores = jnp.einsum("thd,kd->htk", query_rot, ctx_keys, preferred_element_type=F32)
    scores = jnp.where(allowed[None], raw_scores * score_scale, MASKED)
    exp_scores = jnp.exp(scores - jnp.max(scores, axis=-1, keepdims=True))
    attn_prob = exp_scores / jnp.sum(exp_scores, axis=-1, keepdims=True)
    prob_low = attn_prob.astype(BF16)
    attended = jnp.einsum("htk,kd->thd", prob_low, ctx_values, preferred_element_type=F32)
    attn_low = attended.reshape(tok_count, query_width).astype(BF16)
    attn_proj = project(attn_low, full_output)
    middle = resid_in + normed(attn_proj, full_gain_attn)
    ffn_in = normed(middle, full_gain_ffn).astype(BF16)

    (ffn_in_all,) = square_gather(2, ffn_in)
    ffn_in_all = ffn_in_all.reshape(all_tok, model_width)
    gate_pre, up_pre, mixed_low, mixed_turned = hidden_mix(256, ffn_in_all, part_both)
    mixed_low, act_in_late, attn_late = lax.optimization_barrier((mixed_low, act_in, attn_low))
    act_in_all, attn_all = square_gather(13, act_in_late, attn_late)
    ffn_in_turned = ffn_in_all.T
    mixed_low, act_in_all, attn_all, mixed_turned, ffn_in_turned = lax.optimization_barrier(
        (mixed_low, act_in_all, attn_all, mixed_turned, ffn_in_turned)
    )
    act_in_all = act_in_all.reshape(all_tok, model_width)
    attn_all = attn_all.reshape(all_tok, query_width)
    block_out, grad_ffn_low, grad_gain_final = turn_round(
        mixed_low, part_down, middle, cotangent, valid_mask, full_gain_final
    )

    grad_final = cotangent.astype(F32) * valid_mask
    grad_ffn_low = grad_ffn_low.reshape(all_tok, model_width)
    down_grad = product_low(384, mixed_turned, grad_ffn_low)
    down_grad, grad_ffn_low = lax.optimization_barrier((down_grad, grad_ffn_low))
    grad_w_down = scattered(down_grad)
    grad_gate_low, grad_up_low, back_part = hidden_back(
        256, grad_ffn_low, part_down, gate_pre, up_pre, part_both
    )
    (back_parts,) = batch_exchange(
        5, n_batch, slots=(back_part.reshape(n_batch, tok_count, model_width),)
    )
    back_parts, grad_gate_low, grad_up_low = lax.optimization_barrier(
        (back_parts, grad_gate_low, grad_up_low)
    )
    both_grad = product_pair(256, ffn_in_turned, grad_gate_low, grad_up_low, UP_FIRST)
    up_grad = product_low(256, ffn_in_turned, grad_up_low, UP_FIRST, hidden_part - UP_FIRST)
    back_parts, both_grad, up_grad = lax.optimization_barrier((back_parts, both_grad, up_grad))
    grad_w_both = scattered(both_grad)
    grad_ffn_in = jnp.sum(back_parts.astype(F32), axis=0)
    _, pull_ffn_norm = jax.vjp(normed, middle, full_gain_ffn)
    grad_middle_part, grad_gain_ffn = pull_ffn_norm(grad_ffn_in)
    grad_middle = grad_final + grad_middle_part
    _, pull_attn_norm = jax.vjp(normed, attn_proj, full_gain_attn)
    grad_attn_proj, grad_gain_attn = pull_attn_norm(grad_middle)

    grad_proj_low = grad_attn_proj.astype(BF16)
    grad_attended = (
        project_back(grad_proj_low, full_output)
        .astype(BF16)
        .reshape(tok_count, head_count, head_size)
    )
    grad_prob = jnp.einsum("thd,kd->htk", grad_attended, ctx_values, preferred_element_type=F32)
    row_delta = jnp.sum(attn_prob * grad_prob, axis=-1, keepdims=True)
    grad_scores = (attn_prob * (grad_prob - row_delta)).astype(BF16)
    grad_queries = (
        jnp.einsum("htk,kd->thd", grad_scores, ctx_keys, preferred_element_type=F32) * score_scale
    )
    grad_ctx_keys = (
        jnp.einsum("htk,thd->kd", grad_scores, query_rot, preferred_element_type=F32) * score_scale
    )
    grad_ctx_values = jnp.einsum("htk,thd->kd", prob_low, grad_attended, preferred_element_type=F32)
    grad_context = jnp.concatenate([grad_ctx_keys, grad_ctx_values], axis=-1)
    halo_rows = halo_depth * tok_count
    returned, down_all = halo_back(
        n_ctx,
        grad_context[:halo_rows].astype(BF16).reshape(halo_depth, tok_count, 2 * head_size),
        grad_w_down,
    )
    own_grad = grad_context[halo_rows:] + returned
    grad_value_low = own_grad[:, head_size:].astype(BF16)
    _, pull_key = jax.vjp(key_path, key_raw, full_gain_k)
    grad_key_raw, grad_gain_key = pull_key(own_grad[:, :head_size])
    _, pull_query = jax.vjp(query_path, query_raw, full_gain_q)
    grad_query_raw, grad_gain_query = pull_query(grad_queries)
    grad_qkv_low = jnp.concatenate(
        [
            grad_query_raw.astype(BF16).reshape(tok_count, query_width),
            grad_key_raw.astype(BF16),
            grad_value_low,
        ],
        axis=1,
    )
    grad_act_in = sum(
        project_back(grad_qkv_low[:, i * quarter : (i + 1) * quarter], qkv_full[i])
        for i in range(n_batch)
    )
    _, pull_input = jax.vjp(normed, resid_in, full_gain_in)
    grad_in_part, grad_gain_input = pull_input(grad_act_in)
    grad_in = (grad_middle + grad_in_part).astype(BF16)

    def column_slots(upstream):
        return upstream.reshape(tok_count, n_batch, -1).transpose(1, 0, 2)

    gain_rows = jnp.concatenate(
        [
            grad.reshape(n_ctx, -1)
            for grad in (
                grad_gain_input,
                grad_gain_attn,
                grad_gain_ffn,
                grad_gain_final,
                grad_gain_query,
                grad_gain_key,
            )
        ],
        axis=1,
    )
    gain_parts, qkv_slots, proj_slots = batch_exchange(
        7,
        n_batch,
        whole=(gain_rows,),
        slots=(column_slots(grad_qkv_low), column_slots(grad_proj_low)),
    )
    proj_rows = w_output.shape[0]
    gain_count = gain_rows.shape[1]
    gain_lines = -(-gain_count // quarter)
    used = width_shard + proj_rows + gain_lines
    lines = -(-used // 16) * 16
    grad_w_output = weight_grad(attn_all, proj_slots.reshape(all_tok, -1)).astype(BF16)
    grad_w_qkv = weight_grad(act_in_all, qkv_slots.reshape(all_tok, -1)).astype(BF16)
    output_part = model_width // n_batch
    gain_sum = jnp.sum(gain_parts, axis=0).astype(BF16)
    packed = jnp.concatenate(
        [
            grad_w_qkv.reshape(n_ctx, width_shard, quarter),
            jnp.pad(
                grad_w_output.reshape(n_ctx, proj_rows, output_part),
                ((0, 0), (0, 0), (0, quarter - output_part)),
            ),
            jnp.pad(gain_sum, ((0, 0), (0, gain_lines * quarter - gain_count))).reshape(
                n_ctx, gain_lines, quarter
            ),
            jnp.zeros((n_ctx, lines - used, quarter), BF16),
        ],
        axis=1,
    )
    gate_all, up_all, attn_grads = tail_round(
        n_ctx,
        hidden_part,
        grad_w_both,
        up_grad.reshape(n_ctx, width_shard, hidden_part - UP_FIRST),
        packed,
    )
    shapes = (
        (width_shard, w_gate.shape[1]),
        (width_shard, w_gate.shape[1]),
        (hidden_shard, model_width),
        (width_shard, query_width),
        (width_shard, head_size),
        (width_shard, head_size),
        (proj_rows, model_width),
        (gain_lines, quarter),
    )
    (
        grad_gate_shard,
        grad_up_shard,
        grad_down_shard,
        grad_query_shard,
        grad_key_shard,
        grad_value_shard,
        grad_output_shard,
        gain_block,
    ) = finish_round(
        n_batch, n_ctx, piece, padded, output_part, gate_all, up_all, down_all, attn_grads, shapes
    )
    gain_mine = gain_block.reshape(-1)

    return (
        block_out[None],
        grad_in[None],
        gain_mine[:width_shard],
        grad_query_shard,
        grad_key_shard,
        grad_value_shard,
        gain_mine[4 * width_shard : 4 * width_shard + head_shard],
        gain_mine[4 * width_shard + head_shard : gain_count],
        grad_output_shard,
        gain_mine[width_shard : 2 * width_shard],
        gain_mine[2 * width_shard : 3 * width_shard],
        grad_gate_shard,
        grad_up_shard,
        grad_down_shard,
        gain_mine[3 * width_shard : 4 * width_shard],
    )


def solution(mesh):
    matrix = P("ctx", None)
    vector = P("ctx")
    tokens = P("batch", "ctx", None)

    def step(*arrays):
        return local(mesh.shape["batch"], mesh.shape["ctx"], *arrays)

    return jax.shard_map(
        step,
        mesh=mesh,
        in_specs=(
            tokens,
            P("batch", "ctx"),
            P("batch"),
            tokens,
            vector,
            matrix,
            matrix,
            matrix,
            vector,
            vector,
            matrix,
            vector,
            vector,
            matrix,
            matrix,
            matrix,
            vector,
        ),
        out_specs=(
            tokens,
            tokens,
            vector,
            matrix,
            matrix,
            matrix,
            vector,
            vector,
            matrix,
            vector,
            vector,
            matrix,
            matrix,
            matrix,
            vector,
        ),
        check_vma=False,
    )
```

```python
import functools

import jax
import jax.numpy as jnp
from jax import lax
from jax.experimental import pallas as pl
from jax.experimental.pallas import tpu as pltpu
from jax.sharding import PartitionSpec as P

WINDOW = 512
UP_FIRST = 512


EPS = 1e-06
BASE = 10000.0
MASKED = -1e30
BF16 = jnp.bfloat16
F32 = jnp.float32
MESH = pl.DeviceIdType.MESH


def normed(vector, gain_vec):
    return vector * lax.rsqrt(jnp.mean(vector * vector, axis=-1, keepdims=True) + EPS) * gain_vec


def rotate(vector, angles):
    half_size = vector.shape[-1] // 2
    cosine = jnp.cos(angles)
    sine_part = jnp.sin(angles)
    first_half = vector[..., :half_size]
    second = vector[..., half_size:]
    return jnp.concatenate(
        [first_half * cosine - second * sine_part, second * cosine + first_half * sine_part],
        axis=-1,
    )


def project(inputs, weight):
    return lax.dot_general(inputs, weight, (((1,), (0,)), ((), ())), preferred_element_type=F32)


def project_back(upstream, weight):
    return lax.dot_general(upstream, weight, (((1,), (1,)), ((), ())), preferred_element_type=F32)


def weight_grad(inputs, upstream):
    return lax.dot_general(inputs, upstream, (((0,), (0,)), ((), ())), preferred_element_type=F32)


def gated_gelu(gate_val, up_val):
    return jax.nn.gelu(gate_val, approximate=True) * up_val


def batch_kernel(size, kinds, *refs):
    count = len(kinds)
    sources, results = refs[:count], refs[count : 2 * count]
    send_sem, recv_sem, own_sem = refs[2 * count :]
    me = lax.axis_index("batch")
    barrier = pltpu.get_barrier_semaphore()
    for step in range(1, size):
        pl.semaphore_signal(
            barrier, inc=1, device_id={"batch": lax.rem(me + step, size)}, device_id_type=MESH
        )
    pl.semaphore_wait(barrier, size - 1)
    copies = []
    for step in range(1, size):
        peer = lax.rem(me + step, size)
        for item in range(count):
            source = sources[item].at[peer] if kinds[item] else sources[item]
            copies.append(
                pltpu.make_async_remote_copy(
                    src_ref=source,
                    dst_ref=results[item].at[me],
                    send_sem=send_sem.at[item, step - 1],
                    recv_sem=recv_sem.at[item, step - 1],
                    device_id={"batch": peer},
                    device_id_type=MESH,
                )
            )
    for copy in copies:
        copy.start()
    own = []
    for item in range(count):
        source = sources[item].at[me] if kinds[item] else sources[item]
        own.append(pltpu.make_async_copy(source, results[item].at[me], own_sem.at[item]))
    for copy in own:
        copy.start()
    for copy in own:
        copy.wait()
    for copy in copies:
        copy.wait()


def batch_exchange(collective_id, size, whole=(), slots=()):
    arrays = list(whole) + list(slots)
    kinds = [0] * len(whole) + [1] * len(slots)
    count = len(arrays)
    shapes = [
        jax.ShapeDtypeStruct(a.shape if k else (size, *a.shape), a.dtype)
        for a, k in zip(arrays, kinds)
    ]
    return pl.pallas_call(
        functools.partial(batch_kernel, size, kinds),
        out_shape=shapes,
        in_specs=[pl.BlockSpec(memory_space=pltpu.VMEM)] * count,
        out_specs=[pl.BlockSpec(memory_space=pltpu.VMEM)] * count,
        scratch_shapes=[
            pltpu.SemaphoreType.DMA((count, size - 1)),
            pltpu.SemaphoreType.DMA((count, size - 1)),
            pltpu.SemaphoreType.DMA((count,)),
        ],
        compiler_params=pltpu.CompilerParams(collective_id=collective_id, has_side_effects=True),
    )(*arrays)


def square_kernel(count, *refs):
    sources, results = refs[:count], refs[count : 2 * count]
    send_sem, recv_sem, own_sem = refs[2 * count :]
    me = lax.axis_index("batch")
    across = me + 1 - 2 * lax.rem(me, 2)
    along = lax.rem(me + 2, 4)
    barrier = pltpu.get_barrier_semaphore()
    for peer in (across, along):
        pl.semaphore_signal(barrier, inc=1, device_id={"batch": peer}, device_id_type=MESH)
    pl.semaphore_wait(barrier, 2)

    def remote(source, target, item, turn, peer):
        copy = pltpu.make_async_remote_copy(
            src_ref=source,
            dst_ref=target,
            send_sem=send_sem.at[item, turn],
            recv_sem=recv_sem.at[item, turn],
            device_id={"batch": peer},
            device_id_type=MESH,
        )
        copy.start()
        return copy

    firsts = [
        [
            remote(sources[item], results[item].at[me], item, turn, peer)
            for turn, peer in enumerate((across, along))
        ]
        for item in range(count)
    ]
    own = [
        pltpu.make_async_copy(sources[item], results[item].at[me], own_sem.at[item])
        for item in range(count)
    ]
    for copy in own:
        copy.start()
    seconds = []
    for item in range(count):
        columns = sources[item].shape[-1]
        cut = columns // 256 * 128
        halves = (pl.ds(0, cut), pl.ds(cut, columns - cut))
        for turn, (giver, taker) in enumerate(((across, along), (along, across))):
            firsts[item][turn].wait_recv()
            block = results[item].at[giver, :, halves[turn]]
            seconds.append(remote(block, block, item, 2 + turn, taker))
    for copy in own:
        copy.wait()
    for copy in seconds:
        copy.wait()
    for pair in firsts:
        for copy in pair:
            copy.wait_send()


def square_gather(collective_id, *arrays):
    count = len(arrays)
    return pl.pallas_call(
        functools.partial(square_kernel, count),
        out_shape=[jax.ShapeDtypeStruct((4, *a.shape), a.dtype) for a in arrays],
        in_specs=[pl.BlockSpec(memory_space=pltpu.VMEM)] * count,
        out_specs=[pl.BlockSpec(memory_space=pltpu.VMEM)] * count,
        scratch_shapes=[
            pltpu.SemaphoreType.DMA((count, 4)),
            pltpu.SemaphoreType.DMA((count, 4)),
            pltpu.SemaphoreType.DMA((count,)),
        ],
        compiler_params=pltpu.CompilerParams(collective_id=collective_id, has_side_effects=True),
    )(*arrays)


def turn_kernel(
    mixed_ref,
    down_ref,
    middle_ref,
    upstream_ref,
    valid_ref,
    gain_ref,
    out_ref,
    grads_ref,
    gain_grad_ref,
    part_ref,
    taken_ref,
    send_sem,
    recv_sem,
    pass_sem,
    take_sem,
):
    me = lax.axis_index("batch")
    across = me + 1 - 2 * lax.rem(me, 2)
    along = lax.rem(me + 2, 4)
    corner = lax.rem(across + 2, 4)
    order = (corner, across, along)
    tok_count = middle_ref.shape[0]
    barrier = pltpu.get_barrier_semaphore()
    for peer in order:
        pl.semaphore_signal(barrier, inc=1, device_id={"batch": peer}, device_id_type=MESH)
    pl.semaphore_wait(barrier, 3)

    def product(place):
        rows = pl.ds(pl.multiple_of(place * tok_count, tok_count), tok_count)
        return jnp.dot(mixed_ref[rows, :], down_ref[...], preferred_element_type=F32)

    copies = [
        pltpu.make_async_remote_copy(
            src_ref=part_ref.at[turn],
            dst_ref=taken_ref.at[turn],
            send_sem=send_sem.at[turn],
            recv_sem=recv_sem.at[turn],
            device_id={"batch": peer},
            device_id_type=MESH,
        )
        for turn, peer in enumerate(order)
    ]
    for turn, peer in enumerate(order):
        part_ref[turn] = product(peer).astype(BF16)
        if turn > 0:
            copies[turn - 1].start()
    total = product(me)
    copies[2].start()
    for turn in range(3):
        copies[turn].wait_recv()
        total = total + taken_ref[turn].astype(F32)
    gain = gain_ref[...]
    valid = valid_ref[...]
    scale = lax.rsqrt(jnp.mean(total * total, axis=-1, keepdims=True) + EPS)
    upstream = upstream_ref[...].astype(F32) * valid
    gained = upstream * gain
    back = scale * gained - total * (
        scale * scale * scale * jnp.mean(total * gained, axis=-1, keepdims=True)
    )
    grads_ref[me] = back.astype(BF16)
    unit = total * scale
    out_ref[...] = ((middle_ref[...] + unit * gain) * valid).astype(BF16)
    gain_grad_ref[...] = jnp.sum(upstream * unit, axis=0, keepdims=True)

    def remote(block, turn, peer):
        copy = pltpu.make_async_remote_copy(
            src_ref=block,
            dst_ref=block,
            send_sem=pass_sem.at[turn],
            recv_sem=take_sem.at[turn],
            device_id={"batch": peer},
            device_id_type=MESH,
        )
        copy.start()
        return copy

    firsts = [remote(grads_ref.at[me], turn, peer) for turn, peer in enumerate((across, along))]
    columns = grads_ref.shape[-1]
    cut = columns // 256 * 128
    halves = (pl.ds(0, cut), pl.ds(cut, columns - cut))
    seconds = []
    for turn, (giver, taker) in enumerate(((across, along), (along, across))):
        firsts[turn].wait_recv()
        seconds.append(remote(grads_ref.at[giver, :, halves[turn]], 2 + turn, taker))
    for copy in seconds:
        copy.wait()
    for copy in firsts + copies:
        copy.wait_send()


def turn_round(mixed, down, middle, upstream, valid, gain):
    tok_count, width = middle.shape
    dma = pltpu.SemaphoreType.DMA
    vmem = pl.BlockSpec(memory_space=pltpu.VMEM)
    flops = 2 * mixed.shape[0] * mixed.shape[1] * width
    return pl.pallas_call(
        turn_kernel,
        name="turn_round",
        out_shape=(
            jax.ShapeDtypeStruct((tok_count, width), BF16),
            jax.ShapeDtypeStruct((4, tok_count, width), BF16),
            jax.ShapeDtypeStruct((1, width), F32),
        ),
        in_specs=[vmem] * 6,
        out_specs=[vmem] * 3,
        scratch_shapes=[
            pltpu.VMEM((3, tok_count, width), BF16),
            pltpu.VMEM((3, tok_count, width), BF16),
            dma((3,)),
            dma((3,)),
            dma((4,)),
            dma((4,)),
        ],
        cost_estimate=pl.CostEstimate(flops=flops, bytes_accessed=8 << 20, transcendentals=0),
        compiler_params=pltpu.CompilerParams(collective_id=3, has_side_effects=True),
    )(mixed, down, middle, upstream, valid, gain)


def product_kernel(left_ref, right_ref, out_ref):
    out_ref[...] = jnp.dot(left_ref[...], right_ref[...], preferred_element_type=F32).astype(BF16)


def product_low(tile, left, right):
    rows, depth = left.shape
    columns = right.shape[1]
    return pl.pallas_call(
        product_kernel,
        grid=(columns // tile,),
        out_shape=jax.ShapeDtypeStruct((rows, columns), BF16),
        in_specs=[
            pl.BlockSpec((rows, depth), lambda i: (0, 0)),
            pl.BlockSpec((depth, tile), lambda i: (0, i)),
        ],
        out_specs=pl.BlockSpec((rows, tile), lambda i: (0, i)),
        cost_estimate=pl.CostEstimate(
            flops=2 * rows * depth * columns, bytes_accessed=8 << 20, transcendentals=0
        ),
    )(left, right)


def mix_kernel(tokens_ref, w_gate_ref, w_up_ref, gate_ref, up_ref, mixed_ref, turned_ref):
    gate = project(tokens_ref[...], w_gate_ref[...])
    up = project(tokens_ref[...], w_up_ref[...])
    gate_ref[...] = gate
    up_ref[...] = up
    mixed = gated_gelu(gate, up)
    mixed_ref[...] = mixed.astype(BF16)
    turned_ref[...] = mixed.T.astype(BF16)


def hidden_mix(tile, tokens, both_weights):
    count, width = tokens.shape
    hidden = both_weights.shape[1] // 2
    steps = hidden // tile
    wide = jax.ShapeDtypeStruct((count, hidden), F32)
    column = pl.BlockSpec((count, tile), lambda i: (0, i))
    return pl.pallas_call(
        mix_kernel,
        name="hidden_mix",
        grid=(steps,),
        out_shape=(
            wide,
            wide,
            jax.ShapeDtypeStruct((count, hidden), BF16),
            jax.ShapeDtypeStruct((hidden, count), BF16),
        ),
        in_specs=[
            pl.BlockSpec((count, width), lambda i: (0, 0)),
            pl.BlockSpec((width, tile), lambda i: (0, i)),
            pl.BlockSpec((width, tile), lambda i: (0, i + steps)),
        ],
        out_specs=[column, column, column, pl.BlockSpec((tile, count), lambda i: (i, 0))],
        cost_estimate=pl.CostEstimate(
            flops=4 * count * hidden * width, bytes_accessed=24 << 20, transcendentals=0
        ),
    )(tokens, both_weights, both_weights)


def back_kernel(
    upstream_ref, down_ref, gate_ref, up_ref, w_gate_ref, w_up_ref, gate_out, up_out, back_ref, total
):
    step = pl.program_id(0)
    grad_mixed = project_back(upstream_ref[...], down_ref[...])
    _, pull_gelu = jax.vjp(gated_gelu, gate_ref[...], up_ref[...])
    grad_gate, grad_up = pull_gelu(grad_mixed)
    grad_gate, grad_up = grad_gate.astype(BF16), grad_up.astype(BF16)
    gate_out[...] = grad_gate
    up_out[...] = grad_up
    part = project_back(grad_gate, w_gate_ref[...]) + project_back(grad_up, w_up_ref[...])

    @pl.when(step == 0)
    def _():
        total[...] = part

    @pl.when(step > 0)
    def _():
        total[...] += part

    @pl.when(step == pl.num_programs(0) - 1)
    def _():
        back_ref[...] = total[...].astype(BF16)


def hidden_back(tile, upstream, down, gate_pre, up_pre, both_weights):
    tokens, width = upstream.shape
    hidden = down.shape[0]
    count = hidden // tile
    low = jax.ShapeDtypeStruct((tokens, hidden), BF16)
    return pl.pallas_call(
        back_kernel,
        name="hidden_back",
        grid=(count,),
        out_shape=(low, low, jax.ShapeDtypeStruct((tokens, width), BF16)),
        in_specs=[
            pl.BlockSpec((tokens, width), lambda i: (0, 0)),
            pl.BlockSpec((tile, width), lambda i: (i, 0)),
            pl.BlockSpec((tokens, tile), lambda i: (0, i)),
            pl.BlockSpec((tokens, tile), lambda i: (0, i)),
            pl.BlockSpec((width, tile), lambda i: (0, i)),
            pl.BlockSpec((width, tile), lambda i: (0, i + count)),
        ],
        out_specs=[
            pl.BlockSpec((tokens, tile), lambda i: (0, i)),
            pl.BlockSpec((tokens, tile), lambda i: (0, i)),
            pl.BlockSpec((tokens, width), lambda i: (0, 0)),
        ],
        scratch_shapes=[pltpu.VMEM((tokens, width), F32)],
        cost_estimate=pl.CostEstimate(
            flops=6 * tokens * hidden * width, bytes_accessed=24 << 20, transcendentals=0
        ),
    )(upstream, down, gate_pre, up_pre, both_weights, both_weights)


def multiply_tiles(tile, first, last, left, right, out, target, sems):
    def step(index, carry):
        columns = pl.ds(pl.multiple_of(index * tile, tile), tile)
        out[:, columns] = jnp.dot(
            left[...], right[:, columns], preferred_element_type=F32
        ).astype(BF16)
        pltpu.make_async_copy(out.at[:, columns], target.at[:, columns], sems.at[index]).start()
        return carry

    lax.fori_loop(first, last, step, 0)


def await_tiles(tile, count, out, target, sems):
    for index in range(count):
        columns = pl.ds(index * tile, tile)
        pltpu.make_async_copy(out.at[:, columns], target.at[:, columns], sems.at[index]).wait()


def sum_back_kernel(
    tile,
    slots_ref,
    left_ref,
    gate_ref,
    up_ref,
    sum_ref,
    both_ref,
    left,
    right,
    both,
    taken_ref,
    send_sem,
    recv_sem,
    load_sem,
    store_sem,
):
    me = lax.axis_index("batch")
    across = me + 1 - 2 * lax.rem(me, 2)
    along = lax.rem(me + 2, 4)
    order = (lax.rem(across + 2, 4), across, along)
    hidden = gate_ref.shape[1]
    width = right.shape[1]
    loads = [
        pltpu.make_async_copy(left_ref, left, load_sem.at[0]),
        pltpu.make_async_copy(gate_ref, right.at[:, pl.ds(0, hidden)], load_sem.at[1]),
        pltpu.make_async_copy(
            up_ref.at[:, pl.ds(0, width - hidden)],
            right.at[:, pl.ds(hidden, width - hidden)],
            load_sem.at[2],
        ),
    ]
    for load in loads:
        load.start()
    barrier = pltpu.get_barrier_semaphore()
    for peer in order:
        pl.semaphore_signal(barrier, inc=1, device_id={"batch": peer}, device_id_type=MESH)
    pl.semaphore_wait(barrier, 3)
    copies = [
        pltpu.make_async_remote_copy(
            src_ref=slots_ref.at[peer],
            dst_ref=taken_ref.at[turn],
            send_sem=send_sem.at[turn],
            recv_sem=recv_sem.at[turn],
            device_id={"batch": peer},
            device_id_type=MESH,
        )
        for turn, peer in enumerate(order)
    ]
    for copy in copies:
        copy.start()
    for load in loads:
        load.wait()
    multiply_tiles(tile, 0, width // tile, left, right, both, both_ref, store_sem)
    total = slots_ref[me].astype(F32)
    for turn in range(3):
        copies[turn].wait_recv()
        total = total + taken_ref[turn].astype(F32)
    sum_ref[...] = total
    for copy in copies:
        copy.wait_send()
    await_tiles(tile, width // tile, both, both_ref, store_sem)


def sum_back(tile, slots, left, gate, up, columns):
    rows, depth = left.shape
    width = gate.shape[1] + columns
    dma = pltpu.SemaphoreType.DMA
    vmem = pl.BlockSpec(memory_space=pltpu.VMEM)
    anywhere = pl.BlockSpec(memory_space=pl.ANY)
    return pl.pallas_call(
        functools.partial(sum_back_kernel, tile),
        name="sum_back",
        out_shape=[
            jax.ShapeDtypeStruct(slots.shape[1:], F32),
            jax.ShapeDtypeStruct((rows, width), BF16),
        ],
        in_specs=[vmem, anywhere, anywhere, anywhere],
        out_specs=[vmem, anywhere],
        scratch_shapes=[
            pltpu.VMEM((rows, depth), BF16),
            pltpu.VMEM((depth, width), BF16),
            pltpu.VMEM((rows, width), BF16),
            pltpu.VMEM((3, *slots.shape[1:]), BF16),
            dma((3,)),
            dma((3,)),
            dma((3,)),
            dma((width // tile,)),
        ],
        cost_estimate=pl.CostEstimate(
            flops=2 * rows * depth * width, bytes_accessed=12 << 20, transcendentals=0
        ),
        compiler_params=pltpu.CompilerParams(collective_id=5, has_side_effects=True),
    )(slots, left, gate, up)


def halo_out_kernel(n_chip, source_ref, result_ref, send_sem, recv_sem):
    me = lax.axis_index("ctx")
    chip, core = me // 2, lax.rem(me, 2)
    near = {"ctx": me + 1 - 2 * core}
    after = {"ctx": jnp.minimum(me + 2, 2 * n_chip - 1)}
    has_after = chip < n_chip - 1
    barrier = pltpu.get_barrier_semaphore()
    pl.semaphore_signal(barrier, inc=1, device_id=near, device_id_type=MESH)

    @pl.when(chip > 0)
    def _():
        before = {"ctx": jnp.maximum(me - 2, 0)}
        pl.semaphore_signal(barrier, inc=1, device_id=before, device_id_type=MESH)

    pl.semaphore_wait(barrier, 1 + jnp.minimum(n_chip - 1 - chip, 1))

    def remote(source, slot, turn, peer):
        return pltpu.make_async_remote_copy(
            src_ref=source,
            dst_ref=result_ref.at[slot],
            send_sem=send_sem.at[turn],
            recv_sem=recv_sem.at[turn],
            device_id=peer,
            device_id_type=MESH,
        )

    one_on = remote(source_ref, 2, 0, after)
    two_on = remote(result_ref.at[2], 0, 1, after)
    own_near = remote(source_ref, 3, 2, near)
    before_near = remote(result_ref.at[2], 3 - 2 * (1 - core), 3, near)
    far_near = remote(result_ref.at[0], 1, 4, near)

    @pl.when(has_after)
    def _():
        one_on.start()

    @pl.when(core == 0)
    def _():
        own_near.start()

    def blank(slot):
        result_ref[slot] = jnp.zeros(result_ref.shape[1:], result_ref.dtype)

    @pl.when(chip == 0)
    def _():
        blank(2)
        blank(0)
        blank(1)

    @pl.when((chip == 0) & (core == 0))
    def _():
        blank(3)

    @pl.when(chip == 1)
    def _():
        blank(0)

    @pl.when((chip == 1) & (core == 0))
    def _():
        blank(1)

    @pl.when(chip > 0)
    def _():
        one_on.wait_recv()

    @pl.when((chip > 0) & has_after)
    def _():
        two_on.start()

    @pl.when(chip > 0)
    def _():
        before_near.start()

    @pl.when(chip > 1)
    def _():
        two_on.wait_recv()

    @pl.when((chip > 1) & (core == 1))
    def _():
        far_near.start()

    @pl.when(core == 1)
    def _():
        own_near.wait_recv()

    @pl.when(core == 0)
    def _():
        own_near.wait_send()

    @pl.when(chip > 0)
    def _():
        before_near.wait()

    @pl.when((chip > 1) & (core == 0))
    def _():
        far_near.wait_recv()

    @pl.when((chip > 1) & (core == 1))
    def _():
        far_near.wait_send()

    @pl.when(has_after)
    def _():
        one_on.wait_send()

    @pl.when((chip > 0) & has_after)
    def _():
        two_on.wait_send()


def halo_back_kernel(
    tile,
    n_chip,
    source_ref,
    shard_ref,
    left_ref,
    up_ref,
    result_ref,
    shards_ref,
    rest_ref,
    near_ref,
    far_ref,
    way_ref,
    left,
    right,
    rest,
    send_sem,
    recv_sem,
    pass_sem,
    take_sem,
    own_sem,
    store_sem,
):
    me = lax.axis_index("ctx")
    spot = lax.axis_index("batch")
    across = spot + 1 - 2 * lax.rem(spot, 2)
    along = lax.rem(spot + 2, 4)
    chip, core = me // 2, lax.rem(me, 2)
    near = {"ctx": me + 1 - 2 * core}
    before = {"ctx": jnp.maximum(me - 2, 0)}
    has_after = chip < n_chip - 1
    barrier = pltpu.get_barrier_semaphore()
    pl.semaphore_signal(barrier, inc=1, device_id=near, device_id_type=MESH)

    @pl.when(has_after)
    def _():
        after = {"ctx": jnp.minimum(me + 2, 2 * n_chip - 1)}
        pl.semaphore_signal(barrier, inc=1, device_id=after, device_id_type=MESH)

    for peer in (across, along):
        pl.semaphore_signal(barrier, inc=1, device_id={"batch": peer}, device_id_type=MESH)
    pl.semaphore_wait(barrier, 3 + jnp.minimum(chip, 1))

    def beside(source, target, turn, peer):
        copy = pltpu.make_async_remote_copy(
            src_ref=source,
            dst_ref=target,
            send_sem=pass_sem.at[turn],
            recv_sem=take_sem.at[turn],
            device_id={"batch": peer},
            device_id_type=MESH,
        )
        copy.start()
        return copy

    def remote(source, target, turn, peer):
        return pltpu.make_async_remote_copy(
            src_ref=source,
            dst_ref=target,
            send_sem=send_sem.at[turn],
            recv_sem=recv_sem.at[turn],
            device_id=peer,
            device_id_type=MESH,
        )

    to_before = remote(source_ref.at[3 - 2 * core], near_ref.at[0], 0, near)
    to_other = remote(source_ref.at[1 + 2 * core], near_ref.at[1], 1, near)
    to_before.start()
    to_other.start()
    width = right.shape[1]
    count = width // tile
    loads = [
        pltpu.make_async_copy(left_ref, left, own_sem.at[1]),
        pltpu.make_async_copy(
            up_ref.at[:, pl.ds(up_ref.shape[1] - width, width)], right, own_sem.at[2]
        ),
    ]
    for load in loads:
        load.start()
    firsts = [
        beside(shard_ref, shards_ref.at[spot], turn, peer)
        for turn, peer in enumerate((across, along))
    ]
    own = pltpu.make_async_copy(shard_ref, shards_ref.at[spot], own_sem.at[0])
    own.start()

    @pl.when((chip == 0) | jnp.logical_not(has_after))
    def _():
        way_ref[0] = jnp.zeros(way_ref.shape[1:], way_ref.dtype)

    @pl.when(jnp.logical_not(has_after))
    def _():
        way_ref[1] = jnp.zeros(way_ref.shape[1:], way_ref.dtype)

    to_other.wait_recv()
    theirs = near_ref[1].astype(F32)
    far_ref[0] = (source_ref[0].astype(F32) + jnp.where(core == 1, theirs, 0.0)).astype(BF16)
    two_back = remote(far_ref.at[0], way_ref.at[0], 2, before)
    one_back = remote(far_ref.at[1], way_ref.at[1], 3, before)

    @pl.when(chip > 1)
    def _():
        two_back.start()

    to_before.wait_recv()
    due = source_ref[2].astype(F32) + near_ref[0].astype(F32)

    for load in loads:
        load.wait()
    multiply_tiles(tile, 0, count // 3, left, right, rest, rest_ref, store_sem)

    @pl.when((chip > 0) & has_after)
    def _():
        two_back.wait_recv()

    far_ref[1] = (due + way_ref[0].astype(F32)).astype(BF16)

    @pl.when(chip > 0)
    def _():
        one_back.start()

    multiply_tiles(tile, count // 3, count, left, right, rest, rest_ref, store_sem)
    columns = shard_ref.shape[-1]
    cut = columns // 256 * 128
    halves = (pl.ds(0, cut), pl.ds(cut, columns - cut))
    seconds = []
    for turn, (giver, taker) in enumerate(((across, along), (along, across))):
        firsts[turn].wait_recv()
        block = shards_ref.at[giver, :, halves[turn]]
        seconds.append(beside(block, block, 2 + turn, taker))

    @pl.when(has_after)
    def _():
        one_back.wait_recv()

    result_ref[...] = way_ref[1].astype(F32) + jnp.where(core == 0, theirs, 0.0)
    own.wait()
    for copy in seconds:
        copy.wait()
    for copy in firsts + [to_before, to_other]:
        copy.wait_send()
    await_tiles(tile, count, rest, rest_ref, store_sem)

    @pl.when(chip > 1)
    def _():
        two_back.wait_send()

    @pl.when(chip > 0)
    def _():
        one_back.wait_send()


def halo_call(collective_id, kernel, arrays, in_vmem, out_shape, out_vmem, buffers, counts):
    dma = pltpu.SemaphoreType.DMA
    vmem = pl.BlockSpec(memory_space=pltpu.VMEM)
    anywhere = pl.BlockSpec(memory_space=pl.ANY)
    return pl.pallas_call(
        kernel,
        out_shape=out_shape,
        in_specs=[vmem if i < in_vmem else anywhere for i in range(len(arrays))],
        out_specs=[vmem if i < out_vmem else anywhere for i in range(len(out_shape))],
        scratch_shapes=[*buffers, *(dma((count,)) for count in counts)],
        compiler_params=pltpu.CompilerParams(collective_id=collective_id, has_side_effects=True),
    )(*arrays)


def halo_out(n_ctx, block):
    out_shape = [jax.ShapeDtypeStruct((4, *block.shape), block.dtype)]
    kernel = functools.partial(halo_out_kernel, n_ctx // 2)
    return halo_call(1, kernel, (block,), 1, out_shape, 1, (), (5, 5))[0]


def halo_back(tile, n_ctx, blocks, shard, left, up, columns):
    shape = blocks.shape[1:]
    rows, depth = left.shape
    buffers = [pltpu.VMEM((2, *shape), blocks.dtype)] * 3
    buffers += [
        pltpu.VMEM((rows, depth), BF16),
        pltpu.VMEM((depth, columns), BF16),
        pltpu.VMEM((rows, columns), BF16),
    ]
    out_shape = [
        jax.ShapeDtypeStruct(shape, F32),
        jax.ShapeDtypeStruct((4, *shard.shape), shard.dtype),
        jax.ShapeDtypeStruct((rows, columns), BF16),
    ]
    kernel = functools.partial(halo_back_kernel, tile, n_ctx // 2)
    arrays = (blocks, shard, left, up)
    counts = (4, 4, 4, 4, 3, columns // tile)
    return halo_call(6, kernel, arrays, 2, out_shape, 2, buffers, counts)


def pick_kernel(n_batch, n_ctx, piece, padded, gate_ref, up_ref, out_ref):
    me = lax.axis_index("batch")
    out_ref[...] = jnp.zeros_like(out_ref)
    for spot in range(n_batch):

        @pl.when(me == spot)
        def _():
            for shard in range(n_ctx):
                start = (shard * n_batch + spot) * piece
                for half, ref in enumerate((gate_ref, up_ref)):
                    place = (half * n_ctx + shard) * padded
                    out_ref[:, place : place + piece] = ref[:, start : start + piece]


def row_block(rows):
    return 48 if rows % 48 == 0 else rows


def pick_columns(n_batch, n_ctx, piece, padded, w_gate, w_up):
    rows, hidden = w_gate.shape
    block = row_block(rows)
    spec = pl.BlockSpec((block, hidden), lambda i: (i, 0))
    return pl.pallas_call(
        functools.partial(pick_kernel, n_batch, n_ctx, piece, padded),
        name="pick_columns",
        grid=(rows // block,),
        out_shape=jax.ShapeDtypeStruct((rows, 2 * n_ctx * padded), w_gate.dtype),
        in_specs=[spec, spec],
        out_specs=pl.BlockSpec((block, 2 * n_ctx * padded), lambda i: (i, 0)),
    )(w_gate, w_up)


def finish_kernel(n_batch, n_ctx, piece, padded, proj_part, gate_ref, up_ref, down_ref, attn_ref, *refs):
    outs, bufs, sems = refs[:8], refs[8:16], refs[16]
    gate_buf, up_buf, down_buf, query_buf, key_buf, value_buf, proj_buf, gain_buf = bufs
    copies = [pltpu.make_async_copy(bufs[i], outs[i], sems.at[i]) for i in range(8)]
    rows = gate_ref.shape[1]
    block = row_block(rows)

    for ref, buf, copy in ((gate_ref, gate_buf, copies[0]), (up_ref, up_buf, copies[1])):

        def place_rows(step, carry):
            lines = pl.ds(pl.multiple_of(step * block, block), block)
            for shard in range(n_ctx):
                for spot in range(n_batch):
                    start = (shard * n_batch + spot) * piece
                    place = shard * padded
                    buf[lines, start : start + piece] = ref[
                        spot, lines, place : place + piece
                    ].astype(F32)
            return carry

        lax.fori_loop(0, rows // block, place_rows, 0)
        copy.start()
    for spot in range(n_batch):
        down_buf[spot * piece : (spot + 1) * piece, :] = down_ref[spot, :piece, :].astype(F32)
    copies[2].start()
    quarter = attn_ref.shape[-1]
    proj_rows = proj_buf.shape[0]
    for spot in range(n_batch):
        for tile in range(0, quarter, 128):
            column = spot * quarter + tile
            for buf in (query_buf, key_buf, value_buf):
                if 0 <= column < buf.shape[-1]:
                    buf[:, column : column + 128] = attn_ref[
                        spot, :rows, tile : tile + 128
                    ].astype(F32)
                column -= buf.shape[-1]
        proj_buf[:, spot * proj_part : (spot + 1) * proj_part] = attn_ref[
            spot, rows : rows + proj_rows, :proj_part
        ].astype(F32)
    gain_buf[...] = attn_ref[0, rows + proj_rows : rows + proj_rows + gain_buf.shape[0], :].astype(F32)
    for copy in copies[3:]:
        copy.start()
    for copy in copies:
        copy.wait()


def finish_round(n_batch, n_ctx, piece, padded, proj_part, gate, up, down, attn, shapes):
    outs = [jax.ShapeDtypeStruct(shape, F32) for shape in shapes]
    return pl.pallas_call(
        functools.partial(finish_kernel, n_batch, n_ctx, piece, padded, proj_part),
        name="finish_round",
        out_shape=outs,
        in_specs=[pl.BlockSpec(memory_space=pltpu.VMEM)] * 4,
        out_specs=[pl.BlockSpec(memory_space=pl.ANY)] * 8,
        scratch_shapes=[pltpu.VMEM(shape, F32) for shape in shapes] + [pltpu.SemaphoreType.DMA((8,))],
    )(gate, up, down, attn)


def weights_kernel(n_batch, n_ctx, qkv_ref, proj_ref, gain_ref, qkv_all, proj_all, gain_all, *sems):
    send_far, recv_far, send_side, recv_side, send_near, recv_near, own_sem = sems
    spot = lax.axis_index("batch")
    me = lax.axis_index("ctx")
    n_chip = n_ctx // 2
    chip, core = me // 2, lax.rem(me, 2)
    near = {"ctx": me + 1 - 2 * core}
    barrier = pltpu.get_barrier_semaphore()

    def far_at(step):
        return {"ctx": 2 * lax.rem(chip + step, n_chip) + core}

    def side_at(step):
        return {"batch": lax.rem(spot + step, n_batch)}

    peers = [near]
    peers += [far_at(step) for step in range(1, n_chip)]
    peers += [side_at(step) for step in range(1, n_batch)]
    for peer in peers:
        pl.semaphore_signal(barrier, inc=1, device_id=peer, device_id_type=MESH)
    pl.semaphore_wait(barrier, len(peers))

    def remote(source, target, send, recv, peer):
        return pltpu.make_async_remote_copy(
            src_ref=source,
            dst_ref=target,
            send_sem=send,
            recv_sem=recv,
            device_id=peer,
            device_id_type=MESH,
        )

    waits = []
    far = []
    for step in range(1, n_chip):
        triple = [
            remote(source, target, send_far.at[step - 1, item], recv_far.at[step - 1, item], far_at(step))
            for item, (source, target) in enumerate(
                (
                    (qkv_ref.at[spot], qkv_all.at[spot, me]),
                    (proj_ref.at[spot], proj_all.at[me, spot]),
                    (gain_ref, gain_all.at[me]),
                )
            )
        ]
        for copy in triple:
            copy.start()
        far.append(triple)
    own = [
        pltpu.make_async_copy(qkv_ref, qkv_all.at[:, me], own_sem.at[0]),
        pltpu.make_async_copy(proj_ref, proj_all.at[me], own_sem.at[1]),
        pltpu.make_async_copy(gain_ref, gain_all.at[me], own_sem.at[2]),
    ]
    for copy in own:
        copy.start()
    first = n_chip - 1
    pairs = [
        remote(source, target, send_near.at[first, 0, item], recv_near.at[first, 0, item], near)
        for item, (source, target) in enumerate(
            (
                (qkv_ref, qkv_all.at[:, me]),
                (proj_ref, proj_all.at[me]),
                (gain_ref, gain_all.at[me]),
            )
        )
    ]
    for copy in pairs:
        copy.start()
    waits += pairs

    def hand_near(step, turn):
        origin = 2 * lax.rem(chip + n_chip - step, n_chip) + core
        quarter = lax.rem(spot + n_batch - turn, n_batch)
        blocks = [qkv_all.at[quarter, origin], proj_all.at[origin, quarter]]
        blocks += [gain_all.at[origin]] if turn == 0 else []
        for item, block in enumerate(blocks):
            copy = remote(
                block,
                block,
                send_near.at[step - 1, turn, item],
                recv_near.at[step - 1, turn, item],
                near,
            )
            copy.start()
            waits.append(copy)

    side = []
    for step in range(1, n_chip):
        for copy in far[step - 1]:
            copy.wait_recv()
        origin = 2 * lax.rem(chip + n_chip - step, n_chip) + core
        for turn in range(1, n_batch):
            pair = [
                remote(
                    block,
                    block,
                    send_side.at[step - 1, turn - 1, item],
                    recv_side.at[step - 1, turn - 1, item],
                    side_at(turn),
                )
                for item, block in enumerate((qkv_all.at[spot, origin], proj_all.at[origin, spot]))
            ]
            for copy in pair:
                copy.start()
            side.append((step, turn, pair))
        hand_near(step, 0)
    for step, turn, pair in side:
        for copy in pair:
            copy.wait_recv()
        hand_near(step, turn)
    for copy in waits:
        copy.wait()
    for copy in own:
        copy.wait()
    for triple in far:
        for copy in triple:
            copy.wait_send()
    for _, _, pair in side:
        for copy in pair:
            copy.wait_send()


def gather_weights(n_batch, n_ctx, qkv, proj, gains):
    n_chip = n_ctx // 2
    dma = pltpu.SemaphoreType.DMA
    vmem = pl.BlockSpec(memory_space=pltpu.VMEM)
    return pl.pallas_call(
        functools.partial(weights_kernel, n_batch, n_ctx),
        name="gather_weights",
        out_shape=(
            jax.ShapeDtypeStruct((n_batch, n_ctx, *qkv.shape[1:]), qkv.dtype),
            jax.ShapeDtypeStruct((n_ctx, *proj.shape), proj.dtype),
            jax.ShapeDtypeStruct((n_ctx, *gains.shape), gains.dtype),
        ),
        in_specs=[vmem] * 3,
        out_specs=[vmem] * 3,
        scratch_shapes=[
            dma((n_chip - 1, 3)),
            dma((n_chip - 1, 3)),
            dma((n_chip - 1, n_batch - 1, 2)),
            dma((n_chip - 1, n_batch - 1, 2)),
            dma((n_chip, n_batch, 3)),
            dma((n_chip, n_batch, 3)),
            dma((3,)),
        ],
        compiler_params=pltpu.CompilerParams(collective_id=12, has_side_effects=True),
    )(qkv, proj, gains)


def tail_kernel(
    n_ctx,
    both_ref,
    up_ref,
    attn_ref,
    gate_all,
    up_all,
    attn_all,
    pair_up,
    pair_attn,
    way_up,
    way_attn,
    pair_send,
    pair_recv,
    way_send,
    way_recv,
    side_send,
    side_recv,
    own_sem,
):
    n_chip = n_ctx // 2
    spot = lax.axis_index("batch")
    me = lax.axis_index("ctx")
    chip, core = me // 2, lax.rem(me, 2)
    across = {"batch": spot + 1 - 2 * lax.rem(spot, 2)}
    along = {"batch": lax.rem(spot + 2, 4)}
    near = {"ctx": me + 1 - 2 * core}
    beyond = ({"ctx": jnp.minimum(me + 2, n_ctx - 1)}, {"ctx": jnp.maximum(me - 2, 0)})
    inner = (chip > 0, chip < n_chip - 1)
    barrier = pltpu.get_barrier_semaphore()
    for peer in (near, across, along):
        pl.semaphore_signal(barrier, inc=1, device_id=peer, device_id_type=MESH)
    for has_giver, giver in zip(inner, (beyond[1], beyond[0])):

        @pl.when(has_giver)
        def _():
            pl.semaphore_signal(barrier, inc=1, device_id=giver, device_id_type=MESH)

    pl.semaphore_wait(barrier, 3 + jnp.minimum(chip, 1) + jnp.minimum(n_chip - 1 - chip, 1))

    def remote(source, target, send, recv, peer):
        return pltpu.make_async_remote_copy(
            src_ref=source,
            dst_ref=target,
            send_sem=send,
            recv_sem=recv,
            device_id=peer,
            device_id_type=MESH,
        )

    width = up_ref.shape[-1]
    cut = width // 256 * 128
    chains = (
        (up_ref, pair_up, way_up, up_all, pl.ds(0, cut)),
        (up_ref, pair_up, way_up, up_all, pl.ds(cut, width - cut)),
        (attn_ref, pair_attn, way_attn, attn_all, pl.ds(0, attn_ref.shape[-1])),
    )
    gate_width = gate_all.shape[-1]
    offset = both_ref.shape[-1] - gate_width
    spread_columns = (pl.ds(offset, cut), pl.ds(offset + cut, width - cut), chains[2][4])
    numbers = range(len(chains))

    def pair_copy(number, place):
        source, pair, _, _, columns = chains[number]
        return remote(
            source.at[2 * place + 1 - core, :, columns],
            pair.at[place, :, columns],
            pair_send.at[number, place],
            pair_recv.at[number, place],
            near,
        )

    def way_copy(number, direction, step, source):
        _, _, way, _, columns = chains[number]
        return remote(
            source,
            way.at[direction, step - 1, :, columns],
            way_send.at[number, direction, step - 1],
            way_recv.at[number, direction, step - 1],
            beyond[direction],
        )

    def passes(direction, step):
        return chip <= step - 1 if direction == 0 else chip >= n_chip - step

    def bound_for(direction, step):
        place = chip + n_chip - step if direction == 0 else chip - n_chip + step
        return jnp.clip(place, 0, n_chip - 1)

    def side_pair(item, sources, target, columns):
        return [
            remote(
                sources,
                target.at[spot, :, columns],
                side_send.at[item, turn],
                side_recv.at[item, turn],
                peer,
            )
            for turn, peer in enumerate((across, along))
        ]

    def side_pass(item, firsts, target, start, length):
        half = length // 256 * 128
        halves = (pl.ds(start, half), pl.ds(start + half, length - half))
        copies = []
        for turn, (giver, taker) in enumerate(((across, along), (along, across))):
            firsts[turn].wait_recv()
            block = target.at[giver["batch"], :, halves[turn]]
            copies.append(
                remote(block, block, side_send.at[item, 2 + turn], side_recv.at[item, 2 + turn], taker)
            )
            copies[-1].start()
        return copies

    for number in numbers:
        for place in range(n_chip):
            pair_copy(number, place).start()
    early = (
        (both_ref.at[:, pl.ds(0, gate_width)], gate_all),
        (both_ref.at[:, pl.ds(gate_width, offset)], up_all),
    )
    side_firsts = []
    for item, (source, target) in enumerate(early):
        side_firsts.append(side_pair(item, source, target, pl.ds(0, source.shape[-1])))
        for copy in side_firsts[-1]:
            copy.start()
    own = [
        pltpu.make_async_copy(
            source, target.at[spot, :, pl.ds(0, source.shape[-1])], own_sem.at[item]
        )
        for item, (source, target) in enumerate(early)
    ]
    for copy in own:
        copy.start()
    for _, _, way, _, columns in chains:
        for direction in range(2):

            @pl.when(jnp.logical_not(inner[direction]))
            def _():
                way[direction, n_chip - 2, :, columns] = jnp.zeros(
                    (way.shape[2], columns.size), way.dtype
                )

    for number in numbers:
        source, pair, _, _, columns = chains[number]
        for place in range(n_chip):
            pair_copy(number, place).wait_recv()
            pair[place, :, columns] = (
                pair[place, :, columns].astype(F32)
                + source[2 * place + core, :, columns].astype(F32)
            ).astype(BF16)
        for direction in range(2):

            @pl.when(passes(direction, 1))
            def _():
                place = bound_for(direction, 1)
                way_copy(number, direction, 1, pair.at[place, :, columns]).start()

    side_seconds = []
    for step in range(2, n_chip + 1):
        if step <= 3:
            item = step - 2
            source, target = early[item]
            side_seconds += side_pass(item, side_firsts[item], target, 0, source.shape[-1])
        if step == n_chip:
            break
        for number in numbers:
            _, pair, way, _, columns = chains[number]
            for direction in range(2):
                place = bound_for(direction, step)

                @pl.when(passes(direction, step) & inner[direction])
                def _():
                    way_copy(number, direction, step - 1, pair.at[place, :, columns]).wait_recv()
                    way[direction, step - 2, :, columns] = (
                        way[direction, step - 2, :, columns].astype(F32)
                        + pair[place, :, columns].astype(F32)
                    ).astype(BF16)

            for direction in range(2):
                place = bound_for(direction, step)

                @pl.when(passes(direction, step) & inner[direction])
                def _():
                    way_copy(number, direction, step, way.at[direction, step - 2, :, columns]).start()

                @pl.when(passes(direction, step) & jnp.logical_not(inner[direction]))
                def _():
                    way_copy(number, direction, step, pair.at[place, :, columns]).start()

    chain_firsts = []
    for number in numbers:
        _, pair, way, target, columns = chains[number]
        for direction in range(2):

            @pl.when(inner[direction])
            def _():
                way_copy(number, direction, n_chip - 1, pair.at[0, :, columns]).wait_recv()

        spread = spread_columns[number]
        target[spot, :, spread] = (
            pair[chip, :, columns].astype(F32)
            + way[0, n_chip - 2, :, columns].astype(F32)
            + way[1, n_chip - 2, :, columns].astype(F32)
        ).astype(BF16)
        firsts = side_pair(2 + number, target.at[spot, :, spread], target, spread)
        for copy in firsts:
            copy.start()
        chain_firsts.append(firsts)
    for number in numbers:
        target, spread = chains[number][3], spread_columns[number]
        side_seconds += side_pass(
            2 + number, chain_firsts[number], target, spread.start, spread.size
        )
    for copy in own:
        copy.wait()
    for copy in side_seconds:
        copy.wait()
    for firsts in side_firsts + chain_firsts:
        for copy in firsts:
            copy.wait_send()
    for number in numbers:
        _, pair, _, _, columns = chains[number]
        for place in range(n_chip):
            pair_copy(number, place).wait_send()
        for direction in range(2):
            for step in range(1, n_chip):

                @pl.when(passes(direction, step))
                def _():
                    way_copy(number, direction, step, pair.at[0, :, columns]).wait_send()


def tail_round(n_ctx, hidden, both, up, attn):
    n_chip = n_ctx // 2
    dma = pltpu.SemaphoreType.DMA
    vmem = pl.BlockSpec(memory_space=pltpu.VMEM)
    wide = (up.shape[1], hidden)
    shapes = (wide, wide, attn.shape[1:])
    return pl.pallas_call(
        functools.partial(tail_kernel, n_ctx),
        name="tail_round",
        out_shape=[jax.ShapeDtypeStruct((4, *shape), BF16) for shape in shapes],
        in_specs=[vmem] * 3,
        out_specs=[vmem] * 3,
        scratch_shapes=[
            pltpu.VMEM((n_chip, *up.shape[1:]), BF16),
            pltpu.VMEM((n_chip, *attn.shape[1:]), BF16),
            pltpu.VMEM((2, n_chip - 1, *up.shape[1:]), BF16),
            pltpu.VMEM((2, n_chip - 1, *attn.shape[1:]), BF16),
            dma((3, n_chip)),
            dma((3, n_chip)),
            dma((3, 2, n_chip - 1)),
            dma((3, 2, n_chip - 1)),
            dma((5, 4)),
            dma((5, 4)),
            dma((2,)),
        ],
        compiler_params=pltpu.CompilerParams(collective_id=8, has_side_effects=True),
    )(both, up, attn)


def gathered(shard):
    return lax.all_gather(shard, "ctx", axis=0, tiled=True)


def scattered(whole):
    return lax.psum_scatter(whole, "ctx", scatter_dimension=0, tiled=True)


def local(
    n_batch,
    n_ctx,
    block_in,
    positions,
    counts,
    cotangent,
    gain_input,
    w_query,
    w_key,
    w_value,
    gain_query,
    gain_key,
    w_output,
    gain_attn,
    gain_ffn,
    w_gate,
    w_up,
    w_down,
    gain_final,
):
    block_in = block_in[0]
    positions = positions[0]
    cotangent = cotangent[0]
    tok_count, model_width = block_in.shape
    width_shard = w_query.shape[0]
    query_width = w_query.shape[1]
    head_size = w_key.shape[1]
    head_count = query_width // head_size
    hidden_shard = w_down.shape[0]
    piece = hidden_shard // n_batch
    hidden_part = -(-piece * n_ctx // 128) * 128
    padded = hidden_part // n_ctx
    halo_depth = (WINDOW + tok_count - 2) // tok_count
    assert halo_depth == 4
    batch_at = lax.axis_index("batch")
    ctx_at = lax.axis_index("ctx")
    all_tok = n_batch * tok_count

    gains = jnp.concatenate(
        [gain_input, gain_attn, gain_ffn, gain_final, gain_query, gain_key]
    )
    slots_of = query_width + 2 * head_size
    quarter = slots_of // n_batch
    qkv_full, proj_full, gains_all = gather_weights(
        n_batch,
        n_ctx,
        jnp.concatenate([w_query, w_key, w_value], axis=1)
        .reshape(width_shard, n_batch, quarter)
        .transpose(1, 0, 2),
        w_output.reshape(n_batch, -1, model_width),
        gains[None],
    )
    qkv_full = qkv_full.reshape(n_batch, model_width, quarter)
    full_output = proj_full.reshape(query_width, model_width)
    gains_all = gains_all[:, 0].astype(F32)

    def gain_at(start, length):
        return gains_all[:, start : start + length].reshape(1, -1)

    head_shard = gain_query.shape[0]
    full_gain_in = gain_at(0, width_shard)
    full_gain_attn = gain_at(width_shard, width_shard)
    full_gain_ffn = gain_at(2 * width_shard, width_shard)
    full_gain_final = gain_at(3 * width_shard, width_shard)
    full_gain_q = gain_at(4 * width_shard, head_shard)
    full_gain_k = gain_at(4 * width_shard + head_shard, head_shard)

    part_both = gathered(pick_columns(n_batch, n_ctx, piece, padded, w_gate, w_up))
    own_down = lax.dynamic_slice_in_dim(w_down, batch_at * piece, piece, 0)
    part_down = gathered(jnp.pad(own_down, ((0, padded - piece), (0, 0))))

    first_token = ctx_at * tok_count
    token_place = first_token + jnp.arange(tok_count, dtype=jnp.int32)
    valid_mask = (token_place < counts[0]).astype(F32)[:, None]
    resid_in = block_in.astype(F32)
    act_in = normed(resid_in, full_gain_in).astype(BF16)
    qkv_raw = jnp.concatenate([project(act_in, qkv_full[i]) for i in range(n_batch)], axis=1)
    query_raw = qkv_raw[:, :query_width].reshape(tok_count, head_count, head_size)
    key_raw = qkv_raw[:, query_width : query_width + head_size]
    value_low = qkv_raw[:, query_width + head_size :].astype(BF16)
    inv_freq = BASE ** (-jnp.arange(0, head_size, 2, dtype=F32) / head_size)
    angles = positions.astype(F32)[:, None] * inv_freq

    def query_path(raw_query, gain_vec):
        return rotate(normed(raw_query, gain_vec), angles[:, None, :])

    def key_path(raw_key, gain_vec):
        return rotate(normed(raw_key, gain_vec), angles)

    query_rot = query_path(query_raw, full_gain_q).astype(BF16)
    key_rot = key_path(key_raw, full_gain_k).astype(BF16)
    own_pair = jnp.concatenate([key_rot, value_low], axis=-1)
    halo = halo_out(n_ctx, own_pair)
    context = jnp.concatenate([halo.reshape(halo_depth * tok_count, -1), own_pair], axis=0)
    ctx_keys = context[:, :head_size]
    ctx_values = context[:, head_size:]
    key_total = (halo_depth + 1) * tok_count
    distance = (
        jnp.arange(tok_count, dtype=jnp.int32)[:, None]
        + halo_depth * tok_count
        - jnp.arange(key_total, dtype=jnp.int32)[None, :]
    )
    allowed = (distance >= 0) & (distance < WINDOW) & (distance <= positions[:, None])
    score_scale = head_size ** (-0.5)
    raw_scores = jnp.einsum("thd,kd->htk", query_rot, ctx_keys, preferred_element_type=F32)
    scores = jnp.where(allowed[None], raw_scores * score_scale, MASKED)
    exp_scores = jnp.exp(scores - jnp.max(scores, axis=-1, keepdims=True))
    attn_prob = exp_scores / jnp.sum(exp_scores, axis=-1, keepdims=True)
    prob_low = attn_prob.astype(BF16)
    attended = jnp.einsum("htk,kd->thd", prob_low, ctx_values, preferred_element_type=F32)
    attn_low = attended.reshape(tok_count, query_width).astype(BF16)
    attn_proj = project(attn_low, full_output)
    middle = resid_in + normed(attn_proj, full_gain_attn)
    ffn_in = normed(middle, full_gain_ffn).astype(BF16)

    (ffn_in_all,) = square_gather(2, ffn_in)
    ffn_in_all = ffn_in_all.reshape(all_tok, model_width)
    gate_pre, up_pre, mixed_low, mixed_turned = hidden_mix(256, ffn_in_all, part_both)
    mixed_low, act_in_late, attn_late = lax.optimization_barrier((mixed_low, act_in, attn_low))
    act_in_all, attn_all = square_gather(13, act_in_late, attn_late)
    ffn_in_turned = ffn_in_all.T
    mixed_low, act_in_all, attn_all, mixed_turned, ffn_in_turned = lax.optimization_barrier(
        (mixed_low, act_in_all, attn_all, mixed_turned, ffn_in_turned)
    )
    act_in_all = act_in_all.reshape(all_tok, model_width)
    attn_all = attn_all.reshape(all_tok, query_width)
    block_out, grad_ffn_low, grad_gain_final = turn_round(
        mixed_low, part_down, middle, cotangent, valid_mask, full_gain_final
    )

    grad_final = cotangent.astype(F32) * valid_mask
    grad_ffn_low = grad_ffn_low.reshape(all_tok, model_width)
    down_grad = product_low(384, mixed_turned, grad_ffn_low)
    down_grad, grad_ffn_low = lax.optimization_barrier((down_grad, grad_ffn_low))
    grad_w_down = scattered(down_grad)
    grad_gate_low, grad_up_low, back_part = hidden_back(
        256, grad_ffn_low, part_down, gate_pre, up_pre, part_both
    )
    grad_ffn_in, both_grad = sum_back(
        256,
        back_part.reshape(n_batch, tok_count, model_width),
        ffn_in_turned,
        grad_gate_low,
        grad_up_low,
        UP_FIRST,
    )
    grad_w_both = scattered(both_grad)
    _, pull_ffn_norm = jax.vjp(normed, middle, full_gain_ffn)
    grad_middle_part, grad_gain_ffn = pull_ffn_norm(grad_ffn_in)
    grad_middle = grad_final + grad_middle_part
    _, pull_attn_norm = jax.vjp(normed, attn_proj, full_gain_attn)
    grad_attn_proj, grad_gain_attn = pull_attn_norm(grad_middle)

    grad_proj_low = grad_attn_proj.astype(BF16)
    grad_attended = (
        project_back(grad_proj_low, full_output)
        .astype(BF16)
        .reshape(tok_count, head_count, head_size)
    )
    grad_prob = jnp.einsum("thd,kd->htk", grad_attended, ctx_values, preferred_element_type=F32)
    row_delta = jnp.sum(attn_prob * grad_prob, axis=-1, keepdims=True)
    grad_scores = (attn_prob * (grad_prob - row_delta)).astype(BF16)
    grad_queries = (
        jnp.einsum("htk,kd->thd", grad_scores, ctx_keys, preferred_element_type=F32) * score_scale
    )
    grad_ctx_keys = (
        jnp.einsum("htk,thd->kd", grad_scores, query_rot, preferred_element_type=F32) * score_scale
    )
    grad_ctx_values = jnp.einsum("htk,thd->kd", prob_low, grad_attended, preferred_element_type=F32)
    grad_context = jnp.concatenate([grad_ctx_keys, grad_ctx_values], axis=-1)
    halo_rows = halo_depth * tok_count
    returned, down_all, up_grad = halo_back(
        256,
        n_ctx,
        grad_context[:halo_rows].astype(BF16).reshape(halo_depth, tok_count, 2 * head_size),
        grad_w_down,
        ffn_in_turned,
        grad_up_low,
        hidden_part - UP_FIRST,
    )
    own_grad = grad_context[halo_rows:] + returned
    grad_value_low = own_grad[:, head_size:].astype(BF16)
    _, pull_key = jax.vjp(key_path, key_raw, full_gain_k)
    grad_key_raw, grad_gain_key = pull_key(own_grad[:, :head_size])
    _, pull_query = jax.vjp(query_path, query_raw, full_gain_q)
    grad_query_raw, grad_gain_query = pull_query(grad_queries)
    grad_qkv_low = jnp.concatenate(
        [
            grad_query_raw.astype(BF16).reshape(tok_count, query_width),
            grad_key_raw.astype(BF16),
            grad_value_low,
        ],
        axis=1,
    )
    grad_act_in = sum(
        project_back(grad_qkv_low[:, i * quarter : (i + 1) * quarter], qkv_full[i])
        for i in range(n_batch)
    )
    _, pull_input = jax.vjp(normed, resid_in, full_gain_in)
    grad_in_part, grad_gain_input = pull_input(grad_act_in)
    grad_in = (grad_middle + grad_in_part).astype(BF16)

    def column_slots(upstream):
        return upstream.reshape(tok_count, n_batch, -1).transpose(1, 0, 2)

    gain_rows = jnp.concatenate(
        [
            grad.reshape(n_ctx, -1)
            for grad in (
                grad_gain_input,
                grad_gain_attn,
                grad_gain_ffn,
                grad_gain_final,
                grad_gain_query,
                grad_gain_key,
            )
        ],
        axis=1,
    )
    gain_parts, qkv_slots, proj_slots = batch_exchange(
        7,
        n_batch,
        whole=(gain_rows,),
        slots=(column_slots(grad_qkv_low), column_slots(grad_proj_low)),
    )
    proj_rows = w_output.shape[0]
    gain_count = gain_rows.shape[1]
    gain_lines = -(-gain_count // quarter)
    used = width_shard + proj_rows + gain_lines
    lines = -(-used // 16) * 16
    grad_w_output = weight_grad(attn_all, proj_slots.reshape(all_tok, -1)).astype(BF16)
    grad_w_qkv = weight_grad(act_in_all, qkv_slots.reshape(all_tok, -1)).astype(BF16)
    output_part = model_width // n_batch
    gain_sum = jnp.sum(gain_parts, axis=0).astype(BF16)
    packed = jnp.concatenate(
        [
            grad_w_qkv.reshape(n_ctx, width_shard, quarter),
            jnp.pad(
                grad_w_output.reshape(n_ctx, proj_rows, output_part),
                ((0, 0), (0, 0), (0, quarter - output_part)),
            ),
            jnp.pad(gain_sum, ((0, 0), (0, gain_lines * quarter - gain_count))).reshape(
                n_ctx, gain_lines, quarter
            ),
            jnp.zeros((n_ctx, lines - used, quarter), BF16),
        ],
        axis=1,
    )
    gate_all, up_all, attn_grads = tail_round(
        n_ctx,
        hidden_part,
        grad_w_both,
        up_grad.reshape(n_ctx, width_shard, hidden_part - UP_FIRST),
        packed,
    )
    shapes = (
        (width_shard, w_gate.shape[1]),
        (width_shard, w_gate.shape[1]),
        (hidden_shard, model_width),
        (width_shard, query_width),
        (width_shard, head_size),
        (width_shard, head_size),
        (proj_rows, model_width),
        (gain_lines, quarter),
    )
    (
        grad_gate_shard,
        grad_up_shard,
        grad_down_shard,
        grad_query_shard,
        grad_key_shard,
        grad_value_shard,
        grad_output_shard,
        gain_block,
    ) = finish_round(
        n_batch, n_ctx, piece, padded, output_part, gate_all, up_all, down_all, attn_grads, shapes
    )
    gain_mine = gain_block.reshape(-1)

    return (
        block_out[None],
        grad_in[None],
        gain_mine[:width_shard],
        grad_query_shard,
        grad_key_shard,
        grad_value_shard,
        gain_mine[4 * width_shard : 4 * width_shard + head_shard],
        gain_mine[4 * width_shard + head_shard : gain_count],
        grad_output_shard,
        gain_mine[width_shard : 2 * width_shard],
        gain_mine[2 * width_shard : 3 * width_shard],
        grad_gate_shard,
        grad_up_shard,
        grad_down_shard,
        gain_mine[3 * width_shard : 4 * width_shard],
    )


def solution(mesh):
    matrix = P("ctx", None)
    vector = P("ctx")
    tokens = P("batch", "ctx", None)

    def step(*arrays):
        return local(mesh.shape["batch"], mesh.shape["ctx"], *arrays)

    return jax.shard_map(
        step,
        mesh=mesh,
        in_specs=(
            tokens,
            P("batch", "ctx"),
            P("batch"),
            tokens,
            vector,
            matrix,
            matrix,
            matrix,
            vector,
            vector,
            matrix,
            vector,
            vector,
            matrix,
            matrix,
            matrix,
            vector,
        ),
        out_specs=(
            tokens,
            tokens,
            vector,
            matrix,
            matrix,
            matrix,
            vector,
            vector,
            matrix,
            vector,
            vector,
            matrix,
            matrix,
            matrix,
            vector,
        ),
        check_vma=False,
    )
```

```python
import functools

import jax
import jax.numpy as jnp
from jax import lax
from jax.experimental import pallas as pl
from jax.experimental.pallas import tpu as pltpu
from jax.sharding import PartitionSpec as P

WINDOW = 512
UP_FIRST = 256


EPS = 1e-06
BASE = 10000.0
MASKED = -1e30
BF16 = jnp.bfloat16
F32 = jnp.float32
MESH = pl.DeviceIdType.MESH


def normed(vector, gain_vec):
    return vector * lax.rsqrt(jnp.mean(vector * vector, axis=-1, keepdims=True) + EPS) * gain_vec


def rotate(vector, angles):
    half_size = vector.shape[-1] // 2
    cosine = jnp.cos(angles)
    sine_part = jnp.sin(angles)
    first_half = vector[..., :half_size]
    second = vector[..., half_size:]
    return jnp.concatenate(
        [first_half * cosine - second * sine_part, second * cosine + first_half * sine_part],
        axis=-1,
    )


def project(inputs, weight):
    return lax.dot_general(inputs, weight, (((1,), (0,)), ((), ())), preferred_element_type=F32)


def project_back(upstream, weight):
    return lax.dot_general(upstream, weight, (((1,), (1,)), ((), ())), preferred_element_type=F32)


def weight_grad(inputs, upstream):
    return lax.dot_general(inputs, upstream, (((0,), (0,)), ((), ())), preferred_element_type=F32)


def gated_gelu(gate_val, up_val):
    return jax.nn.gelu(gate_val, approximate=True) * up_val


def batch_kernel(size, kinds, *refs):
    count = len(kinds)
    sources, results = refs[:count], refs[count : 2 * count]
    send_sem, recv_sem, own_sem = refs[2 * count :]
    me = lax.axis_index("batch")
    barrier = pltpu.get_barrier_semaphore()
    for step in range(1, size):
        pl.semaphore_signal(
            barrier, inc=1, device_id={"batch": lax.rem(me + step, size)}, device_id_type=MESH
        )
    pl.semaphore_wait(barrier, size - 1)
    copies = []
    for step in range(1, size):
        peer = lax.rem(me + step, size)
        for item in range(count):
            source = sources[item].at[peer] if kinds[item] else sources[item]
            copies.append(
                pltpu.make_async_remote_copy(
                    src_ref=source,
                    dst_ref=results[item].at[me],
                    send_sem=send_sem.at[item, step - 1],
                    recv_sem=recv_sem.at[item, step - 1],
                    device_id={"batch": peer},
                    device_id_type=MESH,
                )
            )
    for copy in copies:
        copy.start()
    own = []
    for item in range(count):
        source = sources[item].at[me] if kinds[item] else sources[item]
        own.append(pltpu.make_async_copy(source, results[item].at[me], own_sem.at[item]))
    for copy in own:
        copy.start()
    for copy in own:
        copy.wait()
    for copy in copies:
        copy.wait()


def batch_exchange(collective_id, size, whole=(), slots=()):
    arrays = list(whole) + list(slots)
    kinds = [0] * len(whole) + [1] * len(slots)
    count = len(arrays)
    shapes = [
        jax.ShapeDtypeStruct(a.shape if k else (size, *a.shape), a.dtype)
        for a, k in zip(arrays, kinds)
    ]
    return pl.pallas_call(
        functools.partial(batch_kernel, size, kinds),
        out_shape=shapes,
        in_specs=[pl.BlockSpec(memory_space=pltpu.VMEM)] * count,
        out_specs=[pl.BlockSpec(memory_space=pltpu.VMEM)] * count,
        scratch_shapes=[
            pltpu.SemaphoreType.DMA((count, size - 1)),
            pltpu.SemaphoreType.DMA((count, size - 1)),
            pltpu.SemaphoreType.DMA((count,)),
        ],
        compiler_params=pltpu.CompilerParams(collective_id=collective_id, has_side_effects=True),
    )(*arrays)


def square_kernel(count, *refs):
    sources, results = refs[:count], refs[count : 2 * count]
    send_sem, recv_sem, own_sem = refs[2 * count :]
    me = lax.axis_index("batch")
    across = me + 1 - 2 * lax.rem(me, 2)
    along = lax.rem(me + 2, 4)
    barrier = pltpu.get_barrier_semaphore()
    for peer in (across, along):
        pl.semaphore_signal(barrier, inc=1, device_id={"batch": peer}, device_id_type=MESH)
    pl.semaphore_wait(barrier, 2)

    def remote(source, target, item, turn, peer):
        copy = pltpu.make_async_remote_copy(
            src_ref=source,
            dst_ref=target,
            send_sem=send_sem.at[item, turn],
            recv_sem=recv_sem.at[item, turn],
            device_id={"batch": peer},
            device_id_type=MESH,
        )
        copy.start()
        return copy

    firsts = [
        [
            remote(sources[item], results[item].at[me], item, turn, peer)
            for turn, peer in enumerate((across, along))
        ]
        for item in range(count)
    ]
    own = [
        pltpu.make_async_copy(sources[item], results[item].at[me], own_sem.at[item])
        for item in range(count)
    ]
    for copy in own:
        copy.start()
    seconds = []
    for item in range(count):
        columns = sources[item].shape[-1]
        cut = columns // 256 * 128
        halves = (pl.ds(0, cut), pl.ds(cut, columns - cut))
        for turn, (giver, taker) in enumerate(((across, along), (along, across))):
            firsts[item][turn].wait_recv()
            block = results[item].at[giver, :, halves[turn]]
            seconds.append(remote(block, block, item, 2 + turn, taker))
    for copy in own:
        copy.wait()
    for copy in seconds:
        copy.wait()
    for pair in firsts:
        for copy in pair:
            copy.wait_send()


def square_gather(collective_id, *arrays):
    count = len(arrays)
    return pl.pallas_call(
        functools.partial(square_kernel, count),
        out_shape=[jax.ShapeDtypeStruct((4, *a.shape), a.dtype) for a in arrays],
        in_specs=[pl.BlockSpec(memory_space=pltpu.VMEM)] * count,
        out_specs=[pl.BlockSpec(memory_space=pltpu.VMEM)] * count,
        scratch_shapes=[
            pltpu.SemaphoreType.DMA((count, 4)),
            pltpu.SemaphoreType.DMA((count, 4)),
            pltpu.SemaphoreType.DMA((count,)),
        ],
        compiler_params=pltpu.CompilerParams(collective_id=collective_id, has_side_effects=True),
    )(*arrays)


def turn_kernel(
    mixed_ref,
    down_ref,
    middle_ref,
    upstream_ref,
    valid_ref,
    gain_ref,
    out_ref,
    grads_ref,
    gain_grad_ref,
    part_ref,
    taken_ref,
    send_sem,
    recv_sem,
    pass_sem,
    take_sem,
):
    me = lax.axis_index("batch")
    across = me + 1 - 2 * lax.rem(me, 2)
    along = lax.rem(me + 2, 4)
    corner = lax.rem(across + 2, 4)
    order = (corner, across, along)
    tok_count = middle_ref.shape[0]
    barrier = pltpu.get_barrier_semaphore()
    for peer in order:
        pl.semaphore_signal(barrier, inc=1, device_id={"batch": peer}, device_id_type=MESH)
    pl.semaphore_wait(barrier, 3)

    columns = grads_ref.shape[-1]
    cut = columns // 256 * 128
    halves = (pl.ds(0, cut), pl.ds(cut, columns - cut))

    def product(place, stretch):
        rows = pl.ds(pl.multiple_of(place * tok_count, tok_count), tok_count)
        return jnp.dot(mixed_ref[rows, :], down_ref[:, stretch], preferred_element_type=F32)

    copies = [
        pltpu.make_async_remote_copy(
            src_ref=part_ref.at[turn, :, stretch],
            dst_ref=taken_ref.at[turn, :, stretch],
            send_sem=send_sem.at[turn, half],
            recv_sem=recv_sem.at[turn, half],
            device_id={"batch": peer},
            device_id_type=MESH,
        )
        for turn, peer in enumerate(order)
        for half, stretch in enumerate(halves)
    ]
    for index in range(len(copies)):
        turn, stretch = index // 2, halves[index % 2]
        part_ref[turn, :, stretch] = product(order[turn], stretch).astype(BF16)
        if index > 0:
            copies[index - 1].start()
    total = product(me, pl.ds(0, columns))
    copies[-1].start()
    for turn in range(3):
        for copy in copies[2 * turn : 2 * turn + 2]:
            copy.wait_recv()
        total = total + taken_ref[turn].astype(F32)
    gain = gain_ref[...]
    valid = valid_ref[...]
    scale = lax.rsqrt(jnp.mean(total * total, axis=-1, keepdims=True) + EPS)
    upstream = upstream_ref[...].astype(F32) * valid
    gained = upstream * gain
    back = scale * gained - total * (
        scale * scale * scale * jnp.mean(total * gained, axis=-1, keepdims=True)
    )
    grads_ref[me] = back.astype(BF16)
    unit = total * scale
    out_ref[...] = ((middle_ref[...] + unit * gain) * valid).astype(BF16)
    gain_grad_ref[...] = jnp.sum(upstream * unit, axis=0, keepdims=True)

    def remote(block, turn, peer):
        copy = pltpu.make_async_remote_copy(
            src_ref=block,
            dst_ref=block,
            send_sem=pass_sem.at[turn],
            recv_sem=take_sem.at[turn],
            device_id={"batch": peer},
            device_id_type=MESH,
        )
        copy.start()
        return copy

    firsts = [remote(grads_ref.at[me], turn, peer) for turn, peer in enumerate((across, along))]
    seconds = []
    for turn, (giver, taker) in enumerate(((across, along), (along, across))):
        firsts[turn].wait_recv()
        seconds.append(remote(grads_ref.at[giver, :, halves[turn]], 2 + turn, taker))
    for copy in seconds:
        copy.wait()
    for copy in firsts + copies:
        copy.wait_send()


def turn_round(mixed, down, middle, upstream, valid, gain):
    tok_count, width = middle.shape
    dma = pltpu.SemaphoreType.DMA
    vmem = pl.BlockSpec(memory_space=pltpu.VMEM)
    flops = 2 * mixed.shape[0] * mixed.shape[1] * width
    return pl.pallas_call(
        turn_kernel,
        name="turn_round",
        out_shape=(
            jax.ShapeDtypeStruct((tok_count, width), BF16),
            jax.ShapeDtypeStruct((4, tok_count, width), BF16),
            jax.ShapeDtypeStruct((1, width), F32),
        ),
        in_specs=[vmem] * 6,
        out_specs=[vmem] * 3,
        scratch_shapes=[
            pltpu.VMEM((3, tok_count, width), BF16),
            pltpu.VMEM((3, tok_count, width), BF16),
            dma((3, 2)),
            dma((3, 2)),
            dma((4,)),
            dma((4,)),
        ],
        cost_estimate=pl.CostEstimate(flops=flops, bytes_accessed=8 << 20, transcendentals=0),
        compiler_params=pltpu.CompilerParams(collective_id=3, has_side_effects=True),
    )(mixed, down, middle, upstream, valid, gain)


def product_kernel(left_ref, right_ref, out_ref):
    out_ref[...] = jnp.dot(left_ref[...], right_ref[...], preferred_element_type=F32).astype(BF16)


def product_low(tile, left, right):
    rows, depth = left.shape
    columns = right.shape[1]
    return pl.pallas_call(
        product_kernel,
        grid=(columns // tile,),
        out_shape=jax.ShapeDtypeStruct((rows, columns), BF16),
        in_specs=[
            pl.BlockSpec((rows, depth), lambda i: (0, 0)),
            pl.BlockSpec((depth, tile), lambda i: (0, i)),
        ],
        out_specs=pl.BlockSpec((rows, tile), lambda i: (0, i)),
        cost_estimate=pl.CostEstimate(
            flops=2 * rows * depth * columns, bytes_accessed=8 << 20, transcendentals=0
        ),
    )(left, right)


def mix_kernel(tokens_ref, w_gate_ref, w_up_ref, gate_ref, up_ref, mixed_ref, turned_ref):
    gate = project(tokens_ref[...], w_gate_ref[...])
    up = project(tokens_ref[...], w_up_ref[...])
    gate_ref[...] = gate
    up_ref[...] = up
    mixed = gated_gelu(gate, up)
    mixed_ref[...] = mixed.astype(BF16)
    turned_ref[...] = mixed.T.astype(BF16)


def hidden_mix(tile, tokens, both_weights):
    count, width = tokens.shape
    hidden = both_weights.shape[1] // 2
    steps = hidden // tile
    wide = jax.ShapeDtypeStruct((count, hidden), F32)
    column = pl.BlockSpec((count, tile), lambda i: (0, i))
    return pl.pallas_call(
        mix_kernel,
        name="hidden_mix",
        grid=(steps,),
        out_shape=(
            wide,
            wide,
            jax.ShapeDtypeStruct((count, hidden), BF16),
            jax.ShapeDtypeStruct((hidden, count), BF16),
        ),
        in_specs=[
            pl.BlockSpec((count, width), lambda i: (0, 0)),
            pl.BlockSpec((width, tile), lambda i: (0, i)),
            pl.BlockSpec((width, tile), lambda i: (0, i + steps)),
        ],
        out_specs=[column, column, column, pl.BlockSpec((tile, count), lambda i: (i, 0))],
        cost_estimate=pl.CostEstimate(
            flops=4 * count * hidden * width, bytes_accessed=24 << 20, transcendentals=0
        ),
    )(tokens, both_weights, both_weights)


def back_kernel(
    upstream_ref, down_ref, gate_ref, up_ref, w_gate_ref, w_up_ref, gate_out, up_out, back_ref, total
):
    step = pl.program_id(0)
    grad_mixed = project_back(upstream_ref[...], down_ref[...])
    _, pull_gelu = jax.vjp(gated_gelu, gate_ref[...], up_ref[...])
    grad_gate, grad_up = pull_gelu(grad_mixed)
    grad_gate, grad_up = grad_gate.astype(BF16), grad_up.astype(BF16)
    gate_out[...] = grad_gate
    up_out[...] = grad_up
    part = project_back(grad_gate, w_gate_ref[...]) + project_back(grad_up, w_up_ref[...])

    @pl.when(step == 0)
    def _():
        total[...] = part

    @pl.when(step > 0)
    def _():
        total[...] += part

    @pl.when(step == pl.num_programs(0) - 1)
    def _():
        back_ref[...] = total[...].astype(BF16)


def hidden_back(tile, upstream, down, gate_pre, up_pre, both_weights):
    tokens, width = upstream.shape
    hidden = down.shape[0]
    count = hidden // tile
    low = jax.ShapeDtypeStruct((tokens, hidden), BF16)
    return pl.pallas_call(
        back_kernel,
        name="hidden_back",
        grid=(count,),
        out_shape=(low, low, jax.ShapeDtypeStruct((tokens, width), BF16)),
        in_specs=[
            pl.BlockSpec((tokens, width), lambda i: (0, 0)),
            pl.BlockSpec((tile, width), lambda i: (i, 0)),
            pl.BlockSpec((tokens, tile), lambda i: (0, i)),
            pl.BlockSpec((tokens, tile), lambda i: (0, i)),
            pl.BlockSpec((width, tile), lambda i: (0, i)),
            pl.BlockSpec((width, tile), lambda i: (0, i + count)),
        ],
        out_specs=[
            pl.BlockSpec((tokens, tile), lambda i: (0, i)),
            pl.BlockSpec((tokens, tile), lambda i: (0, i)),
            pl.BlockSpec((tokens, width), lambda i: (0, 0)),
        ],
        scratch_shapes=[pltpu.VMEM((tokens, width), F32)],
        cost_estimate=pl.CostEstimate(
            flops=6 * tokens * hidden * width, bytes_accessed=24 << 20, transcendentals=0
        ),
    )(upstream, down, gate_pre, up_pre, both_weights, both_weights)


def multiply_tiles(tile, first, last, left, right, out, target, sems):
    def step(index, carry):
        columns = pl.ds(pl.multiple_of(index * tile, tile), tile)
        out[:, columns] = jnp.dot(
            left[...], right[:, columns], preferred_element_type=F32
        ).astype(BF16)
        pltpu.make_async_copy(out.at[:, columns], target.at[:, columns], sems.at[index]).start()
        return carry

    lax.fori_loop(first, last, step, 0)


def await_tiles(tile, count, out, target, sems):
    for index in range(count):
        columns = pl.ds(index * tile, tile)
        pltpu.make_async_copy(out.at[:, columns], target.at[:, columns], sems.at[index]).wait()


def sum_back_kernel(
    tile,
    slots_ref,
    left_ref,
    gate_ref,
    up_ref,
    sum_ref,
    both_ref,
    left,
    right,
    both,
    taken_ref,
    send_sem,
    recv_sem,
    load_sem,
    store_sem,
):
    me = lax.axis_index("batch")
    across = me + 1 - 2 * lax.rem(me, 2)
    along = lax.rem(me + 2, 4)
    order = (lax.rem(across + 2, 4), across, along)
    hidden = gate_ref.shape[1]
    width = right.shape[1]
    loads = [
        pltpu.make_async_copy(left_ref, left, load_sem.at[0]),
        pltpu.make_async_copy(gate_ref, right.at[:, pl.ds(0, hidden)], load_sem.at[1]),
        pltpu.make_async_copy(
            up_ref.at[:, pl.ds(0, width - hidden)],
            right.at[:, pl.ds(hidden, width - hidden)],
            load_sem.at[2],
        ),
    ]
    for load in loads:
        load.start()
    barrier = pltpu.get_barrier_semaphore()
    for peer in order:
        pl.semaphore_signal(barrier, inc=1, device_id={"batch": peer}, device_id_type=MESH)
    pl.semaphore_wait(barrier, 3)
    copies = [
        pltpu.make_async_remote_copy(
            src_ref=slots_ref.at[peer],
            dst_ref=taken_ref.at[turn],
            send_sem=send_sem.at[turn],
            recv_sem=recv_sem.at[turn],
            device_id={"batch": peer},
            device_id_type=MESH,
        )
        for turn, peer in enumerate(order)
    ]
    for copy in copies:
        copy.start()
    for load in loads:
        load.wait()
    multiply_tiles(tile, 0, width // tile, left, right, both, both_ref, store_sem)
    total = slots_ref[me].astype(F32)
    for turn in range(3):
        copies[turn].wait_recv()
        total = total + taken_ref[turn].astype(F32)
    sum_ref[...] = total
    for copy in copies:
        copy.wait_send()
    await_tiles(tile, width // tile, both, both_ref, store_sem)


def sum_back(tile, slots, left, gate, up, columns):
    rows, depth = left.shape
    width = gate.shape[1] + columns
    dma = pltpu.SemaphoreType.DMA
    vmem = pl.BlockSpec(memory_space=pltpu.VMEM)
    anywhere = pl.BlockSpec(memory_space=pl.ANY)
    return pl.pallas_call(
        functools.partial(sum_back_kernel, tile),
        name="sum_back",
        out_shape=[
            jax.ShapeDtypeStruct(slots.shape[1:], F32),
            jax.ShapeDtypeStruct((rows, width), BF16),
        ],
        in_specs=[vmem, anywhere, anywhere, anywhere],
        out_specs=[vmem, anywhere],
        scratch_shapes=[
            pltpu.VMEM((rows, depth), BF16),
            pltpu.VMEM((depth, width), BF16),
            pltpu.VMEM((rows, width), BF16),
            pltpu.VMEM((3, *slots.shape[1:]), BF16),
            dma((3,)),
            dma((3,)),
            dma((3,)),
            dma((width // tile,)),
        ],
        cost_estimate=pl.CostEstimate(
            flops=2 * rows * depth * width, bytes_accessed=12 << 20, transcendentals=0
        ),
        compiler_params=pltpu.CompilerParams(collective_id=5, has_side_effects=True),
    )(slots, left, gate, up)


def halo_out_kernel(n_chip, source_ref, result_ref, send_sem, recv_sem):
    me = lax.axis_index("ctx")
    chip, core = me // 2, lax.rem(me, 2)
    near = {"ctx": me + 1 - 2 * core}
    after = {"ctx": jnp.minimum(me + 2, 2 * n_chip - 1)}
    has_after = chip < n_chip - 1
    barrier = pltpu.get_barrier_semaphore()
    pl.semaphore_signal(barrier, inc=1, device_id=near, device_id_type=MESH)

    @pl.when(chip > 0)
    def _():
        before = {"ctx": jnp.maximum(me - 2, 0)}
        pl.semaphore_signal(barrier, inc=1, device_id=before, device_id_type=MESH)

    pl.semaphore_wait(barrier, 1 + jnp.minimum(n_chip - 1 - chip, 1))

    def remote(source, slot, turn, peer):
        return pltpu.make_async_remote_copy(
            src_ref=source,
            dst_ref=result_ref.at[slot],
            send_sem=send_sem.at[turn],
            recv_sem=recv_sem.at[turn],
            device_id=peer,
            device_id_type=MESH,
        )

    one_on = remote(source_ref, 2, 0, after)
    two_on = remote(result_ref.at[2], 0, 1, after)
    own_near = remote(source_ref, 3, 2, near)
    before_near = remote(result_ref.at[2], 3 - 2 * (1 - core), 3, near)
    far_near = remote(result_ref.at[0], 1, 4, near)

    @pl.when(has_after)
    def _():
        one_on.start()

    @pl.when(core == 0)
    def _():
        own_near.start()

    def blank(slot):
        result_ref[slot] = jnp.zeros(result_ref.shape[1:], result_ref.dtype)

    @pl.when(chip == 0)
    def _():
        blank(2)
        blank(0)
        blank(1)

    @pl.when((chip == 0) & (core == 0))
    def _():
        blank(3)

    @pl.when(chip == 1)
    def _():
        blank(0)

    @pl.when((chip == 1) & (core == 0))
    def _():
        blank(1)

    @pl.when(chip > 0)
    def _():
        one_on.wait_recv()

    @pl.when((chip > 0) & has_after)
    def _():
        two_on.start()

    @pl.when(chip > 0)
    def _():
        before_near.start()

    @pl.when(chip > 1)
    def _():
        two_on.wait_recv()

    @pl.when((chip > 1) & (core == 1))
    def _():
        far_near.start()

    @pl.when(core == 1)
    def _():
        own_near.wait_recv()

    @pl.when(core == 0)
    def _():
        own_near.wait_send()

    @pl.when(chip > 0)
    def _():
        before_near.wait()

    @pl.when((chip > 1) & (core == 0))
    def _():
        far_near.wait_recv()

    @pl.when((chip > 1) & (core == 1))
    def _():
        far_near.wait_send()

    @pl.when(has_after)
    def _():
        one_on.wait_send()

    @pl.when((chip > 0) & has_after)
    def _():
        two_on.wait_send()


def halo_back_kernel(
    tile,
    n_chip,
    source_ref,
    shard_ref,
    left_ref,
    up_ref,
    result_ref,
    shards_ref,
    rest_ref,
    near_ref,
    far_ref,
    way_ref,
    left,
    right,
    rest,
    send_sem,
    recv_sem,
    pass_sem,
    take_sem,
    own_sem,
    store_sem,
):
    me = lax.axis_index("ctx")
    spot = lax.axis_index("batch")
    across = spot + 1 - 2 * lax.rem(spot, 2)
    along = lax.rem(spot + 2, 4)
    chip, core = me // 2, lax.rem(me, 2)
    near = {"ctx": me + 1 - 2 * core}
    before = {"ctx": jnp.maximum(me - 2, 0)}
    has_after = chip < n_chip - 1
    barrier = pltpu.get_barrier_semaphore()
    pl.semaphore_signal(barrier, inc=1, device_id=near, device_id_type=MESH)

    @pl.when(has_after)
    def _():
        after = {"ctx": jnp.minimum(me + 2, 2 * n_chip - 1)}
        pl.semaphore_signal(barrier, inc=1, device_id=after, device_id_type=MESH)

    for peer in (across, along):
        pl.semaphore_signal(barrier, inc=1, device_id={"batch": peer}, device_id_type=MESH)
    pl.semaphore_wait(barrier, 3 + jnp.minimum(chip, 1))

    def beside(source, target, turn, peer):
        copy = pltpu.make_async_remote_copy(
            src_ref=source,
            dst_ref=target,
            send_sem=pass_sem.at[turn],
            recv_sem=take_sem.at[turn],
            device_id={"batch": peer},
            device_id_type=MESH,
        )
        copy.start()
        return copy

    def remote(source, target, turn, peer):
        return pltpu.make_async_remote_copy(
            src_ref=source,
            dst_ref=target,
            send_sem=send_sem.at[turn],
            recv_sem=recv_sem.at[turn],
            device_id=peer,
            device_id_type=MESH,
        )

    to_before = remote(source_ref.at[3 - 2 * core], near_ref.at[0], 0, near)
    to_other = remote(source_ref.at[1 + 2 * core], near_ref.at[1], 1, near)
    to_before.start()
    to_other.start()
    width = right.shape[1]
    count = width // tile
    loads = [
        pltpu.make_async_copy(left_ref, left, own_sem.at[1]),
        pltpu.make_async_copy(
            up_ref.at[:, pl.ds(up_ref.shape[1] - width, width)], right, own_sem.at[2]
        ),
    ]
    for load in loads:
        load.start()
    firsts = [
        beside(shard_ref, shards_ref.at[spot], turn, peer)
        for turn, peer in enumerate((across, along))
    ]
    own = pltpu.make_async_copy(shard_ref, shards_ref.at[spot], own_sem.at[0])
    own.start()

    @pl.when((chip == 0) | jnp.logical_not(has_after))
    def _():
        way_ref[0] = jnp.zeros(way_ref.shape[1:], way_ref.dtype)

    @pl.when(jnp.logical_not(has_after))
    def _():
        way_ref[1] = jnp.zeros(way_ref.shape[1:], way_ref.dtype)

    to_other.wait_recv()
    theirs = near_ref[1].astype(F32)
    far_ref[0] = (source_ref[0].astype(F32) + jnp.where(core == 1, theirs, 0.0)).astype(BF16)
    two_back = remote(far_ref.at[0], way_ref.at[0], 2, before)
    one_back = remote(far_ref.at[1], way_ref.at[1], 3, before)

    @pl.when(chip > 1)
    def _():
        two_back.start()

    to_before.wait_recv()
    due = source_ref[2].astype(F32) + near_ref[0].astype(F32)

    for load in loads:
        load.wait()
    multiply_tiles(tile, 0, count // 3, left, right, rest, rest_ref, store_sem)

    @pl.when((chip > 0) & has_after)
    def _():
        two_back.wait_recv()

    far_ref[1] = (due + way_ref[0].astype(F32)).astype(BF16)

    @pl.when(chip > 0)
    def _():
        one_back.start()

    multiply_tiles(tile, count // 3, count, left, right, rest, rest_ref, store_sem)
    columns = shard_ref.shape[-1]
    cut = columns // 256 * 128
    halves = (pl.ds(0, cut), pl.ds(cut, columns - cut))
    seconds = []
    for turn, (giver, taker) in enumerate(((across, along), (along, across))):
        firsts[turn].wait_recv()
        block = shards_ref.at[giver, :, halves[turn]]
        seconds.append(beside(block, block, 2 + turn, taker))

    @pl.when(has_after)
    def _():
        one_back.wait_recv()

    result_ref[...] = way_ref[1].astype(F32) + jnp.where(core == 0, theirs, 0.0)
    own.wait()
    for copy in seconds:
        copy.wait()
    for copy in firsts + [to_before, to_other]:
        copy.wait_send()
    await_tiles(tile, count, rest, rest_ref, store_sem)

    @pl.when(chip > 1)
    def _():
        two_back.wait_send()

    @pl.when(chip > 0)
    def _():
        one_back.wait_send()


def halo_call(collective_id, kernel, arrays, in_vmem, out_shape, out_vmem, buffers, counts):
    dma = pltpu.SemaphoreType.DMA
    vmem = pl.BlockSpec(memory_space=pltpu.VMEM)
    anywhere = pl.BlockSpec(memory_space=pl.ANY)
    return pl.pallas_call(
        kernel,
        out_shape=out_shape,
        in_specs=[vmem if i < in_vmem else anywhere for i in range(len(arrays))],
        out_specs=[vmem if i < out_vmem else anywhere for i in range(len(out_shape))],
        scratch_shapes=[*buffers, *(dma((count,)) for count in counts)],
        compiler_params=pltpu.CompilerParams(collective_id=collective_id, has_side_effects=True),
    )(*arrays)


def halo_out(n_ctx, block):
    out_shape = [jax.ShapeDtypeStruct((4, *block.shape), block.dtype)]
    kernel = functools.partial(halo_out_kernel, n_ctx // 2)
    return halo_call(1, kernel, (block,), 1, out_shape, 1, (), (5, 5))[0]


def halo_back(tile, n_ctx, blocks, shard, left, up, columns):
    shape = blocks.shape[1:]
    rows, depth = left.shape
    buffers = [pltpu.VMEM((2, *shape), blocks.dtype)] * 3
    buffers += [
        pltpu.VMEM((rows, depth), BF16),
        pltpu.VMEM((depth, columns), BF16),
        pltpu.VMEM((rows, columns), BF16),
    ]
    out_shape = [
        jax.ShapeDtypeStruct(shape, F32),
        jax.ShapeDtypeStruct((4, *shard.shape), shard.dtype),
        jax.ShapeDtypeStruct((rows, columns), BF16),
    ]
    kernel = functools.partial(halo_back_kernel, tile, n_ctx // 2)
    arrays = (blocks, shard, left, up)
    counts = (4, 4, 4, 4, 3, columns // tile)
    return halo_call(6, kernel, arrays, 2, out_shape, 2, buffers, counts)


def pick_kernel(n_batch, n_ctx, piece, padded, gate_ref, up_ref, out_ref):
    me = lax.axis_index("batch")
    out_ref[...] = jnp.zeros_like(out_ref)
    for spot in range(n_batch):

        @pl.when(me == spot)
        def _():
            for shard in range(n_ctx):
                start = (shard * n_batch + spot) * piece
                for half, ref in enumerate((gate_ref, up_ref)):
                    place = (half * n_ctx + shard) * padded
                    out_ref[:, place : place + piece] = ref[:, start : start + piece]


def row_block(rows):
    return 48 if rows % 48 == 0 else rows


def pick_columns(n_batch, n_ctx, piece, padded, w_gate, w_up):
    rows, hidden = w_gate.shape
    block = row_block(rows)
    spec = pl.BlockSpec((block, hidden), lambda i: (i, 0))
    return pl.pallas_call(
        functools.partial(pick_kernel, n_batch, n_ctx, piece, padded),
        name="pick_columns",
        grid=(rows // block,),
        out_shape=jax.ShapeDtypeStruct((rows, 2 * n_ctx * padded), w_gate.dtype),
        in_specs=[spec, spec],
        out_specs=pl.BlockSpec((block, 2 * n_ctx * padded), lambda i: (i, 0)),
    )(w_gate, w_up)


def finish_kernel(n_batch, n_ctx, piece, padded, proj_part, gate_ref, up_ref, down_ref, attn_ref, *refs):
    outs, bufs, sems = refs[:8], refs[8:16], refs[16]
    gate_buf, up_buf, down_buf, query_buf, key_buf, value_buf, proj_buf, gain_buf = bufs
    copies = [pltpu.make_async_copy(bufs[i], outs[i], sems.at[i]) for i in range(8)]
    rows = gate_ref.shape[1]
    block = row_block(rows)

    for ref, buf, copy in ((gate_ref, gate_buf, copies[0]), (up_ref, up_buf, copies[1])):

        def place_rows(step, carry):
            lines = pl.ds(pl.multiple_of(step * block, block), block)
            for shard in range(n_ctx):
                for spot in range(n_batch):
                    start = (shard * n_batch + spot) * piece
                    place = shard * padded
                    buf[lines, start : start + piece] = ref[
                        spot, lines, place : place + piece
                    ].astype(F32)
            return carry

        lax.fori_loop(0, rows // block, place_rows, 0)
        copy.start()
    for spot in range(n_batch):
        down_buf[spot * piece : (spot + 1) * piece, :] = down_ref[spot, :piece, :].astype(F32)
    copies[2].start()
    quarter = attn_ref.shape[-1]
    proj_rows = proj_buf.shape[0]
    for spot in range(n_batch):
        for tile in range(0, quarter, 128):
            column = spot * quarter + tile
            for buf in (query_buf, key_buf, value_buf):
                if 0 <= column < buf.shape[-1]:
                    buf[:, column : column + 128] = attn_ref[
                        spot, :rows, tile : tile + 128
                    ].astype(F32)
                column -= buf.shape[-1]
        proj_buf[:, spot * proj_part : (spot + 1) * proj_part] = attn_ref[
            spot, rows : rows + proj_rows, :proj_part
        ].astype(F32)
    gain_buf[...] = attn_ref[0, rows + proj_rows : rows + proj_rows + gain_buf.shape[0], :].astype(F32)
    for copy in copies[3:]:
        copy.start()
    for copy in copies:
        copy.wait()


def finish_round(n_batch, n_ctx, piece, padded, proj_part, gate, up, down, attn, shapes):
    outs = [jax.ShapeDtypeStruct(shape, F32) for shape in shapes]
    return pl.pallas_call(
        functools.partial(finish_kernel, n_batch, n_ctx, piece, padded, proj_part),
        name="finish_round",
        out_shape=outs,
        in_specs=[pl.BlockSpec(memory_space=pltpu.VMEM)] * 4,
        out_specs=[pl.BlockSpec(memory_space=pl.ANY)] * 8,
        scratch_shapes=[pltpu.VMEM(shape, F32) for shape in shapes] + [pltpu.SemaphoreType.DMA((8,))],
    )(gate, up, down, attn)


def weights_kernel(n_batch, n_ctx, qkv_ref, proj_ref, gain_ref, qkv_all, proj_all, gain_all, *sems):
    send_far, recv_far, send_side, recv_side, send_near, recv_near, own_sem = sems
    spot = lax.axis_index("batch")
    me = lax.axis_index("ctx")
    n_chip = n_ctx // 2
    chip, core = me // 2, lax.rem(me, 2)
    near = {"ctx": me + 1 - 2 * core}
    barrier = pltpu.get_barrier_semaphore()

    def far_at(step):
        return {"ctx": 2 * lax.rem(chip + step, n_chip) + core}

    def side_at(step):
        return {"batch": lax.rem(spot + step, n_batch)}

    peers = [near]
    peers += [far_at(step) for step in range(1, n_chip)]
    peers += [side_at(step) for step in range(1, n_batch)]
    for peer in peers:
        pl.semaphore_signal(barrier, inc=1, device_id=peer, device_id_type=MESH)
    pl.semaphore_wait(barrier, len(peers))

    def remote(source, target, send, recv, peer):
        return pltpu.make_async_remote_copy(
            src_ref=source,
            dst_ref=target,
            send_sem=send,
            recv_sem=recv,
            device_id=peer,
            device_id_type=MESH,
        )

    waits = []
    far = []
    for step in range(1, n_chip):
        triple = [
            remote(source, target, send_far.at[step - 1, item], recv_far.at[step - 1, item], far_at(step))
            for item, (source, target) in enumerate(
                (
                    (qkv_ref.at[spot], qkv_all.at[spot, me]),
                    (proj_ref.at[spot], proj_all.at[me, spot]),
                    (gain_ref, gain_all.at[me]),
                )
            )
        ]
        for copy in triple:
            copy.start()
        far.append(triple)
    own = [
        pltpu.make_async_copy(qkv_ref, qkv_all.at[:, me], own_sem.at[0]),
        pltpu.make_async_copy(proj_ref, proj_all.at[me], own_sem.at[1]),
        pltpu.make_async_copy(gain_ref, gain_all.at[me], own_sem.at[2]),
    ]
    for copy in own:
        copy.start()
    first = n_chip - 1
    pairs = [
        remote(source, target, send_near.at[first, 0, item], recv_near.at[first, 0, item], near)
        for item, (source, target) in enumerate(
            (
                (qkv_ref, qkv_all.at[:, me]),
                (proj_ref, proj_all.at[me]),
                (gain_ref, gain_all.at[me]),
            )
        )
    ]
    for copy in pairs:
        copy.start()
    waits += pairs

    def hand_near(step, turn):
        origin = 2 * lax.rem(chip + n_chip - step, n_chip) + core
        quarter = lax.rem(spot + n_batch - turn, n_batch)
        blocks = [qkv_all.at[quarter, origin], proj_all.at[origin, quarter]]
        blocks += [gain_all.at[origin]] if turn == 0 else []
        for item, block in enumerate(blocks):
            copy = remote(
                block,
                block,
                send_near.at[step - 1, turn, item],
                recv_near.at[step - 1, turn, item],
                near,
            )
            copy.start()
            waits.append(copy)

    side = []
    for step in range(1, n_chip):
        for copy in far[step - 1]:
            copy.wait_recv()
        origin = 2 * lax.rem(chip + n_chip - step, n_chip) + core
        for turn in range(1, n_batch):
            pair = [
                remote(
                    block,
                    block,
                    send_side.at[step - 1, turn - 1, item],
                    recv_side.at[step - 1, turn - 1, item],
                    side_at(turn),
                )
                for item, block in enumerate((qkv_all.at[spot, origin], proj_all.at[origin, spot]))
            ]
            for copy in pair:
                copy.start()
            side.append((step, turn, pair))
        hand_near(step, 0)
    for step, turn, pair in side:
        for copy in pair:
            copy.wait_recv()
        hand_near(step, turn)
    for copy in waits:
        copy.wait()
    for copy in own:
        copy.wait()
    for triple in far:
        for copy in triple:
            copy.wait_send()
    for _, _, pair in side:
        for copy in pair:
            copy.wait_send()


def gather_weights(n_batch, n_ctx, qkv, proj, gains):
    n_chip = n_ctx // 2
    dma = pltpu.SemaphoreType.DMA
    vmem = pl.BlockSpec(memory_space=pltpu.VMEM)
    return pl.pallas_call(
        functools.partial(weights_kernel, n_batch, n_ctx),
        name="gather_weights",
        out_shape=(
            jax.ShapeDtypeStruct((n_batch, n_ctx, *qkv.shape[1:]), qkv.dtype),
            jax.ShapeDtypeStruct((n_ctx, *proj.shape), proj.dtype),
            jax.ShapeDtypeStruct((n_ctx, *gains.shape), gains.dtype),
        ),
        in_specs=[vmem] * 3,
        out_specs=[vmem] * 3,
        scratch_shapes=[
            dma((n_chip - 1, 3)),
            dma((n_chip - 1, 3)),
            dma((n_chip - 1, n_batch - 1, 2)),
            dma((n_chip - 1, n_batch - 1, 2)),
            dma((n_chip, n_batch, 3)),
            dma((n_chip, n_batch, 3)),
            dma((3,)),
        ],
        compiler_params=pltpu.CompilerParams(collective_id=12, has_side_effects=True),
    )(qkv, proj, gains)


def tail_kernel(
    n_ctx,
    both_ref,
    up_ref,
    attn_ref,
    gate_all,
    up_all,
    attn_all,
    pair_up,
    pair_attn,
    way_up,
    way_attn,
    pair_send,
    pair_recv,
    way_send,
    way_recv,
    side_send,
    side_recv,
    own_sem,
):
    n_chip = n_ctx // 2
    spot = lax.axis_index("batch")
    me = lax.axis_index("ctx")
    chip, core = me // 2, lax.rem(me, 2)
    across = {"batch": spot + 1 - 2 * lax.rem(spot, 2)}
    along = {"batch": lax.rem(spot + 2, 4)}
    near = {"ctx": me + 1 - 2 * core}
    beyond = ({"ctx": jnp.minimum(me + 2, n_ctx - 1)}, {"ctx": jnp.maximum(me - 2, 0)})
    inner = (chip > 0, chip < n_chip - 1)
    barrier = pltpu.get_barrier_semaphore()
    for peer in (near, across, along):
        pl.semaphore_signal(barrier, inc=1, device_id=peer, device_id_type=MESH)
    for has_giver, giver in zip(inner, (beyond[1], beyond[0])):

        @pl.when(has_giver)
        def _():
            pl.semaphore_signal(barrier, inc=1, device_id=giver, device_id_type=MESH)

    pl.semaphore_wait(barrier, 3 + jnp.minimum(chip, 1) + jnp.minimum(n_chip - 1 - chip, 1))

    def remote(source, target, send, recv, peer):
        return pltpu.make_async_remote_copy(
            src_ref=source,
            dst_ref=target,
            send_sem=send,
            recv_sem=recv,
            device_id=peer,
            device_id_type=MESH,
        )

    width = up_ref.shape[-1]
    cut = width // 256 * 128
    chains = (
        (up_ref, pair_up, way_up, up_all, pl.ds(0, cut)),
        (up_ref, pair_up, way_up, up_all, pl.ds(cut, width - cut)),
        (attn_ref, pair_attn, way_attn, attn_all, pl.ds(0, attn_ref.shape[-1])),
    )
    gate_width = gate_all.shape[-1]
    offset = both_ref.shape[-1] - gate_width
    spread_columns = (pl.ds(offset, cut), pl.ds(offset + cut, width - cut), chains[2][4])
    numbers = range(len(chains))

    def pair_copy(number, place):
        source, pair, _, _, columns = chains[number]
        return remote(
            source.at[2 * place + 1 - core, :, columns],
            pair.at[place, :, columns],
            pair_send.at[number, place],
            pair_recv.at[number, place],
            near,
        )

    def way_copy(number, direction, step, source):
        _, _, way, _, columns = chains[number]
        return remote(
            source,
            way.at[direction, step - 1, :, columns],
            way_send.at[number, direction, step - 1],
            way_recv.at[number, direction, step - 1],
            beyond[direction],
        )

    def passes(direction, step):
        return chip <= step - 1 if direction == 0 else chip >= n_chip - step

    def bound_for(direction, step):
        place = chip + n_chip - step if direction == 0 else chip - n_chip + step
        return jnp.clip(place, 0, n_chip - 1)

    def side_pair(item, sources, target, columns):
        return [
            remote(
                sources,
                target.at[spot, :, columns],
                side_send.at[item, turn],
                side_recv.at[item, turn],
                peer,
            )
            for turn, peer in enumerate((across, along))
        ]

    def side_pass(item, firsts, target, start, length):
        half = length // 256 * 128
        halves = (pl.ds(start, half), pl.ds(start + half, length - half))
        copies = []
        for turn, (giver, taker) in enumerate(((across, along), (along, across))):
            firsts[turn].wait_recv()
            block = target.at[giver["batch"], :, halves[turn]]
            copies.append(
                remote(block, block, side_send.at[item, 2 + turn], side_recv.at[item, 2 + turn], taker)
            )
            copies[-1].start()
        return copies

    for number in numbers:
        for place in range(n_chip):
            pair_copy(number, place).start()
    early = (
        (both_ref.at[:, pl.ds(0, gate_width)], gate_all),
        (both_ref.at[:, pl.ds(gate_width, offset)], up_all),
    )
    side_firsts = []
    for item, (source, target) in enumerate(early):
        side_firsts.append(side_pair(item, source, target, pl.ds(0, source.shape[-1])))
        for copy in side_firsts[-1]:
            copy.start()
    own = [
        pltpu.make_async_copy(
            source, target.at[spot, :, pl.ds(0, source.shape[-1])], own_sem.at[item]
        )
        for item, (source, target) in enumerate(early)
    ]
    for copy in own:
        copy.start()
    for _, _, way, _, columns in chains:
        for direction in range(2):

            @pl.when(jnp.logical_not(inner[direction]))
            def _():
                way[direction, n_chip - 2, :, columns] = jnp.zeros(
                    (way.shape[2], columns.size), way.dtype
                )

    for number in numbers:
        source, pair, _, _, columns = chains[number]
        for place in range(n_chip):
            pair_copy(number, place).wait_recv()
            pair[place, :, columns] = (
                pair[place, :, columns].astype(F32)
                + source[2 * place + core, :, columns].astype(F32)
            ).astype(BF16)
        for direction in range(2):

            @pl.when(passes(direction, 1))
            def _():
                place = bound_for(direction, 1)
                way_copy(number, direction, 1, pair.at[place, :, columns]).start()

    side_seconds = []
    for step in range(2, n_chip + 1):
        if step <= 3:
            item = step - 2
            source, target = early[item]
            side_seconds += side_pass(item, side_firsts[item], target, 0, source.shape[-1])
        if step == n_chip:
            break
        for number in numbers:
            _, pair, way, _, columns = chains[number]
            for direction in range(2):
                place = bound_for(direction, step)

                @pl.when(passes(direction, step) & inner[direction])
                def _():
                    way_copy(number, direction, step - 1, pair.at[place, :, columns]).wait_recv()
                    way[direction, step - 2, :, columns] = (
                        way[direction, step - 2, :, columns].astype(F32)
                        + pair[place, :, columns].astype(F32)
                    ).astype(BF16)

            for direction in range(2):
                place = bound_for(direction, step)

                @pl.when(passes(direction, step) & inner[direction])
                def _():
                    way_copy(number, direction, step, way.at[direction, step - 2, :, columns]).start()

                @pl.when(passes(direction, step) & jnp.logical_not(inner[direction]))
                def _():
                    way_copy(number, direction, step, pair.at[place, :, columns]).start()

    chain_firsts = []
    for number in numbers:
        _, pair, way, target, columns = chains[number]
        for direction in range(2):

            @pl.when(inner[direction])
            def _():
                way_copy(number, direction, n_chip - 1, pair.at[0, :, columns]).wait_recv()

        spread = spread_columns[number]
        target[spot, :, spread] = (
            pair[chip, :, columns].astype(F32)
            + way[0, n_chip - 2, :, columns].astype(F32)
            + way[1, n_chip - 2, :, columns].astype(F32)
        ).astype(BF16)
        firsts = side_pair(2 + number, target.at[spot, :, spread], target, spread)
        for copy in firsts:
            copy.start()
        chain_firsts.append(firsts)
    for number in numbers:
        target, spread = chains[number][3], spread_columns[number]
        side_seconds += side_pass(
            2 + number, chain_firsts[number], target, spread.start, spread.size
        )
    for copy in own:
        copy.wait()
    for copy in side_seconds:
        copy.wait()
    for firsts in side_firsts + chain_firsts:
        for copy in firsts:
            copy.wait_send()
    for number in numbers:
        _, pair, _, _, columns = chains[number]
        for place in range(n_chip):
            pair_copy(number, place).wait_send()
        for direction in range(2):
            for step in range(1, n_chip):

                @pl.when(passes(direction, step))
                def _():
                    way_copy(number, direction, step, pair.at[0, :, columns]).wait_send()


def tail_round(n_ctx, hidden, both, up, attn):
    n_chip = n_ctx // 2
    dma = pltpu.SemaphoreType.DMA
    vmem = pl.BlockSpec(memory_space=pltpu.VMEM)
    wide = (up.shape[1], hidden)
    shapes = (wide, wide, attn.shape[1:])
    return pl.pallas_call(
        functools.partial(tail_kernel, n_ctx),
        name="tail_round",
        out_shape=[jax.ShapeDtypeStruct((4, *shape), BF16) for shape in shapes],
        in_specs=[vmem] * 3,
        out_specs=[vmem] * 3,
        scratch_shapes=[
            pltpu.VMEM((n_chip, *up.shape[1:]), BF16),
            pltpu.VMEM((n_chip, *attn.shape[1:]), BF16),
            pltpu.VMEM((2, n_chip - 1, *up.shape[1:]), BF16),
            pltpu.VMEM((2, n_chip - 1, *attn.shape[1:]), BF16),
            dma((3, n_chip)),
            dma((3, n_chip)),
            dma((3, 2, n_chip - 1)),
            dma((3, 2, n_chip - 1)),
            dma((5, 4)),
            dma((5, 4)),
            dma((2,)),
        ],
        compiler_params=pltpu.CompilerParams(collective_id=8, has_side_effects=True),
    )(both, up, attn)


def gathered(shard):
    return lax.all_gather(shard, "ctx", axis=0, tiled=True)


def scattered(whole):
    return lax.psum_scatter(whole, "ctx", scatter_dimension=0, tiled=True)


def local(
    n_batch,
    n_ctx,
    block_in,
    positions,
    counts,
    cotangent,
    gain_input,
    w_query,
    w_key,
    w_value,
    gain_query,
    gain_key,
    w_output,
    gain_attn,
    gain_ffn,
    w_gate,
    w_up,
    w_down,
    gain_final,
):
    block_in = block_in[0]
    positions = positions[0]
    cotangent = cotangent[0]
    tok_count, model_width = block_in.shape
    width_shard = w_query.shape[0]
    query_width = w_query.shape[1]
    head_size = w_key.shape[1]
    head_count = query_width // head_size
    hidden_shard = w_down.shape[0]
    piece = hidden_shard // n_batch
    hidden_part = -(-piece * n_ctx // 128) * 128
    padded = hidden_part // n_ctx
    halo_depth = (WINDOW + tok_count - 2) // tok_count
    assert halo_depth == 4
    batch_at = lax.axis_index("batch")
    ctx_at = lax.axis_index("ctx")
    all_tok = n_batch * tok_count

    gains = jnp.concatenate(
        [gain_input, gain_attn, gain_ffn, gain_final, gain_query, gain_key]
    )
    slots_of = query_width + 2 * head_size
    quarter = slots_of // n_batch
    qkv_full, proj_full, gains_all = gather_weights(
        n_batch,
        n_ctx,
        jnp.concatenate([w_query, w_key, w_value], axis=1)
        .reshape(width_shard, n_batch, quarter)
        .transpose(1, 0, 2),
        w_output.reshape(n_batch, -1, model_width),
        gains[None],
    )
    qkv_full = qkv_full.reshape(n_batch, model_width, quarter)
    full_output = proj_full.reshape(query_width, model_width)
    gains_all = gains_all[:, 0].astype(F32)

    def gain_at(start, length):
        return gains_all[:, start : start + length].reshape(1, -1)

    head_shard = gain_query.shape[0]
    full_gain_in = gain_at(0, width_shard)
    full_gain_attn = gain_at(width_shard, width_shard)
    full_gain_ffn = gain_at(2 * width_shard, width_shard)
    full_gain_final = gain_at(3 * width_shard, width_shard)
    full_gain_q = gain_at(4 * width_shard, head_shard)
    full_gain_k = gain_at(4 * width_shard + head_shard, head_shard)

    part_both = gathered(pick_columns(n_batch, n_ctx, piece, padded, w_gate, w_up))
    own_down = lax.dynamic_slice_in_dim(w_down, batch_at * piece, piece, 0)
    part_down = gathered(jnp.pad(own_down, ((0, padded - piece), (0, 0))))

    first_token = ctx_at * tok_count
    token_place = first_token + jnp.arange(tok_count, dtype=jnp.int32)
    valid_mask = (token_place < counts[0]).astype(F32)[:, None]
    resid_in = block_in.astype(F32)
    act_in = normed(resid_in, full_gain_in).astype(BF16)
    qkv_raw = jnp.concatenate([project(act_in, qkv_full[i]) for i in range(n_batch)], axis=1)
    query_raw = qkv_raw[:, :query_width].reshape(tok_count, head_count, head_size)
    key_raw = qkv_raw[:, query_width : query_width + head_size]
    value_low = qkv_raw[:, query_width + head_size :].astype(BF16)
    inv_freq = BASE ** (-jnp.arange(0, head_size, 2, dtype=F32) / head_size)
    angles = positions.astype(F32)[:, None] * inv_freq

    def query_path(raw_query, gain_vec):
        return rotate(normed(raw_query, gain_vec), angles[:, None, :])

    def key_path(raw_key, gain_vec):
        return rotate(normed(raw_key, gain_vec), angles)

    query_rot = query_path(query_raw, full_gain_q).astype(BF16)
    key_rot = key_path(key_raw, full_gain_k).astype(BF16)
    own_pair = jnp.concatenate([key_rot, value_low], axis=-1)
    halo = halo_out(n_ctx, own_pair)
    context = jnp.concatenate([halo.reshape(halo_depth * tok_count, -1), own_pair], axis=0)
    ctx_keys = context[:, :head_size]
    ctx_values = context[:, head_size:]
    key_total = (halo_depth + 1) * tok_count
    distance = (
        jnp.arange(tok_count, dtype=jnp.int32)[:, None]
        + halo_depth * tok_count
        - jnp.arange(key_total, dtype=jnp.int32)[None, :]
    )
    allowed = (distance >= 0) & (distance < WINDOW) & (distance <= positions[:, None])
    score_scale = head_size ** (-0.5)
    raw_scores = jnp.einsum("thd,kd->htk", query_rot, ctx_keys, preferred_element_type=F32)
    scores = jnp.where(allowed[None], raw_scores * score_scale, MASKED)
    exp_scores = jnp.exp(scores - jnp.max(scores, axis=-1, keepdims=True))
    attn_prob = exp_scores / jnp.sum(exp_scores, axis=-1, keepdims=True)
    prob_low = attn_prob.astype(BF16)
    attended = jnp.einsum("htk,kd->thd", prob_low, ctx_values, preferred_element_type=F32)
    attn_low = attended.reshape(tok_count, query_width).astype(BF16)
    attn_proj = project(attn_low, full_output)
    middle = resid_in + normed(attn_proj, full_gain_attn)
    ffn_in = normed(middle, full_gain_ffn).astype(BF16)

    (ffn_in_all,) = square_gather(2, ffn_in)
    ffn_in_all = ffn_in_all.reshape(all_tok, model_width)
    gate_pre, up_pre, mixed_low, mixed_turned = hidden_mix(256, ffn_in_all, part_both)
    mixed_low, act_in_late, attn_late = lax.optimization_barrier((mixed_low, act_in, attn_low))
    act_in_all, attn_all = square_gather(13, act_in_late, attn_late)
    ffn_in_turned = ffn_in_all.T
    mixed_low, act_in_all, attn_all, mixed_turned, ffn_in_turned = lax.optimization_barrier(
        (mixed_low, act_in_all, attn_all, mixed_turned, ffn_in_turned)
    )
    act_in_all = act_in_all.reshape(all_tok, model_width)
    attn_all = attn_all.reshape(all_tok, query_width)
    block_out, grad_ffn_low, grad_gain_final = turn_round(
        mixed_low, part_down, middle, cotangent, valid_mask, full_gain_final
    )

    grad_final = cotangent.astype(F32) * valid_mask
    grad_ffn_low = grad_ffn_low.reshape(all_tok, model_width)
    down_grad = product_low(384, mixed_turned, grad_ffn_low)
    down_grad, grad_ffn_low = lax.optimization_barrier((down_grad, grad_ffn_low))
    grad_w_down = scattered(down_grad)
    grad_gate_low, grad_up_low, back_part = hidden_back(
        256, grad_ffn_low, part_down, gate_pre, up_pre, part_both
    )
    grad_ffn_in, both_grad = sum_back(
        256,
        back_part.reshape(n_batch, tok_count, model_width),
        ffn_in_turned,
        grad_gate_low,
        grad_up_low,
        UP_FIRST,
    )
    grad_w_both = scattered(both_grad)
    _, pull_ffn_norm = jax.vjp(normed, middle, full_gain_ffn)
    grad_middle_part, grad_gain_ffn = pull_ffn_norm(grad_ffn_in)
    grad_middle = grad_final + grad_middle_part
    _, pull_attn_norm = jax.vjp(normed, attn_proj, full_gain_attn)
    grad_attn_proj, grad_gain_attn = pull_attn_norm(grad_middle)

    grad_proj_low = grad_attn_proj.astype(BF16)
    grad_attended = (
        project_back(grad_proj_low, full_output)
        .astype(BF16)
        .reshape(tok_count, head_count, head_size)
    )
    grad_prob = jnp.einsum("thd,kd->htk", grad_attended, ctx_values, preferred_element_type=F32)
    row_delta = jnp.sum(attn_prob * grad_prob, axis=-1, keepdims=True)
    grad_scores = (attn_prob * (grad_prob - row_delta)).astype(BF16)
    grad_queries = (
        jnp.einsum("htk,kd->thd", grad_scores, ctx_keys, preferred_element_type=F32) * score_scale
    )
    grad_ctx_keys = (
        jnp.einsum("htk,thd->kd", grad_scores, query_rot, preferred_element_type=F32) * score_scale
    )
    grad_ctx_values = jnp.einsum("htk,thd->kd", prob_low, grad_attended, preferred_element_type=F32)
    grad_context = jnp.concatenate([grad_ctx_keys, grad_ctx_values], axis=-1)
    halo_rows = halo_depth * tok_count
    returned, down_all, up_grad = halo_back(
        256,
        n_ctx,
        grad_context[:halo_rows].astype(BF16).reshape(halo_depth, tok_count, 2 * head_size),
        grad_w_down,
        ffn_in_turned,
        grad_up_low,
        hidden_part - UP_FIRST,
    )
    own_grad = grad_context[halo_rows:] + returned
    grad_value_low = own_grad[:, head_size:].astype(BF16)
    _, pull_key = jax.vjp(key_path, key_raw, full_gain_k)
    grad_key_raw, grad_gain_key = pull_key(own_grad[:, :head_size])
    _, pull_query = jax.vjp(query_path, query_raw, full_gain_q)
    grad_query_raw, grad_gain_query = pull_query(grad_queries)
    grad_qkv_low = jnp.concatenate(
        [
            grad_query_raw.astype(BF16).reshape(tok_count, query_width),
            grad_key_raw.astype(BF16),
            grad_value_low,
        ],
        axis=1,
    )
    grad_act_in = sum(
        project_back(grad_qkv_low[:, i * quarter : (i + 1) * quarter], qkv_full[i])
        for i in range(n_batch)
    )
    _, pull_input = jax.vjp(normed, resid_in, full_gain_in)
    grad_in_part, grad_gain_input = pull_input(grad_act_in)
    grad_in = (grad_middle + grad_in_part).astype(BF16)

    def column_slots(upstream):
        return upstream.reshape(tok_count, n_batch, -1).transpose(1, 0, 2)

    gain_rows = jnp.concatenate(
        [
            grad.reshape(n_ctx, -1)
            for grad in (
                grad_gain_input,
                grad_gain_attn,
                grad_gain_ffn,
                grad_gain_final,
                grad_gain_query,
                grad_gain_key,
            )
        ],
        axis=1,
    )
    gain_parts, qkv_slots, proj_slots = batch_exchange(
        7,
        n_batch,
        whole=(gain_rows,),
        slots=(column_slots(grad_qkv_low), column_slots(grad_proj_low)),
    )
    proj_rows = w_output.shape[0]
    gain_count = gain_rows.shape[1]
    gain_lines = -(-gain_count // quarter)
    used = width_shard + proj_rows + gain_lines
    lines = -(-used // 16) * 16
    grad_w_output = weight_grad(attn_all, proj_slots.reshape(all_tok, -1)).astype(BF16)
    grad_w_qkv = weight_grad(act_in_all, qkv_slots.reshape(all_tok, -1)).astype(BF16)
    output_part = model_width // n_batch
    gain_sum = jnp.sum(gain_parts, axis=0).astype(BF16)
    packed = jnp.concatenate(
        [
            grad_w_qkv.reshape(n_ctx, width_shard, quarter),
            jnp.pad(
                grad_w_output.reshape(n_ctx, proj_rows, output_part),
                ((0, 0), (0, 0), (0, quarter - output_part)),
            ),
            jnp.pad(gain_sum, ((0, 0), (0, gain_lines * quarter - gain_count))).reshape(
                n_ctx, gain_lines, quarter
            ),
            jnp.zeros((n_ctx, lines - used, quarter), BF16),
        ],
        axis=1,
    )
    gate_all, up_all, attn_grads = tail_round(
        n_ctx,
        hidden_part,
        grad_w_both,
        up_grad.reshape(n_ctx, width_shard, hidden_part - UP_FIRST),
        packed,
    )
    shapes = (
        (width_shard, w_gate.shape[1]),
        (width_shard, w_gate.shape[1]),
        (hidden_shard, model_width),
        (width_shard, query_width),
        (width_shard, head_size),
        (width_shard, head_size),
        (proj_rows, model_width),
        (gain_lines, quarter),
    )
    (
        grad_gate_shard,
        grad_up_shard,
        grad_down_shard,
        grad_query_shard,
        grad_key_shard,
        grad_value_shard,
        grad_output_shard,
        gain_block,
    ) = finish_round(
        n_batch, n_ctx, piece, padded, output_part, gate_all, up_all, down_all, attn_grads, shapes
    )
    gain_mine = gain_block.reshape(-1)

    return (
        block_out[None],
        grad_in[None],
        gain_mine[:width_shard],
        grad_query_shard,
        grad_key_shard,
        grad_value_shard,
        gain_mine[4 * width_shard : 4 * width_shard + head_shard],
        gain_mine[4 * width_shard + head_shard : gain_count],
        grad_output_shard,
        gain_mine[width_shard : 2 * width_shard],
        gain_mine[2 * width_shard : 3 * width_shard],
        grad_gate_shard,
        grad_up_shard,
        grad_down_shard,
        gain_mine[3 * width_shard : 4 * width_shard],
    )


def solution(mesh):
    matrix = P("ctx", None)
    vector = P("ctx")
    tokens = P("batch", "ctx", None)

    def step(*arrays):
        return local(mesh.shape["batch"], mesh.shape["ctx"], *arrays)

    return jax.shard_map(
        step,
        mesh=mesh,
        in_specs=(
            tokens,
            P("batch", "ctx"),
            P("batch"),
            tokens,
            vector,
            matrix,
            matrix,
            matrix,
            vector,
            vector,
            matrix,
            vector,
            vector,
            matrix,
            matrix,
            matrix,
            vector,
        ),
        out_specs=(
            tokens,
            tokens,
            vector,
            matrix,
            matrix,
            matrix,
            vector,
            vector,
            matrix,
            vector,
            vector,
            matrix,
            matrix,
            matrix,
            vector,
        ),
        check_vma=False,
    )
```

```python
import functools

import jax
import jax.numpy as jnp
from jax import lax
from jax.experimental import pallas as pl
from jax.experimental.pallas import tpu as pltpu
from jax.sharding import PartitionSpec as P

WINDOW = 512
UP_FIRST = 256


EPS = 1e-06
BASE = 10000.0
MASKED = -1e30
BF16 = jnp.bfloat16
F32 = jnp.float32
MESH = pl.DeviceIdType.MESH


def normed(vector, gain_vec):
    return vector * lax.rsqrt(jnp.mean(vector * vector, axis=-1, keepdims=True) + EPS) * gain_vec


def rotate(vector, angles):
    half_size = vector.shape[-1] // 2
    cosine = jnp.cos(angles)
    sine_part = jnp.sin(angles)
    first_half = vector[..., :half_size]
    second = vector[..., half_size:]
    return jnp.concatenate(
        [first_half * cosine - second * sine_part, second * cosine + first_half * sine_part],
        axis=-1,
    )


def project(inputs, weight):
    return lax.dot_general(inputs, weight, (((1,), (0,)), ((), ())), preferred_element_type=F32)


def project_back(upstream, weight):
    return lax.dot_general(upstream, weight, (((1,), (1,)), ((), ())), preferred_element_type=F32)


def weight_grad(inputs, upstream):
    return lax.dot_general(inputs, upstream, (((0,), (0,)), ((), ())), preferred_element_type=F32)


def gated_gelu(gate_val, up_val):
    return jax.nn.gelu(gate_val, approximate=True) * up_val


def batch_kernel(size, kinds, *refs):
    count = len(kinds)
    sources, results = refs[:count], refs[count : 2 * count]
    send_sem, recv_sem, own_sem = refs[2 * count :]
    me = lax.axis_index("batch")
    barrier = pltpu.get_barrier_semaphore()
    for step in range(1, size):
        pl.semaphore_signal(
            barrier, inc=1, device_id={"batch": lax.rem(me + step, size)}, device_id_type=MESH
        )
    pl.semaphore_wait(barrier, size - 1)
    copies = []
    for step in range(1, size):
        peer = lax.rem(me + step, size)
        for item in range(count):
            source = sources[item].at[peer] if kinds[item] else sources[item]
            copies.append(
                pltpu.make_async_remote_copy(
                    src_ref=source,
                    dst_ref=results[item].at[me],
                    send_sem=send_sem.at[item, step - 1],
                    recv_sem=recv_sem.at[item, step - 1],
                    device_id={"batch": peer},
                    device_id_type=MESH,
                )
            )
    for copy in copies:
        copy.start()
    own = []
    for item in range(count):
        source = sources[item].at[me] if kinds[item] else sources[item]
        own.append(pltpu.make_async_copy(source, results[item].at[me], own_sem.at[item]))
    for copy in own:
        copy.start()
    for copy in own:
        copy.wait()
    for copy in copies:
        copy.wait()


def batch_exchange(collective_id, size, whole=(), slots=()):
    arrays = list(whole) + list(slots)
    kinds = [0] * len(whole) + [1] * len(slots)
    count = len(arrays)
    shapes = [
        jax.ShapeDtypeStruct(a.shape if k else (size, *a.shape), a.dtype)
        for a, k in zip(arrays, kinds)
    ]
    return pl.pallas_call(
        functools.partial(batch_kernel, size, kinds),
        out_shape=shapes,
        in_specs=[pl.BlockSpec(memory_space=pltpu.VMEM)] * count,
        out_specs=[pl.BlockSpec(memory_space=pltpu.VMEM)] * count,
        scratch_shapes=[
            pltpu.SemaphoreType.DMA((count, size - 1)),
            pltpu.SemaphoreType.DMA((count, size - 1)),
            pltpu.SemaphoreType.DMA((count,)),
        ],
        compiler_params=pltpu.CompilerParams(collective_id=collective_id, has_side_effects=True),
    )(*arrays)


def square_kernel(count, *refs):
    sources, results = refs[:count], refs[count : 2 * count]
    send_sem, recv_sem, own_sem = refs[2 * count :]
    me = lax.axis_index("batch")
    across = me + 1 - 2 * lax.rem(me, 2)
    along = lax.rem(me + 2, 4)
    barrier = pltpu.get_barrier_semaphore()
    for peer in (across, along):
        pl.semaphore_signal(barrier, inc=1, device_id={"batch": peer}, device_id_type=MESH)
    pl.semaphore_wait(barrier, 2)

    def remote(source, target, item, turn, peer):
        copy = pltpu.make_async_remote_copy(
            src_ref=source,
            dst_ref=target,
            send_sem=send_sem.at[item, turn],
            recv_sem=recv_sem.at[item, turn],
            device_id={"batch": peer},
            device_id_type=MESH,
        )
        copy.start()
        return copy

    firsts = [
        [
            remote(sources[item], results[item].at[me], item, turn, peer)
            for turn, peer in enumerate((across, along))
        ]
        for item in range(count)
    ]
    own = [
        pltpu.make_async_copy(sources[item], results[item].at[me], own_sem.at[item])
        for item in range(count)
    ]
    for copy in own:
        copy.start()
    seconds = []
    for item in range(count):
        columns = sources[item].shape[-1]
        cut = columns // 256 * 128
        halves = (pl.ds(0, cut), pl.ds(cut, columns - cut))
        for turn, (giver, taker) in enumerate(((across, along), (along, across))):
            firsts[item][turn].wait_recv()
            block = results[item].at[giver, :, halves[turn]]
            seconds.append(remote(block, block, item, 2 + turn, taker))
    for copy in own:
        copy.wait()
    for copy in seconds:
        copy.wait()
    for pair in firsts:
        for copy in pair:
            copy.wait_send()


def square_gather(collective_id, *arrays):
    count = len(arrays)
    return pl.pallas_call(
        functools.partial(square_kernel, count),
        out_shape=[jax.ShapeDtypeStruct((4, *a.shape), a.dtype) for a in arrays],
        in_specs=[pl.BlockSpec(memory_space=pltpu.VMEM)] * count,
        out_specs=[pl.BlockSpec(memory_space=pltpu.VMEM)] * count,
        scratch_shapes=[
            pltpu.SemaphoreType.DMA((count, 4)),
            pltpu.SemaphoreType.DMA((count, 4)),
            pltpu.SemaphoreType.DMA((count,)),
        ],
        compiler_params=pltpu.CompilerParams(collective_id=collective_id, has_side_effects=True),
    )(*arrays)


def turn_kernel(
    mixed_ref,
    down_ref,
    middle_ref,
    upstream_ref,
    valid_ref,
    gain_ref,
    out_ref,
    grads_ref,
    gain_grad_ref,
    part_ref,
    taken_ref,
    send_sem,
    recv_sem,
    pass_sem,
    take_sem,
):
    me = lax.axis_index("batch")
    across = me + 1 - 2 * lax.rem(me, 2)
    along = lax.rem(me + 2, 4)
    corner = lax.rem(across + 2, 4)
    order = (corner, across, along)
    tok_count = middle_ref.shape[0]
    barrier = pltpu.get_barrier_semaphore()
    for peer in order:
        pl.semaphore_signal(barrier, inc=1, device_id={"batch": peer}, device_id_type=MESH)
    pl.semaphore_wait(barrier, 3)

    columns = grads_ref.shape[-1]
    cut = columns // 256 * 128
    halves = (pl.ds(0, cut), pl.ds(cut, columns - cut))

    def product(place, stretch):
        start = (place // 2) * 2 * tok_count
        rows = pl.ds(pl.multiple_of(start, 2 * tok_count), 2 * tok_count)
        return jnp.dot(mixed_ref[rows, :], down_ref[:, stretch], preferred_element_type=F32)

    copies = [
        pltpu.make_async_remote_copy(
            src_ref=part_ref.at[base + lax.rem(peer, 2), :, stretch],
            dst_ref=taken_ref.at[turn, :, stretch],
            send_sem=send_sem.at[turn, half],
            recv_sem=recv_sem.at[turn, half],
            device_id={"batch": peer},
            device_id_type=MESH,
        )
        for half, stretch in enumerate(halves)
        for turn, (peer, base) in enumerate(((corner, 0), (along, 0), (across, 2)))
    ]

    def multiply(place, base, half):
        both = product(place, halves[half])
        for row in range(2):
            block = both[row * tok_count : (row + 1) * tok_count]
            part_ref[base + row, :, halves[half]] = block.astype(BF16)
        upper = jnp.broadcast_to(lax.rem(me, 2) == 0, (tok_count, both.shape[1]))
        return jnp.where(upper, both[:tok_count], both[tok_count:])

    multiply(along, 0, 0)
    multiply(along, 0, 1)
    copies[0].start()
    copies[1].start()
    own_first = multiply(me, 2, 0)
    copies[3].start()
    copies[4].start()
    own_second = multiply(me, 2, 1)
    copies[2].start()
    total = jnp.concatenate([own_first, own_second], axis=1)
    copies[5].start()
    for turn in range(3):
        copies[turn].wait_recv()
        copies[3 + turn].wait_recv()
        total = total + taken_ref[turn].astype(F32)
    gain = gain_ref[...]
    valid = valid_ref[...]
    scale = lax.rsqrt(jnp.mean(total * total, axis=-1, keepdims=True) + EPS)
    upstream = upstream_ref[...].astype(F32) * valid
    gained = upstream * gain
    back = scale * gained - total * (
        scale * scale * scale * jnp.mean(total * gained, axis=-1, keepdims=True)
    )
    grads_ref[me] = back.astype(BF16)
    unit = total * scale
    out_ref[...] = ((middle_ref[...] + unit * gain) * valid).astype(BF16)
    gain_grad_ref[...] = jnp.sum(upstream * unit, axis=0, keepdims=True)

    def remote(block, turn, peer):
        copy = pltpu.make_async_remote_copy(
            src_ref=block,
            dst_ref=block,
            send_sem=pass_sem.at[turn],
            recv_sem=take_sem.at[turn],
            device_id={"batch": peer},
            device_id_type=MESH,
        )
        copy.start()
        return copy

    firsts = [remote(grads_ref.at[me], turn, peer) for turn, peer in enumerate((across, along))]
    seconds = []
    for turn, (giver, taker) in enumerate(((across, along), (along, across))):
        firsts[turn].wait_recv()
        seconds.append(remote(grads_ref.at[giver, :, halves[turn]], 2 + turn, taker))
    for copy in seconds:
        copy.wait()
    for copy in firsts + copies:
        copy.wait_send()


def turn_round(mixed, down, middle, upstream, valid, gain):
    tok_count, width = middle.shape
    dma = pltpu.SemaphoreType.DMA
    vmem = pl.BlockSpec(memory_space=pltpu.VMEM)
    flops = 2 * mixed.shape[0] * mixed.shape[1] * width
    return pl.pallas_call(
        turn_kernel,
        name="turn_round",
        out_shape=(
            jax.ShapeDtypeStruct((tok_count, width), BF16),
            jax.ShapeDtypeStruct((4, tok_count, width), BF16),
            jax.ShapeDtypeStruct((1, width), F32),
        ),
        in_specs=[vmem] * 6,
        out_specs=[vmem] * 3,
        scratch_shapes=[
            pltpu.VMEM((4, tok_count, width), BF16),
            pltpu.VMEM((3, tok_count, width), BF16),
            dma((3, 2)),
            dma((3, 2)),
            dma((4,)),
            dma((4,)),
        ],
        cost_estimate=pl.CostEstimate(flops=flops, bytes_accessed=8 << 20, transcendentals=0),
        compiler_params=pltpu.CompilerParams(collective_id=3, has_side_effects=True),
    )(mixed, down, middle, upstream, valid, gain)


def product_kernel(left_ref, right_ref, out_ref):
    out_ref[...] = jnp.dot(left_ref[...], right_ref[...], preferred_element_type=F32).astype(BF16)


def product_low(tile, left, right):
    rows, depth = left.shape
    columns = right.shape[1]
    return pl.pallas_call(
        product_kernel,
        grid=(columns // tile,),
        out_shape=jax.ShapeDtypeStruct((rows, columns), BF16),
        in_specs=[
            pl.BlockSpec((rows, depth), lambda i: (0, 0)),
            pl.BlockSpec((depth, tile), lambda i: (0, i)),
        ],
        out_specs=pl.BlockSpec((rows, tile), lambda i: (0, i)),
        cost_estimate=pl.CostEstimate(
            flops=2 * rows * depth * columns, bytes_accessed=8 << 20, transcendentals=0
        ),
    )(left, right)


def mix_kernel(tokens_ref, w_gate_ref, w_up_ref, gate_ref, up_ref, mixed_ref, turned_ref):
    gate = project(tokens_ref[...], w_gate_ref[...])
    up = project(tokens_ref[...], w_up_ref[...])
    gate_ref[...] = gate
    up_ref[...] = up
    mixed = gated_gelu(gate, up)
    mixed_ref[...] = mixed.astype(BF16)
    turned_ref[...] = mixed.T.astype(BF16)


def hidden_mix(tile, tokens, both_weights):
    count, width = tokens.shape
    hidden = both_weights.shape[1] // 2
    steps = hidden // tile
    wide = jax.ShapeDtypeStruct((count, hidden), F32)
    column = pl.BlockSpec((count, tile), lambda i: (0, i))
    return pl.pallas_call(
        mix_kernel,
        name="hidden_mix",
        grid=(steps,),
        out_shape=(
            wide,
            wide,
            jax.ShapeDtypeStruct((count, hidden), BF16),
            jax.ShapeDtypeStruct((hidden, count), BF16),
        ),
        in_specs=[
            pl.BlockSpec((count, width), lambda i: (0, 0)),
            pl.BlockSpec((width, tile), lambda i: (0, i)),
            pl.BlockSpec((width, tile), lambda i: (0, i + steps)),
        ],
        out_specs=[column, column, column, pl.BlockSpec((tile, count), lambda i: (i, 0))],
        cost_estimate=pl.CostEstimate(
            flops=4 * count * hidden * width, bytes_accessed=24 << 20, transcendentals=0
        ),
    )(tokens, both_weights, both_weights)


def back_kernel(
    upstream_ref, down_ref, gate_ref, up_ref, w_gate_ref, w_up_ref, gate_out, up_out, back_ref, total
):
    step = pl.program_id(0)
    grad_mixed = project_back(upstream_ref[...], down_ref[...])
    _, pull_gelu = jax.vjp(gated_gelu, gate_ref[...], up_ref[...])
    grad_gate, grad_up = pull_gelu(grad_mixed)
    grad_gate, grad_up = grad_gate.astype(BF16), grad_up.astype(BF16)
    gate_out[...] = grad_gate
    up_out[...] = grad_up
    part = project_back(grad_gate, w_gate_ref[...]) + project_back(grad_up, w_up_ref[...])

    @pl.when(step == 0)
    def _():
        total[...] = part

    @pl.when(step > 0)
    def _():
        total[...] += part

    @pl.when(step == pl.num_programs(0) - 1)
    def _():
        back_ref[...] = total[...].astype(BF16)


def hidden_back(tile, upstream, down, gate_pre, up_pre, both_weights):
    tokens, width = upstream.shape
    hidden = down.shape[0]
    count = hidden // tile
    low = jax.ShapeDtypeStruct((tokens, hidden), BF16)
    return pl.pallas_call(
        back_kernel,
        name="hidden_back",
        grid=(count,),
        out_shape=(low, low, jax.ShapeDtypeStruct((tokens, width), BF16)),
        in_specs=[
            pl.BlockSpec((tokens, width), lambda i: (0, 0)),
            pl.BlockSpec((tile, width), lambda i: (i, 0)),
            pl.BlockSpec((tokens, tile), lambda i: (0, i)),
            pl.BlockSpec((tokens, tile), lambda i: (0, i)),
            pl.BlockSpec((width, tile), lambda i: (0, i)),
            pl.BlockSpec((width, tile), lambda i: (0, i + count)),
        ],
        out_specs=[
            pl.BlockSpec((tokens, tile), lambda i: (0, i)),
            pl.BlockSpec((tokens, tile), lambda i: (0, i)),
            pl.BlockSpec((tokens, width), lambda i: (0, 0)),
        ],
        scratch_shapes=[pltpu.VMEM((tokens, width), F32)],
        cost_estimate=pl.CostEstimate(
            flops=6 * tokens * hidden * width, bytes_accessed=24 << 20, transcendentals=0
        ),
    )(upstream, down, gate_pre, up_pre, both_weights, both_weights)


def multiply_tiles(tile, first, last, left, right, out, target, sems):
    def step(index, carry):
        columns = pl.ds(pl.multiple_of(index * tile, tile), tile)
        out[:, columns] = jnp.dot(
            left[...], right[:, columns], preferred_element_type=F32
        ).astype(BF16)
        pltpu.make_async_copy(out.at[:, columns], target.at[:, columns], sems.at[index]).start()
        return carry

    lax.fori_loop(first, last, step, 0)


def await_tiles(tile, count, out, target, sems):
    for index in range(count):
        columns = pl.ds(index * tile, tile)
        pltpu.make_async_copy(out.at[:, columns], target.at[:, columns], sems.at[index]).wait()


def sum_back_kernel(
    tile,
    slots_ref,
    left_ref,
    gate_ref,
    up_ref,
    sum_ref,
    both_ref,
    left,
    right,
    both,
    taken_ref,
    send_sem,
    recv_sem,
    load_sem,
    store_sem,
):
    me = lax.axis_index("batch")
    across = me + 1 - 2 * lax.rem(me, 2)
    along = lax.rem(me + 2, 4)
    order = (lax.rem(across + 2, 4), across, along)
    hidden = gate_ref.shape[1]
    width = right.shape[1]
    loads = [
        pltpu.make_async_copy(left_ref, left, load_sem.at[0]),
        pltpu.make_async_copy(gate_ref, right.at[:, pl.ds(0, hidden)], load_sem.at[1]),
        pltpu.make_async_copy(
            up_ref.at[:, pl.ds(0, width - hidden)],
            right.at[:, pl.ds(hidden, width - hidden)],
            load_sem.at[2],
        ),
    ]
    for load in loads:
        load.start()
    barrier = pltpu.get_barrier_semaphore()
    for peer in order:
        pl.semaphore_signal(barrier, inc=1, device_id={"batch": peer}, device_id_type=MESH)
    pl.semaphore_wait(barrier, 3)
    copies = [
        pltpu.make_async_remote_copy(
            src_ref=slots_ref.at[peer],
            dst_ref=taken_ref.at[turn],
            send_sem=send_sem.at[turn],
            recv_sem=recv_sem.at[turn],
            device_id={"batch": peer},
            device_id_type=MESH,
        )
        for turn, peer in enumerate(order)
    ]
    for copy in copies:
        copy.start()
    for load in loads:
        load.wait()
    multiply_tiles(tile, 0, width // tile, left, right, both, both_ref, store_sem)
    total = slots_ref[me].astype(F32)
    for turn in range(3):
        copies[turn].wait_recv()
        total = total + taken_ref[turn].astype(F32)
    sum_ref[...] = total
    for copy in copies:
        copy.wait_send()
    await_tiles(tile, width // tile, both, both_ref, store_sem)


def sum_back(tile, slots, left, gate, up, columns):
    rows, depth = left.shape
    width = gate.shape[1] + columns
    dma = pltpu.SemaphoreType.DMA
    vmem = pl.BlockSpec(memory_space=pltpu.VMEM)
    anywhere = pl.BlockSpec(memory_space=pl.ANY)
    return pl.pallas_call(
        functools.partial(sum_back_kernel, tile),
        name="sum_back",
        out_shape=[
            jax.ShapeDtypeStruct(slots.shape[1:], F32),
            jax.ShapeDtypeStruct((rows, width), BF16),
        ],
        in_specs=[vmem, anywhere, anywhere, anywhere],
        out_specs=[vmem, anywhere],
        scratch_shapes=[
            pltpu.VMEM((rows, depth), BF16),
            pltpu.VMEM((depth, width), BF16),
            pltpu.VMEM((rows, width), BF16),
            pltpu.VMEM((3, *slots.shape[1:]), BF16),
            dma((3,)),
            dma((3,)),
            dma((3,)),
            dma((width // tile,)),
        ],
        cost_estimate=pl.CostEstimate(
            flops=2 * rows * depth * width, bytes_accessed=12 << 20, transcendentals=0
        ),
        compiler_params=pltpu.CompilerParams(collective_id=5, has_side_effects=True),
    )(slots, left, gate, up)


def halo_out_kernel(n_chip, source_ref, result_ref, send_sem, recv_sem):
    me = lax.axis_index("ctx")
    chip, core = me // 2, lax.rem(me, 2)
    near = {"ctx": me + 1 - 2 * core}
    after = {"ctx": jnp.minimum(me + 2, 2 * n_chip - 1)}
    has_after = chip < n_chip - 1
    barrier = pltpu.get_barrier_semaphore()
    pl.semaphore_signal(barrier, inc=1, device_id=near, device_id_type=MESH)

    @pl.when(chip > 0)
    def _():
        before = {"ctx": jnp.maximum(me - 2, 0)}
        pl.semaphore_signal(barrier, inc=1, device_id=before, device_id_type=MESH)

    pl.semaphore_wait(barrier, 1 + jnp.minimum(n_chip - 1 - chip, 1))

    def remote(source, slot, turn, peer):
        return pltpu.make_async_remote_copy(
            src_ref=source,
            dst_ref=result_ref.at[slot],
            send_sem=send_sem.at[turn],
            recv_sem=recv_sem.at[turn],
            device_id=peer,
            device_id_type=MESH,
        )

    one_on = remote(source_ref, 2, 0, after)
    two_on = remote(result_ref.at[2], 0, 1, after)
    own_near = remote(source_ref, 3, 2, near)
    before_near = remote(result_ref.at[2], 3 - 2 * (1 - core), 3, near)
    far_near = remote(result_ref.at[0], 1, 4, near)

    @pl.when(has_after)
    def _():
        one_on.start()

    @pl.when(core == 0)
    def _():
        own_near.start()

    def blank(slot):
        result_ref[slot] = jnp.zeros(result_ref.shape[1:], result_ref.dtype)

    @pl.when(chip == 0)
    def _():
        blank(2)
        blank(0)
        blank(1)

    @pl.when((chip == 0) & (core == 0))
    def _():
        blank(3)

    @pl.when(chip == 1)
    def _():
        blank(0)

    @pl.when((chip == 1) & (core == 0))
    def _():
        blank(1)

    @pl.when(chip > 0)
    def _():
        one_on.wait_recv()

    @pl.when((chip > 0) & has_after)
    def _():
        two_on.start()

    @pl.when(chip > 0)
    def _():
        before_near.start()

    @pl.when(chip > 1)
    def _():
        two_on.wait_recv()

    @pl.when((chip > 1) & (core == 1))
    def _():
        far_near.start()

    @pl.when(core == 1)
    def _():
        own_near.wait_recv()

    @pl.when(core == 0)
    def _():
        own_near.wait_send()

    @pl.when(chip > 0)
    def _():
        before_near.wait()

    @pl.when((chip > 1) & (core == 0))
    def _():
        far_near.wait_recv()

    @pl.when((chip > 1) & (core == 1))
    def _():
        far_near.wait_send()

    @pl.when(has_after)
    def _():
        one_on.wait_send()

    @pl.when((chip > 0) & has_after)
    def _():
        two_on.wait_send()


def halo_back_kernel(
    tile,
    n_chip,
    source_ref,
    shard_ref,
    left_ref,
    up_ref,
    result_ref,
    shards_ref,
    rest_ref,
    near_ref,
    far_ref,
    way_ref,
    left,
    right,
    rest,
    send_sem,
    recv_sem,
    pass_sem,
    take_sem,
    own_sem,
    store_sem,
):
    me = lax.axis_index("ctx")
    spot = lax.axis_index("batch")
    across = spot + 1 - 2 * lax.rem(spot, 2)
    along = lax.rem(spot + 2, 4)
    chip, core = me // 2, lax.rem(me, 2)
    near = {"ctx": me + 1 - 2 * core}
    before = {"ctx": jnp.maximum(me - 2, 0)}
    has_after = chip < n_chip - 1
    barrier = pltpu.get_barrier_semaphore()
    pl.semaphore_signal(barrier, inc=1, device_id=near, device_id_type=MESH)

    @pl.when(has_after)
    def _():
        after = {"ctx": jnp.minimum(me + 2, 2 * n_chip - 1)}
        pl.semaphore_signal(barrier, inc=1, device_id=after, device_id_type=MESH)

    for peer in (across, along):
        pl.semaphore_signal(barrier, inc=1, device_id={"batch": peer}, device_id_type=MESH)
    pl.semaphore_wait(barrier, 3 + jnp.minimum(chip, 1))

    def beside(source, target, turn, peer):
        copy = pltpu.make_async_remote_copy(
            src_ref=source,
            dst_ref=target,
            send_sem=pass_sem.at[turn],
            recv_sem=take_sem.at[turn],
            device_id={"batch": peer},
            device_id_type=MESH,
        )
        copy.start()
        return copy

    def remote(source, target, turn, peer):
        return pltpu.make_async_remote_copy(
            src_ref=source,
            dst_ref=target,
            send_sem=send_sem.at[turn],
            recv_sem=recv_sem.at[turn],
            device_id=peer,
            device_id_type=MESH,
        )

    to_before = remote(source_ref.at[3 - 2 * core], near_ref.at[0], 0, near)
    to_other = remote(source_ref.at[1 + 2 * core], near_ref.at[1], 1, near)
    to_before.start()
    to_other.start()
    width = right.shape[1]
    count = width // tile
    loads = [
        pltpu.make_async_copy(left_ref, left, own_sem.at[1]),
        pltpu.make_async_copy(
            up_ref.at[:, pl.ds(up_ref.shape[1] - width, width)], right, own_sem.at[2]
        ),
    ]
    for load in loads:
        load.start()
    firsts = [
        beside(shard_ref, shards_ref.at[spot], turn, peer)
        for turn, peer in enumerate((across, along))
    ]
    own = pltpu.make_async_copy(shard_ref, shards_ref.at[spot], own_sem.at[0])
    own.start()

    @pl.when((chip == 0) | jnp.logical_not(has_after))
    def _():
        way_ref[0] = jnp.zeros(way_ref.shape[1:], way_ref.dtype)

    @pl.when(jnp.logical_not(has_after))
    def _():
        way_ref[1] = jnp.zeros(way_ref.shape[1:], way_ref.dtype)

    to_other.wait_recv()
    theirs = near_ref[1].astype(F32)
    far_ref[0] = (source_ref[0].astype(F32) + jnp.where(core == 1, theirs, 0.0)).astype(BF16)
    two_back = remote(far_ref.at[0], way_ref.at[0], 2, before)
    one_back = remote(far_ref.at[1], way_ref.at[1], 3, before)

    @pl.when(chip > 1)
    def _():
        two_back.start()

    to_before.wait_recv()
    due = source_ref[2].astype(F32) + near_ref[0].astype(F32)

    for load in loads:
        load.wait()
    multiply_tiles(tile, 0, count // 3, left, right, rest, rest_ref, store_sem)

    @pl.when((chip > 0) & has_after)
    def _():
        two_back.wait_recv()

    far_ref[1] = (due + way_ref[0].astype(F32)).astype(BF16)

    @pl.when(chip > 0)
    def _():
        one_back.start()

    multiply_tiles(tile, count // 3, count, left, right, rest, rest_ref, store_sem)
    columns = shard_ref.shape[-1]
    cut = columns // 256 * 128
    halves = (pl.ds(0, cut), pl.ds(cut, columns - cut))
    seconds = []
    for turn, (giver, taker) in enumerate(((across, along), (along, across))):
        firsts[turn].wait_recv()
        block = shards_ref.at[giver, :, halves[turn]]
        seconds.append(beside(block, block, 2 + turn, taker))

    @pl.when(has_after)
    def _():
        one_back.wait_recv()

    result_ref[...] = way_ref[1].astype(F32) + jnp.where(core == 0, theirs, 0.0)
    own.wait()
    for copy in seconds:
        copy.wait()
    for copy in firsts + [to_before, to_other]:
        copy.wait_send()
    await_tiles(tile, count, rest, rest_ref, store_sem)

    @pl.when(chip > 1)
    def _():
        two_back.wait_send()

    @pl.when(chip > 0)
    def _():
        one_back.wait_send()


def halo_call(collective_id, kernel, arrays, in_vmem, out_shape, out_vmem, buffers, counts):
    dma = pltpu.SemaphoreType.DMA
    vmem = pl.BlockSpec(memory_space=pltpu.VMEM)
    anywhere = pl.BlockSpec(memory_space=pl.ANY)
    return pl.pallas_call(
        kernel,
        out_shape=out_shape,
        in_specs=[vmem if i < in_vmem else anywhere for i in range(len(arrays))],
        out_specs=[vmem if i < out_vmem else anywhere for i in range(len(out_shape))],
        scratch_shapes=[*buffers, *(dma((count,)) for count in counts)],
        compiler_params=pltpu.CompilerParams(collective_id=collective_id, has_side_effects=True),
    )(*arrays)


def halo_out(n_ctx, block):
    out_shape = [jax.ShapeDtypeStruct((4, *block.shape), block.dtype)]
    kernel = functools.partial(halo_out_kernel, n_ctx // 2)
    return halo_call(1, kernel, (block,), 1, out_shape, 1, (), (5, 5))[0]


def halo_back(tile, n_ctx, blocks, shard, left, up, columns):
    shape = blocks.shape[1:]
    rows, depth = left.shape
    buffers = [pltpu.VMEM((2, *shape), blocks.dtype)] * 3
    buffers += [
        pltpu.VMEM((rows, depth), BF16),
        pltpu.VMEM((depth, columns), BF16),
        pltpu.VMEM((rows, columns), BF16),
    ]
    out_shape = [
        jax.ShapeDtypeStruct(shape, F32),
        jax.ShapeDtypeStruct((4, *shard.shape), shard.dtype),
        jax.ShapeDtypeStruct((rows, columns), BF16),
    ]
    kernel = functools.partial(halo_back_kernel, tile, n_ctx // 2)
    arrays = (blocks, shard, left, up)
    counts = (4, 4, 4, 4, 3, columns // tile)
    return halo_call(6, kernel, arrays, 2, out_shape, 2, buffers, counts)


def pick_kernel(n_batch, n_ctx, piece, padded, gate_ref, up_ref, out_ref):
    me = lax.axis_index("batch")
    out_ref[...] = jnp.zeros_like(out_ref)
    for spot in range(n_batch):

        @pl.when(me == spot)
        def _():
            for shard in range(n_ctx):
                start = (shard * n_batch + spot) * piece
                for half, ref in enumerate((gate_ref, up_ref)):
                    place = (half * n_ctx + shard) * padded
                    out_ref[:, place : place + piece] = ref[:, start : start + piece]


def row_block(rows):
    return 48 if rows % 48 == 0 else rows


def pick_columns(n_batch, n_ctx, piece, padded, w_gate, w_up):
    rows, hidden = w_gate.shape
    block = row_block(rows)
    spec = pl.BlockSpec((block, hidden), lambda i: (i, 0))
    return pl.pallas_call(
        functools.partial(pick_kernel, n_batch, n_ctx, piece, padded),
        name="pick_columns",
        grid=(rows // block,),
        out_shape=jax.ShapeDtypeStruct((rows, 2 * n_ctx * padded), w_gate.dtype),
        in_specs=[spec, spec],
        out_specs=pl.BlockSpec((block, 2 * n_ctx * padded), lambda i: (i, 0)),
    )(w_gate, w_up)


def finish_kernel(n_batch, n_ctx, piece, padded, proj_part, gate_ref, up_ref, down_ref, attn_ref, *refs):
    outs, bufs, sems = refs[:8], refs[8:16], refs[16]
    gate_buf, up_buf, down_buf, query_buf, key_buf, value_buf, proj_buf, gain_buf = bufs
    copies = [pltpu.make_async_copy(bufs[i], outs[i], sems.at[i]) for i in range(8)]
    rows = gate_ref.shape[1]
    block = row_block(rows)

    for ref, buf, copy in ((gate_ref, gate_buf, copies[0]), (up_ref, up_buf, copies[1])):

        def place_rows(step, carry):
            lines = pl.ds(pl.multiple_of(step * block, block), block)
            for shard in range(n_ctx):
                for spot in range(n_batch):
                    start = (shard * n_batch + spot) * piece
                    place = shard * padded
                    buf[lines, start : start + piece] = ref[
                        spot, lines, place : place + piece
                    ].astype(F32)
            return carry

        lax.fori_loop(0, rows // block, place_rows, 0)
        copy.start()
    for spot in range(n_batch):
        down_buf[spot * piece : (spot + 1) * piece, :] = down_ref[spot, :piece, :].astype(F32)
    copies[2].start()
    quarter = attn_ref.shape[-1]
    proj_rows = proj_buf.shape[0]
    for spot in range(n_batch):
        for tile in range(0, quarter, 128):
            column = spot * quarter + tile
            for buf in (query_buf, key_buf, value_buf):
                if 0 <= column < buf.shape[-1]:
                    buf[:, column : column + 128] = attn_ref[
                        spot, :rows, tile : tile + 128
                    ].astype(F32)
                column -= buf.shape[-1]
        proj_buf[:, spot * proj_part : (spot + 1) * proj_part] = attn_ref[
            spot, rows : rows + proj_rows, :proj_part
        ].astype(F32)
    gain_buf[...] = attn_ref[0, rows + proj_rows : rows + proj_rows + gain_buf.shape[0], :].astype(F32)
    for copy in copies[3:]:
        copy.start()
    for copy in copies:
        copy.wait()


def finish_round(n_batch, n_ctx, piece, padded, proj_part, gate, up, down, attn, shapes):
    outs = [jax.ShapeDtypeStruct(shape, F32) for shape in shapes]
    return pl.pallas_call(
        functools.partial(finish_kernel, n_batch, n_ctx, piece, padded, proj_part),
        name="finish_round",
        out_shape=outs,
        in_specs=[pl.BlockSpec(memory_space=pltpu.VMEM)] * 4,
        out_specs=[pl.BlockSpec(memory_space=pl.ANY)] * 8,
        scratch_shapes=[pltpu.VMEM(shape, F32) for shape in shapes] + [pltpu.SemaphoreType.DMA((8,))],
    )(gate, up, down, attn)


def weights_kernel(n_batch, n_ctx, qkv_ref, proj_ref, gain_ref, qkv_all, proj_all, gain_all, *sems):
    send_far, recv_far, send_side, recv_side, send_near, recv_near, own_sem = sems
    spot = lax.axis_index("batch")
    me = lax.axis_index("ctx")
    n_chip = n_ctx // 2
    chip, core = me // 2, lax.rem(me, 2)
    near = {"ctx": me + 1 - 2 * core}
    barrier = pltpu.get_barrier_semaphore()

    def far_at(step):
        return {"ctx": 2 * lax.rem(chip + step, n_chip) + core}

    def side_at(step):
        return {"batch": lax.rem(spot + step, n_batch)}

    peers = [near]
    peers += [far_at(step) for step in range(1, n_chip)]
    peers += [side_at(step) for step in range(1, n_batch)]
    for peer in peers:
        pl.semaphore_signal(barrier, inc=1, device_id=peer, device_id_type=MESH)
    pl.semaphore_wait(barrier, len(peers))

    def remote(source, target, send, recv, peer):
        return pltpu.make_async_remote_copy(
            src_ref=source,
            dst_ref=target,
            send_sem=send,
            recv_sem=recv,
            device_id=peer,
            device_id_type=MESH,
        )

    waits = []
    far = []
    for step in range(1, n_chip):
        triple = [
            remote(source, target, send_far.at[step - 1, item], recv_far.at[step - 1, item], far_at(step))
            for item, (source, target) in enumerate(
                (
                    (qkv_ref.at[spot], qkv_all.at[spot, me]),
                    (proj_ref.at[spot], proj_all.at[me, spot]),
                    (gain_ref, gain_all.at[me]),
                )
            )
        ]
        for copy in triple:
            copy.start()
        far.append(triple)
    own = [
        pltpu.make_async_copy(qkv_ref, qkv_all.at[:, me], own_sem.at[0]),
        pltpu.make_async_copy(proj_ref, proj_all.at[me], own_sem.at[1]),
        pltpu.make_async_copy(gain_ref, gain_all.at[me], own_sem.at[2]),
    ]
    for copy in own:
        copy.start()
    first = n_chip - 1
    pairs = [
        remote(source, target, send_near.at[first, 0, item], recv_near.at[first, 0, item], near)
        for item, (source, target) in enumerate(
            (
                (qkv_ref, qkv_all.at[:, me]),
                (proj_ref, proj_all.at[me]),
                (gain_ref, gain_all.at[me]),
            )
        )
    ]
    for copy in pairs:
        copy.start()
    waits += pairs

    def hand_near(step, turn):
        origin = 2 * lax.rem(chip + n_chip - step, n_chip) + core
        quarter = lax.rem(spot + n_batch - turn, n_batch)
        blocks = [qkv_all.at[quarter, origin], proj_all.at[origin, quarter]]
        blocks += [gain_all.at[origin]] if turn == 0 else []
        for item, block in enumerate(blocks):
            copy = remote(
                block,
                block,
                send_near.at[step - 1, turn, item],
                recv_near.at[step - 1, turn, item],
                near,
            )
            copy.start()
            waits.append(copy)

    side = []
    for step in range(1, n_chip):
        for copy in far[step - 1]:
            copy.wait_recv()
        origin = 2 * lax.rem(chip + n_chip - step, n_chip) + core
        for turn in range(1, n_batch):
            pair = [
                remote(
                    block,
                    block,
                    send_side.at[step - 1, turn - 1, item],
                    recv_side.at[step - 1, turn - 1, item],
                    side_at(turn),
                )
                for item, block in enumerate((qkv_all.at[spot, origin], proj_all.at[origin, spot]))
            ]
            for copy in pair:
                copy.start()
            side.append((step, turn, pair))
        hand_near(step, 0)
    for step, turn, pair in side:
        for copy in pair:
            copy.wait_recv()
        hand_near(step, turn)
    for copy in waits:
        copy.wait()
    for copy in own:
        copy.wait()
    for triple in far:
        for copy in triple:
            copy.wait_send()
    for _, _, pair in side:
        for copy in pair:
            copy.wait_send()


def gather_weights(n_batch, n_ctx, qkv, proj, gains):
    n_chip = n_ctx // 2
    dma = pltpu.SemaphoreType.DMA
    vmem = pl.BlockSpec(memory_space=pltpu.VMEM)
    return pl.pallas_call(
        functools.partial(weights_kernel, n_batch, n_ctx),
        name="gather_weights",
        out_shape=(
            jax.ShapeDtypeStruct((n_batch, n_ctx, *qkv.shape[1:]), qkv.dtype),
            jax.ShapeDtypeStruct((n_ctx, *proj.shape), proj.dtype),
            jax.ShapeDtypeStruct((n_ctx, *gains.shape), gains.dtype),
        ),
        in_specs=[vmem] * 3,
        out_specs=[vmem] * 3,
        scratch_shapes=[
            dma((n_chip - 1, 3)),
            dma((n_chip - 1, 3)),
            dma((n_chip - 1, n_batch - 1, 2)),
            dma((n_chip - 1, n_batch - 1, 2)),
            dma((n_chip, n_batch, 3)),
            dma((n_chip, n_batch, 3)),
            dma((3,)),
        ],
        compiler_params=pltpu.CompilerParams(collective_id=12, has_side_effects=True),
    )(qkv, proj, gains)


def tail_kernel(
    n_ctx,
    both_ref,
    up_ref,
    attn_ref,
    gate_all,
    up_all,
    attn_all,
    pair_up,
    pair_attn,
    way_up,
    way_attn,
    pair_send,
    pair_recv,
    way_send,
    way_recv,
    side_send,
    side_recv,
    own_sem,
):
    n_chip = n_ctx // 2
    spot = lax.axis_index("batch")
    me = lax.axis_index("ctx")
    chip, core = me // 2, lax.rem(me, 2)
    across = {"batch": spot + 1 - 2 * lax.rem(spot, 2)}
    along = {"batch": lax.rem(spot + 2, 4)}
    near = {"ctx": me + 1 - 2 * core}
    beyond = ({"ctx": jnp.minimum(me + 2, n_ctx - 1)}, {"ctx": jnp.maximum(me - 2, 0)})
    inner = (chip > 0, chip < n_chip - 1)
    barrier = pltpu.get_barrier_semaphore()
    for peer in (near, across, along):
        pl.semaphore_signal(barrier, inc=1, device_id=peer, device_id_type=MESH)
    for has_giver, giver in zip(inner, (beyond[1], beyond[0])):

        @pl.when(has_giver)
        def _():
            pl.semaphore_signal(barrier, inc=1, device_id=giver, device_id_type=MESH)

    pl.semaphore_wait(barrier, 3 + jnp.minimum(chip, 1) + jnp.minimum(n_chip - 1 - chip, 1))

    def remote(source, target, send, recv, peer):
        return pltpu.make_async_remote_copy(
            src_ref=source,
            dst_ref=target,
            send_sem=send,
            recv_sem=recv,
            device_id=peer,
            device_id_type=MESH,
        )

    width = up_ref.shape[-1]
    cut = width // 256 * 128
    chains = (
        (up_ref, pair_up, way_up, up_all, pl.ds(0, cut)),
        (up_ref, pair_up, way_up, up_all, pl.ds(cut, width - cut)),
        (attn_ref, pair_attn, way_attn, attn_all, pl.ds(0, attn_ref.shape[-1])),
    )
    gate_width = gate_all.shape[-1]
    offset = both_ref.shape[-1] - gate_width
    spread_columns = (pl.ds(offset, cut), pl.ds(offset + cut, width - cut), chains[2][4])
    numbers = range(len(chains))

    def pair_copy(number, place):
        source, pair, _, _, columns = chains[number]
        return remote(
            source.at[2 * place + 1 - core, :, columns],
            pair.at[place, :, columns],
            pair_send.at[number, place],
            pair_recv.at[number, place],
            near,
        )

    def way_copy(number, direction, step, source):
        _, _, way, _, columns = chains[number]
        return remote(
            source,
            way.at[direction, step - 1, :, columns],
            way_send.at[number, direction, step - 1],
            way_recv.at[number, direction, step - 1],
            beyond[direction],
        )

    def passes(direction, step):
        return chip <= step - 1 if direction == 0 else chip >= n_chip - step

    def bound_for(direction, step):
        place = chip + n_chip - step if direction == 0 else chip - n_chip + step
        return jnp.clip(place, 0, n_chip - 1)

    def side_pair(item, sources, target, columns):
        return [
            remote(
                sources,
                target.at[spot, :, columns],
                side_send.at[item, turn],
                side_recv.at[item, turn],
                peer,
            )
            for turn, peer in enumerate((across, along))
        ]

    def side_pass(item, firsts, target, start, length):
        half = length // 256 * 128
        halves = (pl.ds(start, half), pl.ds(start + half, length - half))
        copies = []
        for turn, (giver, taker) in enumerate(((across, along), (along, across))):
            firsts[turn].wait_recv()
            block = target.at[giver["batch"], :, halves[turn]]
            copies.append(
                remote(block, block, side_send.at[item, 2 + turn], side_recv.at[item, 2 + turn], taker)
            )
            copies[-1].start()
        return copies

    for number in numbers:
        for place in range(n_chip):
            pair_copy(number, place).start()
    early = (
        (both_ref.at[:, pl.ds(0, gate_width)], gate_all),
        (both_ref.at[:, pl.ds(gate_width, offset)], up_all),
    )
    side_firsts = []
    for item, (source, target) in enumerate(early):
        side_firsts.append(side_pair(item, source, target, pl.ds(0, source.shape[-1])))
        for copy in side_firsts[-1]:
            copy.start()
    own = [
        pltpu.make_async_copy(
            source, target.at[spot, :, pl.ds(0, source.shape[-1])], own_sem.at[item]
        )
        for item, (source, target) in enumerate(early)
    ]
    for copy in own:
        copy.start()
    for _, _, way, _, columns in chains:
        for direction in range(2):

            @pl.when(jnp.logical_not(inner[direction]))
            def _():
                way[direction, n_chip - 2, :, columns] = jnp.zeros(
                    (way.shape[2], columns.size), way.dtype
                )

    for number in numbers:
        source, pair, _, _, columns = chains[number]
        for place in range(n_chip):
            pair_copy(number, place).wait_recv()
            pair[place, :, columns] = (
                pair[place, :, columns].astype(F32)
                + source[2 * place + core, :, columns].astype(F32)
            ).astype(BF16)
        for direction in range(2):

            @pl.when(passes(direction, 1))
            def _():
                place = bound_for(direction, 1)
                way_copy(number, direction, 1, pair.at[place, :, columns]).start()

    side_seconds = []
    for step in range(2, n_chip + 1):
        if step <= 3:
            item = step - 2
            source, target = early[item]
            side_seconds += side_pass(item, side_firsts[item], target, 0, source.shape[-1])
        if step == n_chip:
            break
        for number in numbers:
            _, pair, way, _, columns = chains[number]
            for direction in range(2):
                place = bound_for(direction, step)

                @pl.when(passes(direction, step) & inner[direction])
                def _():
                    way_copy(number, direction, step - 1, pair.at[place, :, columns]).wait_recv()
                    way[direction, step - 2, :, columns] = (
                        way[direction, step - 2, :, columns].astype(F32)
                        + pair[place, :, columns].astype(F32)
                    ).astype(BF16)

            for direction in range(2):
                place = bound_for(direction, step)

                @pl.when(passes(direction, step) & inner[direction])
                def _():
                    way_copy(number, direction, step, way.at[direction, step - 2, :, columns]).start()

                @pl.when(passes(direction, step) & jnp.logical_not(inner[direction]))
                def _():
                    way_copy(number, direction, step, pair.at[place, :, columns]).start()

    chain_firsts = []
    for number in numbers:
        _, pair, way, target, columns = chains[number]
        for direction in range(2):

            @pl.when(inner[direction])
            def _():
                way_copy(number, direction, n_chip - 1, pair.at[0, :, columns]).wait_recv()

        spread = spread_columns[number]
        target[spot, :, spread] = (
            pair[chip, :, columns].astype(F32)
            + way[0, n_chip - 2, :, columns].astype(F32)
            + way[1, n_chip - 2, :, columns].astype(F32)
        ).astype(BF16)
        firsts = side_pair(2 + number, target.at[spot, :, spread], target, spread)
        for copy in firsts:
            copy.start()
        chain_firsts.append(firsts)
    for number in numbers:
        target, spread = chains[number][3], spread_columns[number]
        side_seconds += side_pass(
            2 + number, chain_firsts[number], target, spread.start, spread.size
        )
    for copy in own:
        copy.wait()
    for copy in side_seconds:
        copy.wait()
    for firsts in side_firsts + chain_firsts:
        for copy in firsts:
            copy.wait_send()
    for number in numbers:
        _, pair, _, _, columns = chains[number]
        for place in range(n_chip):
            pair_copy(number, place).wait_send()
        for direction in range(2):
            for step in range(1, n_chip):

                @pl.when(passes(direction, step))
                def _():
                    way_copy(number, direction, step, pair.at[0, :, columns]).wait_send()


def tail_round(n_ctx, hidden, both, up, attn):
    n_chip = n_ctx // 2
    dma = pltpu.SemaphoreType.DMA
    vmem = pl.BlockSpec(memory_space=pltpu.VMEM)
    wide = (up.shape[1], hidden)
    shapes = (wide, wide, attn.shape[1:])
    return pl.pallas_call(
        functools.partial(tail_kernel, n_ctx),
        name="tail_round",
        out_shape=[jax.ShapeDtypeStruct((4, *shape), BF16) for shape in shapes],
        in_specs=[vmem] * 3,
        out_specs=[vmem] * 3,
        scratch_shapes=[
            pltpu.VMEM((n_chip, *up.shape[1:]), BF16),
            pltpu.VMEM((n_chip, *attn.shape[1:]), BF16),
            pltpu.VMEM((2, n_chip - 1, *up.shape[1:]), BF16),
            pltpu.VMEM((2, n_chip - 1, *attn.shape[1:]), BF16),
            dma((3, n_chip)),
            dma((3, n_chip)),
            dma((3, 2, n_chip - 1)),
            dma((3, 2, n_chip - 1)),
            dma((5, 4)),
            dma((5, 4)),
            dma((2,)),
        ],
        compiler_params=pltpu.CompilerParams(collective_id=8, has_side_effects=True),
    )(both, up, attn)


def gathered(shard):
    return lax.all_gather(shard, "ctx", axis=0, tiled=True)


def scattered(whole):
    return lax.psum_scatter(whole, "ctx", scatter_dimension=0, tiled=True)


def local(
    n_batch,
    n_ctx,
    block_in,
    positions,
    counts,
    cotangent,
    gain_input,
    w_query,
    w_key,
    w_value,
    gain_query,
    gain_key,
    w_output,
    gain_attn,
    gain_ffn,
    w_gate,
    w_up,
    w_down,
    gain_final,
):
    block_in = block_in[0]
    positions = positions[0]
    cotangent = cotangent[0]
    tok_count, model_width = block_in.shape
    width_shard = w_query.shape[0]
    query_width = w_query.shape[1]
    head_size = w_key.shape[1]
    head_count = query_width // head_size
    hidden_shard = w_down.shape[0]
    piece = hidden_shard // n_batch
    hidden_part = -(-piece * n_ctx // 128) * 128
    padded = hidden_part // n_ctx
    halo_depth = (WINDOW + tok_count - 2) // tok_count
    assert halo_depth == 4
    batch_at = lax.axis_index("batch")
    ctx_at = lax.axis_index("ctx")
    all_tok = n_batch * tok_count

    gains = jnp.concatenate(
        [gain_input, gain_attn, gain_ffn, gain_final, gain_query, gain_key]
    )
    slots_of = query_width + 2 * head_size
    quarter = slots_of // n_batch
    qkv_full, proj_full, gains_all = gather_weights(
        n_batch,
        n_ctx,
        jnp.concatenate([w_query, w_key, w_value], axis=1)
        .reshape(width_shard, n_batch, quarter)
        .transpose(1, 0, 2),
        w_output.reshape(n_batch, -1, model_width),
        gains[None],
    )
    qkv_full = qkv_full.reshape(n_batch, model_width, quarter)
    full_output = proj_full.reshape(query_width, model_width)
    gains_all = gains_all[:, 0].astype(F32)

    def gain_at(start, length):
        return gains_all[:, start : start + length].reshape(1, -1)

    head_shard = gain_query.shape[0]
    full_gain_in = gain_at(0, width_shard)
    full_gain_attn = gain_at(width_shard, width_shard)
    full_gain_ffn = gain_at(2 * width_shard, width_shard)
    full_gain_final = gain_at(3 * width_shard, width_shard)
    full_gain_q = gain_at(4 * width_shard, head_shard)
    full_gain_k = gain_at(4 * width_shard + head_shard, head_shard)

    part_both = gathered(pick_columns(n_batch, n_ctx, piece, padded, w_gate, w_up))
    own_down = lax.dynamic_slice_in_dim(w_down, batch_at * piece, piece, 0)
    part_down = gathered(jnp.pad(own_down, ((0, padded - piece), (0, 0))))

    first_token = ctx_at * tok_count
    token_place = first_token + jnp.arange(tok_count, dtype=jnp.int32)
    valid_mask = (token_place < counts[0]).astype(F32)[:, None]
    resid_in = block_in.astype(F32)
    act_in = normed(resid_in, full_gain_in).astype(BF16)
    qkv_raw = jnp.concatenate([project(act_in, qkv_full[i]) for i in range(n_batch)], axis=1)
    query_raw = qkv_raw[:, :query_width].reshape(tok_count, head_count, head_size)
    key_raw = qkv_raw[:, query_width : query_width + head_size]
    value_low = qkv_raw[:, query_width + head_size :].astype(BF16)
    inv_freq = BASE ** (-jnp.arange(0, head_size, 2, dtype=F32) / head_size)
    angles = positions.astype(F32)[:, None] * inv_freq

    def query_path(raw_query, gain_vec):
        return rotate(normed(raw_query, gain_vec), angles[:, None, :])

    def key_path(raw_key, gain_vec):
        return rotate(normed(raw_key, gain_vec), angles)

    query_rot = query_path(query_raw, full_gain_q).astype(BF16)
    key_rot = key_path(key_raw, full_gain_k).astype(BF16)
    own_pair = jnp.concatenate([key_rot, value_low], axis=-1)
    halo = halo_out(n_ctx, own_pair)
    context = jnp.concatenate([halo.reshape(halo_depth * tok_count, -1), own_pair], axis=0)
    ctx_keys = context[:, :head_size]
    ctx_values = context[:, head_size:]
    key_total = (halo_depth + 1) * tok_count
    distance = (
        jnp.arange(tok_count, dtype=jnp.int32)[:, None]
        + halo_depth * tok_count
        - jnp.arange(key_total, dtype=jnp.int32)[None, :]
    )
    allowed = (distance >= 0) & (distance < WINDOW) & (distance <= positions[:, None])
    score_scale = head_size ** (-0.5)
    raw_scores = jnp.einsum("thd,kd->htk", query_rot, ctx_keys, preferred_element_type=F32)
    scores = jnp.where(allowed[None], raw_scores * score_scale, MASKED)
    exp_scores = jnp.exp(scores - jnp.max(scores, axis=-1, keepdims=True))
    attn_prob = exp_scores / jnp.sum(exp_scores, axis=-1, keepdims=True)
    prob_low = attn_prob.astype(BF16)
    attended = jnp.einsum("htk,kd->thd", prob_low, ctx_values, preferred_element_type=F32)
    attn_low = attended.reshape(tok_count, query_width).astype(BF16)
    attn_proj = project(attn_low, full_output)
    middle = resid_in + normed(attn_proj, full_gain_attn)
    ffn_in = normed(middle, full_gain_ffn).astype(BF16)

    (ffn_in_all,) = square_gather(2, ffn_in)
    ffn_in_all = ffn_in_all.reshape(all_tok, model_width)
    gate_pre, up_pre, mixed_low, mixed_turned = hidden_mix(256, ffn_in_all, part_both)
    mixed_low, act_in_late, attn_late = lax.optimization_barrier((mixed_low, act_in, attn_low))
    act_in_all, attn_all = square_gather(13, act_in_late, attn_late)
    ffn_in_turned = ffn_in_all.T
    mixed_low, act_in_all, attn_all, mixed_turned, ffn_in_turned = lax.optimization_barrier(
        (mixed_low, act_in_all, attn_all, mixed_turned, ffn_in_turned)
    )
    act_in_all = act_in_all.reshape(all_tok, model_width)
    attn_all = attn_all.reshape(all_tok, query_width)
    block_out, grad_ffn_low, grad_gain_final = turn_round(
        mixed_low, part_down, middle, cotangent, valid_mask, full_gain_final
    )

    grad_final = cotangent.astype(F32) * valid_mask
    grad_ffn_low = grad_ffn_low.reshape(all_tok, model_width)
    down_grad = product_low(384, mixed_turned, grad_ffn_low)
    down_grad, grad_ffn_low = lax.optimization_barrier((down_grad, grad_ffn_low))
    grad_w_down = scattered(down_grad)
    grad_gate_low, grad_up_low, back_part = hidden_back(
        256, grad_ffn_low, part_down, gate_pre, up_pre, part_both
    )
    grad_ffn_in, both_grad = sum_back(
        256,
        back_part.reshape(n_batch, tok_count, model_width),
        ffn_in_turned,
        grad_gate_low,
        grad_up_low,
        UP_FIRST,
    )
    grad_w_both = scattered(both_grad)
    _, pull_ffn_norm = jax.vjp(normed, middle, full_gain_ffn)
    grad_middle_part, grad_gain_ffn = pull_ffn_norm(grad_ffn_in)
    grad_middle = grad_final + grad_middle_part
    _, pull_attn_norm = jax.vjp(normed, attn_proj, full_gain_attn)
    grad_attn_proj, grad_gain_attn = pull_attn_norm(grad_middle)

    grad_proj_low = grad_attn_proj.astype(BF16)
    grad_attended = (
        project_back(grad_proj_low, full_output)
        .astype(BF16)
        .reshape(tok_count, head_count, head_size)
    )
    grad_prob = jnp.einsum("thd,kd->htk", grad_attended, ctx_values, preferred_element_type=F32)
    row_delta = jnp.sum(attn_prob * grad_prob, axis=-1, keepdims=True)
    grad_scores = (attn_prob * (grad_prob - row_delta)).astype(BF16)
    grad_queries = (
        jnp.einsum("htk,kd->thd", grad_scores, ctx_keys, preferred_element_type=F32) * score_scale
    )
    grad_ctx_keys = (
        jnp.einsum("htk,thd->kd", grad_scores, query_rot, preferred_element_type=F32) * score_scale
    )
    grad_ctx_values = jnp.einsum("htk,thd->kd", prob_low, grad_attended, preferred_element_type=F32)
    grad_context = jnp.concatenate([grad_ctx_keys, grad_ctx_values], axis=-1)
    halo_rows = halo_depth * tok_count
    returned, down_all, up_grad = halo_back(
        256,
        n_ctx,
        grad_context[:halo_rows].astype(BF16).reshape(halo_depth, tok_count, 2 * head_size),
        grad_w_down,
        ffn_in_turned,
        grad_up_low,
        hidden_part - UP_FIRST,
    )
    own_grad = grad_context[halo_rows:] + returned
    grad_value_low = own_grad[:, head_size:].astype(BF16)
    _, pull_key = jax.vjp(key_path, key_raw, full_gain_k)
    grad_key_raw, grad_gain_key = pull_key(own_grad[:, :head_size])
    _, pull_query = jax.vjp(query_path, query_raw, full_gain_q)
    grad_query_raw, grad_gain_query = pull_query(grad_queries)
    grad_qkv_low = jnp.concatenate(
        [
            grad_query_raw.astype(BF16).reshape(tok_count, query_width),
            grad_key_raw.astype(BF16),
            grad_value_low,
        ],
        axis=1,
    )
    grad_act_in = sum(
        project_back(grad_qkv_low[:, i * quarter : (i + 1) * quarter], qkv_full[i])
        for i in range(n_batch)
    )
    _, pull_input = jax.vjp(normed, resid_in, full_gain_in)
    grad_in_part, grad_gain_input = pull_input(grad_act_in)
    grad_in = (grad_middle + grad_in_part).astype(BF16)

    def column_slots(upstream):
        return upstream.reshape(tok_count, n_batch, -1).transpose(1, 0, 2)

    gain_rows = jnp.concatenate(
        [
            grad.reshape(n_ctx, -1)
            for grad in (
                grad_gain_input,
                grad_gain_attn,
                grad_gain_ffn,
                grad_gain_final,
                grad_gain_query,
                grad_gain_key,
            )
        ],
        axis=1,
    )
    gain_parts, qkv_slots, proj_slots = batch_exchange(
        7,
        n_batch,
        whole=(gain_rows,),
        slots=(column_slots(grad_qkv_low), column_slots(grad_proj_low)),
    )
    proj_rows = w_output.shape[0]
    gain_count = gain_rows.shape[1]
    gain_lines = -(-gain_count // quarter)
    used = width_shard + proj_rows + gain_lines
    lines = -(-used // 16) * 16
    grad_w_output = weight_grad(attn_all, proj_slots.reshape(all_tok, -1)).astype(BF16)
    grad_w_qkv = weight_grad(act_in_all, qkv_slots.reshape(all_tok, -1)).astype(BF16)
    output_part = model_width // n_batch
    gain_sum = jnp.sum(gain_parts, axis=0).astype(BF16)
    packed = jnp.concatenate(
        [
            grad_w_qkv.reshape(n_ctx, width_shard, quarter),
            jnp.pad(
                grad_w_output.reshape(n_ctx, proj_rows, output_part),
                ((0, 0), (0, 0), (0, quarter - output_part)),
            ),
            jnp.pad(gain_sum, ((0, 0), (0, gain_lines * quarter - gain_count))).reshape(
                n_ctx, gain_lines, quarter
            ),
            jnp.zeros((n_ctx, lines - used, quarter), BF16),
        ],
        axis=1,
    )
    gate_all, up_all, attn_grads = tail_round(
        n_ctx,
        hidden_part,
        grad_w_both,
        up_grad.reshape(n_ctx, width_shard, hidden_part - UP_FIRST),
        packed,
    )
    shapes = (
        (width_shard, w_gate.shape[1]),
        (width_shard, w_gate.shape[1]),
        (hidden_shard, model_width),
        (width_shard, query_width),
        (width_shard, head_size),
        (width_shard, head_size),
        (proj_rows, model_width),
        (gain_lines, quarter),
    )
    (
        grad_gate_shard,
        grad_up_shard,
        grad_down_shard,
        grad_query_shard,
        grad_key_shard,
        grad_value_shard,
        grad_output_shard,
        gain_block,
    ) = finish_round(
        n_batch, n_ctx, piece, padded, output_part, gate_all, up_all, down_all, attn_grads, shapes
    )
    gain_mine = gain_block.reshape(-1)

    return (
        block_out[None],
        grad_in[None],
        gain_mine[:width_shard],
        grad_query_shard,
        grad_key_shard,
        grad_value_shard,
        gain_mine[4 * width_shard : 4 * width_shard + head_shard],
        gain_mine[4 * width_shard + head_shard : gain_count],
        grad_output_shard,
        gain_mine[width_shard : 2 * width_shard],
        gain_mine[2 * width_shard : 3 * width_shard],
        grad_gate_shard,
        grad_up_shard,
        grad_down_shard,
        gain_mine[3 * width_shard : 4 * width_shard],
    )


def solution(mesh):
    matrix = P("ctx", None)
    vector = P("ctx")
    tokens = P("batch", "ctx", None)

    def step(*arrays):
        return local(mesh.shape["batch"], mesh.shape["ctx"], *arrays)

    return jax.shard_map(
        step,
        mesh=mesh,
        in_specs=(
            tokens,
            P("batch", "ctx"),
            P("batch"),
            tokens,
            vector,
            matrix,
            matrix,
            matrix,
            vector,
            vector,
            matrix,
            vector,
            vector,
            matrix,
            matrix,
            matrix,
            vector,
        ),
        out_specs=(
            tokens,
            tokens,
            vector,
            matrix,
            matrix,
            matrix,
            vector,
            vector,
            matrix,
            vector,
            vector,
            matrix,
            matrix,
            matrix,
            vector,
        ),
        check_vma=False,
    )
```

```python
import functools

import jax
import jax.numpy as jnp
from jax import lax
from jax.experimental import pallas as pl
from jax.experimental.pallas import tpu as pltpu
from jax.sharding import PartitionSpec as P

WINDOW = 512
UP_FIRST = 256


EPS = 1e-06
BASE = 10000.0
MASKED = -1e30
BF16 = jnp.bfloat16
F32 = jnp.float32
MESH = pl.DeviceIdType.MESH


def normed(vector, gain_vec):
    return vector * lax.rsqrt(jnp.mean(vector * vector, axis=-1, keepdims=True) + EPS) * gain_vec


def rotate(vector, angles):
    half_size = vector.shape[-1] // 2
    cosine = jnp.cos(angles)
    sine_part = jnp.sin(angles)
    first_half = vector[..., :half_size]
    second = vector[..., half_size:]
    return jnp.concatenate(
        [first_half * cosine - second * sine_part, second * cosine + first_half * sine_part],
        axis=-1,
    )


def project(inputs, weight):
    return lax.dot_general(inputs, weight, (((1,), (0,)), ((), ())), preferred_element_type=F32)


def project_back(upstream, weight):
    return lax.dot_general(upstream, weight, (((1,), (1,)), ((), ())), preferred_element_type=F32)


def weight_grad(inputs, upstream):
    return lax.dot_general(inputs, upstream, (((0,), (0,)), ((), ())), preferred_element_type=F32)


def gated_gelu(gate_val, up_val):
    return jax.nn.gelu(gate_val, approximate=True) * up_val


def spread_kernel(
    n_chip,
    gain_ref,
    first_ref,
    second_ref,
    up_ref,
    gain_out,
    first_out,
    second_out,
    sums_ref,
    own_ref,
    taken_ref,
    send_sem,
    recv_sem,
    own_sem,
    pair_send,
    pair_recv,
    load_sem,
):
    me = lax.axis_index("batch")
    place_at = lax.axis_index("ctx")
    core = lax.rem(place_at, 2)
    near = {"ctx": place_at + 1 - 2 * core}
    barrier = pltpu.get_barrier_semaphore()
    for step in range(1, 4):
        pl.semaphore_signal(
            barrier, inc=1, device_id={"batch": lax.rem(me + step, 4)}, device_id_type=MESH
        )
    pl.semaphore_signal(barrier, inc=1, device_id=near, device_id_type=MESH)
    pl.semaphore_wait(barrier, 4)

    def remote(source, target, send, recv, peer):
        copy = pltpu.make_async_remote_copy(
            src_ref=source,
            dst_ref=target,
            send_sem=send,
            recv_sem=recv,
            device_id=peer,
            device_id_type=MESH,
        )
        copy.start()
        return copy

    items = ((gain_ref, gain_out), (first_ref, first_out), (second_ref, second_out))
    copies = []
    for step in range(1, 4):
        peer = lax.rem(me + step, 4)
        for item, (source, target) in enumerate(items):
            block = source.at[peer] if item else source
            copies.append(
                remote(
                    block,
                    target.at[me],
                    send_sem.at[item, step - 1],
                    recv_sem.at[item, step - 1],
                    {"batch": peer},
                )
            )
    pairs = [
        remote(
            up_ref.at[2 * place + 1 - core],
            taken_ref.at[place],
            pair_send.at[place],
            pair_recv.at[place],
            near,
        )
        for place in range(n_chip)
    ]
    own = [
        pltpu.make_async_copy(
            source.at[me] if item else source, target.at[me], own_sem.at[item]
        )
        for item, (source, target) in enumerate(items)
    ]
    own += [
        pltpu.make_async_copy(up_ref.at[2 * place + core], own_ref.at[place], load_sem.at[place])
        for place in range(n_chip)
    ]
    for copy in own:
        copy.start()
    for copy in own:
        copy.wait()
    for place in range(n_chip):
        pairs[place].wait_recv()
        sums_ref[place] = (own_ref[place].astype(F32) + taken_ref[place].astype(F32)).astype(BF16)
    for copy in copies:
        copy.wait()
    for copy in pairs:
        copy.wait_send()


def spread_grads(n_ctx, gains, first, second, up):
    n_chip = n_ctx // 2
    dma = pltpu.SemaphoreType.DMA
    vmem = pl.BlockSpec(memory_space=pltpu.VMEM)
    half = (n_chip, *up.shape[1:])
    return pl.pallas_call(
        functools.partial(spread_kernel, n_chip),
        name="spread_grads",
        out_shape=[
            jax.ShapeDtypeStruct((4, *gains.shape), gains.dtype),
            jax.ShapeDtypeStruct(first.shape, first.dtype),
            jax.ShapeDtypeStruct(second.shape, second.dtype),
            jax.ShapeDtypeStruct(half, up.dtype),
        ],
        in_specs=[vmem, vmem, vmem, pl.BlockSpec(memory_space=pl.ANY)],
        out_specs=[vmem] * 4,
        scratch_shapes=[
            pltpu.VMEM(half, up.dtype),
            pltpu.VMEM(half, up.dtype),
            dma((3, 3)),
            dma((3, 3)),
            dma((3,)),
            dma((n_chip,)),
            dma((n_chip,)),
            dma((n_chip,)),
        ],
        compiler_params=pltpu.CompilerParams(collective_id=7, has_side_effects=True),
    )(gains, first, second, up)


def square_kernel(count, *refs):
    sources, results = refs[:count], refs[count : 2 * count]
    send_sem, recv_sem, own_sem = refs[2 * count :]
    me = lax.axis_index("batch")
    across = me + 1 - 2 * lax.rem(me, 2)
    along = lax.rem(me + 2, 4)
    barrier = pltpu.get_barrier_semaphore()
    for peer in (across, along):
        pl.semaphore_signal(barrier, inc=1, device_id={"batch": peer}, device_id_type=MESH)
    pl.semaphore_wait(barrier, 2)

    def remote(source, target, item, turn, peer):
        copy = pltpu.make_async_remote_copy(
            src_ref=source,
            dst_ref=target,
            send_sem=send_sem.at[item, turn],
            recv_sem=recv_sem.at[item, turn],
            device_id={"batch": peer},
            device_id_type=MESH,
        )
        copy.start()
        return copy

    firsts = [
        [
            remote(sources[item], results[item].at[me], item, turn, peer)
            for turn, peer in enumerate((across, along))
        ]
        for item in range(count)
    ]
    own = [
        pltpu.make_async_copy(sources[item], results[item].at[me], own_sem.at[item])
        for item in range(count)
    ]
    for copy in own:
        copy.start()
    seconds = []
    for item in range(count):
        columns = sources[item].shape[-1]
        cut = columns // 256 * 128
        halves = (pl.ds(0, cut), pl.ds(cut, columns - cut))
        for turn, (giver, taker) in enumerate(((across, along), (along, across))):
            firsts[item][turn].wait_recv()
            block = results[item].at[giver, :, halves[turn]]
            seconds.append(remote(block, block, item, 2 + turn, taker))
    for copy in own:
        copy.wait()
    for copy in seconds:
        copy.wait()
    for pair in firsts:
        for copy in pair:
            copy.wait_send()


def square_gather(collective_id, *arrays):
    count = len(arrays)
    return pl.pallas_call(
        functools.partial(square_kernel, count),
        out_shape=[jax.ShapeDtypeStruct((4, *a.shape), a.dtype) for a in arrays],
        in_specs=[pl.BlockSpec(memory_space=pltpu.VMEM)] * count,
        out_specs=[pl.BlockSpec(memory_space=pltpu.VMEM)] * count,
        scratch_shapes=[
            pltpu.SemaphoreType.DMA((count, 4)),
            pltpu.SemaphoreType.DMA((count, 4)),
            pltpu.SemaphoreType.DMA((count,)),
        ],
        compiler_params=pltpu.CompilerParams(collective_id=collective_id, has_side_effects=True),
    )(*arrays)


def turn_kernel(
    mixed_ref,
    down_ref,
    middle_ref,
    upstream_ref,
    valid_ref,
    gain_ref,
    out_ref,
    grads_ref,
    gain_grad_ref,
    part_ref,
    taken_ref,
    send_sem,
    recv_sem,
    pass_sem,
    take_sem,
):
    me = lax.axis_index("batch")
    across = me + 1 - 2 * lax.rem(me, 2)
    along = lax.rem(me + 2, 4)
    corner = lax.rem(across + 2, 4)
    order = (corner, across, along)
    tok_count = middle_ref.shape[0]
    barrier = pltpu.get_barrier_semaphore()
    for peer in order:
        pl.semaphore_signal(barrier, inc=1, device_id={"batch": peer}, device_id_type=MESH)
    pl.semaphore_wait(barrier, 3)

    columns = grads_ref.shape[-1]
    cut = columns // 256 * 128
    halves = (pl.ds(0, cut), pl.ds(cut, columns - cut))

    def product(place, stretch):
        start = (place // 2) * 2 * tok_count
        rows = pl.ds(pl.multiple_of(start, 2 * tok_count), 2 * tok_count)
        return jnp.dot(mixed_ref[rows, :], down_ref[:, stretch], preferred_element_type=F32)

    copies = [
        pltpu.make_async_remote_copy(
            src_ref=part_ref.at[base + lax.rem(peer, 2), :, stretch],
            dst_ref=taken_ref.at[turn, :, stretch],
            send_sem=send_sem.at[turn, half],
            recv_sem=recv_sem.at[turn, half],
            device_id={"batch": peer},
            device_id_type=MESH,
        )
        for half, stretch in enumerate(halves)
        for turn, (peer, base) in enumerate(((corner, 0), (along, 0), (across, 2)))
    ]

    def multiply(place, base, half):
        both = product(place, halves[half])
        for row in range(2):
            block = both[row * tok_count : (row + 1) * tok_count]
            part_ref[base + row, :, halves[half]] = block.astype(BF16)
        upper = jnp.broadcast_to(lax.rem(me, 2) == 0, (tok_count, both.shape[1]))
        return jnp.where(upper, both[:tok_count], both[tok_count:])

    multiply(along, 0, 0)
    multiply(along, 0, 1)
    copies[0].start()
    copies[1].start()
    own_first = multiply(me, 2, 0)
    copies[3].start()
    copies[4].start()
    own_second = multiply(me, 2, 1)
    copies[2].start()
    total = jnp.concatenate([own_first, own_second], axis=1)
    copies[5].start()
    for turn in range(3):
        copies[turn].wait_recv()
        copies[3 + turn].wait_recv()
        total = total + taken_ref[turn].astype(F32)
    gain = gain_ref[...]
    valid = valid_ref[...]
    scale = lax.rsqrt(jnp.mean(total * total, axis=-1, keepdims=True) + EPS)
    upstream = upstream_ref[...].astype(F32) * valid
    gained = upstream * gain
    back = scale * gained - total * (
        scale * scale * scale * jnp.mean(total * gained, axis=-1, keepdims=True)
    )
    grads_ref[me] = back.astype(BF16)
    unit = total * scale
    out_ref[...] = ((middle_ref[...] + unit * gain) * valid).astype(BF16)
    gain_grad_ref[...] = jnp.sum(upstream * unit, axis=0, keepdims=True)

    def remote(block, turn, peer):
        copy = pltpu.make_async_remote_copy(
            src_ref=block,
            dst_ref=block,
            send_sem=pass_sem.at[turn],
            recv_sem=take_sem.at[turn],
            device_id={"batch": peer},
            device_id_type=MESH,
        )
        copy.start()
        return copy

    firsts = [remote(grads_ref.at[me], turn, peer) for turn, peer in enumerate((across, along))]
    seconds = []
    for turn, (giver, taker) in enumerate(((across, along), (along, across))):
        firsts[turn].wait_recv()
        seconds.append(remote(grads_ref.at[giver, :, halves[turn]], 2 + turn, taker))
    for copy in seconds:
        copy.wait()
    for copy in firsts + copies:
        copy.wait_send()


def turn_round(mixed, down, middle, upstream, valid, gain):
    tok_count, width = middle.shape
    dma = pltpu.SemaphoreType.DMA
    vmem = pl.BlockSpec(memory_space=pltpu.VMEM)
    flops = 2 * mixed.shape[0] * mixed.shape[1] * width
    return pl.pallas_call(
        turn_kernel,
        name="turn_round",
        out_shape=(
            jax.ShapeDtypeStruct((tok_count, width), BF16),
            jax.ShapeDtypeStruct((4, tok_count, width), BF16),
            jax.ShapeDtypeStruct((1, width), F32),
        ),
        in_specs=[vmem] * 6,
        out_specs=[vmem] * 3,
        scratch_shapes=[
            pltpu.VMEM((4, tok_count, width), BF16),
            pltpu.VMEM((3, tok_count, width), BF16),
            dma((3, 2)),
            dma((3, 2)),
            dma((4,)),
            dma((4,)),
        ],
        cost_estimate=pl.CostEstimate(flops=flops, bytes_accessed=8 << 20, transcendentals=0),
        compiler_params=pltpu.CompilerParams(collective_id=3, has_side_effects=True),
    )(mixed, down, middle, upstream, valid, gain)


def product_kernel(left_ref, right_ref, out_ref):
    out_ref[...] = jnp.dot(left_ref[...], right_ref[...], preferred_element_type=F32).astype(BF16)


def product_low(tile, left, right):
    rows, depth = left.shape
    columns = right.shape[1]
    return pl.pallas_call(
        product_kernel,
        grid=(columns // tile,),
        out_shape=jax.ShapeDtypeStruct((rows, columns), BF16),
        in_specs=[
            pl.BlockSpec((rows, depth), lambda i: (0, 0)),
            pl.BlockSpec((depth, tile), lambda i: (0, i)),
        ],
        out_specs=pl.BlockSpec((rows, tile), lambda i: (0, i)),
        cost_estimate=pl.CostEstimate(
            flops=2 * rows * depth * columns, bytes_accessed=8 << 20, transcendentals=0
        ),
    )(left, right)


def mix_kernel(tokens_ref, w_gate_ref, w_up_ref, gate_ref, up_ref, mixed_ref, turned_ref):
    gate = project(tokens_ref[...], w_gate_ref[...])
    up = project(tokens_ref[...], w_up_ref[...])
    gate_ref[...] = gate
    up_ref[...] = up
    mixed = gated_gelu(gate, up)
    mixed_ref[...] = mixed.astype(BF16)
    turned_ref[...] = mixed.T.astype(BF16)


def hidden_mix(tile, tokens, both_weights):
    count, width = tokens.shape
    hidden = both_weights.shape[1] // 2
    steps = hidden // tile
    wide = jax.ShapeDtypeStruct((count, hidden), F32)
    column = pl.BlockSpec((count, tile), lambda i: (0, i))
    return pl.pallas_call(
        mix_kernel,
        name="hidden_mix",
        grid=(steps,),
        out_shape=(
            wide,
            wide,
            jax.ShapeDtypeStruct((count, hidden), BF16),
            jax.ShapeDtypeStruct((hidden, count), BF16),
        ),
        in_specs=[
            pl.BlockSpec((count, width), lambda i: (0, 0)),
            pl.BlockSpec((width, tile), lambda i: (0, i)),
            pl.BlockSpec((width, tile), lambda i: (0, i + steps)),
        ],
        out_specs=[column, column, column, pl.BlockSpec((tile, count), lambda i: (i, 0))],
        cost_estimate=pl.CostEstimate(
            flops=4 * count * hidden * width, bytes_accessed=24 << 20, transcendentals=0
        ),
    )(tokens, both_weights, both_weights)


def back_kernel(
    upstream_ref, down_ref, gate_ref, up_ref, w_gate_ref, w_up_ref, gate_out, up_out, back_ref, total
):
    step = pl.program_id(0)
    grad_mixed = project_back(upstream_ref[...], down_ref[...])
    _, pull_gelu = jax.vjp(gated_gelu, gate_ref[...], up_ref[...])
    grad_gate, grad_up = pull_gelu(grad_mixed)
    grad_gate, grad_up = grad_gate.astype(BF16), grad_up.astype(BF16)
    gate_out[...] = grad_gate
    up_out[...] = grad_up
    part = project_back(grad_gate, w_gate_ref[...]) + project_back(grad_up, w_up_ref[...])

    @pl.when(step == 0)
    def _():
        total[...] = part

    @pl.when(step > 0)
    def _():
        total[...] += part

    @pl.when(step == pl.num_programs(0) - 1)
    def _():
        back_ref[...] = total[...].astype(BF16)


def hidden_back(tile, upstream, down, gate_pre, up_pre, both_weights):
    tokens, width = upstream.shape
    hidden = down.shape[0]
    count = hidden // tile
    low = jax.ShapeDtypeStruct((tokens, hidden), BF16)
    return pl.pallas_call(
        back_kernel,
        name="hidden_back",
        grid=(count,),
        out_shape=(low, low, jax.ShapeDtypeStruct((tokens, width), BF16)),
        in_specs=[
            pl.BlockSpec((tokens, width), lambda i: (0, 0)),
            pl.BlockSpec((tile, width), lambda i: (i, 0)),
            pl.BlockSpec((tokens, tile), lambda i: (0, i)),
            pl.BlockSpec((tokens, tile), lambda i: (0, i)),
            pl.BlockSpec((width, tile), lambda i: (0, i)),
            pl.BlockSpec((width, tile), lambda i: (0, i + count)),
        ],
        out_specs=[
            pl.BlockSpec((tokens, tile), lambda i: (0, i)),
            pl.BlockSpec((tokens, tile), lambda i: (0, i)),
            pl.BlockSpec((tokens, width), lambda i: (0, 0)),
        ],
        scratch_shapes=[pltpu.VMEM((tokens, width), F32)],
        cost_estimate=pl.CostEstimate(
            flops=6 * tokens * hidden * width, bytes_accessed=24 << 20, transcendentals=0
        ),
    )(upstream, down, gate_pre, up_pre, both_weights, both_weights)


def multiply_tiles(tile, first, last, left, right, out, target, sems):
    def step(index, carry):
        columns = pl.ds(pl.multiple_of(index * tile, tile), tile)
        out[:, columns] = jnp.dot(
            left[...], right[:, columns], preferred_element_type=F32
        ).astype(BF16)
        pltpu.make_async_copy(out.at[:, columns], target.at[:, columns], sems.at[index]).start()
        return carry

    lax.fori_loop(first, last, step, 0)


def await_tiles(tile, count, out, target, sems):
    for index in range(count):
        columns = pl.ds(index * tile, tile)
        pltpu.make_async_copy(out.at[:, columns], target.at[:, columns], sems.at[index]).wait()


def sum_back_kernel(
    tile,
    slots_ref,
    left_ref,
    gate_ref,
    up_ref,
    sum_ref,
    both_ref,
    left,
    right,
    both,
    taken_ref,
    send_sem,
    recv_sem,
    load_sem,
    store_sem,
):
    me = lax.axis_index("batch")
    across = me + 1 - 2 * lax.rem(me, 2)
    along = lax.rem(me + 2, 4)
    order = (lax.rem(across + 2, 4), across, along)
    hidden = gate_ref.shape[1]
    width = right.shape[1]
    loads = [
        pltpu.make_async_copy(left_ref, left, load_sem.at[0]),
        pltpu.make_async_copy(gate_ref, right.at[:, pl.ds(0, hidden)], load_sem.at[1]),
        pltpu.make_async_copy(
            up_ref.at[:, pl.ds(0, width - hidden)],
            right.at[:, pl.ds(hidden, width - hidden)],
            load_sem.at[2],
        ),
    ]
    for load in loads:
        load.start()
    barrier = pltpu.get_barrier_semaphore()
    for peer in order:
        pl.semaphore_signal(barrier, inc=1, device_id={"batch": peer}, device_id_type=MESH)
    pl.semaphore_wait(barrier, 3)
    copies = [
        pltpu.make_async_remote_copy(
            src_ref=slots_ref.at[peer],
            dst_ref=taken_ref.at[turn],
            send_sem=send_sem.at[turn],
            recv_sem=recv_sem.at[turn],
            device_id={"batch": peer},
            device_id_type=MESH,
        )
        for turn, peer in enumerate(order)
    ]
    for copy in copies:
        copy.start()
    for load in loads:
        load.wait()
    multiply_tiles(tile, 0, width // tile, left, right, both, both_ref, store_sem)
    total = slots_ref[me].astype(F32)
    for turn in range(3):
        copies[turn].wait_recv()
        total = total + taken_ref[turn].astype(F32)
    sum_ref[...] = total
    for copy in copies:
        copy.wait_send()
    await_tiles(tile, width // tile, both, both_ref, store_sem)


def sum_back(tile, slots, left, gate, up, columns):
    rows, depth = left.shape
    width = gate.shape[1] + columns
    dma = pltpu.SemaphoreType.DMA
    vmem = pl.BlockSpec(memory_space=pltpu.VMEM)
    anywhere = pl.BlockSpec(memory_space=pl.ANY)
    return pl.pallas_call(
        functools.partial(sum_back_kernel, tile),
        name="sum_back",
        out_shape=[
            jax.ShapeDtypeStruct(slots.shape[1:], F32),
            jax.ShapeDtypeStruct((rows, width), BF16),
        ],
        in_specs=[vmem, anywhere, anywhere, anywhere],
        out_specs=[vmem, anywhere],
        scratch_shapes=[
            pltpu.VMEM((rows, depth), BF16),
            pltpu.VMEM((depth, width), BF16),
            pltpu.VMEM((rows, width), BF16),
            pltpu.VMEM((3, *slots.shape[1:]), BF16),
            dma((3,)),
            dma((3,)),
            dma((3,)),
            dma((width // tile,)),
        ],
        cost_estimate=pl.CostEstimate(
            flops=2 * rows * depth * width, bytes_accessed=12 << 20, transcendentals=0
        ),
        compiler_params=pltpu.CompilerParams(collective_id=5, has_side_effects=True),
    )(slots, left, gate, up)


def halo_out_kernel(n_chip, source_ref, result_ref, send_sem, recv_sem):
    me = lax.axis_index("ctx")
    chip, core = me // 2, lax.rem(me, 2)
    near = {"ctx": me + 1 - 2 * core}
    after = {"ctx": jnp.minimum(me + 2, 2 * n_chip - 1)}
    has_after = chip < n_chip - 1
    barrier = pltpu.get_barrier_semaphore()
    pl.semaphore_signal(barrier, inc=1, device_id=near, device_id_type=MESH)

    @pl.when(chip > 0)
    def _():
        before = {"ctx": jnp.maximum(me - 2, 0)}
        pl.semaphore_signal(barrier, inc=1, device_id=before, device_id_type=MESH)

    pl.semaphore_wait(barrier, 1 + jnp.minimum(n_chip - 1 - chip, 1))

    def remote(source, slot, turn, peer):
        return pltpu.make_async_remote_copy(
            src_ref=source,
            dst_ref=result_ref.at[slot],
            send_sem=send_sem.at[turn],
            recv_sem=recv_sem.at[turn],
            device_id=peer,
            device_id_type=MESH,
        )

    one_on = remote(source_ref, 2, 0, after)
    two_on = remote(result_ref.at[2], 0, 1, after)
    own_near = remote(source_ref, 3, 2, near)
    before_near = remote(result_ref.at[2], 3 - 2 * (1 - core), 3, near)
    far_near = remote(result_ref.at[0], 1, 4, near)

    @pl.when(has_after)
    def _():
        one_on.start()

    @pl.when(core == 0)
    def _():
        own_near.start()

    def blank(slot):
        result_ref[slot] = jnp.zeros(result_ref.shape[1:], result_ref.dtype)

    @pl.when(chip == 0)
    def _():
        blank(2)
        blank(0)
        blank(1)

    @pl.when((chip == 0) & (core == 0))
    def _():
        blank(3)

    @pl.when(chip == 1)
    def _():
        blank(0)

    @pl.when((chip == 1) & (core == 0))
    def _():
        blank(1)

    @pl.when(chip > 0)
    def _():
        one_on.wait_recv()

    @pl.when((chip > 0) & has_after)
    def _():
        two_on.start()

    @pl.when(chip > 0)
    def _():
        before_near.start()

    @pl.when(chip > 1)
    def _():
        two_on.wait_recv()

    @pl.when((chip > 1) & (core == 1))
    def _():
        far_near.start()

    @pl.when(core == 1)
    def _():
        own_near.wait_recv()

    @pl.when(core == 0)
    def _():
        own_near.wait_send()

    @pl.when(chip > 0)
    def _():
        before_near.wait()

    @pl.when((chip > 1) & (core == 0))
    def _():
        far_near.wait_recv()

    @pl.when((chip > 1) & (core == 1))
    def _():
        far_near.wait_send()

    @pl.when(has_after)
    def _():
        one_on.wait_send()

    @pl.when((chip > 0) & has_after)
    def _():
        two_on.wait_send()


def halo_back_kernel(
    tile,
    n_chip,
    source_ref,
    shard_ref,
    left_ref,
    up_ref,
    result_ref,
    shards_ref,
    rest_ref,
    near_ref,
    far_ref,
    way_ref,
    left,
    right,
    rest,
    send_sem,
    recv_sem,
    pass_sem,
    take_sem,
    own_sem,
    store_sem,
):
    me = lax.axis_index("ctx")
    spot = lax.axis_index("batch")
    across = spot + 1 - 2 * lax.rem(spot, 2)
    along = lax.rem(spot + 2, 4)
    chip, core = me // 2, lax.rem(me, 2)
    near = {"ctx": me + 1 - 2 * core}
    before = {"ctx": jnp.maximum(me - 2, 0)}
    has_after = chip < n_chip - 1
    barrier = pltpu.get_barrier_semaphore()
    pl.semaphore_signal(barrier, inc=1, device_id=near, device_id_type=MESH)

    @pl.when(has_after)
    def _():
        after = {"ctx": jnp.minimum(me + 2, 2 * n_chip - 1)}
        pl.semaphore_signal(barrier, inc=1, device_id=after, device_id_type=MESH)

    for peer in (across, along):
        pl.semaphore_signal(barrier, inc=1, device_id={"batch": peer}, device_id_type=MESH)
    pl.semaphore_wait(barrier, 3 + jnp.minimum(chip, 1))

    def beside(source, target, turn, peer):
        copy = pltpu.make_async_remote_copy(
            src_ref=source,
            dst_ref=target,
            send_sem=pass_sem.at[turn],
            recv_sem=take_sem.at[turn],
            device_id={"batch": peer},
            device_id_type=MESH,
        )
        copy.start()
        return copy

    def remote(source, target, turn, peer):
        return pltpu.make_async_remote_copy(
            src_ref=source,
            dst_ref=target,
            send_sem=send_sem.at[turn],
            recv_sem=recv_sem.at[turn],
            device_id=peer,
            device_id_type=MESH,
        )

    to_before = remote(source_ref.at[3 - 2 * core], near_ref.at[0], 0, near)
    to_other = remote(source_ref.at[1 + 2 * core], near_ref.at[1], 1, near)
    to_before.start()
    to_other.start()
    width = right.shape[1]
    count = width // tile
    loads = [
        pltpu.make_async_copy(left_ref, left, own_sem.at[1]),
        pltpu.make_async_copy(
            up_ref.at[:, pl.ds(up_ref.shape[1] - width, width)], right, own_sem.at[2]
        ),
    ]
    for load in loads:
        load.start()
    firsts = [
        beside(shard_ref, shards_ref.at[spot], turn, peer)
        for turn, peer in enumerate((across, along))
    ]
    own = pltpu.make_async_copy(shard_ref, shards_ref.at[spot], own_sem.at[0])
    own.start()

    @pl.when((chip == 0) | jnp.logical_not(has_after))
    def _():
        way_ref[0] = jnp.zeros(way_ref.shape[1:], way_ref.dtype)

    @pl.when(jnp.logical_not(has_after))
    def _():
        way_ref[1] = jnp.zeros(way_ref.shape[1:], way_ref.dtype)

    to_other.wait_recv()
    theirs = near_ref[1].astype(F32)
    far_ref[0] = (source_ref[0].astype(F32) + jnp.where(core == 1, theirs, 0.0)).astype(BF16)
    two_back = remote(far_ref.at[0], way_ref.at[0], 2, before)
    one_back = remote(far_ref.at[1], way_ref.at[1], 3, before)

    @pl.when(chip > 1)
    def _():
        two_back.start()

    to_before.wait_recv()
    due = source_ref[2].astype(F32) + near_ref[0].astype(F32)

    for load in loads:
        load.wait()
    multiply_tiles(tile, 0, count // 3, left, right, rest, rest_ref, store_sem)

    @pl.when((chip > 0) & has_after)
    def _():
        two_back.wait_recv()

    far_ref[1] = (due + way_ref[0].astype(F32)).astype(BF16)

    @pl.when(chip > 0)
    def _():
        one_back.start()

    multiply_tiles(tile, count // 3, count, left, right, rest, rest_ref, store_sem)
    columns = shard_ref.shape[-1]
    cut = columns // 256 * 128
    halves = (pl.ds(0, cut), pl.ds(cut, columns - cut))
    seconds = []
    for turn, (giver, taker) in enumerate(((across, along), (along, across))):
        firsts[turn].wait_recv()
        block = shards_ref.at[giver, :, halves[turn]]
        seconds.append(beside(block, block, 2 + turn, taker))

    @pl.when(has_after)
    def _():
        one_back.wait_recv()

    result_ref[...] = way_ref[1].astype(F32) + jnp.where(core == 0, theirs, 0.0)
    own.wait()
    for copy in seconds:
        copy.wait()
    for copy in firsts + [to_before, to_other]:
        copy.wait_send()
    await_tiles(tile, count, rest, rest_ref, store_sem)

    @pl.when(chip > 1)
    def _():
        two_back.wait_send()

    @pl.when(chip > 0)
    def _():
        one_back.wait_send()


def halo_call(collective_id, kernel, arrays, in_vmem, out_shape, out_vmem, buffers, counts):
    dma = pltpu.SemaphoreType.DMA
    vmem = pl.BlockSpec(memory_space=pltpu.VMEM)
    anywhere = pl.BlockSpec(memory_space=pl.ANY)
    return pl.pallas_call(
        kernel,
        out_shape=out_shape,
        in_specs=[vmem if i < in_vmem else anywhere for i in range(len(arrays))],
        out_specs=[vmem if i < out_vmem else anywhere for i in range(len(out_shape))],
        scratch_shapes=[*buffers, *(dma((count,)) for count in counts)],
        compiler_params=pltpu.CompilerParams(collective_id=collective_id, has_side_effects=True),
    )(*arrays)


def halo_out(n_ctx, block):
    out_shape = [jax.ShapeDtypeStruct((4, *block.shape), block.dtype)]
    kernel = functools.partial(halo_out_kernel, n_ctx // 2)
    return halo_call(1, kernel, (block,), 1, out_shape, 1, (), (5, 5))[0]


def halo_back(tile, n_ctx, blocks, shard, left, up, columns):
    shape = blocks.shape[1:]
    rows, depth = left.shape
    buffers = [pltpu.VMEM((2, *shape), blocks.dtype)] * 3
    buffers += [
        pltpu.VMEM((rows, depth), BF16),
        pltpu.VMEM((depth, columns), BF16),
        pltpu.VMEM((rows, columns), BF16),
    ]
    out_shape = [
        jax.ShapeDtypeStruct(shape, F32),
        jax.ShapeDtypeStruct((4, *shard.shape), shard.dtype),
        jax.ShapeDtypeStruct((rows, columns), BF16),
    ]
    kernel = functools.partial(halo_back_kernel, tile, n_ctx // 2)
    arrays = (blocks, shard, left, up)
    counts = (4, 4, 4, 4, 3, columns // tile)
    return halo_call(6, kernel, arrays, 2, out_shape, 2, buffers, counts)


def pick_kernel(n_batch, n_ctx, piece, padded, gate_ref, up_ref, out_ref):
    me = lax.axis_index("batch")
    out_ref[...] = jnp.zeros_like(out_ref)
    for spot in range(n_batch):

        @pl.when(me == spot)
        def _():
            for shard in range(n_ctx):
                start = (shard * n_batch + spot) * piece
                for half, ref in enumerate((gate_ref, up_ref)):
                    place = (half * n_ctx + shard) * padded
                    out_ref[:, place : place + piece] = ref[:, start : start + piece]


def row_block(rows):
    return 48 if rows % 48 == 0 else rows


def pick_columns(n_batch, n_ctx, piece, padded, w_gate, w_up):
    rows, hidden = w_gate.shape
    block = row_block(rows)
    spec = pl.BlockSpec((block, hidden), lambda i: (i, 0))
    return pl.pallas_call(
        functools.partial(pick_kernel, n_batch, n_ctx, piece, padded),
        name="pick_columns",
        grid=(rows // block,),
        out_shape=jax.ShapeDtypeStruct((rows, 2 * n_ctx * padded), w_gate.dtype),
        in_specs=[spec, spec],
        out_specs=pl.BlockSpec((block, 2 * n_ctx * padded), lambda i: (i, 0)),
    )(w_gate, w_up)


def finish_kernel(n_batch, n_ctx, piece, padded, proj_part, gate_ref, up_ref, down_ref, attn_ref, *refs):
    outs, bufs, sems = refs[:8], refs[8:16], refs[16]
    gate_buf, up_buf, down_buf, query_buf, key_buf, value_buf, proj_buf, gain_buf = bufs
    copies = [pltpu.make_async_copy(bufs[i], outs[i], sems.at[i]) for i in range(8)]
    rows = gate_ref.shape[1]
    block = row_block(rows)

    for ref, buf, copy in ((gate_ref, gate_buf, copies[0]), (up_ref, up_buf, copies[1])):

        def place_rows(step, carry):
            lines = pl.ds(pl.multiple_of(step * block, block), block)
            for shard in range(n_ctx):
                for spot in range(n_batch):
                    start = (shard * n_batch + spot) * piece
                    place = shard * padded
                    buf[lines, start : start + piece] = ref[
                        spot, lines, place : place + piece
                    ].astype(F32)
            return carry

        lax.fori_loop(0, rows // block, place_rows, 0)
        copy.start()
    for spot in range(n_batch):
        down_buf[spot * piece : (spot + 1) * piece, :] = down_ref[spot, :piece, :].astype(F32)
    copies[2].start()
    quarter = attn_ref.shape[-1]
    proj_rows = proj_buf.shape[0]
    for spot in range(n_batch):
        for tile in range(0, quarter, 128):
            column = spot * quarter + tile
            for buf in (query_buf, key_buf, value_buf):
                if 0 <= column < buf.shape[-1]:
                    buf[:, column : column + 128] = attn_ref[
                        spot, :rows, tile : tile + 128
                    ].astype(F32)
                column -= buf.shape[-1]
        proj_buf[:, spot * proj_part : (spot + 1) * proj_part] = attn_ref[
            spot, rows : rows + proj_rows, :proj_part
        ].astype(F32)
    gain_buf[...] = attn_ref[0, rows + proj_rows : rows + proj_rows + gain_buf.shape[0], :].astype(F32)
    for copy in copies[3:]:
        copy.start()
    for copy in copies:
        copy.wait()


def finish_round(n_batch, n_ctx, piece, padded, proj_part, gate, up, down, attn, shapes):
    outs = [jax.ShapeDtypeStruct(shape, F32) for shape in shapes]
    return pl.pallas_call(
        functools.partial(finish_kernel, n_batch, n_ctx, piece, padded, proj_part),
        name="finish_round",
        out_shape=outs,
        in_specs=[pl.BlockSpec(memory_space=pltpu.VMEM)] * 4,
        out_specs=[pl.BlockSpec(memory_space=pl.ANY)] * 8,
        scratch_shapes=[pltpu.VMEM(shape, F32) for shape in shapes] + [pltpu.SemaphoreType.DMA((8,))],
    )(gate, up, down, attn)


def weights_kernel(n_batch, n_ctx, qkv_ref, proj_ref, gain_ref, qkv_all, proj_all, gain_all, *sems):
    send_far, recv_far, send_side, recv_side, send_near, recv_near, own_sem = sems
    spot = lax.axis_index("batch")
    me = lax.axis_index("ctx")
    n_chip = n_ctx // 2
    chip, core = me // 2, lax.rem(me, 2)
    near = {"ctx": me + 1 - 2 * core}
    barrier = pltpu.get_barrier_semaphore()

    def far_at(step):
        return {"ctx": 2 * lax.rem(chip + step, n_chip) + core}

    def side_at(step):
        return {"batch": lax.rem(spot + step, n_batch)}

    peers = [near]
    peers += [far_at(step) for step in range(1, n_chip)]
    peers += [side_at(step) for step in range(1, n_batch)]
    for peer in peers:
        pl.semaphore_signal(barrier, inc=1, device_id=peer, device_id_type=MESH)
    pl.semaphore_wait(barrier, len(peers))

    def remote(source, target, send, recv, peer):
        return pltpu.make_async_remote_copy(
            src_ref=source,
            dst_ref=target,
            send_sem=send,
            recv_sem=recv,
            device_id=peer,
            device_id_type=MESH,
        )

    waits = []
    far = []
    for step in range(1, n_chip):
        triple = [
            remote(source, target, send_far.at[step - 1, item], recv_far.at[step - 1, item], far_at(step))
            for item, (source, target) in enumerate(
                (
                    (qkv_ref.at[spot], qkv_all.at[spot, me]),
                    (proj_ref.at[spot], proj_all.at[me, spot]),
                    (gain_ref, gain_all.at[me]),
                )
            )
        ]
        for copy in triple:
            copy.start()
        far.append(triple)
    own = [
        pltpu.make_async_copy(qkv_ref, qkv_all.at[:, me], own_sem.at[0]),
        pltpu.make_async_copy(proj_ref, proj_all.at[me], own_sem.at[1]),
        pltpu.make_async_copy(gain_ref, gain_all.at[me], own_sem.at[2]),
    ]
    for copy in own:
        copy.start()
    first = n_chip - 1
    pairs = [
        remote(source, target, send_near.at[first, 0, item], recv_near.at[first, 0, item], near)
        for item, (source, target) in enumerate(
            (
                (qkv_ref, qkv_all.at[:, me]),
                (proj_ref, proj_all.at[me]),
                (gain_ref, gain_all.at[me]),
            )
        )
    ]
    for copy in pairs:
        copy.start()
    waits += pairs

    def hand_near(step, turn):
        origin = 2 * lax.rem(chip + n_chip - step, n_chip) + core
        quarter = lax.rem(spot + n_batch - turn, n_batch)
        blocks = [qkv_all.at[quarter, origin], proj_all.at[origin, quarter]]
        blocks += [gain_all.at[origin]] if turn == 0 else []
        for item, block in enumerate(blocks):
            copy = remote(
                block,
                block,
                send_near.at[step - 1, turn, item],
                recv_near.at[step - 1, turn, item],
                near,
            )
            copy.start()
            waits.append(copy)

    side = []
    for step in range(1, n_chip):
        for copy in far[step - 1]:
            copy.wait_recv()
        origin = 2 * lax.rem(chip + n_chip - step, n_chip) + core
        for turn in range(1, n_batch):
            pair = [
                remote(
                    block,
                    block,
                    send_side.at[step - 1, turn - 1, item],
                    recv_side.at[step - 1, turn - 1, item],
                    side_at(turn),
                )
                for item, block in enumerate((qkv_all.at[spot, origin], proj_all.at[origin, spot]))
            ]
            for copy in pair:
                copy.start()
            side.append((step, turn, pair))
        hand_near(step, 0)
    for step, turn, pair in side:
        for copy in pair:
            copy.wait_recv()
        hand_near(step, turn)
    for copy in waits:
        copy.wait()
    for copy in own:
        copy.wait()
    for triple in far:
        for copy in triple:
            copy.wait_send()
    for _, _, pair in side:
        for copy in pair:
            copy.wait_send()


def gather_weights(n_batch, n_ctx, qkv, proj, gains):
    n_chip = n_ctx // 2
    dma = pltpu.SemaphoreType.DMA
    vmem = pl.BlockSpec(memory_space=pltpu.VMEM)
    return pl.pallas_call(
        functools.partial(weights_kernel, n_batch, n_ctx),
        name="gather_weights",
        out_shape=(
            jax.ShapeDtypeStruct((n_batch, n_ctx, *qkv.shape[1:]), qkv.dtype),
            jax.ShapeDtypeStruct((n_ctx, *proj.shape), proj.dtype),
            jax.ShapeDtypeStruct((n_ctx, *gains.shape), gains.dtype),
        ),
        in_specs=[vmem] * 3,
        out_specs=[vmem] * 3,
        scratch_shapes=[
            dma((n_chip - 1, 3)),
            dma((n_chip - 1, 3)),
            dma((n_chip - 1, n_batch - 1, 2)),
            dma((n_chip - 1, n_batch - 1, 2)),
            dma((n_chip, n_batch, 3)),
            dma((n_chip, n_batch, 3)),
            dma((3,)),
        ],
        compiler_params=pltpu.CompilerParams(collective_id=12, has_side_effects=True),
    )(qkv, proj, gains)


def tail_kernel(
    n_ctx,
    both_ref,
    up_ref,
    attn_ref,
    gate_all,
    up_all,
    attn_all,
    pair_attn,
    way_up,
    way_attn,
    pair_send,
    pair_recv,
    way_send,
    way_recv,
    side_send,
    side_recv,
    own_sem,
):
    n_chip = n_ctx // 2
    spot = lax.axis_index("batch")
    me = lax.axis_index("ctx")
    chip, core = me // 2, lax.rem(me, 2)
    across = {"batch": spot + 1 - 2 * lax.rem(spot, 2)}
    along = {"batch": lax.rem(spot + 2, 4)}
    near = {"ctx": me + 1 - 2 * core}
    beyond = ({"ctx": jnp.minimum(me + 2, n_ctx - 1)}, {"ctx": jnp.maximum(me - 2, 0)})
    inner = (chip > 0, chip < n_chip - 1)
    barrier = pltpu.get_barrier_semaphore()
    for peer in (near, across, along):
        pl.semaphore_signal(barrier, inc=1, device_id=peer, device_id_type=MESH)
    for has_giver, giver in zip(inner, (beyond[1], beyond[0])):

        @pl.when(has_giver)
        def _():
            pl.semaphore_signal(barrier, inc=1, device_id=giver, device_id_type=MESH)

    pl.semaphore_wait(barrier, 3 + jnp.minimum(chip, 1) + jnp.minimum(n_chip - 1 - chip, 1))

    def remote(source, target, send, recv, peer):
        return pltpu.make_async_remote_copy(
            src_ref=source,
            dst_ref=target,
            send_sem=send,
            recv_sem=recv,
            device_id=peer,
            device_id_type=MESH,
        )

    width = up_ref.shape[-1]
    cut = width // 256 * 128
    chains = (
        (None, up_ref, way_up, up_all, pl.ds(0, cut)),
        (None, up_ref, way_up, up_all, pl.ds(cut, width - cut)),
        (attn_ref, pair_attn, way_attn, attn_all, pl.ds(0, attn_ref.shape[-1])),
    )
    gate_width = gate_all.shape[-1]
    offset = both_ref.shape[-1] - gate_width
    spread_columns = (pl.ds(offset, cut), pl.ds(offset + cut, width - cut), chains[2][4])
    numbers = range(len(chains))

    def pair_copy(number, place):
        source, pair, _, _, columns = chains[number]
        return remote(
            source.at[2 * place + 1 - core, :, columns],
            pair.at[place, :, columns],
            pair_send.at[place],
            pair_recv.at[place],
            near,
        )

    def way_copy(number, direction, step, source):
        _, _, way, _, columns = chains[number]
        return remote(
            source,
            way.at[direction, step - 1, :, columns],
            way_send.at[number, direction, step - 1],
            way_recv.at[number, direction, step - 1],
            beyond[direction],
        )

    def passes(direction, step):
        return chip <= step - 1 if direction == 0 else chip >= n_chip - step

    def bound_for(direction, step):
        place = chip + n_chip - step if direction == 0 else chip - n_chip + step
        return jnp.clip(place, 0, n_chip - 1)

    def side_pair(item, sources, target, columns):
        return [
            remote(
                sources,
                target.at[spot, :, columns],
                side_send.at[item, turn],
                side_recv.at[item, turn],
                peer,
            )
            for turn, peer in enumerate((across, along))
        ]

    def side_pass(item, firsts, target, start, length):
        half = length // 256 * 128
        halves = (pl.ds(start, half), pl.ds(start + half, length - half))
        copies = []
        for turn, (giver, taker) in enumerate(((across, along), (along, across))):
            firsts[turn].wait_recv()
            block = target.at[giver["batch"], :, halves[turn]]
            copies.append(
                remote(block, block, side_send.at[item, 2 + turn], side_recv.at[item, 2 + turn], taker)
            )
            copies[-1].start()
        return copies

    for place in range(n_chip):
        pair_copy(2, place).start()
    early = (
        (both_ref.at[:, pl.ds(0, gate_width)], gate_all),
        (both_ref.at[:, pl.ds(gate_width, offset)], up_all),
    )
    side_firsts = []
    for item, (source, target) in enumerate(early):
        side_firsts.append(side_pair(item, source, target, pl.ds(0, source.shape[-1])))
        for copy in side_firsts[-1]:
            copy.start()
    own = [
        pltpu.make_async_copy(
            source, target.at[spot, :, pl.ds(0, source.shape[-1])], own_sem.at[item]
        )
        for item, (source, target) in enumerate(early)
    ]
    for copy in own:
        copy.start()
    for _, _, way, _, columns in chains:
        for direction in range(2):

            @pl.when(jnp.logical_not(inner[direction]))
            def _():
                way[direction, n_chip - 2, :, columns] = jnp.zeros(
                    (way.shape[2], columns.size), way.dtype
                )

    for number in numbers:
        source, pair, _, _, columns = chains[number]
        for place in range(n_chip if source is not None else 0):
            pair_copy(number, place).wait_recv()
            pair[place, :, columns] = (
                pair[place, :, columns].astype(F32)
                + source[2 * place + core, :, columns].astype(F32)
            ).astype(BF16)
        for direction in range(2):

            @pl.when(passes(direction, 1))
            def _():
                place = bound_for(direction, 1)
                way_copy(number, direction, 1, pair.at[place, :, columns]).start()

    side_seconds = []
    for step in range(2, n_chip + 1):
        if step <= 3:
            item = step - 2
            source, target = early[item]
            side_seconds += side_pass(item, side_firsts[item], target, 0, source.shape[-1])
        if step == n_chip:
            break
        for number in numbers:
            _, pair, way, _, columns = chains[number]
            for direction in range(2):
                place = bound_for(direction, step)

                @pl.when(passes(direction, step) & inner[direction])
                def _():
                    way_copy(number, direction, step - 1, pair.at[place, :, columns]).wait_recv()
                    way[direction, step - 2, :, columns] = (
                        way[direction, step - 2, :, columns].astype(F32)
                        + pair[place, :, columns].astype(F32)
                    ).astype(BF16)

            for direction in range(2):
                place = bound_for(direction, step)

                @pl.when(passes(direction, step) & inner[direction])
                def _():
                    way_copy(number, direction, step, way.at[direction, step - 2, :, columns]).start()

                @pl.when(passes(direction, step) & jnp.logical_not(inner[direction]))
                def _():
                    way_copy(number, direction, step, pair.at[place, :, columns]).start()

    chain_firsts = []
    for number in numbers:
        _, pair, way, target, columns = chains[number]
        for direction in range(2):

            @pl.when(inner[direction])
            def _():
                way_copy(number, direction, n_chip - 1, pair.at[0, :, columns]).wait_recv()

        spread = spread_columns[number]
        target[spot, :, spread] = (
            pair[chip, :, columns].astype(F32)
            + way[0, n_chip - 2, :, columns].astype(F32)
            + way[1, n_chip - 2, :, columns].astype(F32)
        ).astype(BF16)
        firsts = side_pair(2 + number, target.at[spot, :, spread], target, spread)
        for copy in firsts:
            copy.start()
        chain_firsts.append(firsts)
    for number in numbers:
        target, spread = chains[number][3], spread_columns[number]
        side_seconds += side_pass(
            2 + number, chain_firsts[number], target, spread.start, spread.size
        )
    for copy in own:
        copy.wait()
    for copy in side_seconds:
        copy.wait()
    for firsts in side_firsts + chain_firsts:
        for copy in firsts:
            copy.wait_send()
    for number in numbers:
        source, pair, _, _, columns = chains[number]
        for place in range(n_chip if source is not None else 0):
            pair_copy(number, place).wait_send()
        for direction in range(2):
            for step in range(1, n_chip):

                @pl.when(passes(direction, step))
                def _():
                    way_copy(number, direction, step, pair.at[0, :, columns]).wait_send()


def tail_round(n_ctx, hidden, both, up, attn):
    n_chip = n_ctx // 2
    dma = pltpu.SemaphoreType.DMA
    vmem = pl.BlockSpec(memory_space=pltpu.VMEM)
    wide = (up.shape[1], hidden)
    shapes = (wide, wide, attn.shape[1:])
    return pl.pallas_call(
        functools.partial(tail_kernel, n_ctx),
        name="tail_round",
        out_shape=[jax.ShapeDtypeStruct((4, *shape), BF16) for shape in shapes],
        in_specs=[vmem] * 3,
        out_specs=[vmem] * 3,
        scratch_shapes=[
            pltpu.VMEM((n_chip, *attn.shape[1:]), BF16),
            pltpu.VMEM((2, n_chip - 1, *up.shape[1:]), BF16),
            pltpu.VMEM((2, n_chip - 1, *attn.shape[1:]), BF16),
            dma((n_chip,)),
            dma((n_chip,)),
            dma((3, 2, n_chip - 1)),
            dma((3, 2, n_chip - 1)),
            dma((5, 4)),
            dma((5, 4)),
            dma((2,)),
        ],
        compiler_params=pltpu.CompilerParams(collective_id=8, has_side_effects=True),
    )(both, up, attn)


def gathered(shard):
    return lax.all_gather(shard, "ctx", axis=0, tiled=True)


def scattered(whole):
    return lax.psum_scatter(whole, "ctx", scatter_dimension=0, tiled=True)


def local(
    n_batch,
    n_ctx,
    block_in,
    positions,
    counts,
    cotangent,
    gain_input,
    w_query,
    w_key,
    w_value,
    gain_query,
    gain_key,
    w_output,
    gain_attn,
    gain_ffn,
    w_gate,
    w_up,
    w_down,
    gain_final,
):
    block_in = block_in[0]
    positions = positions[0]
    cotangent = cotangent[0]
    tok_count, model_width = block_in.shape
    width_shard = w_query.shape[0]
    query_width = w_query.shape[1]
    head_size = w_key.shape[1]
    head_count = query_width // head_size
    hidden_shard = w_down.shape[0]
    piece = hidden_shard // n_batch
    hidden_part = -(-piece * n_ctx // 128) * 128
    padded = hidden_part // n_ctx
    halo_depth = (WINDOW + tok_count - 2) // tok_count
    assert halo_depth == 4
    batch_at = lax.axis_index("batch")
    ctx_at = lax.axis_index("ctx")
    all_tok = n_batch * tok_count

    gains = jnp.concatenate(
        [gain_input, gain_attn, gain_ffn, gain_final, gain_query, gain_key]
    )
    slots_of = query_width + 2 * head_size
    quarter = slots_of // n_batch
    qkv_full, proj_full, gains_all = gather_weights(
        n_batch,
        n_ctx,
        jnp.concatenate([w_query, w_key, w_value], axis=1)
        .reshape(width_shard, n_batch, quarter)
        .transpose(1, 0, 2),
        w_output.reshape(n_batch, -1, model_width),
        gains[None],
    )
    qkv_full = qkv_full.reshape(n_batch, model_width, quarter)
    full_output = proj_full.reshape(query_width, model_width)
    gains_all = gains_all[:, 0].astype(F32)

    def gain_at(start, length):
        return gains_all[:, start : start + length].reshape(1, -1)

    head_shard = gain_query.shape[0]
    full_gain_in = gain_at(0, width_shard)
    full_gain_attn = gain_at(width_shard, width_shard)
    full_gain_ffn = gain_at(2 * width_shard, width_shard)
    full_gain_final = gain_at(3 * width_shard, width_shard)
    full_gain_q = gain_at(4 * width_shard, head_shard)
    full_gain_k = gain_at(4 * width_shard + head_shard, head_shard)

    part_both = gathered(pick_columns(n_batch, n_ctx, piece, padded, w_gate, w_up))
    own_down = lax.dynamic_slice_in_dim(w_down, batch_at * piece, piece, 0)
    part_down = gathered(jnp.pad(own_down, ((0, padded - piece), (0, 0))))

    first_token = ctx_at * tok_count
    token_place = first_token + jnp.arange(tok_count, dtype=jnp.int32)
    valid_mask = (token_place < counts[0]).astype(F32)[:, None]
    resid_in = block_in.astype(F32)
    act_in = normed(resid_in, full_gain_in).astype(BF16)
    qkv_raw = jnp.concatenate([project(act_in, qkv_full[i]) for i in range(n_batch)], axis=1)
    query_raw = qkv_raw[:, :query_width].reshape(tok_count, head_count, head_size)
    key_raw = qkv_raw[:, query_width : query_width + head_size]
    value_low = qkv_raw[:, query_width + head_size :].astype(BF16)
    inv_freq = BASE ** (-jnp.arange(0, head_size, 2, dtype=F32) / head_size)
    angles = positions.astype(F32)[:, None] * inv_freq

    def query_path(raw_query, gain_vec):
        return rotate(normed(raw_query, gain_vec), angles[:, None, :])

    def key_path(raw_key, gain_vec):
        return rotate(normed(raw_key, gain_vec), angles)

    query_rot = query_path(query_raw, full_gain_q).astype(BF16)
    key_rot = key_path(key_raw, full_gain_k).astype(BF16)
    own_pair = jnp.concatenate([key_rot, value_low], axis=-1)
    halo = halo_out(n_ctx, own_pair)
    context = jnp.concatenate([halo.reshape(halo_depth * tok_count, -1), own_pair], axis=0)
    ctx_keys = context[:, :head_size]
    ctx_values = context[:, head_size:]
    key_total = (halo_depth + 1) * tok_count
    distance = (
        jnp.arange(tok_count, dtype=jnp.int32)[:, None]
        + halo_depth * tok_count
        - jnp.arange(key_total, dtype=jnp.int32)[None, :]
    )
    allowed = (distance >= 0) & (distance < WINDOW) & (distance <= positions[:, None])
    score_scale = head_size ** (-0.5)
    raw_scores = jnp.einsum("thd,kd->htk", query_rot, ctx_keys, preferred_element_type=F32)
    scores = jnp.where(allowed[None], raw_scores * score_scale, MASKED)
    exp_scores = jnp.exp(scores - jnp.max(scores, axis=-1, keepdims=True))
    attn_prob = exp_scores / jnp.sum(exp_scores, axis=-1, keepdims=True)
    prob_low = attn_prob.astype(BF16)
    attended = jnp.einsum("htk,kd->thd", prob_low, ctx_values, preferred_element_type=F32)
    attn_low = attended.reshape(tok_count, query_width).astype(BF16)
    attn_proj = project(attn_low, full_output)
    middle = resid_in + normed(attn_proj, full_gain_attn)
    ffn_in = normed(middle, full_gain_ffn).astype(BF16)

    (ffn_in_all,) = square_gather(2, ffn_in)
    ffn_in_all = ffn_in_all.reshape(all_tok, model_width)
    gate_pre, up_pre, mixed_low, mixed_turned = hidden_mix(256, ffn_in_all, part_both)
    mixed_low, act_in_late, attn_late = lax.optimization_barrier((mixed_low, act_in, attn_low))
    act_in_all, attn_all = square_gather(13, act_in_late, attn_late)
    ffn_in_turned = ffn_in_all.T
    mixed_low, act_in_all, attn_all, mixed_turned, ffn_in_turned = lax.optimization_barrier(
        (mixed_low, act_in_all, attn_all, mixed_turned, ffn_in_turned)
    )
    act_in_all = act_in_all.reshape(all_tok, model_width)
    attn_all = attn_all.reshape(all_tok, query_width)
    block_out, grad_ffn_low, grad_gain_final = turn_round(
        mixed_low, part_down, middle, cotangent, valid_mask, full_gain_final
    )

    grad_final = cotangent.astype(F32) * valid_mask
    grad_ffn_low = grad_ffn_low.reshape(all_tok, model_width)
    down_grad = product_low(384, mixed_turned, grad_ffn_low)
    down_grad, grad_ffn_low = lax.optimization_barrier((down_grad, grad_ffn_low))
    grad_w_down = scattered(down_grad)
    grad_gate_low, grad_up_low, back_part = hidden_back(
        256, grad_ffn_low, part_down, gate_pre, up_pre, part_both
    )
    grad_ffn_in, both_grad = sum_back(
        256,
        back_part.reshape(n_batch, tok_count, model_width),
        ffn_in_turned,
        grad_gate_low,
        grad_up_low,
        UP_FIRST,
    )
    grad_w_both = scattered(both_grad)
    _, pull_ffn_norm = jax.vjp(normed, middle, full_gain_ffn)
    grad_middle_part, grad_gain_ffn = pull_ffn_norm(grad_ffn_in)
    grad_middle = grad_final + grad_middle_part
    _, pull_attn_norm = jax.vjp(normed, attn_proj, full_gain_attn)
    grad_attn_proj, grad_gain_attn = pull_attn_norm(grad_middle)

    grad_proj_low = grad_attn_proj.astype(BF16)
    grad_attended = (
        project_back(grad_proj_low, full_output)
        .astype(BF16)
        .reshape(tok_count, head_count, head_size)
    )
    grad_prob = jnp.einsum("thd,kd->htk", grad_attended, ctx_values, preferred_element_type=F32)
    row_delta = jnp.sum(attn_prob * grad_prob, axis=-1, keepdims=True)
    grad_scores = (attn_prob * (grad_prob - row_delta)).astype(BF16)
    grad_queries = (
        jnp.einsum("htk,kd->thd", grad_scores, ctx_keys, preferred_element_type=F32) * score_scale
    )
    grad_ctx_keys = (
        jnp.einsum("htk,thd->kd", grad_scores, query_rot, preferred_element_type=F32) * score_scale
    )
    grad_ctx_values = jnp.einsum("htk,thd->kd", prob_low, grad_attended, preferred_element_type=F32)
    grad_context = jnp.concatenate([grad_ctx_keys, grad_ctx_values], axis=-1)
    halo_rows = halo_depth * tok_count
    returned, down_all, up_grad = halo_back(
        256,
        n_ctx,
        grad_context[:halo_rows].astype(BF16).reshape(halo_depth, tok_count, 2 * head_size),
        grad_w_down,
        ffn_in_turned,
        grad_up_low,
        hidden_part - UP_FIRST,
    )
    own_grad = grad_context[halo_rows:] + returned
    grad_value_low = own_grad[:, head_size:].astype(BF16)
    _, pull_key = jax.vjp(key_path, key_raw, full_gain_k)
    grad_key_raw, grad_gain_key = pull_key(own_grad[:, :head_size])
    _, pull_query = jax.vjp(query_path, query_raw, full_gain_q)
    grad_query_raw, grad_gain_query = pull_query(grad_queries)
    grad_qkv_low = jnp.concatenate(
        [
            grad_query_raw.astype(BF16).reshape(tok_count, query_width),
            grad_key_raw.astype(BF16),
            grad_value_low,
        ],
        axis=1,
    )
    grad_act_in = sum(
        project_back(grad_qkv_low[:, i * quarter : (i + 1) * quarter], qkv_full[i])
        for i in range(n_batch)
    )
    _, pull_input = jax.vjp(normed, resid_in, full_gain_in)
    grad_in_part, grad_gain_input = pull_input(grad_act_in)
    grad_in = (grad_middle + grad_in_part).astype(BF16)

    def column_slots(upstream):
        return upstream.reshape(tok_count, n_batch, -1).transpose(1, 0, 2)

    gain_rows = jnp.concatenate(
        [
            grad.reshape(n_ctx, -1)
            for grad in (
                grad_gain_input,
                grad_gain_attn,
                grad_gain_ffn,
                grad_gain_final,
                grad_gain_query,
                grad_gain_key,
            )
        ],
        axis=1,
    )
    gain_parts, qkv_slots, proj_slots, up_sums = spread_grads(
        n_ctx,
        gain_rows,
        column_slots(grad_qkv_low),
        column_slots(grad_proj_low),
        up_grad.reshape(n_ctx, width_shard, hidden_part - UP_FIRST),
    )
    proj_rows = w_output.shape[0]
    gain_count = gain_rows.shape[1]
    gain_lines = -(-gain_count // quarter)
    used = width_shard + proj_rows + gain_lines
    lines = -(-used // 16) * 16
    grad_w_output = weight_grad(attn_all, proj_slots.reshape(all_tok, -1)).astype(BF16)
    grad_w_qkv = weight_grad(act_in_all, qkv_slots.reshape(all_tok, -1)).astype(BF16)
    output_part = model_width // n_batch
    gain_sum = jnp.sum(gain_parts, axis=0).astype(BF16)
    packed = jnp.concatenate(
        [
            grad_w_qkv.reshape(n_ctx, width_shard, quarter),
            jnp.pad(
                grad_w_output.reshape(n_ctx, proj_rows, output_part),
                ((0, 0), (0, 0), (0, quarter - output_part)),
            ),
            jnp.pad(gain_sum, ((0, 0), (0, gain_lines * quarter - gain_count))).reshape(
                n_ctx, gain_lines, quarter
            ),
            jnp.zeros((n_ctx, lines - used, quarter), BF16),
        ],
        axis=1,
    )
    gate_all, up_all, attn_grads = tail_round(
        n_ctx,
        hidden_part,
        grad_w_both,
        up_sums,
        packed,
    )
    shapes = (
        (width_shard, w_gate.shape[1]),
        (width_shard, w_gate.shape[1]),
        (hidden_shard, model_width),
        (width_shard, query_width),
        (width_shard, head_size),
        (width_shard, head_size),
        (proj_rows, model_width),
        (gain_lines, quarter),
    )
    (
        grad_gate_shard,
        grad_up_shard,
        grad_down_shard,
        grad_query_shard,
        grad_key_shard,
        grad_value_shard,
        grad_output_shard,
        gain_block,
    ) = finish_round(
        n_batch, n_ctx, piece, padded, output_part, gate_all, up_all, down_all, attn_grads, shapes
    )
    gain_mine = gain_block.reshape(-1)

    return (
        block_out[None],
        grad_in[None],
        gain_mine[:width_shard],
        grad_query_shard,
        grad_key_shard,
        grad_value_shard,
        gain_mine[4 * width_shard : 4 * width_shard + head_shard],
        gain_mine[4 * width_shard + head_shard : gain_count],
        grad_output_shard,
        gain_mine[width_shard : 2 * width_shard],
        gain_mine[2 * width_shard : 3 * width_shard],
        grad_gate_shard,
        grad_up_shard,
        grad_down_shard,
        gain_mine[3 * width_shard : 4 * width_shard],
    )


def solution(mesh):
    matrix = P("ctx", None)
    vector = P("ctx")
    tokens = P("batch", "ctx", None)

    def step(*arrays):
        return local(mesh.shape["batch"], mesh.shape["ctx"], *arrays)

    return jax.shard_map(
        step,
        mesh=mesh,
        in_specs=(
            tokens,
            P("batch", "ctx"),
            P("batch"),
            tokens,
            vector,
            matrix,
            matrix,
            matrix,
            vector,
            vector,
            matrix,
            vector,
            vector,
            matrix,
            matrix,
            matrix,
            vector,
        ),
        out_specs=(
            tokens,
            tokens,
            vector,
            matrix,
            matrix,
            matrix,
            vector,
            vector,
            matrix,
            vector,
            vector,
            matrix,
            matrix,
            matrix,
            vector,
        ),
        check_vma=False,
    )
```
